32 devices in a mesh: dp: 4 (over y, x), seq: 4 (over z), fsdp: 2 (over core).
Axes of the slice: x: 2, y: 2, z: 4, core: 2. Of those that a mesh axis runs over, the one named last changes fastest.
Arguments:
- hidden: bfloat16 [8, 2560, 768], P(('dp', 'fsdp'), 'seq'), may hold values from -6 to 6
- teacher_hidden: bfloat16 [8, 2560, 768], P(('dp', 'fsdp'), 'seq'), may hold values from -6 to 6
- segments: int32 [8, 2560], P(('dp', 'fsdp')), may hold values from 0 to 3, as said below
- latent_qkv: float32 [2304, 768], P('fsdp'), may hold values from -0.375 to 0.375
- latent_out: float32 [768, 768], P('fsdp'), may hold values from -1.25 to 1.25
- latent_up: float32 [3072, 768], P('fsdp'), may hold values from -0.21875 to 0.21875
- latent_down: float32 [768, 3072], P('fsdp'), may hold values from -0.109375 to 0.109375
- biases: float32 [4, 768], replicated, may hold values from -2.5 to 2.5
- up_bias: float32 [3072], replicated, may hold values from -2.5 to 2.5
- norm_gains: float32 [2, 768], replicated, may hold values from 0.5 to 1.5
- norm_shifts: float32 [2, 768], replicated, may hold values from -2.5 to 2.5
- teacher_qkv: bfloat16 [2304, 768], P('fsdp'), may hold values from -0.3125 to 0.3125
- teacher_out: bfloat16 [768, 768], P('fsdp'), may hold values from -1.25 to 1.25
- teacher_up: bfloat16 [3072, 768], P('fsdp'), may hold values from -0.21875 to 0.21875
- teacher_down: bfloat16 [768, 3072], P('fsdp'), may hold values from -0.109375 to 0.109375
Outputs:
- student_out: bfloat16 [8, 2560, 768], P(('dp', 'fsdp'), 'seq')
- hidden_grad: bfloat16 [8, 2560, 768], P(('dp', 'fsdp'), 'seq')
- grad_qkv: float32 [2304, 768], P('fsdp')
- grad_out: float32 [768, 768], P('fsdp')
- grad_up: float32 [3072, 768], P('fsdp')
- grad_down: float32 [768, 3072], P('fsdp')
- grad_biases: float32 [4, 768], P(None, 'fsdp')
- grad_up_bias: float32 [3072], P('fsdp')
- grad_gains: float32 [2, 768], P(None, 'fsdp')
- grad_shifts: float32 [2, 768], P(None, 'fsdp')
The draws below stay inside these ranges and needn't reach their ends.
Inputs may be any that keep to these rules, and one draw needn't show every extreme that they name: In every group the first 1024 positions have segment 0 (the prompt). The remaining 1536 positions hold 3 continuations with segments 1 to 3 in order, each of 1 to 1024 positions, one of exactly 1024.
All inputs are finite; a program needn't handle non-finite values.
Results may differ from the reference program's by a relative error of at most 0.012.
The reference program's roundings to bfloat16 on the way count: a program that leaves them out, or rounds other values in their place, can miss the bound.
Values may be sent and summed in bfloat16 or wider, within the bound.
A program may use at most 256 MiB of HBM per device.

```python
import jax
import jax.numpy as jnp
from jax import lax

D = 768
HEADS = 12
HDIM = 64
FF = 3072
PROMPT = 1024
CONTS = 3
CONT_MOST = 1024
CONT_TOK = 1536
BLOCK = 512
GROUPS = 8
TOK_UNIT = 2560


def draw_segments(key, part):
    leftover = CONT_TOK - CONT_MOST

    def one_group(group_key):
        key_long, key_cut = jax.random.split(group_key)
        longest = jax.random.randint(key_long, (), 0, CONTS)
        cut_points = jnp.sort(jax.random.permutation(key_cut, leftover - 1)[:CONTS - 2] + 1).astype(jnp.int32)
        boundary = jnp.concatenate([jnp.zeros((1,), jnp.int32), cut_points, jnp.full((1,), leftover, jnp.int32)])
        others = boundary[1:] - boundary[:-1]
        slot_ids = jnp.arange(CONTS, dtype=jnp.int32)
        source = jnp.clip(slot_ids - (slot_ids > longest).astype(jnp.int32), 0, CONTS - 2)
        lengths = jnp.where(slot_ids == longest, CONT_MOST, others[source]).astype(jnp.int32)
        seg_ends = jnp.cumsum(lengths).astype(jnp.int32)
        position = jnp.arange(CONT_TOK, dtype=jnp.int32)
        cont_ids = 1 + jnp.sum((position[:, None] >= seg_ends[None, :CONTS - 1]).astype(jnp.int32), axis=1)
        return jnp.concatenate([jnp.zeros((PROMPT,), jnp.int32), cont_ids.astype(jnp.int32)])
    return jax.vmap(one_group)(jax.random.split(key, GROUPS))


def steps_of(own_key, extent, shards, low, largest):
    gain = 1.0
    for dim, shards_of in shards:
        heights = jax.random.uniform(jax.random.fold_in(jax.random.fold_in(own_key, 6), dim), (shards_of,), jnp.float32, low / len(shards), largest / len(shards))
        gain = gain * jnp.repeat(jnp.exp(heights), extent[dim] // shards_of).reshape((-1,) + (1,) * (len(extent) - 1 - dim))
    return gain


def noise(rng, dims, width, most, cuts=(), kind=jnp.bfloat16):
    gain = steps_of(rng, dims, cuts, -0.22, 0.18) if cuts else 1.0
    values = jax.random.normal(rng, dims, jnp.float32) * width * gain
    return jnp.minimum(jnp.maximum(values, -most), most).astype(kind)


def setup_inputs(seed: int = 0) -> dict:
    splits = jax.random.split(jax.random.key(seed), 16)
    hidden = noise(splits[0], (GROUPS, TOK_UNIT, D), 1.0, 6.0, ((0, 8), (1, 4)))
    teacher_hidden = noise(splits[1], (GROUPS, TOK_UNIT, D), 1.0, 6.0, ((0, 8), (1, 4)))
    segments = draw_segments(jax.random.fold_in(splits[15], 71), 0)
    latent_qkv = noise(splits[3], (3 * D, D), (D // 3) ** -0.5, 0.375, ((0, 2),), jnp.float32)
    latent_out = noise(splits[4], (D, D), (D // 32) ** -0.5, 1.25, ((0, 2),), jnp.float32)
    latent_up = noise(splits[5], (FF, D), D ** -0.5, 0.21875, ((0, 2),), jnp.float32)
    latent_down = noise(splits[6], (D, FF), FF ** -0.5, 0.109375, ((0, 2),), jnp.float32)
    biases = noise(splits[7], (4, D), 0.3, 2.5, (), jnp.float32)
    up_bias = noise(splits[8], (FF,), 0.3, 2.5, (), jnp.float32)
    norm_gains = jnp.clip(1.0 + 0.1 * jax.random.normal(splits[9], (2, D), jnp.float32), 0.5, 1.5)
    norm_shifts = noise(splits[10], (2, D), 0.3, 2.5, (), jnp.float32)
    teacher_qkv = noise(splits[11], (3 * D, D), (D // 2) ** -0.5, 0.3125, ((0, 2),))
    teacher_out = noise(splits[12], (D, D), (D // 32) ** -0.5, 1.25, ((0, 2),))
    teacher_up = noise(splits[13], (FF, D), D ** -0.5, 0.21875, ((0, 2),))
    teacher_down = noise(splits[14], (D, FF), FF ** -0.5, 0.109375, ((0, 2),))
    return dict(hidden=hidden, teacher_hidden=teacher_hidden, segments=segments, latent_qkv=latent_qkv, latent_out=latent_out, latent_up=latent_up, latent_down=latent_down, biases=biases, up_bias=up_bias, norm_gains=norm_gains, norm_shifts=norm_shifts, teacher_qkv=teacher_qkv, teacher_out=teacher_out, teacher_up=teacher_up, teacher_down=teacher_down)


@jax.custom_vjp
def low(v):
    return lax.optimization_barrier(v.astype(jnp.bfloat16)).astype(jnp.float32)

@jax.custom_vjp
def low_back(v):
    return v

def low_keep(v):
    return (low(v), None)

def low_pass(kept, grad):
    return (grad,)

def back_keep(v):
    return (v, None)

def back_low(kept, grad):
    return (low(grad),)
low.defvjp(low_keep, low_pass)
low_back.defvjp(back_keep, back_low)
CLIP = 2.5
EPS = 1e-05
HIGH = lax.Precision.HIGHEST

def matmul_rows(left, weight):
    return jnp.dot(left, weight.T, precision=HIGH, preferred_element_type=jnp.float32)

def norm_rows(values, gain_row, shift_row):
    centre = lax.optimization_barrier(jnp.mean(values, axis=-1, keepdims=True))
    shifted = values - centre
    spread = lax.optimization_barrier(jnp.mean(shifted * shifted, axis=-1, keepdims=True))
    return shifted * lax.rsqrt(spread + EPS) * gain_row + shift_row

def binarize(latent):
    row_scale = lax.optimization_barrier(jnp.mean(jnp.abs(latent), axis=1, keepdims=True))
    return (row_scale * jnp.sign(latent)).astype(jnp.bfloat16).astype(jnp.float32)

def attend(queries, key_set, value_set, segment):
    row_count = queries.shape[0]
    heads_q = queries.reshape(row_count, HEADS, HDIM)
    heads_k = key_set.reshape(row_count, HEADS, HDIM)
    heads_v = value_set.reshape(row_count, HEADS, HDIM)

    def query_block(row_start):
        query_rows = lax.dynamic_slice_in_dim(heads_q, row_start, BLOCK, 0)
        row_seg = lax.dynamic_slice_in_dim(segment, row_start, BLOCK, 0)
        scores = jnp.einsum('qhd,khd->hqk', query_rows, heads_k, precision=HIGH) * 0.125
        scores = low_back(scores)
        allowed = (segment[None, :] == 0) | (segment[None, :] == row_seg[:, None])
        scores = jnp.where(allowed[None], scores, -1e+30)
        row_max = lax.optimization_barrier(jnp.max(scores, axis=-1, keepdims=True))
        exponent = jnp.exp(scores - row_max)
        softmax_w = low(exponent / lax.optimization_barrier(jnp.sum(exponent, axis=-1, keepdims=True)))
        context = jnp.einsum('hqk,khd->qhd', softmax_w, heads_v, precision=HIGH)
        return context.reshape(BLOCK, HEADS * HDIM)
    starts = (jnp.arange(row_count // BLOCK) * BLOCK).astype(jnp.int32)
    return lax.map(jax.checkpoint(query_block), starts).reshape(row_count, HEADS * HDIM)

def block_layer(inputs, segment, weights, vectors, student):
    qkv_w, out_w, up_w, down_w = weights
    qkv_bias, out_bias, bias_up, down_bias, gain_rows, shift_rows = vectors
    if student:
        matmul_in = low(jnp.clip(inputs, -CLIP, CLIP))
    else:
        matmul_in = inputs
    qkv = low_back(low(matmul_rows(matmul_in, qkv_w) + qkv_bias))
    model_width = inputs.shape[1]
    context = attend(qkv[:, :model_width], qkv[:, model_width:2 * model_width], qkv[:, 2 * model_width:], segment)
    context = low_back(low(context))
    attn_out = low_back(matmul_rows(context, out_w) + out_bias)
    middle = norm_rows(inputs + attn_out, gain_rows[0], shift_rows[0])
    if student:
        ffn_in = low(jnp.clip(middle, -CLIP, CLIP))
    else:
        ffn_in = low(middle)
    pre_gelu = low_back(matmul_rows(ffn_in, up_w) + bias_up)
    gelu_act = low(jax.nn.gelu(pre_gelu, approximate=False))
    ffn_out = low_back(matmul_rows(gelu_act, down_w) + down_bias)
    return norm_rows(middle + ffn_out, gain_rows[1], shift_rows[1])

def reference(hidden, teacher_hidden, segments, latent_qkv, latent_out, latent_up, latent_down, biases, up_bias, norm_gains, norm_shifts, teacher_qkv, teacher_out, teacher_up, teacher_down):
    teach_weights = (teacher_qkv.astype(jnp.float32), teacher_out.astype(jnp.float32), teacher_up.astype(jnp.float32), teacher_down.astype(jnp.float32))
    zero_row = jnp.zeros((D,), jnp.float32)
    teach_vectors = (jnp.zeros((3 * D,), jnp.float32), zero_row, jnp.zeros((FF,), jnp.float32), zero_row, jnp.ones((2, D), jnp.float32), jnp.zeros((2, D), jnp.float32))

    def teach_group(group_data):
        return block_layer(group_data[0].astype(jnp.float32), group_data[1], teach_weights, teach_vectors, False)
    teacher_result = lax.map(teach_group, (teacher_hidden, segments))
    binary = (binarize(latent_qkv), binarize(latent_out), binarize(latent_up), binarize(latent_down))

    def student_loss(inputs, weights, bias_rows, bias_up, gain_rows, shift_rows):
        qkv_bias = jnp.concatenate([bias_rows[0], jnp.zeros_like(bias_rows[0]), bias_rows[1]])
        vectors = (qkv_bias, bias_rows[2], bias_up, bias_rows[3], gain_rows, shift_rows)

        def per_group(running, group_data):
            result = block_layer(group_data[0], group_data[1], weights, vectors, True)
            mismatch = result - group_data[2]
            return (running + 0.5 * jnp.sum(mismatch * mismatch), result)
        return lax.scan(jax.checkpoint(per_group), jnp.zeros((), jnp.float32), (inputs, segments, teacher_result))
    distill_loss, pullback, student_result = jax.vjp(student_loss, hidden.astype(jnp.float32), binary, biases, up_bias, norm_gains, norm_shifts, has_aux=True)
    grad_input, grad_weights, grad_bias_rows, grad_bias_up, grad_gain_rows, grad_shift_rows = pullback(jnp.ones_like(distill_loss))
    return (student_result.astype(jnp.bfloat16), grad_input.astype(jnp.bfloat16), grad_weights[0], grad_weights[1], grad_weights[2], grad_weights[3], grad_bias_rows, grad_bias_up, grad_gain_rows, grad_shift_rows)
```

```python
import jax
import jax.numpy as jnp
from jax import lax
from jax.experimental import pallas as pl
from jax.experimental.pallas import tpu as pltpu
from jax.sharding import PartitionSpec as P

HEADS = 12
PROMPT = 1024
LONG = 1024
CLIP = 2.5
EPS = 1e-05
AXES = ("dp", "seq", "fsdp")
BF = jnp.bfloat16
F32 = jnp.float32
LOG2E = 1.4426950408889634
QB = 512
KC = 256
KB = 512
FC = 512
AUG = 16
VMEM_LIMIT = 56 * 2**20


def dot(left, right, left_dim, right_dim):
    return lax.dot_general(
        left, right, (((left_dim,), (right_dim,)), ((), ())), preferred_element_type=F32
    )


def xor(first, second):
    return lax.bitwise_xor(first, jnp.int32(second))


def sizes():
    return tuple(lax.axis_size(name) for name in AXES)


def permute(values, target):
    dp, seq, fsdp = sizes()
    pairs = []
    for d in range(dp):
        for s in range(seq):
            for f in range(fsdp):
                td, ts, tf = target(d, s, f)
                pairs.append(((d * seq + s) * fsdp + f, (td * seq + ts) * fsdp + tf))
    return lax.ppermute(values, AXES, pairs)


def flip(values, dp=0, seq=0, fsdp=0):
    return permute(values, lambda d, s, f: (d ^ dp, s ^ seq, f ^ fsdp))


def swap_groups(values):
    return permute(
        values, lambda d, s, f: (d, 2 * (f % 2) + s % 2, f - f % 2 + s // 2)
    )


def to_slot(values, slot):
    return flip(values, seq=slot & 1, fsdp=slot >> 1)


def bit_list(name):
    count = lax.axis_size(name)
    out, bit = [], 1
    while bit < count:
        out.append((name, bit))
        bit *= 2
    return out


def flip_bit(values, bit):
    return flip(values, **{bit[0]: bit[1]})


def side(bit):
    return lax.bitwise_and(lax.axis_index(bit[0]), bit[1]) != 0


def halve(values, bit):
    upper = side(bit).astype(jnp.int32)
    half = values.shape[0] // 2
    sent = lax.dynamic_slice_in_dim(values, (1 - upper) * half, half, 0)
    kept = lax.dynamic_slice_in_dim(values, upper * half, half, 0)
    got = flip_bit(sent, bit)
    return (kept.astype(F32) + got.astype(F32)).astype(values.dtype)


def double(values, bit):
    got = flip_bit(values, bit)
    return jnp.where(
        side(bit),
        jnp.concatenate([got, values], axis=0),
        jnp.concatenate([values, got], axis=0),
    )


def gather_rows(values):
    for bit in bit_list("fsdp"):
        values = double(values, bit)
    return values


def all_reduce(values, bits):
    for bit in bits:
        values = halve(values, bit)
    for bit in reversed(bits):
        values = double(values, bit)
    return values


def sum_small(values, bits):
    for bit in bits:
        values = values + flip_bit(values, bit)
    return values


def whole(shape):
    return pl.BlockSpec(shape, lambda *_: (0,) * len(shape))


def call(kernel, pref, args, in_specs, outs, out_specs, grid, scratch, flops, trans=0):
    moved = sum(a.size * a.dtype.itemsize for a in args)
    moved += sum(o.size * o.dtype.itemsize for o in jax.tree.leaves(outs))
    return pl.pallas_call(
        kernel,
        grid_spec=pltpu.PrefetchScalarGridSpec(
            num_scalar_prefetch=1,
            grid=grid,
            in_specs=in_specs,
            out_specs=out_specs,
            scratch_shapes=scratch,
        ),
        out_shape=outs,
        compiler_params=pltpu.CompilerParams(vmem_limit_bytes=VMEM_LIMIT),
        cost_estimate=pl.CostEstimate(flops=flops, bytes_accessed=moved, transcendentals=trans),
    )(pref, *args)


def shape_of(shape, dtype):
    return jax.ShapeDtypeStruct(shape, dtype)


def qkv_kernel(student, pref, x0, x1, x2, x3, wq, wk, wv, *rest):
    slot = pl.program_id(0)
    out = rest[-1]
    rows = wq.shape[0]
    for j, ref in enumerate((x0, x1, x2, x3)):

        @pl.when(slot == j)
        def _():
            act = ref[...]
            if student:
                act = jnp.clip(act, -CLIP, CLIP)
            for part, weight in enumerate((wq, wk, wv)):
                value = dot(weight[...], act, 1, 1)
                if student and part != 1:
                    value = value + rest[0][part // 2]
                out[part * rows : (part + 1) * rows, :] = value.astype(BF)


def qkv_project(pref, slots, weight, bias):
    tok, width = slots[0].shape
    rows = weight.shape[0] // 12
    specs = [whole((tok, width))] * 4
    specs += [
        pl.BlockSpec((rows, width), lambda j, i, o=o: (o * 4 + i[0], 0)) for o in range(3)
    ]
    args = list(slots) + [weight] * 3
    if bias is not None:
        specs.append(pl.BlockSpec((2, rows, 1), lambda j, i: (0, i[0], 0)))
        args.append(bias)
    return call(
        lambda *refs: qkv_kernel(bias is not None, *refs),
        pref,
        args,
        specs,
        shape_of((3 * rows, 4 * tok), BF),
        pl.BlockSpec((3 * rows, tok), lambda j, i: (0, lax.bitwise_xor(i[0], j))),
        (4,),
        [],
        2 * 4 * tok * width * 3 * rows,
    )


def roll_cont(values, shift):
    return jnp.concatenate(
        [values[:, :PROMPT], pltpu.roll(values[:, PROMPT:], shift, 1)], axis=1
    )


def block_list(total, rows):
    blocks = [(i, [(0, PROMPT)]) for i in range(0, PROMPT, rows)]
    blocks += [(i, [(0, PROMPT + LONG)]) for i in range(PROMPT, PROMPT + LONG, rows)]
    blocks += [
        (i, [(0, PROMPT), (PROMPT + LONG, total)]) for i in range(PROMPT + LONG, total, rows)
    ]
    return blocks


def same_segment(shape, key_axis, key_start, query_start, border):
    keys = lax.broadcasted_iota(jnp.int32, shape, key_axis) + key_start
    queries = lax.broadcasted_iota(jnp.int32, shape, 1 - key_axis) + query_start
    return (keys < border) == (queries < border)


def attention_kernel(scale, pref, q_ref, k_ref, v_ref, o0, o1, o2, o3, cf_ref, lse_ref, qs, ks, vs, cs, st):
    own, shift, border = pref[0], pref[1], pref[2]
    total = q_ref.shape[1]
    cont = total - PROMPT
    others = PROMPT + LONG
    back = lax.rem(cont - shift, cont)
    qs[...] = roll_cont(q_ref[...].astype(F32), back).astype(BF)
    ks[...] = roll_cont(k_ref[...].astype(F32), back).astype(BF)
    vs[...] = roll_cont(v_ref[...].astype(F32), back).astype(BF)
    blocks = []
    for start, parts in block_list(total, QB):
        chunks = [key for lo, hi in parts for key in range(lo, hi, KC)]
        blocks.append((start, chunks))
    top, acc, norm = {}, {}, {}

    def scores(n, i):
        start, chunks = blocks[n]
        key = chunks[i]
        value = dot(ks[:, key : key + KC], qs[:, start : start + QB], 0, 0) * scale
        if key >= others:
            mask = same_segment((KC, QB), 0, key - others, start - others, border)
            value = jnp.where(mask, value, -1e30)
        st[n % 2, i * KC : (i + 1) * KC, :] = value
        peak = jnp.max(value, axis=0, keepdims=True)
        top[n] = jnp.maximum(top[n], peak) if n in top else peak

    def weigh(n, i):
        key = blocks[n][1][i]
        prob = jnp.exp2(st[n % 2, i * KC : (i + 1) * KC, :] - top[n])
        part = jnp.sum(prob, axis=0, keepdims=True)
        value = dot(vs[:, key : key + KC], prob.astype(BF), 1, 0)
        acc[n] = acc[n] + value if n in acc else value
        norm[n] = norm[n] + part if n in norm else part

    for i in range(len(blocks[0][1])):
        scores(0, i)
    for n, (start, chunks) in enumerate(blocks):
        ahead = len(blocks[n + 1][1]) if n + 1 < len(blocks) else 0
        for i in range(max(len(chunks), ahead)):
            if i < ahead:
                scores(n + 1, i)
            if i < len(chunks):
                weigh(n, i)
        cf_ref[:, start : start + QB] = acc[n] / norm[n]
        lse_ref[:, start : start + QB] = top[n] + jnp.log2(norm[n])
    cs[...] = roll_cont(cf_ref[...], shift).astype(BF)
    tok = total // 4
    for j, out in enumerate((o0, o1, o2, o3)):
        first = pl.multiple_of(xor(own, j) * tok, 128)
        out[...] = cs[:, pl.ds(first, tok)]


def attention(pref, qkv):
    total = qkv.shape[1]
    heads = HEADS // 4
    hdim = qkv.shape[0] // (3 * heads)
    rows = qkv.shape[0] // 3
    scale = LOG2E / hdim**0.5
    return call(
        lambda *refs: attention_kernel(scale, *refs),
        pref,
        [qkv] * 3,
        [pl.BlockSpec((hdim, total), lambda h, i, o=o: (h + o * heads, 0)) for o in range(3)],
        [shape_of((rows, total // 4), BF)] * 4
        + [shape_of((rows, total), F32), shape_of((heads, 1, total), F32)],
        [pl.BlockSpec((hdim, total // 4), lambda h, i: (h, 0))] * 4
        + [
            pl.BlockSpec((hdim, total), lambda h, i: (h, 0)),
            pl.BlockSpec((None, 1, total), lambda h, i: (h, 0, 0)),
        ],
        (heads,),
        [pltpu.VMEM((hdim, total), BF)] * 4 + [pltpu.VMEM((2, PROMPT + LONG, QB), F32)],
        16 * 10**9,
        12 * 10**6,
    )


def thirds(values):
    high = values.astype(BF).astype(F32)
    middle = (values - high).astype(BF).astype(F32)
    low = values - high - middle
    row = lax.broadcasted_iota(jnp.int32, (AUG, values.shape[1]), 0)
    value = jnp.where(row == 0, high, jnp.where(row == 1, middle, jnp.where(row == 2, low, 0.0)))
    return value.astype(BF)


def attention_back_kernel(
    scale, pref, q_ref, k_ref, v_ref, g0, g1, g2, g3, cf_ref, lse_ref,
    d0, d1, d2, d3, qa, ka, va, ga, gs, dqs, dks, dvs,
):
    own, shift, border = pref[0], pref[1], pref[2]
    hdim, total = q_ref.shape
    tok = total // 4
    cont = total - PROMPT
    others = PROMPT + LONG
    back = lax.rem(cont - shift, cont)
    for j, ref in enumerate((g0, g1, g2, g3)):
        first = pl.multiple_of(xor(own, j) * tok, 128)
        gs[:, pl.ds(first, tok)] = ref[...].astype(F32)
    qa[:hdim, :] = roll_cont(q_ref[...].astype(F32), back).astype(BF)
    ka[:hdim, :] = roll_cont(k_ref[...].astype(F32), back).astype(BF)
    va[:hdim, :] = roll_cont(v_ref[...].astype(F32), back).astype(BF)
    grad = roll_cont(gs[...], back)
    ga[:hdim, :] = grad.astype(BF)
    ga[hdim:, :] = thirds(-jnp.sum(grad * cf_ref[...], axis=0, keepdims=True))
    qa[hdim:, :] = thirds(lse_ref[...] * (-1.0 / scale))
    row = lax.broadcasted_iota(jnp.int32, (AUG, total), 0)
    ones = jnp.where(row < 3, 1.0, 0.0).astype(BF)
    ka[hdim:, :] = ones
    va[hdim:, :] = ones
    seen = set()
    for start, parts in block_list(total, QB):
        queries = slice(start, start + QB)
        grad_q = None
        for lo, hi in parts:
            for key in range(lo, hi, KB):
                keys = slice(key, key + KB)
                value = dot(qa[:, queries], ka[:, keys], 0, 0) * scale
                if lo >= others:
                    mask = same_segment((QB, KB), 1, key - others, start - others, border)
                    value = jnp.where(mask, value, -1e30)
                prob = jnp.exp2(value)
                grad_p = dot(ga[:, queries], va[:, keys], 0, 0)
                grad_s = (prob * grad_p).astype(BF)
                grad_v = dot(ga[:hdim, queries], prob.astype(BF), 1, 0)
                grad_k = dot(qa[:hdim, queries], grad_s, 1, 0)
                part = dot(ka[:hdim, keys], grad_s, 1, 1)
                grad_q = part if grad_q is None else grad_q + part
                if key in seen:
                    dvs[:, keys] += grad_v
                    dks[:, keys] += grad_k
                else:
                    dvs[:, keys] = grad_v
                    dks[:, keys] = grad_k
                    seen.add(key)
        dqs[:, queries] = grad_q
    inv = 1.0 / hdim**0.5
    for part, (ref, factor) in enumerate(((dqs, inv), (dks, inv), (dvs, 1.0))):
        gs[...] = roll_cont(ref[...] * factor, shift)
        for j, out in enumerate((d0, d1, d2, d3)):
            first = pl.multiple_of(xor(own, j) * tok, 128)
            out[part] = gs[:, pl.ds(first, tok)].astype(BF)


def attention_back(pref, qkv, grads, ctx, lse):
    total = qkv.shape[1]
    heads = HEADS // 4
    hdim = qkv.shape[0] // (3 * heads)
    rows = qkv.shape[0] // 3
    scale = LOG2E / hdim**0.5
    quarter = pl.BlockSpec((hdim, total // 4), lambda h, i: (h, 0))
    return call(
        lambda *refs: attention_back_kernel(scale, *refs),
        pref,
        [qkv] * 3 + list(grads) + [ctx, lse],
        [pl.BlockSpec((hdim, total), lambda h, i, o=o: (h + o * heads, 0)) for o in range(3)]
        + [quarter] * 4
        + [
            pl.BlockSpec((hdim, total), lambda h, i: (h, 0)),
            pl.BlockSpec((None, 1, total), lambda h, i: (h, 0, 0)),
        ],
        [shape_of((3, rows, total // 4), BF)] * 4,
        [pl.BlockSpec((3, hdim, total // 4), lambda h, i: (0, h, 0))] * 4,
        (heads,),
        [pltpu.VMEM((hdim + AUG, total), BF)] * 4 + [pltpu.VMEM((hdim, total), F32)] * 4,
        30 * 10**9,
        12 * 10**6,
    )


def normalize(values):
    centre = jnp.mean(values, axis=-1, keepdims=True)
    shifted = values - centre
    spread = jnp.mean(shifted * shifted, axis=-1, keepdims=True)
    inv = lax.rsqrt(spread + EPS)
    return shifted * inv, inv


def normalize_back(grad, normed, inv):
    first = jnp.mean(grad, axis=-1, keepdims=True)
    second = jnp.mean(grad * normed, axis=-1, keepdims=True)
    return (grad - first - normed * second) * inv


def total_rows(values):
    return jnp.sum(values, axis=0, keepdims=True)


def gather_ctx(own, pieces, ctx):
    rows = pieces[0].shape[0]
    for j, ref in enumerate(pieces):
        first = pl.multiple_of(xor(own, j) * rows, 64)
        ctx[pl.ds(first, rows), :] = ref[...]


def student_kernel(
    pref, c0, c1, c2, c3, x, w_out, w_up, w_down, b_out, b_up, b_down, gain, shift,
    ctx, act_one, normed_one, inv_one, gelu, slope, result, normed_two, inv_two,
    acc, mid,
):
    step = pl.program_id(0)

    @pl.when(step == 0)
    def _():
        gather_ctx(pref[0], (c0, c1, c2, c3), ctx)
        res = x[...].astype(F32) + (dot(ctx[...], w_out[...], 0, 1) + b_out[...])
        normed, inv = normalize(res)
        normed_one[...] = normed
        inv_one[...] = inv
        middle = normed * gain[0:1] + shift[0:1]
        mid[...] = middle
        act_one[...] = jnp.clip(middle, -CLIP, CLIP).astype(BF)
        acc[...] = jnp.zeros_like(acc)

    pre = dot(act_one[...], w_up[...], 1, 1) + b_up[...]
    cdf = 0.5 * (1.0 + lax.erf(pre * 0.5**0.5))
    act = (pre * cdf).astype(BF)
    gelu[...] = act
    slope[...] = (cdf + pre * (jnp.exp(pre * pre * -0.5) * 0.3989422804014327)).astype(BF)
    acc[...] += dot(act, w_down[...], 1, 1)

    @pl.when(step == pl.num_programs(0) - 1)
    def _():
        normed, inv = normalize(mid[...] + (acc[...] + b_down[...]))
        normed_two[...] = normed
        inv_two[...] = inv
        result[...] = (normed * gain[1:2] + shift[1:2]).astype(BF)


def ffn_specs(tok, width, hidden):
    up = pl.BlockSpec((FC, width), lambda c, i: (c, 0))
    down = pl.BlockSpec((width, FC), lambda c, i: (0, c))
    wide = pl.BlockSpec((tok, FC), lambda c, i: (0, c))
    row = pl.BlockSpec((1, FC), lambda c, i: (0, c))
    return up, down, wide, row


def student_ffn(pref, pieces, x, w_out, w_up, w_down, b_out, b_up, b_down, gain, shift):
    tok, width = x.shape
    hidden = w_up.shape[0]
    up, down, wide, row = ffn_specs(tok, width, hidden)
    full, one = whole((tok, width)), whole((tok, 1))
    return call(
        student_kernel,
        pref,
        list(pieces) + [x, w_out, w_up, w_down, b_out, b_up, b_down, gain, shift],
        [whole(pieces[0].shape)] * 4
        + [full, whole(w_out.shape), up, down, whole((1, width)), row, whole((1, width))]
        + [whole((2, width))] * 2,
        [
            shape_of((width, tok), BF),
            shape_of((tok, width), BF),
            shape_of((tok, width), F32),
            shape_of((tok, 1), F32),
            shape_of((tok, hidden), BF),
            shape_of((tok, hidden), BF),
            shape_of((tok, width), BF),
            shape_of((tok, width), F32),
            shape_of((tok, 1), F32),
        ],
        [whole((width, tok)), full, full, one, wide, wide, full, full, one],
        (hidden // FC,),
        [pltpu.VMEM((tok, width), F32)] * 2,
        2 * tok * width * (2 * hidden + width),
        2 * tok * hidden,
    )


def teacher_kernel(
    pref, c0, c1, c2, c3, x, w_out, w_up, w_down, gain, shift, normed_two, inv_two,
    grad_sum, grad_ffn, vectors,
    ctx, acc, mid, act_one,
):
    step = pl.program_id(0)

    @pl.when(step == 0)
    def _():
        gather_ctx(pref[0], (c0, c1, c2, c3), ctx)
        res = x[...].astype(F32) + dot(ctx[...], w_out[...], 0, 1)
        normed, inv = normalize(res)
        mid[...] = normed
        act_one[...] = normed.astype(BF)
        acc[...] = jnp.zeros_like(acc)

    pre = dot(act_one[...], w_up[...], 1, 1)
    act = (pre * (0.5 * (1.0 + lax.erf(pre * 0.5**0.5)))).astype(BF)
    acc[...] += dot(act, w_down[...], 1, 1)

    @pl.when(step == pl.num_programs(0) - 1)
    def _():
        target, _unused = normalize(mid[...] + acc[...])
        normed = normed_two[...]
        diff = normed * gain[1:2] + shift[1:2] - target
        back = normalize_back(diff * gain[1:2], normed, inv_two[...])
        grad_sum[...] = back
        low = back.astype(BF)
        grad_ffn[...] = low
        vectors[0:1] = total_rows(diff * normed)
        vectors[1:2] = total_rows(diff)
        vectors[2:3] = total_rows(low.astype(F32))


def teacher_ffn(pref, pieces, x, w_out, w_up, w_down, gain, shift, normed_two, inv_two):
    tok, width = x.shape
    hidden = w_up.shape[0]
    up, down, wide, row = ffn_specs(tok, width, hidden)
    full, one = whole((tok, width)), whole((tok, 1))
    return call(
        teacher_kernel,
        pref,
        list(pieces) + [x, w_out, w_up, w_down, gain, shift, normed_two, inv_two],
        [whole(pieces[0].shape)] * 4
        + [full, whole(w_out.shape), up, down]
        + [whole((2, width))] * 2
        + [full, one],
        [shape_of((tok, width), F32), shape_of((tok, width), BF), shape_of((3, width), F32)],
        [full, full, whole((3, width))],
        (hidden // FC,),
        [pltpu.VMEM((width, tok), BF)]
        + [pltpu.VMEM((tok, width), F32)] * 2
        + [pltpu.VMEM((tok, width), BF)],
        2 * tok * width * (2 * hidden + width),
        tok * hidden,
    )


def back_kernel(
    pref, grad_ffn, slope, w_up, w_down, grad_sum, normed_one, inv_one, gain, shift, w_out,
    grad_hidden, grad_bias, grad_res, grad_attn, g0, g1, g2, g3, vectors,
    acc, ctx,
):
    step = pl.program_id(0)

    @pl.when(step == 0)
    def _():
        acc[...] = jnp.zeros_like(acc)

    low = (dot(grad_ffn[...], w_down[...], 1, 0) * slope[...].astype(F32)).astype(BF)
    grad_hidden[...] = low
    grad_bias[...] = total_rows(low.astype(F32))
    acc[...] += dot(low, w_up[...], 1, 0)

    @pl.when(step == pl.num_programs(0) - 1)
    def _():
        normed = normed_one[...]
        middle = normed * gain[0:1] + shift[0:1]
        grad = grad_sum[...] + jnp.where(jnp.abs(middle) < CLIP, acc[...], 0.0)
        back = normalize_back(grad * gain[0:1], normed, inv_one[...])
        grad_res[...] = back
        attn = back.astype(BF)
        grad_attn[...] = attn
        vectors[0:1] = total_rows(grad * normed)
        vectors[1:2] = total_rows(grad)
        vectors[2:3] = total_rows(attn.astype(F32))
        ctx[...] = dot(w_out[...], attn, 0, 1).astype(BF)
        rows = g0.shape[0]
        for j, ref in enumerate((g0, g1, g2, g3)):
            first = pl.multiple_of(xor(pref[0], j) * rows, 64)
            ref[...] = ctx[pl.ds(first, rows), :]


def student_back(pref, grad_ffn, slope, w_up, w_down, grad_sum, normed_one, inv_one, gain, shift, w_out):
    tok, width = grad_ffn.shape
    hidden = w_up.shape[0]
    up, down, wide, row = ffn_specs(tok, width, hidden)
    full, one = whole((tok, width)), whole((tok, 1))
    return call(
        back_kernel,
        pref,
        [grad_ffn, slope, w_up, w_down, grad_sum, normed_one, inv_one, gain, shift, w_out],
        [full, wide, up, down, full, full, one] + [whole((2, width))] * 2 + [whole(w_out.shape)],
        [
            shape_of((tok, hidden), BF),
            shape_of((1, hidden), F32),
            shape_of((tok, width), F32),
            shape_of((tok, width), BF),
        ]
        + [shape_of((width // 4, tok), BF)] * 4
        + [shape_of((3, width), F32)],
        [wide, row, full, full] + [whole((width // 4, tok))] * 4 + [whole((3, width))],
        (hidden // FC,),
        [pltpu.VMEM((tok, width), F32), pltpu.VMEM((width, tok), BF)],
        2 * tok * width * (2 * hidden + width),
    )


def weight_grad_kernel(
    pref, grad_ffn, gelu, grad_hidden, act_one, grad_attn, ctx, grad_down, grad_up, grad_out
):
    @pl.when(pl.program_id(0) == 0)
    def _():
        grad_out[...] = dot(grad_attn[...], ctx[...], 0, 1).astype(BF)

    grad_down[...] = dot(grad_ffn[...], gelu[...], 0, 0).astype(BF)
    grad_up[...] = dot(grad_hidden[...], act_one[...], 0, 0).astype(BF)


def weight_grads(pref, grad_ffn, gelu, grad_hidden, act_one, grad_attn, ctx):
    tok, width = grad_ffn.shape
    hidden = gelu.shape[1]
    up, down, wide, row = ffn_specs(tok, width, hidden)
    full = whole((tok, width))
    return call(
        weight_grad_kernel,
        pref,
        [grad_ffn, gelu, grad_hidden, act_one, grad_attn, ctx],
        [full, wide, wide, full, full, whole((width, tok))],
        [
            shape_of((width, hidden), BF),
            shape_of((hidden, width), BF),
            shape_of((width, width), BF),
        ],
        [down, up, whole((width, width))],
        (hidden // FC,),
        [],
        2 * tok * width * (2 * hidden + width),
    )


def qkv_grad_kernel(pref, d0, d1, d2, d3, x0, x1, x2, x3, out, sums, acc):
    total = None
    count = None
    for grad, x in zip((d0, d1, d2, d3), (x0, x1, x2, x3)):
        value = grad[...]
        part = dot(value, jnp.clip(x[...], -CLIP, CLIP), 1, 0)
        line = jnp.sum(value.astype(F32), axis=1, keepdims=True)
        total = part if total is None else total + part
        count = line if count is None else count + line
    out[...] = total.astype(BF)
    sums[...] = count


def qkv_grad(pref, grads, slots):
    tok, width = slots[0].shape
    rows = grads[0].shape[1]
    return call(
        qkv_grad_kernel,
        pref,
        list(grads) + list(slots),
        [pl.BlockSpec((None, rows, tok), lambda o, i: (o, 0, 0))] * 4 + [whole((tok, width))] * 4,
        [shape_of((3, rows, width), BF), shape_of((3, rows, 1), F32)],
        [
            pl.BlockSpec((None, rows, width), lambda o, i: (o, 0, 0)),
            pl.BlockSpec((None, rows, 1), lambda o, i: (o, 0, 0)),
        ],
        (3,),
        [pltpu.VMEM((8, 128), F32)],
        2 * 4 * tok * width * 3 * rows,
    )


def input_grad_kernel(pref, e0, e1, e2, e3, wq, wk, wv, grad_res, x, out, acc):
    slot = pl.program_id(0)

    @pl.when(slot == 0)
    def _():
        acc[...] = jnp.zeros_like(acc)

    for j, ref in enumerate((e0, e1, e2, e3)):

        @pl.when(slot == j)
        def _():
            part = dot(ref[0], wq[...], 0, 0)
            part = part + dot(ref[1], wk[...], 0, 0)
            acc[...] += part + dot(ref[2], wv[...], 0, 0)

    @pl.when(slot == 3)
    def _():
        size = jnp.abs(x[...].astype(F32))
        pull = jnp.where(size < CLIP, 1.0, jnp.where(size == CLIP, 0.5, 0.0))
        out[...] = (grad_res[...] + acc[...] * pull).astype(BF)


def input_grad(pref, pieces, weight, grad_res, x):
    tok, width = x.shape
    rows = pieces[0].shape[1]
    full = whole((tok, width))
    return call(
        input_grad_kernel,
        pref,
        list(pieces) + [weight] * 3 + [grad_res, x],
        [whole((3, rows, tok))] * 4
        + [
            pl.BlockSpec((rows, width), lambda j, i, o=o: (o * 4 + lax.bitwise_xor(i[0], j), 0))
            for o in range(3)
        ]
        + [full, full],
        shape_of((tok, width), BF),
        full,
        (4,),
        [pltpu.VMEM((tok, width), F32)],
        2 * 4 * tok * width * 3 * rows,
    )


def binarize(latent):
    row_scale = jnp.mean(jnp.abs(latent), axis=1, keepdims=True)
    return (row_scale * jnp.sign(latent)).astype(BF)


def segment_info(segments):
    sizes_of = [jnp.sum((segments == k).astype(jnp.int32)) for k in (1, 2, 3)]
    first, second, third = sizes_of
    shift = jnp.where(first == LONG, 0, jnp.where(second == LONG, first, first + second))
    border = jnp.where(first == LONG, second, jnp.where(second == LONG, third, first))
    return jnp.stack([shift, border])


def quarters(own):
    along = to_slot(own, 1)
    return (own, along, to_slot(own, 2), to_slot(along, 2))


def exchange(pieces):
    return (pieces[0],) + tuple(to_slot(pieces[j], j) for j in (1, 2, 3))


def on_device(
    hidden, teacher_hidden, segments, latent_qkv, latent_out, latent_up, latent_down,
    biases, up_bias, norm_gains, norm_shifts, teacher_qkv, teacher_out, teacher_up, teacher_down,
):
    seq_at, fsdp_at = lax.axis_index("seq"), lax.axis_index("fsdp")
    fsdp = lax.axis_size("fsdp")
    core = fsdp_at % 2
    own = (seq_at % 2 + 2 * core).astype(jnp.int32)
    width = hidden.shape[2]

    x = swap_groups(hidden[0])
    x_slots = quarters(x)
    bin_qkv = gather_rows(binarize(latent_qkv))
    info = segment_info(segments)
    info = jnp.where(core == seq_at // 2, info, flip(info, fsdp=1))
    pref = jnp.concatenate([own[None], info]).astype(jnp.int32)
    bin_out = gather_rows(binarize(latent_out))
    bin_up = gather_rows(binarize(latent_up))
    bin_down = gather_rows(binarize(latent_down))
    teach = swap_groups(teacher_hidden[0])
    t_slots = quarters(teach)
    t_qkv = gather_rows(teacher_qkv)
    t_out = gather_rows(teacher_out)
    t_up = gather_rows(teacher_up)
    t_down = gather_rows(teacher_down)

    bias_cols = biases[:2].reshape(2, width, 1)
    qkv = qkv_project(pref, x_slots, bin_qkv, bias_cols)
    *ctx_slots, ctx_full, lse = attention(pref, qkv)
    ctx_pieces = exchange(ctx_slots)

    t_heads = qkv_project(pref, t_slots, t_qkv, None)
    *tctx_slots, _unused, _unused_too = attention(pref, t_heads)
    tctx_pieces = exchange(tctx_slots)

    gain, shift = norm_gains, norm_shifts
    (
        ctx, act_one, normed_one, inv_one, gelu, slope, result, normed_two, inv_two,
    ) = student_ffn(
        pref, ctx_pieces, x, bin_out, bin_up, bin_down,
        biases[2:3], up_bias[None], biases[3:4], gain, shift,
    )
    student_out = swap_groups(result)
    grad_sum, grad_ffn, vec_two = teacher_ffn(
        pref, tctx_pieces, teach, t_out, t_up, t_down, gain, shift, normed_two, inv_two
    )
    grad_hidden, grad_up_bias, grad_res, grad_attn, *gctx_slots, vec_one = student_back(
        pref, grad_ffn, slope, bin_up, bin_down, grad_sum, normed_one, inv_one, gain, shift, bin_out
    )
    gctx_pieces = exchange(gctx_slots)
    grad_down, grad_up, grad_out = weight_grads(
        pref, grad_ffn, gelu, grad_hidden, act_one, grad_attn, ctx
    )
    dp_bits, seq_bits, fsdp_bits = bit_list("dp"), bit_list("seq"), bit_list("fsdp")

    def reduce_grad(value, bits):
        for bit in reversed(fsdp_bits):
            value = halve(value, bit)
        return all_reduce(value, bits).astype(F32)

    total_down = reduce_grad(grad_down, dp_bits + seq_bits)
    total_up = reduce_grad(grad_up, dp_bits[::-1] + seq_bits)
    total_out = reduce_grad(grad_out, seq_bits[:1] + dp_bits + seq_bits[1:])

    dqkv_slots = attention_back(pref, qkv, gctx_pieces, ctx_full, lse)
    dqkv_pieces = exchange(dqkv_slots)
    grad_heads, head_sums = qkv_grad(pref, dqkv_slots, x_slots)
    hidden_grad = swap_groups(input_grad(pref, dqkv_pieces, bin_qkv, grad_res, x))

    rows = width // 4
    blocks = all_reduce(grad_heads.reshape(3 * rows, width), dp_bits + seq_bits[1:] + fsdp_bits[1:])
    blocks = blocks.reshape(1, 3, rows, width)
    blocks = double(double(blocks, seq_bits[0]), fsdp_bits[0])
    whole_qkv = blocks.transpose(1, 0, 2, 3).reshape(3 * width, width)
    part = 3 * width // fsdp
    total_qkv = lax.dynamic_slice_in_dim(whole_qkv, fsdp_at * part, part, 0).astype(F32)

    placed = jnp.zeros((2, 4, rows), F32)
    placed = lax.dynamic_update_slice(
        placed, head_sums.reshape(3, 1, rows)[0::2], (0, own, 0)
    ).reshape(2, width)
    vectors = jnp.concatenate(
        [
            placed,
            vec_one[2:3],
            vec_two[2:3],
            vec_one[0:1],
            vec_two[0:1],
            vec_one[1:2],
            vec_two[1:2],
            grad_up_bias.reshape(-1, width),
        ]
    )
    vectors = sum_small(vectors, dp_bits + seq_bits + fsdp_bits)
    hid_bias = vectors[8:].reshape(-1)
    share, hid_share = width // fsdp, hid_bias.shape[0] // fsdp
    cols = lax.dynamic_slice_in_dim(vectors[:8], fsdp_at * share, share, 1)
    return (
        student_out[None],
        hidden_grad[None],
        total_qkv,
        total_out,
        total_up,
        total_down,
        cols[0:4],
        lax.dynamic_slice_in_dim(hid_bias, fsdp_at * hid_share, hid_share, 0),
        cols[4:6],
        cols[6:8],
    )


def solution(mesh):
    tokens = P(("dp", "fsdp"), "seq", None)
    rows = P("fsdp", None)
    return jax.shard_map(
        on_device,
        mesh=mesh,
        in_specs=(tokens, tokens, P(("dp", "fsdp"), None)) + (rows,) * 4 + (P(),) * 4 + (rows,) * 4,
        out_specs=(tokens, tokens)
        + (rows,) * 4
        + (P(None, "fsdp"), P("fsdp"), P(None, "fsdp"), P(None, "fsdp")),
        check_vma=False,
    )
```

```python
import jax
import jax.numpy as jnp
from jax import lax
from jax.experimental import pallas as pl
from jax.experimental.pallas import tpu as pltpu
from jax.sharding import PartitionSpec as P

HEADS = 12
PROMPT = 1024
LONG = 1024
CLIP = 2.5
EPS = 1e-05
AXES = ("dp", "seq", "fsdp")
BF = jnp.bfloat16
F32 = jnp.float32
LOG2E = 1.4426950408889634
QB = 512
KC = 256
KB = 512
FC = 512
AUG = 16
VMEM_LIMIT = 56 * 2**20


def dot(left, right, left_dim, right_dim):
    return lax.dot_general(
        left, right, (((left_dim,), (right_dim,)), ((), ())), preferred_element_type=F32
    )


def xor(first, second):
    return lax.bitwise_xor(first, jnp.int32(second))


def sizes():
    return tuple(lax.axis_size(name) for name in AXES)


def permute(values, target):
    dp, seq, fsdp = sizes()
    pairs = []
    for d in range(dp):
        for s in range(seq):
            for f in range(fsdp):
                td, ts, tf = target(d, s, f)
                pairs.append(((d * seq + s) * fsdp + f, (td * seq + ts) * fsdp + tf))
    return lax.ppermute(values, AXES, pairs)


def flip(values, dp=0, seq=0, fsdp=0):
    return permute(values, lambda d, s, f: (d ^ dp, s ^ seq, f ^ fsdp))


def swap_groups(values):
    return permute(
        values, lambda d, s, f: (d, 2 * (f % 2) + s % 2, f - f % 2 + s // 2)
    )


def to_slot(values, slot):
    return flip(values, seq=slot & 1, fsdp=slot >> 1)


def bit_list(name):
    count = lax.axis_size(name)
    out, bit = [], 1
    while bit < count:
        out.append((name, bit))
        bit *= 2
    return out


def flip_bit(values, bit):
    return flip(values, **{bit[0]: bit[1]})


def side(bit):
    return lax.bitwise_and(lax.axis_index(bit[0]), bit[1]) != 0


def halve(values, bit):
    upper = side(bit).astype(jnp.int32)
    half = values.shape[0] // 2
    sent = lax.dynamic_slice_in_dim(values, (1 - upper) * half, half, 0)
    kept = lax.dynamic_slice_in_dim(values, upper * half, half, 0)
    got = flip_bit(sent, bit)
    return (kept.astype(F32) + got.astype(F32)).astype(values.dtype)


def double(values, bit):
    got = flip_bit(values, bit)
    return jnp.where(
        side(bit),
        jnp.concatenate([got, values], axis=0),
        jnp.concatenate([values, got], axis=0),
    )


def gather_rows(values):
    for bit in bit_list("fsdp"):
        values = double(values, bit)
    return values


def all_reduce(values, bits):
    for bit in bits:
        values = halve(values, bit)
    for bit in reversed(bits):
        values = double(values, bit)
    return values


def sum_small(values, bits):
    for bit in bits:
        values = values + flip_bit(values, bit)
    return values


def whole(shape):
    return pl.BlockSpec(shape, lambda *_: (0,) * len(shape))


def call(kernel, pref, args, in_specs, outs, out_specs, grid, scratch, flops, trans=0):
    moved = sum(a.size * a.dtype.itemsize for a in args)
    moved += sum(o.size * o.dtype.itemsize for o in jax.tree.leaves(outs))
    return pl.pallas_call(
        kernel,
        grid_spec=pltpu.PrefetchScalarGridSpec(
            num_scalar_prefetch=1,
            grid=grid,
            in_specs=in_specs,
            out_specs=out_specs,
            scratch_shapes=scratch,
        ),
        out_shape=outs,
        compiler_params=pltpu.CompilerParams(vmem_limit_bytes=VMEM_LIMIT),
        cost_estimate=pl.CostEstimate(flops=flops, bytes_accessed=moved, transcendentals=trans),
    )(pref, *args)


def shape_of(shape, dtype):
    return jax.ShapeDtypeStruct(shape, dtype)


def qkv_kernel(student, pref, x0, x1, x2, x3, wq, wk, wv, *rest):
    slot = pl.program_id(0)
    out = rest[-1]
    rows = wq.shape[0]
    for j, ref in enumerate((x0, x1, x2, x3)):

        @pl.when(slot == j)
        def _():
            act = ref[...]
            if student:
                act = jnp.clip(act, -CLIP, CLIP)
            for part, weight in enumerate((wq, wk, wv)):
                value = dot(weight[...], act, 1, 1)
                if student and part != 1:
                    value = value + rest[0][part // 2]
                out[part * rows : (part + 1) * rows, :] = value.astype(BF)


def qkv_project(pref, slots, weight, bias):
    tok, width = slots[0].shape
    rows = weight.shape[0] // 12
    specs = [whole((tok, width))] * 4
    specs += [
        pl.BlockSpec((rows, width), lambda j, i, o=o: (o * 4 + i[0], 0)) for o in range(3)
    ]
    args = list(slots) + [weight] * 3
    if bias is not None:
        specs.append(pl.BlockSpec((2, rows, 1), lambda j, i: (0, i[0], 0)))
        args.append(bias)
    return call(
        lambda *refs: qkv_kernel(bias is not None, *refs),
        pref,
        args,
        specs,
        shape_of((3 * rows, 4 * tok), BF),
        pl.BlockSpec((3 * rows, tok), lambda j, i: (0, lax.bitwise_xor(i[0], j))),
        (4,),
        [],
        2 * 4 * tok * width * 3 * rows,
    )


def roll_cont(values, shift):
    return jnp.concatenate(
        [values[:, :PROMPT], pltpu.roll(values[:, PROMPT:], shift, 1)], axis=1
    )


def block_list(total, rows):
    blocks = [(i, [(0, PROMPT)]) for i in range(0, PROMPT, rows)]
    blocks += [(i, [(0, PROMPT + LONG)]) for i in range(PROMPT, PROMPT + LONG, rows)]
    blocks += [
        (i, [(0, PROMPT), (PROMPT + LONG, total)]) for i in range(PROMPT + LONG, total, rows)
    ]
    return blocks


def same_segment(shape, key_axis, key_start, query_start, border):
    keys = lax.broadcasted_iota(jnp.int32, shape, key_axis) + key_start
    queries = lax.broadcasted_iota(jnp.int32, shape, 1 - key_axis) + query_start
    return (keys < border) == (queries < border)


def attention_kernel(scale, pref, q_ref, k_ref, v_ref, o0, o1, o2, o3, cf_ref, lse_ref, qs, ks, vs, cs, st):
    own, shift, border = pref[0], pref[1], pref[2]
    total = q_ref.shape[1]
    cont = total - PROMPT
    others = PROMPT + LONG
    back = lax.rem(cont - shift, cont)
    qs[...] = roll_cont(q_ref[...].astype(F32), back).astype(BF)
    ks[...] = roll_cont(k_ref[...].astype(F32), back).astype(BF)
    vs[...] = roll_cont(v_ref[...].astype(F32), back).astype(BF)
    blocks = []
    for start, parts in block_list(total, QB):
        chunks = [key for lo, hi in parts for key in range(lo, hi, KC)]
        blocks.append((start, chunks))
    top, acc, norm = {}, {}, {}

    def scores(n, i):
        start, chunks = blocks[n]
        key = chunks[i]
        value = dot(ks[:, key : key + KC], qs[:, start : start + QB], 0, 0) * scale
        if key >= others:
            mask = same_segment((KC, QB), 0, key - others, start - others, border)
            value = jnp.where(mask, value, -1e30)
        st[n % 2, i * KC : (i + 1) * KC, :] = value
        peak = jnp.max(value, axis=0, keepdims=True)
        top[n] = jnp.maximum(top[n], peak) if n in top else peak

    def weigh(n, i):
        key = blocks[n][1][i]
        prob = jnp.exp2(st[n % 2, i * KC : (i + 1) * KC, :] - top[n])
        part = jnp.sum(prob, axis=0, keepdims=True)
        value = dot(vs[:, key : key + KC], prob.astype(BF), 1, 0)
        acc[n] = acc[n] + value if n in acc else value
        norm[n] = norm[n] + part if n in norm else part

    for i in range(len(blocks[0][1])):
        scores(0, i)
    for n, (start, chunks) in enumerate(blocks):
        ahead = len(blocks[n + 1][1]) if n + 1 < len(blocks) else 0
        for i in range(max(len(chunks), ahead)):
            if i < ahead:
                scores(n + 1, i)
            if i < len(chunks):
                weigh(n, i)
        cf_ref[:, start : start + QB] = acc[n] / norm[n]
        lse_ref[:, start : start + QB] = top[n] + jnp.log2(norm[n])
    cs[...] = roll_cont(cf_ref[...], shift).astype(BF)
    tok = total // 4
    for j, out in enumerate((o0, o1, o2, o3)):
        first = pl.multiple_of(xor(own, j) * tok, 128)
        out[...] = cs[:, pl.ds(first, tok)]


def attention(pref, qkv):
    total = qkv.shape[1]
    heads = HEADS // 4
    hdim = qkv.shape[0] // (3 * heads)
    rows = qkv.shape[0] // 3
    scale = LOG2E / hdim**0.5
    return call(
        lambda *refs: attention_kernel(scale, *refs),
        pref,
        [qkv] * 3,
        [pl.BlockSpec((hdim, total), lambda h, i, o=o: (h + o * heads, 0)) for o in range(3)],
        [shape_of((rows, total // 4), BF)] * 4
        + [shape_of((rows, total), F32), shape_of((heads, 1, total), F32)],
        [pl.BlockSpec((hdim, total // 4), lambda h, i: (h, 0))] * 4
        + [
            pl.BlockSpec((hdim, total), lambda h, i: (h, 0)),
            pl.BlockSpec((None, 1, total), lambda h, i: (h, 0, 0)),
        ],
        (heads,),
        [pltpu.VMEM((hdim, total), BF)] * 4 + [pltpu.VMEM((2, PROMPT + LONG, QB), F32)],
        16 * 10**9,
        12 * 10**6,
    )


def thirds(values):
    high = values.astype(BF).astype(F32)
    middle = (values - high).astype(BF).astype(F32)
    low = values - high - middle
    row = lax.broadcasted_iota(jnp.int32, (AUG, values.shape[1]), 0)
    value = jnp.where(row == 0, high, jnp.where(row == 1, middle, jnp.where(row == 2, low, 0.0)))
    return value.astype(BF)


def attention_back_kernel(
    scale, pref, q_ref, k_ref, v_ref, g0, g1, g2, g3, cf_ref, lse_ref,
    d0, d1, d2, d3, qa, ka, va, ga, gs, dqs, dks, dvs,
):
    own, shift, border = pref[0], pref[1], pref[2]
    hdim, total = q_ref.shape
    tok = total // 4
    cont = total - PROMPT
    others = PROMPT + LONG
    back = lax.rem(cont - shift, cont)
    for j, ref in enumerate((g0, g1, g2, g3)):
        first = pl.multiple_of(xor(own, j) * tok, 128)
        gs[:, pl.ds(first, tok)] = ref[...].astype(F32)
    qa[:hdim, :] = roll_cont(q_ref[...].astype(F32), back).astype(BF)
    ka[:hdim, :] = roll_cont(k_ref[...].astype(F32), back).astype(BF)
    va[:hdim, :] = roll_cont(v_ref[...].astype(F32), back).astype(BF)
    grad = roll_cont(gs[...], back)
    ga[:hdim, :] = grad.astype(BF)
    ga[hdim:, :] = thirds(-jnp.sum(grad * cf_ref[...], axis=0, keepdims=True))
    qa[hdim:, :] = thirds(lse_ref[...] * (-1.0 / scale))
    row = lax.broadcasted_iota(jnp.int32, (AUG, total), 0)
    ones = jnp.where(row < 3, 1.0, 0.0).astype(BF)
    ka[hdim:, :] = ones
    va[hdim:, :] = ones
    seen = set()
    for start, parts in block_list(total, QB):
        queries = slice(start, start + QB)
        grad_q = None
        for lo, hi in parts:
            for key in range(lo, hi, KB):
                keys = slice(key, key + KB)
                value = dot(qa[:, queries], ka[:, keys], 0, 0) * scale
                if lo >= others:
                    mask = same_segment((QB, KB), 1, key - others, start - others, border)
                    value = jnp.where(mask, value, -1e30)
                prob = jnp.exp2(value)
                grad_p = dot(ga[:, queries], va[:, keys], 0, 0)
                grad_s = (prob * grad_p).astype(BF)
                grad_v = dot(ga[:hdim, queries], prob.astype(BF), 1, 0)
                grad_k = dot(qa[:hdim, queries], grad_s, 1, 0)
                part = dot(ka[:hdim, keys], grad_s, 1, 1)
                grad_q = part if grad_q is None else grad_q + part
                if key in seen:
                    dvs[:, keys] += grad_v
                    dks[:, keys] += grad_k
                else:
                    dvs[:, keys] = grad_v
                    dks[:, keys] = grad_k
                    seen.add(key)
        dqs[:, queries] = grad_q
    inv = 1.0 / hdim**0.5
    for part, (ref, factor) in enumerate(((dqs, inv), (dks, inv), (dvs, 1.0))):
        gs[...] = roll_cont(ref[...] * factor, shift)
        for j, out in enumerate((d0, d1, d2, d3)):
            first = pl.multiple_of(xor(own, j) * tok, 128)
            out[part] = gs[:, pl.ds(first, tok)].astype(BF)


def attention_back(pref, qkv, grads, ctx, lse):
    total = qkv.shape[1]
    heads = HEADS // 4
    hdim = qkv.shape[0] // (3 * heads)
    rows = qkv.shape[0] // 3
    scale = LOG2E / hdim**0.5
    quarter = pl.BlockSpec((hdim, total // 4), lambda h, i: (h, 0))
    return call(
        lambda *refs: attention_back_kernel(scale, *refs),
        pref,
        [qkv] * 3 + list(grads) + [ctx, lse],
        [pl.BlockSpec((hdim, total), lambda h, i, o=o: (h + o * heads, 0)) for o in range(3)]
        + [quarter] * 4
        + [
            pl.BlockSpec((hdim, total), lambda h, i: (h, 0)),
            pl.BlockSpec((None, 1, total), lambda h, i: (h, 0, 0)),
        ],
        [shape_of((3, rows, total // 4), BF)] * 4,
        [pl.BlockSpec((3, hdim, total // 4), lambda h, i: (0, h, 0))] * 4,
        (heads,),
        [pltpu.VMEM((hdim + AUG, total), BF)] * 4 + [pltpu.VMEM((hdim, total), F32)] * 4,
        30 * 10**9,
        12 * 10**6,
    )


def normalize(values):
    centre = jnp.mean(values, axis=-1, keepdims=True)
    shifted = values - centre
    spread = jnp.mean(shifted * shifted, axis=-1, keepdims=True)
    inv = lax.rsqrt(spread + EPS)
    return shifted * inv, inv


def normalize_back(grad, normed, inv):
    first = jnp.mean(grad, axis=-1, keepdims=True)
    second = jnp.mean(grad * normed, axis=-1, keepdims=True)
    return (grad - first - normed * second) * inv


def total_rows(values):
    return jnp.sum(values, axis=0, keepdims=True)


def gather_ctx(own, pieces, ctx):
    rows = pieces[0].shape[0]
    for j, ref in enumerate(pieces):
        first = pl.multiple_of(xor(own, j) * rows, 64)
        ctx[pl.ds(first, rows), :] = ref[...]


def student_kernel(
    pref, c0, c1, c2, c3, x, w_out, w_up, w_down, b_out, b_up, b_down, gain, shift,
    ctx, act_one, normed_one, inv_one, gelu, slope, result, normed_two, inv_two,
    acc, mid,
):
    step = pl.program_id(0)

    @pl.when(step == 0)
    def _():
        gather_ctx(pref[0], (c0, c1, c2, c3), ctx)
        res = x[...].astype(F32) + (dot(ctx[...], w_out[...], 0, 1) + b_out[...])
        normed, inv = normalize(res)
        normed_one[...] = normed
        inv_one[...] = inv
        middle = normed * gain[0:1] + shift[0:1]
        mid[...] = middle
        act_one[...] = jnp.clip(middle, -CLIP, CLIP).astype(BF)
        acc[...] = jnp.zeros_like(acc)

    pre = dot(act_one[...], w_up[...], 1, 1) + b_up[...]
    cdf = 0.5 * (1.0 + lax.erf(pre * 0.5**0.5))
    act = (pre * cdf).astype(BF)
    gelu[...] = act
    slope[...] = (cdf + pre * (jnp.exp(pre * pre * -0.5) * 0.3989422804014327)).astype(BF)
    acc[...] += dot(act, w_down[...], 1, 1)

    @pl.when(step == pl.num_programs(0) - 1)
    def _():
        normed, inv = normalize(mid[...] + (acc[...] + b_down[...]))
        normed_two[...] = normed
        inv_two[...] = inv
        result[...] = (normed * gain[1:2] + shift[1:2]).astype(BF)


def ffn_specs(tok, width, hidden):
    up = pl.BlockSpec((FC, width), lambda c, i: (c, 0))
    down = pl.BlockSpec((width, FC), lambda c, i: (0, c))
    wide = pl.BlockSpec((tok, FC), lambda c, i: (0, c))
    row = pl.BlockSpec((1, FC), lambda c, i: (0, c))
    return up, down, wide, row


def student_ffn(pref, pieces, x, w_out, w_up, w_down, b_out, b_up, b_down, gain, shift):
    tok, width = x.shape
    hidden = w_up.shape[0]
    up, down, wide, row = ffn_specs(tok, width, hidden)
    full, one = whole((tok, width)), whole((tok, 1))
    return call(
        student_kernel,
        pref,
        list(pieces) + [x, w_out, w_up, w_down, b_out, b_up, b_down, gain, shift],
        [whole(pieces[0].shape)] * 4
        + [full, whole(w_out.shape), up, down, whole((1, width)), row, whole((1, width))]
        + [whole((2, width))] * 2,
        [
            shape_of((width, tok), BF),
            shape_of((tok, width), BF),
            shape_of((tok, width), F32),
            shape_of((tok, 1), F32),
            shape_of((tok, hidden), BF),
            shape_of((tok, hidden), BF),
            shape_of((tok, width), BF),
            shape_of((tok, width), F32),
            shape_of((tok, 1), F32),
        ],
        [whole((width, tok)), full, full, one, wide, wide, full, full, one],
        (hidden // FC,),
        [pltpu.VMEM((tok, width), F32)] * 2,
        2 * tok * width * (2 * hidden + width),
        2 * tok * hidden,
    )


def teacher_kernel(
    pref, c0, c1, c2, c3, x, w_out, w_up, w_down, gain, shift, normed_two, inv_two,
    grad_sum, grad_ffn, vectors,
    ctx, acc, mid, act_one,
):
    step = pl.program_id(0)

    @pl.when(step == 0)
    def _():
        gather_ctx(pref[0], (c0, c1, c2, c3), ctx)
        res = x[...].astype(F32) + dot(ctx[...], w_out[...], 0, 1)
        normed, inv = normalize(res)
        mid[...] = normed
        act_one[...] = normed.astype(BF)
        acc[...] = jnp.zeros_like(acc)

    pre = dot(act_one[...], w_up[...], 1, 1)
    act = (pre * (0.5 * (1.0 + lax.erf(pre * 0.5**0.5)))).astype(BF)
    acc[...] += dot(act, w_down[...], 1, 1)

    @pl.when(step == pl.num_programs(0) - 1)
    def _():
        target, _unused = normalize(mid[...] + acc[...])
        normed = normed_two[...]
        diff = normed * gain[1:2] + shift[1:2] - target
        back = normalize_back(diff * gain[1:2], normed, inv_two[...])
        grad_sum[...] = back
        low = back.astype(BF)
        grad_ffn[...] = low
        vectors[0:1] = total_rows(diff * normed)
        vectors[1:2] = total_rows(diff)
        vectors[2:3] = total_rows(low.astype(F32))


def teacher_ffn(pref, pieces, x, w_out, w_up, w_down, gain, shift, normed_two, inv_two):
    tok, width = x.shape
    hidden = w_up.shape[0]
    up, down, wide, row = ffn_specs(tok, width, hidden)
    full, one = whole((tok, width)), whole((tok, 1))
    return call(
        teacher_kernel,
        pref,
        list(pieces) + [x, w_out, w_up, w_down, gain, shift, normed_two, inv_two],
        [whole(pieces[0].shape)] * 4
        + [full, whole(w_out.shape), up, down]
        + [whole((2, width))] * 2
        + [full, one],
        [shape_of((tok, width), F32), shape_of((tok, width), BF), shape_of((3, width), F32)],
        [full, full, whole((3, width))],
        (hidden // FC,),
        [pltpu.VMEM((width, tok), BF)]
        + [pltpu.VMEM((tok, width), F32)] * 2
        + [pltpu.VMEM((tok, width), BF)],
        2 * tok * width * (2 * hidden + width),
        tok * hidden,
    )


def back_kernel(
    pref, grad_ffn, slope, w_up, w_down, grad_sum, normed_one, inv_one, gain, shift, w_out,
    grad_hidden, grad_bias, grad_res, grad_attn, g0, g1, g2, g3, vectors,
    acc, ctx,
):
    step = pl.program_id(0)

    @pl.when(step == 0)
    def _():
        acc[...] = jnp.zeros_like(acc)

    low = (dot(grad_ffn[...], w_down[...], 1, 0) * slope[...].astype(F32)).astype(BF)
    grad_hidden[...] = low
    grad_bias[...] = total_rows(low.astype(F32))
    acc[...] += dot(low, w_up[...], 1, 0)

    @pl.when(step == pl.num_programs(0) - 1)
    def _():
        normed = normed_one[...]
        middle = normed * gain[0:1] + shift[0:1]
        grad = grad_sum[...] + jnp.where(jnp.abs(middle) < CLIP, acc[...], 0.0)
        back = normalize_back(grad * gain[0:1], normed, inv_one[...])
        grad_res[...] = back
        attn = back.astype(BF)
        grad_attn[...] = attn
        vectors[0:1] = total_rows(grad * normed)
        vectors[1:2] = total_rows(grad)
        vectors[2:3] = total_rows(attn.astype(F32))
        ctx[...] = dot(w_out[...], attn, 0, 1).astype(BF)
        rows = g0.shape[0]
        for j, ref in enumerate((g0, g1, g2, g3)):
            first = pl.multiple_of(xor(pref[0], j) * rows, 64)
            ref[...] = ctx[pl.ds(first, rows), :]


def student_back(pref, grad_ffn, slope, w_up, w_down, grad_sum, normed_one, inv_one, gain, shift, w_out):
    tok, width = grad_ffn.shape
    hidden = w_up.shape[0]
    up, down, wide, row = ffn_specs(tok, width, hidden)
    full, one = whole((tok, width)), whole((tok, 1))
    return call(
        back_kernel,
        pref,
        [grad_ffn, slope, w_up, w_down, grad_sum, normed_one, inv_one, gain, shift, w_out],
        [full, wide, up, down, full, full, one] + [whole((2, width))] * 2 + [whole(w_out.shape)],
        [
            shape_of((tok, hidden), BF),
            shape_of((1, hidden), F32),
            shape_of((tok, width), F32),
            shape_of((tok, width), BF),
        ]
        + [shape_of((width // 4, tok), BF)] * 4
        + [shape_of((3, width), F32)],
        [wide, row, full, full] + [whole((width // 4, tok))] * 4 + [whole((3, width))],
        (hidden // FC,),
        [pltpu.VMEM((tok, width), F32), pltpu.VMEM((width, tok), BF)],
        2 * tok * width * (2 * hidden + width),
    )


def weight_grad_kernel(
    pref, grad_ffn, gelu, grad_hidden, act_one, grad_attn, ctx, grad_down, grad_up, grad_out
):
    @pl.when(pl.program_id(0) == 0)
    def _():
        value = dot(grad_attn[...], ctx[...], 0, 1).astype(BF)
        grad_out[...] = value.reshape(grad_out.shape)

    value = dot(grad_ffn[...], gelu[...], 0, 0).astype(BF)
    grad_down[...] = value.reshape(grad_down.shape)
    value = dot(grad_hidden[...], act_one[...], 0, 0).astype(BF)
    grad_up[...] = value.reshape(grad_up.shape)


def weight_grads(pref, grad_ffn, gelu, grad_hidden, act_one, grad_attn, ctx):
    tok, width = grad_ffn.shape
    hidden = gelu.shape[1]
    count, half = hidden // width, width // 2
    wide = pl.BlockSpec((tok, width), lambda c, i: (0, c))
    full = whole((tok, width))
    return call(
        weight_grad_kernel,
        pref,
        [grad_ffn, gelu, grad_hidden, act_one, grad_attn, ctx],
        [full, wide, wide, full, full, whole((width, tok))],
        [
            shape_of((2, count, half, width), BF),
            shape_of((2 * count, half, width), BF),
            shape_of((2, half, width), BF),
        ],
        [
            pl.BlockSpec((2, 1, half, width), lambda c, i: (0, c, 0, 0)),
            pl.BlockSpec((2, half, width), lambda c, i: (c, 0, 0)),
            whole((2, half, width)),
        ],
        (count,),
        [],
        2 * tok * width * (2 * hidden + width),
    )


def qkv_grad_kernel(pref, d0, d1, d2, d3, x0, x1, x2, x3, out, sums):
    own = pref[0]
    total = None
    count = None
    ones = jnp.ones((8, d0.shape[1]), BF)
    for grad, x in zip((d0, d1, d2, d3), (x0, x1, x2, x3)):
        value = grad[...]
        part = dot(value, jnp.clip(x[...], -CLIP, CLIP), 1, 0)
        line = dot(ones, value, 1, 1)
        total = part if total is None else total + part
        count = line if count is None else count + line
    out[...] = total.astype(BF)
    sums[...] = jnp.zeros_like(sums)
    rows = out.shape[0]
    for j in range(4):

        @pl.when(own == j)
        def _():
            sums[:, j * rows : (j + 1) * rows] = count


def qkv_grad(pref, grads, slots):
    tok, width = slots[0].shape
    rows = grads[0].shape[1]
    return call(
        qkv_grad_kernel,
        pref,
        list(grads) + list(slots),
        [pl.BlockSpec((None, rows, tok), lambda o, i: (o, 0, 0))] * 4 + [whole((tok, width))] * 4,
        [shape_of((3, rows, width), BF), shape_of((3, 8, width), F32)],
        [
            pl.BlockSpec((None, rows, width), lambda o, i: (o, 0, 0)),
            pl.BlockSpec((None, 8, width), lambda o, i: (o, 0, 0)),
        ],
        (3,),
        [],
        2 * 4 * tok * width * 3 * rows,
    )


def input_grad_kernel(pref, e0, e1, e2, e3, wq, wk, wv, grad_res, x, out, acc):
    slot = pl.program_id(0)

    @pl.when(slot == 0)
    def _():
        acc[...] = jnp.zeros_like(acc)

    for j, ref in enumerate((e0, e1, e2, e3)):

        @pl.when(slot == j)
        def _():
            part = dot(ref[0], wq[...], 0, 0)
            part = part + dot(ref[1], wk[...], 0, 0)
            acc[...] += part + dot(ref[2], wv[...], 0, 0)

    @pl.when(slot == 3)
    def _():
        size = jnp.abs(x[...].astype(F32))
        pull = jnp.where(size < CLIP, 1.0, jnp.where(size == CLIP, 0.5, 0.0))
        out[...] = (grad_res[...] + acc[...] * pull).astype(BF)


def input_grad(pref, pieces, weight, grad_res, x):
    tok, width = x.shape
    rows = pieces[0].shape[1]
    full = whole((tok, width))
    return call(
        input_grad_kernel,
        pref,
        list(pieces) + [weight] * 3 + [grad_res, x],
        [whole((3, rows, tok))] * 4
        + [
            pl.BlockSpec((rows, width), lambda j, i, o=o: (o * 4 + lax.bitwise_xor(i[0], j), 0))
            for o in range(3)
        ]
        + [full, full],
        shape_of((tok, width), BF),
        full,
        (4,),
        [pltpu.VMEM((tok, width), F32)],
        2 * 4 * tok * width * 3 * rows,
    )


def place(bit):
    name, mask = bit
    at = lax.axis_index(name)
    upper = lax.rem(lax.div(at, jnp.int32(mask)), jnp.int32(2))
    return upper, {name: at + mask * (1 - 2 * upper)}


def greet(bits):
    barrier = pltpu.get_barrier_semaphore()
    for bit in bits:
        pl.semaphore_signal(
            barrier, inc=1, device_id=place(bit)[1], device_id_type=pl.DeviceIdType.MESH
        )
    pl.semaphore_wait(barrier, len(bits))


class Copies:
    def __init__(self, send, recv, local):
        self.send, self.recv, self.local_sem = send, recv, local
        self.sent, self.kept = [], 0

    def remote(self, source, target, device):
        n = len(self.sent)
        copy = pltpu.make_async_remote_copy(
            src_ref=source,
            dst_ref=target,
            send_sem=self.send.at[n],
            recv_sem=self.recv.at[n],
            device_id=device,
            device_id_type=pl.DeviceIdType.MESH,
        )
        copy.start()
        self.sent.append(copy)
        return copy

    def local(self, source, target):
        copy = pltpu.make_async_copy(source, target, self.local_sem.at[self.kept])
        self.kept += 1
        copy.start()
        return copy

    def finish(self):
        for copy in self.sent:
            copy.wait_send()


def window(ref, region):
    row, rows, col, cols = region
    return ref.at[pl.ds(row, rows), pl.ds(col, cols)]


def add_window(target, left, right, region, start):
    row, rows, col, cols = region
    step = 48 if rows % 48 == 0 else 16

    def body(i, carry):
        there = pl.ds(pl.multiple_of(row + i * step, 16), step)
        here = pl.ds(pl.multiple_of(start + i * step, 16), step)
        value = left[there, pl.ds(col, cols)].astype(F32) + right[here, :cols].astype(F32)
        target[there, pl.ds(col, cols)] = value.astype(target.dtype)
        return carry

    lax.fori_loop(0, rows // step, body, 0)


def scatter_sum(copies, work, far, full, bits):
    rows, cols = work.shape
    region, used, parts = (0, rows, 0, cols), 0, []
    for n, bit in enumerate(bits):
        upper, device = place(bit)
        row, rows, col, cols = region
        if (rows // 2) % 16 == 0:
            rows //= 2
            kept = (pl.multiple_of(row + upper * rows, 16), rows, col, cols)
            sent = (pl.multiple_of(row + (1 - upper) * rows, 16), rows, col, cols)
        else:
            cols //= 2
            kept = (row, rows, pl.multiple_of(col + upper * cols, 128), cols)
            sent = (row, rows, pl.multiple_of(col + (1 - upper) * cols, 128), cols)
        slot = far.at[pl.ds(used, rows), pl.ds(0, cols)]
        copy = copies.remote(window(work, sent), slot, device)
        yield
        copy.wait_recv()
        add_window(full if n == len(bits) - 1 else work, work, far, kept, used)
        used += rows
        region = kept
        parts.append((bit, kept))
    return parts


def sum_flow(copies, own, other, work, near, far, full, result, core, bits):
    copy = copies.remote(other, near, place(core)[1])
    load = copies.local(own, work)
    yield
    copy.wait_recv()
    load.wait()
    add_window(work, work, near, (0, work.shape[0], 0, work.shape[1]), 0)
    parts = yield from scatter_sum(copies, work, far, full, bits)
    for bit, kept in reversed(parts):
        copy = copies.remote(window(full, kept), window(full, kept), place(bit)[1])
        yield
        copy.wait_recv()
    store = copies.local(full, result)
    yield
    store.wait()


def vector_flow(copies, sums, far, bits):
    for n, bit in enumerate(bits):
        yield
        copy = copies.remote(sums.at[n], far.at[n], place(bit)[1])
        yield
        copy.wait_recv()
        sums[n + 1] = sums[n] + far[n]


def run_flows(flows, step):
    events = []
    for delay, flow in flows:
        next(flow)
        events.append([delay, len(events), flow])
    while events:
        events.sort(key=lambda e: e[:2])
        event = events[0]
        try:
            next(event[2])
            event[0] += step
        except StopIteration:
            events.pop(0)


def rotate(items, count):
    count %= len(items)
    return items[count:] + items[:count]


def sum_kernel(
    dp, seq, core, down, up, out, two, one, bias, heads, down_sum, up_sum, out_sum, totals,
    work, near, far, full, sums, sums_far, send, recv, local,
):
    greet(dp + seq + [core])
    copies = Copies(send, recv, local)
    side_of = place(core)[0]
    count, half, width = down.shape[1:]
    pieces = [(up.at[side_of, p], up.at[1 - side_of, p], up_sum.at[p]) for p in range(count)]
    pieces += [
        (
            down.at[side_of, p],
            down.at[1 - side_of, p],
            down_sum.at[:, pl.ds(p * width, width)],
        )
        for p in range(count)
    ]
    pieces.append((out.at[side_of], out.at[1 - side_of], out_sum))
    first = dp + seq[:1]
    flows = []
    for n, (own, other, result) in enumerate(pieces):
        bits = rotate(first, n) + seq[1:]
        flow = sum_flow(
            copies, own, other, work.at[n], near.at[n], far.at[n], full.at[n], result, core, bits
        )
        flows.append((n // len(first), flow))
    sums[0] = jnp.zeros(sums.shape[1:], F32)
    sums[0, 0:1] = heads[0, 0:1]
    sums[0, 1:2] = heads[2, 0:1]
    sums[0, 2:3] = one[2:3]
    sums[0, 3:4] = two[2:3]
    sums[0, 4:5] = one[0:1]
    sums[0, 5:6] = two[0:1]
    sums[0, 6:7] = one[1:2]
    sums[0, 7:8] = two[1:2]
    for p in range(count):
        sums[0, 8 + p : 9 + p] = bias[:, p * width : (p + 1) * width]
    flows.append((0.5, vector_flow(copies, sums, sums_far, [core] + dp + seq)))
    run_flows(flows, 1.5)
    totals[...] = sums[sums.shape[0] - 1]
    copies.finish()


def remote_call(kernel, args, in_specs, outs, out_specs, scratch, copies, local, number):
    sems = pltpu.SemaphoreType.DMA
    return pl.pallas_call(
        kernel,
        in_specs=in_specs,
        out_specs=out_specs,
        out_shape=outs,
        scratch_shapes=scratch + [sems((copies,)), sems((copies,)), sems((local,))],
        compiler_params=pltpu.CompilerParams(
            vmem_limit_bytes=VMEM_LIMIT, collective_id=number, has_side_effects=True
        ),
        cost_estimate=pl.CostEstimate(flops=5 * 10**10, bytes_accessed=10**8, transcendentals=0),
    )(*args)


ANY = pl.BlockSpec(memory_space=pl.ANY)
IN_VMEM = pl.BlockSpec(memory_space=pltpu.VMEM)


def sum_grads(dp, seq, core, down, up, out, two, one, bias, heads):
    sides, count, half, width = down.shape
    pieces, steps = 2 * count + 1, len(dp) + len(seq)
    lines = 16
    return remote_call(
        lambda *refs: sum_kernel(dp, seq, core, *refs),
        [down, up, out, two, one, bias, heads],
        [ANY] * 3 + [IN_VMEM] * 4,
        [
            shape_of((half, count * width), BF),
            shape_of((count, half, width), BF),
            shape_of((half, width), BF),
            shape_of((lines, width), F32),
        ],
        [ANY] * 3 + [IN_VMEM],
        [pltpu.VMEM((pieces, half, width), BF)] * 4
        + [pltpu.VMEM((steps + 2, lines, width), F32), pltpu.VMEM((steps + 1, lines, width), F32)],
        pieces * (1 + 2 * steps) + steps + 1,
        2 * pieces,
        1,
    )


def head_sum_kernel(dp, seq, core, heads, result, work, far, full, send, recv, local):
    greet(dp + seq + [core])
    copies = Copies(send, recv, local)
    side_of, partner = place(core)
    along = place(seq[0])[0]
    rows = dp + seq[1:]

    def flow(n):
        if n == 1:
            copy = copies.remote(heads.at[2 - 2 * side_of], work.at[n], partner)
            yield
            copy.wait_recv()
        else:
            load = copies.local(heads.at[n // 2 + side_of], work.at[n])
            yield
            load.wait()
        bits = (rotate(dp, n) if n < 2 else dp) + seq[1:]
        mine = full.at[2 * n + along]
        parts = yield from scatter_sum(copies, work.at[n], far.at[n], mine, bits)
        steps = [(bit, kept, False) for bit, kept in reversed(parts)]
        cut = len(steps) if n == 2 else 1
        held = steps[cut][1] if n < 2 else (0, mine.shape[0], 0, mine.shape[1])
        steps = steps[:cut] + [(seq[0], held, False)] + [(b, k, True) for b, k, _ in steps[cut:]]
        for bit, (row, size, col, cols), both in steps:
            first, count = (2 * n, 2) if both else (2 * n + along, 1)
            part = full.at[pl.ds(first, count), pl.ds(row, size), pl.ds(col, cols)]
            copy = copies.remote(part, part, place(bit)[1])
            yield
            copy.wait_recv()
        store = copies.local(full.at[pl.ds(2 * n, 2)], result.at[pl.ds(2 * n, 2)])
        yield
        store.wait()

    run_flows([(0, flow(0)), (0, flow(2)), (0, flow(1))], 1.0)
    copies.finish()


def head_sums_of(dp, seq, core, heads):
    _, rows, width = heads.shape
    steps = len(dp) + len(seq) - 1
    return remote_call(
        lambda *refs: head_sum_kernel(dp, seq, core, *refs),
        [heads],
        [ANY],
        shape_of((6, rows, width), BF),
        ANY,
        [pltpu.VMEM((3, rows, width), BF)] * 2 + [pltpu.VMEM((6, rows, width), BF)],
        3 * (2 * steps + 1) + 1,
        5,
        2,
    )


def binarize(latent):
    row_scale = jnp.mean(jnp.abs(latent), axis=1, keepdims=True)
    return (row_scale * jnp.sign(latent)).astype(BF)


def segment_info(segments):
    sizes_of = [jnp.sum((segments == k).astype(jnp.int32)) for k in (1, 2, 3)]
    first, second, third = sizes_of
    shift = jnp.where(first == LONG, 0, jnp.where(second == LONG, first, first + second))
    border = jnp.where(first == LONG, second, jnp.where(second == LONG, third, first))
    return jnp.stack([shift, border])


def quarters(own):
    along = to_slot(own, 1)
    return (own, along, to_slot(own, 2), to_slot(along, 2))


def exchange(pieces):
    return (pieces[0],) + tuple(to_slot(pieces[j], j) for j in (1, 2, 3))


def on_device(
    hidden, teacher_hidden, segments, latent_qkv, latent_out, latent_up, latent_down,
    biases, up_bias, norm_gains, norm_shifts, teacher_qkv, teacher_out, teacher_up, teacher_down,
):
    seq_at, fsdp_at = lax.axis_index("seq"), lax.axis_index("fsdp")
    fsdp = lax.axis_size("fsdp")
    core = fsdp_at % 2
    own = (seq_at % 2 + 2 * core).astype(jnp.int32)
    width = hidden.shape[2]

    x = swap_groups(hidden[0])
    x_slots = quarters(x)
    bin_qkv = gather_rows(binarize(latent_qkv))
    info = segment_info(segments)
    info = jnp.where(core == seq_at // 2, info, flip(info, fsdp=1))
    pref = jnp.concatenate([own[None], info]).astype(jnp.int32)
    bin_out = gather_rows(binarize(latent_out))
    bin_up = gather_rows(binarize(latent_up))
    bin_down = gather_rows(binarize(latent_down))
    teach = swap_groups(teacher_hidden[0])
    t_slots = quarters(teach)
    t_qkv = gather_rows(teacher_qkv)
    t_out = gather_rows(teacher_out)
    t_up = gather_rows(teacher_up)
    t_down = gather_rows(teacher_down)

    bias_cols = biases[:2].reshape(2, width, 1)
    qkv = qkv_project(pref, x_slots, bin_qkv, bias_cols)
    *ctx_slots, ctx_full, lse = attention(pref, qkv)
    ctx_pieces = exchange(ctx_slots)

    t_heads = qkv_project(pref, t_slots, t_qkv, None)
    *tctx_slots, _unused, _unused_too = attention(pref, t_heads)
    tctx_pieces = exchange(tctx_slots)

    gain, shift = norm_gains, norm_shifts
    (
        ctx, act_one, normed_one, inv_one, gelu, slope, result, normed_two, inv_two,
    ) = student_ffn(
        pref, ctx_pieces, x, bin_out, bin_up, bin_down,
        biases[2:3], up_bias[None], biases[3:4], gain, shift,
    )
    student_out = swap_groups(result)
    grad_sum, grad_ffn, vec_two = teacher_ffn(
        pref, tctx_pieces, teach, t_out, t_up, t_down, gain, shift, normed_two, inv_two
    )
    grad_hidden, grad_up_bias, grad_res, grad_attn, *gctx_slots, vec_one = student_back(
        pref, grad_ffn, slope, bin_up, bin_down, grad_sum, normed_one, inv_one, gain, shift, bin_out
    )
    gctx_pieces = exchange(gctx_slots)
    grad_down, grad_up, grad_out = weight_grads(
        pref, grad_ffn, gelu, grad_hidden, act_one, grad_attn, ctx
    )
    dp_bits, seq_bits, fsdp_bits = bit_list("dp"), bit_list("seq"), bit_list("fsdp")
    dqkv_slots = attention_back(pref, qkv, gctx_pieces, ctx_full, lse)
    dqkv_pieces = exchange(dqkv_slots)
    grad_heads, head_sums = qkv_grad(pref, dqkv_slots, x_slots)
    rows, hidden_units = width // 4, up_bias.shape[0]
    _, count, half, _ = grad_down.shape

    if fsdp == 2:
        total_down, total_up, total_out, vectors = sum_grads(
            dp_bits,
            seq_bits,
            fsdp_bits[0],
            grad_down,
            grad_up.reshape(grad_down.shape),
            grad_out,
            vec_two,
            vec_one,
            grad_up_bias,
            head_sums,
        )
        total_up = total_up.reshape(-1, width)
        hidden_grad = swap_groups(input_grad(pref, dqkv_pieces, bin_qkv, grad_res, x))
        total_qkv = head_sums_of(dp_bits, seq_bits, fsdp_bits[0], grad_heads).reshape(-1, width)
    else:
        hidden_grad = swap_groups(input_grad(pref, dqkv_pieces, bin_qkv, grad_res, x))

        def reduce_grad(value, bits):
            for bit in reversed(fsdp_bits):
                value = halve(value, bit)
            return all_reduce(value, bits)

        grad_down = grad_down.transpose(0, 2, 1, 3).reshape(width, hidden_units)
        total_down = reduce_grad(grad_down, dp_bits + seq_bits)
        total_up = reduce_grad(grad_up.reshape(hidden_units, width), dp_bits[::-1] + seq_bits)
        total_out = reduce_grad(
            grad_out.reshape(width, width), seq_bits[:1] + dp_bits + seq_bits[1:]
        )
        blocks = all_reduce(
            grad_heads.reshape(3 * rows, width), dp_bits + seq_bits[1:] + fsdp_bits[1:]
        )
        blocks = blocks.reshape(1, 3, rows, width)
        blocks = double(double(blocks, seq_bits[0]), fsdp_bits[0])
        whole_qkv = blocks.transpose(1, 0, 2, 3).reshape(3 * width, width)
        part = 3 * width // fsdp
        total_qkv = lax.dynamic_slice_in_dim(whole_qkv, fsdp_at * part, part, 0)
        vectors = jnp.concatenate(
            [
                head_sums[0, :1],
                head_sums[2, :1],
                vec_one[2:3],
                vec_two[2:3],
                vec_one[0:1],
                vec_two[0:1],
                vec_one[1:2],
                vec_two[1:2],
                grad_up_bias.reshape(-1, width),
            ]
        )
        vectors = sum_small(vectors, dp_bits + seq_bits + fsdp_bits)
    hid_bias = vectors[8 : 8 + hidden_units // width].reshape(-1)
    share, hid_share = width // fsdp, hid_bias.shape[0] // fsdp
    cols = lax.dynamic_slice_in_dim(vectors[:8], fsdp_at * share, share, 1)
    return (
        student_out[None],
        hidden_grad[None],
        total_qkv.astype(F32),
        total_out.astype(F32),
        total_up.astype(F32),
        total_down.astype(F32),
        cols[0:4],
        lax.dynamic_slice_in_dim(hid_bias, fsdp_at * hid_share, hid_share, 0),
        cols[4:6],
        cols[6:8],
    )


def solution(mesh):
    tokens = P(("dp", "fsdp"), "seq", None)
    rows = P("fsdp", None)
    return jax.shard_map(
        on_device,
        mesh=mesh,
        in_specs=(tokens, tokens, P(("dp", "fsdp"), None)) + (rows,) * 4 + (P(),) * 4 + (rows,) * 4,
        out_specs=(tokens, tokens)
        + (rows,) * 4
        + (P(None, "fsdp"), P("fsdp"), P(None, "fsdp"), P(None, "fsdp")),
        check_vma=False,
    )
```

```python
import jax
import jax.numpy as jnp
from jax import lax
from jax.experimental import pallas as pl
from jax.experimental.pallas import tpu as pltpu
from jax.sharding import PartitionSpec as P

HEADS = 12
PROMPT = 1024
LONG = 1024
CLIP = 2.5
EPS = 1e-05
AXES = ("dp", "seq", "fsdp")
BF = jnp.bfloat16
F32 = jnp.float32
LOG2E = 1.4426950408889634
QB = 512
KC = 256
KB = 512
FC = 512
AUG = 16
VMEM_LIMIT = 56 * 2**20


def dot(left, right, left_dim, right_dim):
    return lax.dot_general(
        left, right, (((left_dim,), (right_dim,)), ((), ())), preferred_element_type=F32
    )


def xor(first, second):
    return lax.bitwise_xor(first, jnp.int32(second))


def sizes():
    return tuple(lax.axis_size(name) for name in AXES)


def permute(values, target):
    dp, seq, fsdp = sizes()
    pairs = []
    for d in range(dp):
        for s in range(seq):
            for f in range(fsdp):
                td, ts, tf = target(d, s, f)
                pairs.append(((d * seq + s) * fsdp + f, (td * seq + ts) * fsdp + tf))
    return lax.ppermute(values, AXES, pairs)


def flip(values, dp=0, seq=0, fsdp=0):
    return permute(values, lambda d, s, f: (d ^ dp, s ^ seq, f ^ fsdp))


def swap_groups(values):
    return permute(
        values, lambda d, s, f: (d, 2 * (f % 2) + s % 2, f - f % 2 + s // 2)
    )


def to_slot(values, slot):
    return flip(values, seq=slot & 1, fsdp=slot >> 1)


def bit_list(name):
    count = lax.axis_size(name)
    out, bit = [], 1
    while bit < count:
        out.append((name, bit))
        bit *= 2
    return out


def flip_bit(values, bit):
    return flip(values, **{bit[0]: bit[1]})


def side(bit):
    return lax.bitwise_and(lax.axis_index(bit[0]), bit[1]) != 0


def halve(values, bit):
    upper = side(bit).astype(jnp.int32)
    half = values.shape[0] // 2
    sent = lax.dynamic_slice_in_dim(values, (1 - upper) * half, half, 0)
    kept = lax.dynamic_slice_in_dim(values, upper * half, half, 0)
    got = flip_bit(sent, bit)
    return (kept.astype(F32) + got.astype(F32)).astype(values.dtype)


def double(values, bit):
    got = flip_bit(values, bit)
    return jnp.where(
        side(bit),
        jnp.concatenate([got, values], axis=0),
        jnp.concatenate([values, got], axis=0),
    )


def gather_rows(values):
    for bit in bit_list("fsdp"):
        values = double(values, bit)
    return values


def all_reduce(values, bits):
    for bit in bits:
        values = halve(values, bit)
    for bit in reversed(bits):
        values = double(values, bit)
    return values


def sum_small(values, bits):
    for bit in bits:
        values = values + flip_bit(values, bit)
    return values


def whole(shape):
    return pl.BlockSpec(shape, lambda *_: (0,) * len(shape))


def call(kernel, pref, args, in_specs, outs, out_specs, grid, scratch, flops, trans=0):
    moved = sum(a.size * a.dtype.itemsize for a in args)
    moved += sum(o.size * o.dtype.itemsize for o in jax.tree.leaves(outs))
    return pl.pallas_call(
        kernel,
        grid_spec=pltpu.PrefetchScalarGridSpec(
            num_scalar_prefetch=1,
            grid=grid,
            in_specs=in_specs,
            out_specs=out_specs,
            scratch_shapes=scratch,
        ),
        out_shape=outs,
        compiler_params=pltpu.CompilerParams(vmem_limit_bytes=VMEM_LIMIT),
        cost_estimate=pl.CostEstimate(flops=flops, bytes_accessed=moved, transcendentals=trans),
    )(pref, *args)


def shape_of(shape, dtype):
    return jax.ShapeDtypeStruct(shape, dtype)


def qkv_kernel(student, pref, x0, x1, x2, x3, wq, wk, wv, *rest):
    slot = pl.program_id(0)
    out = rest[-1]
    rows = wq.shape[0]
    for j, ref in enumerate((x0, x1, x2, x3)):

        @pl.when(slot == j)
        def _():
            act = ref[...]
            if student:
                act = jnp.clip(act, -CLIP, CLIP)
            for part, weight in enumerate((wq, wk, wv)):
                value = dot(weight[...], act, 1, 1)
                if student and part != 1:
                    value = value + rest[0][part // 2]
                out[part * rows : (part + 1) * rows, :] = value.astype(BF)


def qkv_project(pref, slots, weight, bias):
    tok, width = slots[0].shape
    rows = weight.shape[0] // 12
    specs = [whole((tok, width))] * 4
    specs += [
        pl.BlockSpec((rows, width), lambda j, i, o=o: (o * 4 + i[0], 0)) for o in range(3)
    ]
    args = list(slots) + [weight] * 3
    if bias is not None:
        specs.append(pl.BlockSpec((2, rows, 1), lambda j, i: (0, i[0], 0)))
        args.append(bias)
    return call(
        lambda *refs: qkv_kernel(bias is not None, *refs),
        pref,
        args,
        specs,
        shape_of((3 * rows, 4 * tok), BF),
        pl.BlockSpec((3 * rows, tok), lambda j, i: (0, lax.bitwise_xor(i[0], j))),
        (4,),
        [],
        2 * 4 * tok * width * 3 * rows,
    )


def roll_cont(values, shift):
    return jnp.concatenate(
        [values[:, :PROMPT], pltpu.roll(values[:, PROMPT:], shift, 1)], axis=1
    )


def block_list(total, rows):
    blocks = [(i, [(0, PROMPT)]) for i in range(0, PROMPT, rows)]
    blocks += [(i, [(0, PROMPT + LONG)]) for i in range(PROMPT, PROMPT + LONG, rows)]
    blocks += [
        (i, [(0, PROMPT), (PROMPT + LONG, total)]) for i in range(PROMPT + LONG, total, rows)
    ]
    return blocks


def same_segment(shape, key_axis, key_start, query_start, border):
    keys = lax.broadcasted_iota(jnp.int32, shape, key_axis) + key_start
    queries = lax.broadcasted_iota(jnp.int32, shape, 1 - key_axis) + query_start
    return (keys < border) == (queries < border)


def attention_kernel(scale, pref, q_ref, k_ref, v_ref, o0, o1, o2, o3, cf_ref, lse_ref, qs, ks, vs, cs, st):
    own, shift, border = pref[0], pref[1], pref[2]
    total = q_ref.shape[1]
    cont = total - PROMPT
    others = PROMPT + LONG
    back = lax.rem(cont - shift, cont)
    qs[...] = roll_cont(q_ref[...].astype(F32), back).astype(BF)
    ks[...] = roll_cont(k_ref[...].astype(F32), back).astype(BF)
    vs[...] = roll_cont(v_ref[...].astype(F32), back).astype(BF)
    blocks = []
    for start, parts in block_list(total, QB):
        chunks = [key for lo, hi in parts for key in range(lo, hi, KC)]
        blocks.append((start, chunks))
    top, acc, norm = {}, {}, {}

    def scores(n, i):
        start, chunks = blocks[n]
        key = chunks[i]
        value = dot(ks[:, key : key + KC], qs[:, start : start + QB], 0, 0) * scale
        if key >= others:
            mask = same_segment((KC, QB), 0, key - others, start - others, border)
            value = jnp.where(mask, value, -1e30)
        st[n % 2, i * KC : (i + 1) * KC, :] = value
        peak = jnp.max(value, axis=0, keepdims=True)
        top[n] = jnp.maximum(top[n], peak) if n in top else peak

    def weigh(n, i):
        key = blocks[n][1][i]
        prob = jnp.exp2(st[n % 2, i * KC : (i + 1) * KC, :] - top[n])
        part = jnp.sum(prob, axis=0, keepdims=True)
        value = dot(vs[:, key : key + KC], prob.astype(BF), 1, 0)
        acc[n] = acc[n] + value if n in acc else value
        norm[n] = norm[n] + part if n in norm else part

    for i in range(len(blocks[0][1])):
        scores(0, i)
    for n, (start, chunks) in enumerate(blocks):
        ahead = len(blocks[n + 1][1]) if n + 1 < len(blocks) else 0
        for i in range(max(len(chunks), ahead)):
            if i < ahead:
                scores(n + 1, i)
            if i < len(chunks):
                weigh(n, i)
        cf_ref[:, start : start + QB] = acc[n] / norm[n]
        lse_ref[:, start : start + QB] = top[n] + jnp.log2(norm[n])
    cs[...] = roll_cont(cf_ref[...], shift).astype(BF)
    tok = total // 4
    for j, out in enumerate((o0, o1, o2, o3)):
        first = pl.multiple_of(xor(own, j) * tok, 128)
        out[...] = cs[:, pl.ds(first, tok)]


def attention(pref, qkv):
    total = qkv.shape[1]
    heads = HEADS // 4
    hdim = qkv.shape[0] // (3 * heads)
    rows = qkv.shape[0] // 3
    scale = LOG2E / hdim**0.5
    return call(
        lambda *refs: attention_kernel(scale, *refs),
        pref,
        [qkv] * 3,
        [pl.BlockSpec((hdim, total), lambda h, i, o=o: (h + o * heads, 0)) for o in range(3)],
        [shape_of((rows, total // 4), BF)] * 4
        + [shape_of((rows, total), F32), shape_of((heads, 1, total), F32)],
        [pl.BlockSpec((hdim, total // 4), lambda h, i: (h, 0))] * 4
        + [
            pl.BlockSpec((hdim, total), lambda h, i: (h, 0)),
            pl.BlockSpec((None, 1, total), lambda h, i: (h, 0, 0)),
        ],
        (heads,),
        [pltpu.VMEM((hdim, total), BF)] * 4 + [pltpu.VMEM((2, PROMPT + LONG, QB), F32)],
        16 * 10**9,
        12 * 10**6,
    )


def thirds(values):
    high = values.astype(BF).astype(F32)
    middle = (values - high).astype(BF).astype(F32)
    low = values - high - middle
    row = lax.broadcasted_iota(jnp.int32, (AUG, values.shape[1]), 0)
    value = jnp.where(row == 0, high, jnp.where(row == 1, middle, jnp.where(row == 2, low, 0.0)))
    return value.astype(BF)


def attention_back_kernel(
    scale, pref, q_ref, k_ref, v_ref, g0, g1, g2, g3, cf_ref, lse_ref,
    d0, d1, d2, d3, qa, ka, va, ga, gs, dqs, dks, dvs,
):
    own, shift, border = pref[0], pref[1], pref[2]
    hdim, total = q_ref.shape
    tok = total // 4
    cont = total - PROMPT
    others = PROMPT + LONG
    back = lax.rem(cont - shift, cont)
    for j, ref in enumerate((g0, g1, g2, g3)):
        first = pl.multiple_of(xor(own, j) * tok, 128)
        gs[:, pl.ds(first, tok)] = ref[...].astype(F32)
    qa[:hdim, :] = roll_cont(q_ref[...].astype(F32), back).astype(BF)
    ka[:hdim, :] = roll_cont(k_ref[...].astype(F32), back).astype(BF)
    va[:hdim, :] = roll_cont(v_ref[...].astype(F32), back).astype(BF)
    grad = roll_cont(gs[...], back)
    ga[:hdim, :] = grad.astype(BF)
    ga[hdim:, :] = thirds(-jnp.sum(grad * cf_ref[...], axis=0, keepdims=True))
    qa[hdim:, :] = thirds(lse_ref[...] * (-1.0 / scale))
    row = lax.broadcasted_iota(jnp.int32, (AUG, total), 0)
    ones = jnp.where(row < 3, 1.0, 0.0).astype(BF)
    ka[hdim:, :] = ones
    va[hdim:, :] = ones
    seen = set()
    for start, parts in block_list(total, QB):
        queries = slice(start, start + QB)
        grad_q = None
        for lo, hi in parts:
            for key in range(lo, hi, KB):
                keys = slice(key, key + KB)
                value = dot(qa[:, queries], ka[:, keys], 0, 0) * scale
                if lo >= others:
                    mask = same_segment((QB, KB), 1, key - others, start - others, border)
                    value = jnp.where(mask, value, -1e30)
                prob = jnp.exp2(value)
                grad_p = dot(ga[:, queries], va[:, keys], 0, 0)
                grad_s = (prob * grad_p).astype(BF)
                grad_v = dot(ga[:hdim, queries], prob.astype(BF), 1, 0)
                grad_k = dot(qa[:hdim, queries], grad_s, 1, 0)
                part = dot(ka[:hdim, keys], grad_s, 1, 1)
                grad_q = part if grad_q is None else grad_q + part
                if key in seen:
                    dvs[:, keys] += grad_v
                    dks[:, keys] += grad_k
                else:
                    dvs[:, keys] = grad_v
                    dks[:, keys] = grad_k
                    seen.add(key)
        dqs[:, queries] = grad_q
    inv = 1.0 / hdim**0.5
    for part, (ref, factor) in enumerate(((dqs, inv), (dks, inv), (dvs, 1.0))):
        gs[...] = roll_cont(ref[...] * factor, shift)
        for j, out in enumerate((d0, d1, d2, d3)):
            first = pl.multiple_of(xor(own, j) * tok, 128)
            out[part] = gs[:, pl.ds(first, tok)].astype(BF)


def attention_back(pref, qkv, grads, ctx, lse):
    total = qkv.shape[1]
    heads = HEADS // 4
    hdim = qkv.shape[0] // (3 * heads)
    rows = qkv.shape[0] // 3
    scale = LOG2E / hdim**0.5
    quarter = pl.BlockSpec((hdim, total // 4), lambda h, i: (h, 0))
    return call(
        lambda *refs: attention_back_kernel(scale, *refs),
        pref,
        [qkv] * 3 + list(grads) + [ctx, lse],
        [pl.BlockSpec((hdim, total), lambda h, i, o=o: (h + o * heads, 0)) for o in range(3)]
        + [quarter] * 4
        + [
            pl.BlockSpec((hdim, total), lambda h, i: (h, 0)),
            pl.BlockSpec((None, 1, total), lambda h, i: (h, 0, 0)),
        ],
        [shape_of((3, rows, total // 4), BF)] * 4,
        [pl.BlockSpec((3, hdim, total // 4), lambda h, i: (0, h, 0))] * 4,
        (heads,),
        [pltpu.VMEM((hdim + AUG, total), BF)] * 4 + [pltpu.VMEM((hdim, total), F32)] * 4,
        30 * 10**9,
        12 * 10**6,
    )


def normalize(values):
    centre = jnp.mean(values, axis=-1, keepdims=True)
    shifted = values - centre
    spread = jnp.mean(shifted * shifted, axis=-1, keepdims=True)
    inv = lax.rsqrt(spread + EPS)
    return shifted * inv, inv


def normalize_back(grad, normed, inv):
    first = jnp.mean(grad, axis=-1, keepdims=True)
    second = jnp.mean(grad * normed, axis=-1, keepdims=True)
    return (grad - first - normed * second) * inv


def total_rows(values):
    return jnp.sum(values, axis=0, keepdims=True)


def gather_ctx(own, pieces, ctx):
    rows = pieces[0].shape[0]
    for j, ref in enumerate(pieces):
        first = pl.multiple_of(xor(own, j) * rows, 64)
        ctx[pl.ds(first, rows), :] = ref[...]


def student_kernel(
    pref, c0, c1, c2, c3, x, w_out, w_up, w_down, b_out, b_up, b_down, gain, shift,
    ctx, act_one, normed_one, inv_one, gelu, slope, result, normed_two, inv_two,
    acc, mid,
):
    step = pl.program_id(0)

    @pl.when(step == 0)
    def _():
        gather_ctx(pref[0], (c0, c1, c2, c3), ctx)
        res = x[...].astype(F32) + (dot(ctx[...], w_out[...], 0, 1) + b_out[...])
        normed, inv = normalize(res)
        normed_one[...] = normed
        inv_one[...] = inv
        middle = normed * gain[0:1] + shift[0:1]
        mid[...] = middle
        act_one[...] = jnp.clip(middle, -CLIP, CLIP).astype(BF)
        acc[...] = jnp.zeros_like(acc)

    pre = dot(act_one[...], w_up[...], 1, 1) + b_up[...]
    cdf = 0.5 * (1.0 + lax.erf(pre * 0.5**0.5))
    act = (pre * cdf).astype(BF)
    gelu[...] = act
    slope[...] = (cdf + pre * (jnp.exp(pre * pre * -0.5) * 0.3989422804014327)).astype(BF)
    acc[...] += dot(act, w_down[...], 1, 1)

    @pl.when(step == pl.num_programs(0) - 1)
    def _():
        normed, inv = normalize(mid[...] + (acc[...] + b_down[...]))
        normed_two[...] = normed
        inv_two[...] = inv
        result[...] = (normed * gain[1:2] + shift[1:2]).astype(BF)


def ffn_specs(tok, width, hidden):
    up = pl.BlockSpec((FC, width), lambda c, i: (c, 0))
    down = pl.BlockSpec((width, FC), lambda c, i: (0, c))
    wide = pl.BlockSpec((tok, FC), lambda c, i: (0, c))
    row = pl.BlockSpec((1, FC), lambda c, i: (0, c))
    return up, down, wide, row


def student_ffn(pref, pieces, x, w_out, w_up, w_down, b_out, b_up, b_down, gain, shift):
    tok, width = x.shape
    hidden = w_up.shape[0]
    up, down, wide, row = ffn_specs(tok, width, hidden)
    full, one = whole((tok, width)), whole((tok, 1))
    return call(
        student_kernel,
        pref,
        list(pieces) + [x, w_out, w_up, w_down, b_out, b_up, b_down, gain, shift],
        [whole(pieces[0].shape)] * 4
        + [full, whole(w_out.shape), up, down, whole((1, width)), row, whole((1, width))]
        + [whole((2, width))] * 2,
        [
            shape_of((width, tok), BF),
            shape_of((tok, width), BF),
            shape_of((tok, width), F32),
            shape_of((tok, 1), F32),
            shape_of((tok, hidden), BF),
            shape_of((tok, hidden), BF),
            shape_of((tok, width), BF),
            shape_of((tok, width), F32),
            shape_of((tok, 1), F32),
        ],
        [whole((width, tok)), full, full, one, wide, wide, full, full, one],
        (hidden // FC,),
        [pltpu.VMEM((tok, width), F32)] * 2,
        2 * tok * width * (2 * hidden + width),
        2 * tok * hidden,
    )


def teacher_kernel(
    pref, c0, c1, c2, c3, x, w_out, w_up, w_down, gain, shift, normed_two, inv_two,
    grad_sum, grad_ffn, vectors,
    ctx, acc, mid, act_one,
):
    step = pl.program_id(0)

    @pl.when(step == 0)
    def _():
        gather_ctx(pref[0], (c0, c1, c2, c3), ctx)
        res = x[...].astype(F32) + dot(ctx[...], w_out[...], 0, 1)
        normed, inv = normalize(res)
        mid[...] = normed
        act_one[...] = normed.astype(BF)
        acc[...] = jnp.zeros_like(acc)

    pre = dot(act_one[...], w_up[...], 1, 1)
    act = (pre * (0.5 * (1.0 + lax.erf(pre * 0.5**0.5)))).astype(BF)
    acc[...] += dot(act, w_down[...], 1, 1)

    @pl.when(step == pl.num_programs(0) - 1)
    def _():
        target, _unused = normalize(mid[...] + acc[...])
        normed = normed_two[...]
        diff = normed * gain[1:2] + shift[1:2] - target
        back = normalize_back(diff * gain[1:2], normed, inv_two[...])
        grad_sum[...] = back
        low = back.astype(BF)
        grad_ffn[...] = low
        vectors[0:1] = total_rows(diff * normed)
        vectors[1:2] = total_rows(diff)
        vectors[2:3] = total_rows(low.astype(F32))


def teacher_ffn(pref, pieces, x, w_out, w_up, w_down, gain, shift, normed_two, inv_two):
    tok, width = x.shape
    hidden = w_up.shape[0]
    up, down, wide, row = ffn_specs(tok, width, hidden)
    full, one = whole((tok, width)), whole((tok, 1))
    return call(
        teacher_kernel,
        pref,
        list(pieces) + [x, w_out, w_up, w_down, gain, shift, normed_two, inv_two],
        [whole(pieces[0].shape)] * 4
        + [full, whole(w_out.shape), up, down]
        + [whole((2, width))] * 2
        + [full, one],
        [shape_of((tok, width), F32), shape_of((tok, width), BF), shape_of((3, width), F32)],
        [full, full, whole((3, width))],
        (hidden // FC,),
        [pltpu.VMEM((width, tok), BF)]
        + [pltpu.VMEM((tok, width), F32)] * 2
        + [pltpu.VMEM((tok, width), BF)],
        2 * tok * width * (2 * hidden + width),
        tok * hidden,
    )


def back_kernel(
    pref, grad_ffn, slope, w_up, w_down, grad_sum, normed_one, inv_one, gain, shift, w_out,
    grad_hidden, grad_bias, grad_res, grad_attn, g0, g1, g2, g3, vectors,
    acc, ctx,
):
    step = pl.program_id(0)

    @pl.when(step == 0)
    def _():
        acc[...] = jnp.zeros_like(acc)

    low = (dot(grad_ffn[...], w_down[...], 1, 0) * slope[...].astype(F32)).astype(BF)
    grad_hidden[...] = low
    grad_bias[...] = total_rows(low.astype(F32))
    acc[...] += dot(low, w_up[...], 1, 0)

    @pl.when(step == pl.num_programs(0) - 1)
    def _():
        normed = normed_one[...]
        middle = normed * gain[0:1] + shift[0:1]
        grad = grad_sum[...] + jnp.where(jnp.abs(middle) < CLIP, acc[...], 0.0)
        back = normalize_back(grad * gain[0:1], normed, inv_one[...])
        grad_res[...] = back
        attn = back.astype(BF)
        grad_attn[...] = attn
        vectors[0:1] = total_rows(grad * normed)
        vectors[1:2] = total_rows(grad)
        vectors[2:3] = total_rows(attn.astype(F32))
        ctx[...] = dot(w_out[...], attn, 0, 1).astype(BF)
        rows = g0.shape[0]
        for j, ref in enumerate((g0, g1, g2, g3)):
            first = pl.multiple_of(xor(pref[0], j) * rows, 64)
            ref[...] = ctx[pl.ds(first, rows), :]


def student_back(pref, grad_ffn, slope, w_up, w_down, grad_sum, normed_one, inv_one, gain, shift, w_out):
    tok, width = grad_ffn.shape
    hidden = w_up.shape[0]
    up, down, wide, row = ffn_specs(tok, width, hidden)
    full, one = whole((tok, width)), whole((tok, 1))
    return call(
        back_kernel,
        pref,
        [grad_ffn, slope, w_up, w_down, grad_sum, normed_one, inv_one, gain, shift, w_out],
        [full, wide, up, down, full, full, one] + [whole((2, width))] * 2 + [whole(w_out.shape)],
        [
            shape_of((tok, hidden), BF),
            shape_of((1, hidden), F32),
            shape_of((tok, width), F32),
            shape_of((tok, width), BF),
        ]
        + [shape_of((width // 4, tok), BF)] * 4
        + [shape_of((3, width), F32)],
        [wide, row, full, full] + [whole((width // 4, tok))] * 4 + [whole((3, width))],
        (hidden // FC,),
        [pltpu.VMEM((tok, width), F32), pltpu.VMEM((width, tok), BF)],
        2 * tok * width * (2 * hidden + width),
    )


def weight_grad_kernel(
    pref, grad_ffn, gelu, grad_hidden, act_one, grad_attn, ctx, grad_down, grad_up, grad_out
):
    @pl.when(pl.program_id(0) == 0)
    def _():
        value = dot(grad_attn[...], ctx[...], 0, 1).astype(BF)
        grad_out[...] = value.reshape(grad_out.shape)

    value = dot(grad_ffn[...], gelu[...], 0, 0).astype(BF)
    grad_down[...] = value.reshape(grad_down.shape)
    value = dot(grad_hidden[...], act_one[...], 0, 0).astype(BF)
    grad_up[...] = value.reshape(grad_up.shape)


def weight_grads(pref, grad_ffn, gelu, grad_hidden, act_one, grad_attn, ctx):
    tok, width = grad_ffn.shape
    hidden = gelu.shape[1]
    count, half = hidden // width, width // 2
    wide = pl.BlockSpec((tok, width), lambda c, i: (0, c))
    full = whole((tok, width))
    return call(
        weight_grad_kernel,
        pref,
        [grad_ffn, gelu, grad_hidden, act_one, grad_attn, ctx],
        [full, wide, wide, full, full, whole((width, tok))],
        [
            shape_of((2, count, half, width), BF),
            shape_of((2 * count, half, width), BF),
            shape_of((2, half, width), BF),
        ],
        [
            pl.BlockSpec((2, 1, half, width), lambda c, i: (0, c, 0, 0)),
            pl.BlockSpec((2, half, width), lambda c, i: (c, 0, 0)),
            whole((2, half, width)),
        ],
        (count,),
        [],
        2 * tok * width * (2 * hidden + width),
    )


def qkv_grad_kernel(pref, d0, d1, d2, d3, x0, x1, x2, x3, out, sums):
    own = pref[0]
    total = None
    count = None
    ones = jnp.ones((8, d0.shape[1]), BF)
    for grad, x in zip((d0, d1, d2, d3), (x0, x1, x2, x3)):
        value = grad[...]
        part = dot(value, jnp.clip(x[...], -CLIP, CLIP), 1, 0)
        line = dot(ones, value, 1, 1)
        total = part if total is None else total + part
        count = line if count is None else count + line
    out[...] = total.astype(BF)
    sums[...] = jnp.zeros_like(sums)
    rows = out.shape[0]
    for j in range(4):

        @pl.when(own == j)
        def _():
            sums[:, j * rows : (j + 1) * rows] = count


def qkv_grad(pref, grads, slots):
    tok, width = slots[0].shape
    rows = grads[0].shape[1]
    return call(
        qkv_grad_kernel,
        pref,
        list(grads) + list(slots),
        [pl.BlockSpec((None, rows, tok), lambda o, i: (o, 0, 0))] * 4 + [whole((tok, width))] * 4,
        [shape_of((3, rows, width), BF), shape_of((3, 8, width), F32)],
        [
            pl.BlockSpec((None, rows, width), lambda o, i: (o, 0, 0)),
            pl.BlockSpec((None, 8, width), lambda o, i: (o, 0, 0)),
        ],
        (3,),
        [],
        2 * 4 * tok * width * 3 * rows,
    )


def input_grad_kernel(pref, e0, e1, e2, e3, wq, wk, wv, grad_res, x, out, acc):
    slot = pl.program_id(0)

    @pl.when(slot == 0)
    def _():
        acc[...] = jnp.zeros_like(acc)

    for j, ref in enumerate((e0, e1, e2, e3)):

        @pl.when(slot == j)
        def _():
            part = dot(ref[0], wq[...], 0, 0)
            part = part + dot(ref[1], wk[...], 0, 0)
            acc[...] += part + dot(ref[2], wv[...], 0, 0)

    @pl.when(slot == 3)
    def _():
        size = jnp.abs(x[...].astype(F32))
        pull = jnp.where(size < CLIP, 1.0, jnp.where(size == CLIP, 0.5, 0.0))
        out[...] = (grad_res[...] + acc[...] * pull).astype(BF)


def input_grad(pref, pieces, weight, grad_res, x):
    tok, width = x.shape
    rows = pieces[0].shape[1]
    full = whole((tok, width))
    return call(
        input_grad_kernel,
        pref,
        list(pieces) + [weight] * 3 + [grad_res, x],
        [whole((3, rows, tok))] * 4
        + [
            pl.BlockSpec((rows, width), lambda j, i, o=o: (o * 4 + lax.bitwise_xor(i[0], j), 0))
            for o in range(3)
        ]
        + [full, full],
        shape_of((tok, width), BF),
        full,
        (4,),
        [pltpu.VMEM((tok, width), F32)],
        2 * 4 * tok * width * 3 * rows,
    )


def place(bit):
    name, mask = bit
    at = lax.axis_index(name)
    upper = lax.rem(lax.div(at, jnp.int32(mask)), jnp.int32(2))
    return upper, {name: at + mask * (1 - 2 * upper)}


def greet(bits):
    barrier = pltpu.get_barrier_semaphore()
    for bit in bits:
        pl.semaphore_signal(
            barrier, inc=1, device_id=place(bit)[1], device_id_type=pl.DeviceIdType.MESH
        )
    pl.semaphore_wait(barrier, len(bits))


class Copies:
    def __init__(self, send, recv, local):
        self.send, self.recv, self.local_sem = send, recv, local
        self.sent, self.planned, self.kept = [], 0, 0

    def plan(self, source, target, device):
        n = self.planned
        self.planned += 1
        return pltpu.make_async_remote_copy(
            src_ref=source,
            dst_ref=target,
            send_sem=self.send.at[n],
            recv_sem=self.recv.at[n],
            device_id=device,
            device_id_type=pl.DeviceIdType.MESH,
        )

    def remote(self, source, target, device):
        copy = self.plan(source, target, device)
        copy.start()
        self.sent.append(copy)
        return copy

    def plan_local(self, source, target):
        self.kept += 1
        return pltpu.make_async_copy(source, target, self.local_sem.at[self.kept - 1])

    def local(self, source, target):
        copy = self.plan_local(source, target)
        copy.start()
        return copy

    def finish(self):
        for copy in self.sent:
            copy.wait_send()


def window(ref, region):
    row, rows, col, cols = region
    return ref.at[pl.ds(row, rows), pl.ds(col, cols)]


def add_window(target, left, right, region, start):
    row, rows, col, cols = region
    step = 48 if rows % 48 == 0 else 16

    def body(i, carry):
        there = pl.ds(pl.multiple_of(row + i * step, 16), step)
        here = pl.ds(pl.multiple_of(start + i * step, 16), step)
        value = left[there, pl.ds(col, cols)].astype(F32) + right[here, :cols].astype(F32)
        target[there, pl.ds(col, cols)] = value.astype(target.dtype)
        return carry

    lax.fori_loop(0, rows // step, body, 0)


def scatter_sum(copies, work, far, full, bits):
    rows, cols = work.shape
    region, used, parts = (0, rows, 0, cols), 0, []
    for n, bit in enumerate(bits):
        upper, device = place(bit)
        row, rows, col, cols = region
        if (rows // 2) % 16 == 0:
            rows //= 2
            kept = (pl.multiple_of(row + upper * rows, 16), rows, col, cols)
            sent = (pl.multiple_of(row + (1 - upper) * rows, 16), rows, col, cols)
        else:
            cols //= 2
            kept = (row, rows, pl.multiple_of(col + upper * cols, 128), cols)
            sent = (row, rows, pl.multiple_of(col + (1 - upper) * cols, 128), cols)
        slot = far.at[pl.ds(used, rows), pl.ds(0, cols)]
        copy = copies.remote(window(work, sent), slot, device)
        yield
        copy.wait_recv()
        add_window(full if n == len(bits) - 1 else work, work, far, kept, used)
        used += rows
        region = kept
        parts.append((bit, kept))
    return parts


def sum_flow(copies, own, other, work, near, far, full, result, core, bits):
    copy = copies.remote(other, near, place(core)[1])
    load = copies.local(own, work)
    yield
    copy.wait_recv()
    load.wait()
    add_window(work, work, near, (0, work.shape[0], 0, work.shape[1]), 0)
    parts = yield from scatter_sum(copies, work, far, full, bits)
    for bit, kept in reversed(parts):
        copy = copies.remote(window(full, kept), window(full, kept), place(bit)[1])
        yield
        copy.wait_recv()
    store = copies.local(full, result)
    yield
    store.wait()


def vector_flow(copies, sums, far, bits):
    for n, bit in enumerate(bits):
        yield
        copy = copies.remote(sums.at[n], far.at[n], place(bit)[1])
        yield
        copy.wait_recv()
        sums[n + 1] = sums[n] + far[n]


def run_flows(flows, step):
    events = []
    for delay, flow in flows:
        next(flow)
        events.append([delay, len(events), flow])
    while events:
        events.sort(key=lambda e: e[:2])
        event = events[0]
        try:
            next(event[2])
            event[0] += step
        except StopIteration:
            events.pop(0)


def rotate(items, count):
    count %= len(items)
    return items[count:] + items[:count]


def sum_kernel(
    dp, seq, core, down, up, out, two, one, bias, heads, down_sum, up_sum, out_sum, totals,
    work, near, far, full, sums, sums_far, send, recv, local,
):
    greet(dp + seq + [core])
    copies = Copies(send, recv, local)
    side_of = place(core)[0]
    count, half, width = down.shape[1:]
    pieces = [(up.at[side_of, p], up.at[1 - side_of, p], up_sum.at[p]) for p in range(count)]
    pieces += [
        (
            down.at[side_of, p],
            down.at[1 - side_of, p],
            down_sum.at[:, pl.ds(p * width, width)],
        )
        for p in range(count)
    ]
    pieces.append((out.at[side_of], out.at[1 - side_of], out_sum))
    first = dp + seq[:1]
    flows = []
    for n, (own, other, result) in enumerate(pieces):
        bits = rotate(first, n) + seq[1:]
        flow = sum_flow(
            copies, own, other, work.at[n], near.at[n], far.at[n], full.at[n], result, core, bits
        )
        flows.append((n // len(first), flow))
    sums[0] = jnp.zeros(sums.shape[1:], F32)
    sums[0, 0:1] = heads[0, 0:1]
    sums[0, 1:2] = heads[2, 0:1]
    sums[0, 2:3] = one[2:3]
    sums[0, 3:4] = two[2:3]
    sums[0, 4:5] = one[0:1]
    sums[0, 5:6] = two[0:1]
    sums[0, 6:7] = one[1:2]
    sums[0, 7:8] = two[1:2]
    for p in range(count):
        sums[0, 8 + p : 9 + p] = bias[:, p * width : (p + 1) * width]
    flows.append((0.5, vector_flow(copies, sums, sums_far, [core] + dp + seq)))
    run_flows(flows, 1.5)
    totals[...] = sums[sums.shape[0] - 1]
    copies.finish()


def remote_call(kernel, args, in_specs, outs, out_specs, scratch, copies, local, number):
    sems = pltpu.SemaphoreType.DMA
    return pl.pallas_call(
        kernel,
        in_specs=in_specs,
        out_specs=out_specs,
        out_shape=outs,
        scratch_shapes=scratch + [sems((copies,)), sems((copies,)), sems((local,))],
        compiler_params=pltpu.CompilerParams(
            vmem_limit_bytes=VMEM_LIMIT, collective_id=number, has_side_effects=True
        ),
        cost_estimate=pl.CostEstimate(flops=5 * 10**10, bytes_accessed=10**8, transcendentals=0),
    )(*args)


ANY = pl.BlockSpec(memory_space=pl.ANY)
IN_VMEM = pl.BlockSpec(memory_space=pltpu.VMEM)


def sum_grads(dp, seq, core, down, up, out, two, one, bias, heads):
    sides, count, half, width = down.shape
    pieces, steps = 2 * count + 1, len(dp) + len(seq)
    lines = 16
    return remote_call(
        lambda *refs: sum_kernel(dp, seq, core, *refs),
        [down, up, out, two, one, bias, heads],
        [ANY] * 3 + [IN_VMEM] * 4,
        [
            shape_of((half, count * width), BF),
            shape_of((count, half, width), BF),
            shape_of((half, width), BF),
            shape_of((lines, width), F32),
        ],
        [ANY] * 3 + [IN_VMEM],
        [pltpu.VMEM((pieces, half, width), BF)] * 4
        + [pltpu.VMEM((steps + 2, lines, width), F32), pltpu.VMEM((steps + 1, lines, width), F32)],
        pieces * (1 + 2 * steps) + steps + 1,
        2 * pieces,
        1,
    )


def head_sum_kernel(dp, seq, core, heads, result, work, far, full, send, recv, local):
    greet(dp + seq + [core])
    copies = Copies(send, recv, local)
    side_of, partner = place(core)
    along = place(seq[0])[0]
    rows = dp + seq[1:]

    def flow(n):
        if n == 1:
            copy = copies.remote(heads.at[2 - 2 * side_of], work.at[n], partner)
            yield
            copy.wait_recv()
        else:
            load = copies.local(heads.at[n // 2 + side_of], work.at[n])
            yield
            load.wait()
        bits = (rotate(dp, n) if n < 2 else dp) + seq[1:]
        mine = full.at[2 * n + along]
        parts = yield from scatter_sum(copies, work.at[n], far.at[n], mine, bits)
        steps = [(bit, kept, False) for bit, kept in reversed(parts)]
        cut = len(steps) if n == 2 else 1
        held = steps[cut][1] if n < 2 else (0, mine.shape[0], 0, mine.shape[1])
        steps = steps[:cut] + [(seq[0], held, False)] + [(b, k, True) for b, k, _ in steps[cut:]]
        for bit, (row, size, col, cols), both in steps:
            first, count = (2 * n, 2) if both else (2 * n + along, 1)
            part = full.at[pl.ds(first, count), pl.ds(row, size), pl.ds(col, cols)]
            copy = copies.remote(part, part, place(bit)[1])
            yield
            copy.wait_recv()
        store = copies.local(full.at[pl.ds(2 * n, 2)], result.at[pl.ds(2 * n, 2)])
        yield
        store.wait()

    run_flows([(0, flow(0)), (0, flow(2)), (0, flow(1))], 1.0)
    copies.finish()


def head_sums_of(dp, seq, core, heads):
    _, rows, width = heads.shape
    steps = len(dp) + len(seq) - 1
    return remote_call(
        lambda *refs: head_sum_kernel(dp, seq, core, *refs),
        [heads],
        [ANY],
        shape_of((6, rows, width), BF),
        ANY,
        [pltpu.VMEM((3, rows, width), BF)] * 2 + [pltpu.VMEM((6, rows, width), BF)],
        3 * (2 * steps + 1) + 1,
        5,
        2,
    )


def binarize_rows(source, target):
    rows, cols = target.shape
    step = 96 if cols < 2048 else 32

    def body(i, carry):
        at = pl.ds(pl.multiple_of(i * step, 16), step)
        value = source[at, :]
        scale = jnp.sum(jnp.abs(value), axis=1, keepdims=True) * (1.0 / cols)
        signed = jnp.where(value > 0, scale, jnp.where(value < 0, -scale, 0.0))
        target[at, :] = signed.astype(BF)
        return carry

    lax.fori_loop(0, rows // step, body, 0)


def entry_kernel(
    seq, core, hidden, teach, l_qkv, l_out, l_up, l_down, t_qkv, t_out, t_up, t_down, bias,
    o_qkv, x0, x1, x2, x3, o_teach, b_qkv, b_out, b_up, b_down, e_qkv, e_out, e_up, e_down,
    xs, held, w_qkv, w_out, w_up, w_down, f_qkv, f_out, f_up, f_down,
    s_qkv, s_out, s_up, s_down, proj, send, recv, local,
):
    tok, width = hidden.shape
    parts, size = 4, tok // 4
    along, next_chip = place(seq[0])
    side_of, sibling = place(core)
    half = lax.div(lax.axis_index("seq"), jnp.int32(2))
    stays = half == side_of
    moves = half != side_of
    partner = {"seq": 2 * side_of + along, "fsdp": half}
    mesh = pl.DeviceIdType.MESH

    barrier = pltpu.get_barrier_semaphore()
    for device in (next_chip, sibling):
        pl.semaphore_signal(barrier, inc=1, device_id=device, device_id_type=mesh)

    @pl.when(moves)
    def _():
        pl.semaphore_signal(barrier, inc=1, device_id=partner, device_id_type=mesh)
        pl.semaphore_wait(barrier, 3)

    @pl.when(stays)
    def _():
        pl.semaphore_wait(barrier, 2)

    copies = Copies(send, recv, local)
    cuts = [pl.ds(c * size, size) for c in range(parts)]
    swap = [copies.plan(hidden.at[cut], xs.at[0, cut], partner) for cut in cuts]
    load = [copies.plan_local(hidden.at[cut], xs.at[0, cut]) for cut in cuts]
    over = [copies.plan(xs.at[0, cut], xs.at[1, cut], next_chip) for cut in cuts]
    beside = [copies.plan(xs.at[0, cut], xs.at[2, cut], sibling) for cut in cuts]
    relay = [copies.plan(xs.at[1, cut], xs.at[3, cut], sibling) for cut in cuts]
    t_swap = copies.plan(teach, held, partner)
    t_load = copies.plan_local(teach, held)

    @pl.when(moves)
    def _():
        for copy in swap:
            copy.start()

    @pl.when(stays)
    def _():
        for copy in load:
            copy.start()
        t_load.start()

    latent = [
        (copies.local(source, target), target)
        for source, target in ((l_qkv, f_qkv), (l_out, f_out), (l_up, f_up), (l_down, f_down))
    ]
    staged = [
        (copies.local(source, target), target, result)
        for source, target, result in (
            (t_qkv, s_qkv, e_qkv),
            (t_out, s_out, e_out),
            (t_up, s_up, e_up),
            (t_down, s_down, e_down),
        )
    ]

    @pl.when(stays)
    def _():
        for c in range(parts):
            load[c].wait()
            over[c].start()
            beside[c].start()

    rows_qkv = l_qkv.shape[0]
    mine = w_qkv.at[pl.ds(pl.multiple_of(side_of * rows_qkv, 16), rows_qkv)]
    latent[0][0].wait()
    binarize_rows(f_qkv, mine)
    qkv_copy = copies.remote(mine, mine, sibling)
    stores, arrivals = [], []
    for (copy, source), target, result in zip(
        latent[1:], (w_out, w_up, w_down), (b_out, b_up, b_down)
    ):
        copy.wait()
        binarize_rows(source, target)
        arrivals.append(copies.remote(target, result.at[side_of], sibling))
        stores.append(copies.local(target, result.at[side_of]))
    for source, (_, _, result) in zip((t_qkv, t_out, t_up, t_down), staged):
        arrivals.append(copies.remote(source, result.at[side_of], sibling))
    for copy, target, result in staged:
        copy.wait()
        stores.append(copies.local(target, result.at[side_of]))

    @pl.when(moves)
    def _():
        for c in range(parts):
            swap[c].wait_recv()
            over[c].start()
            beside[c].start()
        t_swap.start()

    qkv_copy.wait_recv()
    stores.append(copies.local(w_qkv, b_qkv))
    rows = width // 4
    own = along + 2 * side_of

    def project(slot):
        act = jnp.clip(xs[slot], -CLIP, CLIP)
        first = (1 - along if slot % 2 else along) + 2 * (1 - side_of if slot // 2 else side_of)
        there = pl.ds(pl.multiple_of(first * tok, 128), tok)
        for part in range(3):
            at = pl.multiple_of(part * width + own * rows, 16)
            value = dot(w_qkv[pl.ds(at, rows), :], act, 1, 1)
            if part != 1:
                value = value + bias[part // 2, pl.ds(pl.multiple_of(own * rows, 8), rows), :]
            proj[part * rows : (part + 1) * rows, there] = value.astype(BF)
        stores.append(copies.local(proj.at[:, there], o_qkv.at[:, there]))
        stores.append(copies.local(xs.at[slot], (x0, x1, x2, x3)[slot]))

    project(0)
    for copy in beside:
        copy.wait_recv()
    project(2)
    for c in range(parts):
        over[c].wait_recv()
        relay[c].start()
    project(1)
    for copy in relay:
        copy.wait_recv()
    project(3)

    @pl.when(moves)
    def _():
        t_swap.wait_recv()

    @pl.when(stays)
    def _():
        t_load.wait()

    stores.append(copies.local(held, o_teach))
    for copy in arrivals:
        copy.wait_recv()
    for copy in stores:
        copy.wait()

    @pl.when(moves)
    def _():
        for copy in swap + [t_swap]:
            copy.wait_send()

    for copy in over + beside + relay:
        copy.wait_send()
    copies.finish()


def entry(seq, core, hidden, teach, latents, teachers, bias):
    tok, width = hidden.shape
    halves = [w.shape for w in latents]
    sides = [shape_of((2,) + shape, BF) for shape in halves]
    own = [pltpu.VMEM(shape, BF) for shape in halves]
    sides[0] = shape_of((2 * halves[0][0], halves[0][1]), BF)
    sides_t = [shape_of((2,) + shape, BF) for shape in halves]
    outs = remote_call(
        lambda *refs: entry_kernel(seq, core, *refs),
        [hidden, teach] + list(latents) + list(teachers) + [bias],
        [ANY] * 10 + [IN_VMEM],
        [shape_of((3 * width // 4, 4 * tok), BF)]
        + [shape_of((tok, width), BF)] * 5
        + sides
        + sides_t,
        [ANY] * 14,
        [pltpu.VMEM((4, tok, width), BF), pltpu.VMEM((tok, width), BF)]
        + [pltpu.VMEM(sides[0].shape, BF)]
        + own[1:]
        + [pltpu.VMEM(shape, F32) for shape in halves]
        + own
        + [pltpu.VMEM((3 * width // 4, 4 * tok), BF)],
        25,
        30,
        3,
    )
    qkv, x0, x1, x2, x3, teach = outs[:6]
    weights = [w.reshape((-1, w.shape[-1])) for w in outs[6:]]
    return qkv, (x0, x1, x2, x3), teach, weights[:4], weights[4:]


def binarize(latent):
    row_scale = jnp.mean(jnp.abs(latent), axis=1, keepdims=True)
    return (row_scale * jnp.sign(latent)).astype(BF)


def segment_info(segments):
    sizes_of = [jnp.sum((segments == k).astype(jnp.int32)) for k in (1, 2, 3)]
    first, second, third = sizes_of
    shift = jnp.where(first == LONG, 0, jnp.where(second == LONG, first, first + second))
    border = jnp.where(first == LONG, second, jnp.where(second == LONG, third, first))
    return jnp.stack([shift, border])


def quarters(own):
    along = to_slot(own, 1)
    return (own, along, to_slot(own, 2), to_slot(along, 2))


def exchange(pieces):
    return (pieces[0],) + tuple(to_slot(pieces[j], j) for j in (1, 2, 3))


def on_device(
    hidden, teacher_hidden, segments, latent_qkv, latent_out, latent_up, latent_down,
    biases, up_bias, norm_gains, norm_shifts, teacher_qkv, teacher_out, teacher_up, teacher_down,
):
    seq_at, fsdp_at = lax.axis_index("seq"), lax.axis_index("fsdp")
    fsdp = lax.axis_size("fsdp")
    core = fsdp_at % 2
    own = (seq_at % 2 + 2 * core).astype(jnp.int32)
    width = hidden.shape[2]

    info = segment_info(segments)
    info = jnp.where(core == seq_at // 2, info, flip(info, fsdp=1))
    pref = jnp.concatenate([own[None], info]).astype(jnp.int32)
    bias_cols = biases[:2].reshape(2, width, 1)
    latents = (latent_qkv, latent_out, latent_up, latent_down)
    teachers = (teacher_qkv, teacher_out, teacher_up, teacher_down)
    if fsdp == 2:
        qkv, x_slots, teach, bins, t_weights = entry(
            bit_list("seq"), bit_list("fsdp")[0], hidden[0], teacher_hidden[0],
            latents, teachers, bias_cols,
        )
        x = x_slots[0]
    else:
        x = swap_groups(hidden[0])
        x_slots = quarters(x)
        bins = [gather_rows(binarize(w)) for w in latents]
        teach = swap_groups(teacher_hidden[0])
        t_weights = [gather_rows(w) for w in teachers]
        qkv = qkv_project(pref, x_slots, bins[0], bias_cols)
    bin_qkv, bin_out, bin_up, bin_down = bins
    t_qkv, t_out, t_up, t_down = t_weights
    t_slots = quarters(teach)

    *ctx_slots, ctx_full, lse = attention(pref, qkv)
    ctx_pieces = exchange(ctx_slots)

    t_heads = qkv_project(pref, t_slots, t_qkv, None)
    *tctx_slots, _unused, _unused_too = attention(pref, t_heads)
    tctx_pieces = exchange(tctx_slots)

    gain, shift = norm_gains, norm_shifts
    (
        ctx, act_one, normed_one, inv_one, gelu, slope, result, normed_two, inv_two,
    ) = student_ffn(
        pref, ctx_pieces, x, bin_out, bin_up, bin_down,
        biases[2:3], up_bias[None], biases[3:4], gain, shift,
    )
    student_out = swap_groups(result)
    grad_sum, grad_ffn, vec_two = teacher_ffn(
        pref, tctx_pieces, teach, t_out, t_up, t_down, gain, shift, normed_two, inv_two
    )
    grad_hidden, grad_up_bias, grad_res, grad_attn, *gctx_slots, vec_one = student_back(
        pref, grad_ffn, slope, bin_up, bin_down, grad_sum, normed_one, inv_one, gain, shift, bin_out
    )
    gctx_pieces = exchange(gctx_slots)
    grad_down, grad_up, grad_out = weight_grads(
        pref, grad_ffn, gelu, grad_hidden, act_one, grad_attn, ctx
    )
    dp_bits, seq_bits, fsdp_bits = bit_list("dp"), bit_list("seq"), bit_list("fsdp")
    dqkv_slots = attention_back(pref, qkv, gctx_pieces, ctx_full, lse)
    dqkv_pieces = exchange(dqkv_slots)
    grad_heads, head_sums = qkv_grad(pref, dqkv_slots, x_slots)
    rows, hidden_units = width // 4, up_bias.shape[0]
    _, count, half, _ = grad_down.shape

    if fsdp == 2:
        total_down, total_up, total_out, vectors = sum_grads(
            dp_bits,
            seq_bits,
            fsdp_bits[0],
            grad_down,
            grad_up.reshape(grad_down.shape),
            grad_out,
            vec_two,
            vec_one,
            grad_up_bias,
            head_sums,
        )
        total_up = total_up.reshape(-1, width)
        hidden_grad = swap_groups(input_grad(pref, dqkv_pieces, bin_qkv, grad_res, x))
        total_qkv = head_sums_of(dp_bits, seq_bits, fsdp_bits[0], grad_heads).reshape(-1, width)
    else:
        hidden_grad = swap_groups(input_grad(pref, dqkv_pieces, bin_qkv, grad_res, x))

        def reduce_grad(value, bits):
            for bit in reversed(fsdp_bits):
                value = halve(value, bit)
            return all_reduce(value, bits)

        grad_down = grad_down.transpose(0, 2, 1, 3).reshape(width, hidden_units)
        total_down = reduce_grad(grad_down, dp_bits + seq_bits)
        total_up = reduce_grad(grad_up.reshape(hidden_units, width), dp_bits[::-1] + seq_bits)
        total_out = reduce_grad(
            grad_out.reshape(width, width), seq_bits[:1] + dp_bits + seq_bits[1:]
        )
        blocks = all_reduce(
            grad_heads.reshape(3 * rows, width), dp_bits + seq_bits[1:] + fsdp_bits[1:]
        )
        blocks = blocks.reshape(1, 3, rows, width)
        blocks = double(double(blocks, seq_bits[0]), fsdp_bits[0])
        whole_qkv = blocks.transpose(1, 0, 2, 3).reshape(3 * width, width)
        part = 3 * width // fsdp
        total_qkv = lax.dynamic_slice_in_dim(whole_qkv, fsdp_at * part, part, 0)
        vectors = jnp.concatenate(
            [
                head_sums[0, :1],
                head_sums[2, :1],
                vec_one[2:3],
                vec_two[2:3],
                vec_one[0:1],
                vec_two[0:1],
                vec_one[1:2],
                vec_two[1:2],
                grad_up_bias.reshape(-1, width),
            ]
        )
        vectors = sum_small(vectors, dp_bits + seq_bits + fsdp_bits)
    hid_bias = vectors[8 : 8 + hidden_units // width].reshape(-1)
    share, hid_share = width // fsdp, hid_bias.shape[0] // fsdp
    cols = lax.dynamic_slice_in_dim(vectors[:8], fsdp_at * share, share, 1)
    return (
        student_out[None],
        hidden_grad[None],
        total_qkv.astype(F32),
        total_out.astype(F32),
        total_up.astype(F32),
        total_down.astype(F32),
        cols[0:4],
        lax.dynamic_slice_in_dim(hid_bias, fsdp_at * hid_share, hid_share, 0),
        cols[4:6],
        cols[6:8],
    )


def solution(mesh):
    tokens = P(("dp", "fsdp"), "seq", None)
    rows = P("fsdp", None)
    return jax.shard_map(
        on_device,
        mesh=mesh,
        in_specs=(tokens, tokens, P(("dp", "fsdp"), None)) + (rows,) * 4 + (P(),) * 4 + (rows,) * 4,
        out_specs=(tokens, tokens)
        + (rows,) * 4
        + (P(None, "fsdp"), P("fsdp"), P(None, "fsdp"), P(None, "fsdp")),
        check_vma=False,
    )
```

```python
import jax
import jax.numpy as jnp
from jax import lax
from jax.experimental import pallas as pl
from jax.experimental.pallas import tpu as pltpu
from jax.sharding import PartitionSpec as P

HEADS = 12
PROMPT = 1024
LONG = 1024
CLIP = 2.5
EPS = 1e-05
AXES = ("dp", "seq", "fsdp")
BF = jnp.bfloat16
F32 = jnp.float32
LOG2E = 1.4426950408889634
QB = 512
KC = 256
KB = 512
FC = 512
AUG = 16
VMEM_LIMIT = 56 * 2**20


def dot(left, right, left_dim, right_dim):
    return lax.dot_general(
        left, right, (((left_dim,), (right_dim,)), ((), ())), preferred_element_type=F32
    )


def xor(first, second):
    return lax.bitwise_xor(first, jnp.int32(second))


def sizes():
    return tuple(lax.axis_size(name) for name in AXES)


def permute(values, target):
    dp, seq, fsdp = sizes()
    pairs = []
    for d in range(dp):
        for s in range(seq):
            for f in range(fsdp):
                td, ts, tf = target(d, s, f)
                pairs.append(((d * seq + s) * fsdp + f, (td * seq + ts) * fsdp + tf))
    return lax.ppermute(values, AXES, pairs)


def flip(values, dp=0, seq=0, fsdp=0):
    return permute(values, lambda d, s, f: (d ^ dp, s ^ seq, f ^ fsdp))


def swap_groups(values):
    return permute(
        values, lambda d, s, f: (d, 2 * (f % 2) + s % 2, f - f % 2 + s // 2)
    )


def to_slot(values, slot):
    return flip(values, seq=slot & 1, fsdp=slot >> 1)


def bit_list(name):
    count = lax.axis_size(name)
    out, bit = [], 1
    while bit < count:
        out.append((name, bit))
        bit *= 2
    return out


def flip_bit(values, bit):
    return flip(values, **{bit[0]: bit[1]})


def side(bit):
    return lax.bitwise_and(lax.axis_index(bit[0]), bit[1]) != 0


def halve(values, bit):
    upper = side(bit).astype(jnp.int32)
    half = values.shape[0] // 2
    sent = lax.dynamic_slice_in_dim(values, (1 - upper) * half, half, 0)
    kept = lax.dynamic_slice_in_dim(values, upper * half, half, 0)
    got = flip_bit(sent, bit)
    return (kept.astype(F32) + got.astype(F32)).astype(values.dtype)


def double(values, bit):
    got = flip_bit(values, bit)
    return jnp.where(
        side(bit),
        jnp.concatenate([got, values], axis=0),
        jnp.concatenate([values, got], axis=0),
    )


def gather_rows(values):
    for bit in bit_list("fsdp"):
        values = double(values, bit)
    return values


def all_reduce(values, bits):
    for bit in bits:
        values = halve(values, bit)
    for bit in reversed(bits):
        values = double(values, bit)
    return values


def sum_small(values, bits):
    for bit in bits:
        values = values + flip_bit(values, bit)
    return values


def whole(shape):
    return pl.BlockSpec(shape, lambda *_: (0,) * len(shape))


def call(kernel, pref, args, in_specs, outs, out_specs, grid, scratch, flops, trans=0):
    moved = sum(a.size * a.dtype.itemsize for a in args)
    moved += sum(o.size * o.dtype.itemsize for o in jax.tree.leaves(outs))
    return pl.pallas_call(
        kernel,
        grid_spec=pltpu.PrefetchScalarGridSpec(
            num_scalar_prefetch=1,
            grid=grid,
            in_specs=in_specs,
            out_specs=out_specs,
            scratch_shapes=scratch,
        ),
        out_shape=outs,
        compiler_params=pltpu.CompilerParams(vmem_limit_bytes=VMEM_LIMIT),
        cost_estimate=pl.CostEstimate(flops=flops, bytes_accessed=moved, transcendentals=trans),
    )(pref, *args)


def shape_of(shape, dtype):
    return jax.ShapeDtypeStruct(shape, dtype)


def qkv_kernel(student, pref, x0, x1, x2, x3, wq, wk, wv, *rest):
    slot = pl.program_id(0)
    out = rest[-1]
    rows = wq.shape[0]
    for j, ref in enumerate((x0, x1, x2, x3)):

        @pl.when(slot == j)
        def _():
            act = ref[...]
            if student:
                act = jnp.clip(act, -CLIP, CLIP)
            for part, weight in enumerate((wq, wk, wv)):
                value = dot(weight[...], act, 1, 1)
                if student and part != 1:
                    value = value + rest[0][part // 2]
                out[part * rows : (part + 1) * rows, :] = value.astype(BF)


def qkv_project(pref, slots, weight, bias):
    tok, width = slots[0].shape
    rows = weight.shape[0] // 12
    specs = [whole((tok, width))] * 4
    specs += [
        pl.BlockSpec((rows, width), lambda j, i, o=o: (o * 4 + i[0], 0)) for o in range(3)
    ]
    args = list(slots) + [weight] * 3
    if bias is not None:
        specs.append(pl.BlockSpec((2, rows, 1), lambda j, i: (0, i[0], 0)))
        args.append(bias)
    return call(
        lambda *refs: qkv_kernel(bias is not None, *refs),
        pref,
        args,
        specs,
        shape_of((3 * rows, 4 * tok), BF),
        pl.BlockSpec((3 * rows, tok), lambda j, i: (0, lax.bitwise_xor(i[0], j))),
        (4,),
        [],
        2 * 4 * tok * width * 3 * rows,
    )


def roll_cont(values, shift):
    return jnp.concatenate(
        [values[:, :PROMPT], pltpu.roll(values[:, PROMPT:], shift, 1)], axis=1
    )


def block_list(total, rows):
    blocks = [(i, [(0, PROMPT)]) for i in range(0, PROMPT, rows)]
    blocks += [(i, [(0, PROMPT + LONG)]) for i in range(PROMPT, PROMPT + LONG, rows)]
    blocks += [
        (i, [(0, PROMPT), (PROMPT + LONG, total)]) for i in range(PROMPT + LONG, total, rows)
    ]
    return blocks


def same_segment(shape, key_axis, key_start, query_start, border):
    keys = lax.broadcasted_iota(jnp.int32, shape, key_axis) + key_start
    queries = lax.broadcasted_iota(jnp.int32, shape, 1 - key_axis) + query_start
    return (keys < border) == (queries < border)


def attention_kernel(scale, pref, q_ref, k_ref, v_ref, o0, o1, o2, o3, cf_ref, lse_ref, qs, ks, vs, cs, st):
    own, shift, border = pref[0], pref[1], pref[2]
    total = q_ref.shape[1]
    cont = total - PROMPT
    others = PROMPT + LONG
    back = lax.rem(cont - shift, cont)
    qs[...] = roll_cont(q_ref[...].astype(F32), back).astype(BF)
    ks[...] = roll_cont(k_ref[...].astype(F32), back).astype(BF)
    vs[...] = roll_cont(v_ref[...].astype(F32), back).astype(BF)
    blocks = []
    for start, parts in block_list(total, QB):
        chunks = [key for lo, hi in parts for key in range(lo, hi, KC)]
        blocks.append((start, chunks))
    top, acc, norm = {}, {}, {}

    def scores(n, i):
        start, chunks = blocks[n]
        key = chunks[i]
        value = dot(ks[:, key : key + KC], qs[:, start : start + QB], 0, 0) * scale
        if key >= others:
            mask = same_segment((KC, QB), 0, key - others, start - others, border)
            value = jnp.where(mask, value, -1e30)
        st[n % 2, i * KC : (i + 1) * KC, :] = value
        peak = jnp.max(value, axis=0, keepdims=True)
        top[n] = jnp.maximum(top[n], peak) if n in top else peak

    def weigh(n, i):
        key = blocks[n][1][i]
        prob = jnp.exp2(st[n % 2, i * KC : (i + 1) * KC, :] - top[n])
        part = jnp.sum(prob, axis=0, keepdims=True)
        value = dot(vs[:, key : key + KC], prob.astype(BF), 1, 0)
        acc[n] = acc[n] + value if n in acc else value
        norm[n] = norm[n] + part if n in norm else part

    for i in range(len(blocks[0][1])):
        scores(0, i)
    for n, (start, chunks) in enumerate(blocks):
        ahead = len(blocks[n + 1][1]) if n + 1 < len(blocks) else 0
        for i in range(max(len(chunks), ahead)):
            if i < ahead:
                scores(n + 1, i)
            if i < len(chunks):
                weigh(n, i)
        cf_ref[:, start : start + QB] = acc[n] / norm[n]
        lse_ref[:, start : start + QB] = top[n] + jnp.log2(norm[n])
    cs[...] = roll_cont(cf_ref[...], shift).astype(BF)
    tok = total // 4
    for j, out in enumerate((o0, o1, o2, o3)):
        first = pl.multiple_of(xor(own, j) * tok, 128)
        out[...] = cs[:, pl.ds(first, tok)]


def attention(pref, qkv):
    total = qkv.shape[1]
    heads = HEADS // 4
    hdim = qkv.shape[0] // (3 * heads)
    rows = qkv.shape[0] // 3
    scale = LOG2E / hdim**0.5
    return call(
        lambda *refs: attention_kernel(scale, *refs),
        pref,
        [qkv] * 3,
        [pl.BlockSpec((hdim, total), lambda h, i, o=o: (h + o * heads, 0)) for o in range(3)],
        [shape_of((rows, total // 4), BF)] * 4
        + [shape_of((rows, total), F32), shape_of((heads, 1, total), F32)],
        [pl.BlockSpec((hdim, total // 4), lambda h, i: (h, 0))] * 4
        + [
            pl.BlockSpec((hdim, total), lambda h, i: (h, 0)),
            pl.BlockSpec((None, 1, total), lambda h, i: (h, 0, 0)),
        ],
        (heads,),
        [pltpu.VMEM((hdim, total), BF)] * 4 + [pltpu.VMEM((2, PROMPT + LONG, QB), F32)],
        16 * 10**9,
        12 * 10**6,
    )


def thirds(values):
    high = values.astype(BF).astype(F32)
    middle = (values - high).astype(BF).astype(F32)
    low = values - high - middle
    row = lax.broadcasted_iota(jnp.int32, (AUG, values.shape[1]), 0)
    value = jnp.where(row == 0, high, jnp.where(row == 1, middle, jnp.where(row == 2, low, 0.0)))
    return value.astype(BF)


def attention_back_kernel(
    scale, pref, q_ref, k_ref, v_ref, g0, g1, g2, g3, cf_ref, lse_ref,
    d0, d1, d2, d3, qa, ka, va, ga, gs, dqs, dks, dvs,
):
    own, shift, border = pref[0], pref[1], pref[2]
    hdim, total = q_ref.shape
    tok = total // 4
    cont = total - PROMPT
    others = PROMPT + LONG
    back = lax.rem(cont - shift, cont)
    for j, ref in enumerate((g0, g1, g2, g3)):
        first = pl.multiple_of(xor(own, j) * tok, 128)
        gs[:, pl.ds(first, tok)] = ref[...].astype(F32)
    qa[:hdim, :] = roll_cont(q_ref[...].astype(F32), back).astype(BF)
    ka[:hdim, :] = roll_cont(k_ref[...].astype(F32), back).astype(BF)
    va[:hdim, :] = roll_cont(v_ref[...].astype(F32), back).astype(BF)
    grad = roll_cont(gs[...], back)
    ga[:hdim, :] = grad.astype(BF)
    ga[hdim:, :] = thirds(-jnp.sum(grad * cf_ref[...], axis=0, keepdims=True))
    qa[hdim:, :] = thirds(lse_ref[...] * (-1.0 / scale))
    row = lax.broadcasted_iota(jnp.int32, (AUG, total), 0)
    ones = jnp.where(row < 3, 1.0, 0.0).astype(BF)
    ka[hdim:, :] = ones
    va[hdim:, :] = ones
    seen = set()
    for start, parts in block_list(total, QB):
        queries = slice(start, start + QB)
        grad_q = None
        for lo, hi in parts:
            for key in range(lo, hi, KB):
                keys = slice(key, key + KB)
                value = dot(qa[:, queries], ka[:, keys], 0, 0) * scale
                if lo >= others:
                    mask = same_segment((QB, KB), 1, key - others, start - others, border)
                    value = jnp.where(mask, value, -1e30)
                prob = jnp.exp2(value)
                grad_p = dot(ga[:, queries], va[:, keys], 0, 0)
                grad_s = (prob * grad_p).astype(BF)
                grad_v = dot(ga[:hdim, queries], prob.astype(BF), 1, 0)
                grad_k = dot(qa[:hdim, queries], grad_s, 1, 0)
                part = dot(ka[:hdim, keys], grad_s, 1, 1)
                grad_q = part if grad_q is None else grad_q + part
                if key in seen:
                    dvs[:, keys] += grad_v
                    dks[:, keys] += grad_k
                else:
                    dvs[:, keys] = grad_v
                    dks[:, keys] = grad_k
                    seen.add(key)
        dqs[:, queries] = grad_q
    inv = 1.0 / hdim**0.5
    for part, (ref, factor) in enumerate(((dqs, inv), (dks, inv), (dvs, 1.0))):
        gs[...] = roll_cont(ref[...] * factor, shift)
        for j, out in enumerate((d0, d1, d2, d3)):
            first = pl.multiple_of(xor(own, j) * tok, 128)
            out[part] = gs[:, pl.ds(first, tok)].astype(BF)


def attention_back(pref, qkv, grads, ctx, lse):
    total = qkv.shape[1]
    heads = HEADS // 4
    hdim = qkv.shape[0] // (3 * heads)
    rows = qkv.shape[0] // 3
    scale = LOG2E / hdim**0.5
    quarter = pl.BlockSpec((hdim, total // 4), lambda h, i: (h, 0))
    return call(
        lambda *refs: attention_back_kernel(scale, *refs),
        pref,
        [qkv] * 3 + list(grads) + [ctx, lse],
        [pl.BlockSpec((hdim, total), lambda h, i, o=o: (h + o * heads, 0)) for o in range(3)]
        + [quarter] * 4
        + [
            pl.BlockSpec((hdim, total), lambda h, i: (h, 0)),
            pl.BlockSpec((None, 1, total), lambda h, i: (h, 0, 0)),
        ],
        [shape_of((3, rows, total // 4), BF)] * 4,
        [pl.BlockSpec((3, hdim, total // 4), lambda h, i: (0, h, 0))] * 4,
        (heads,),
        [pltpu.VMEM((hdim + AUG, total), BF)] * 4 + [pltpu.VMEM((hdim, total), F32)] * 4,
        30 * 10**9,
        12 * 10**6,
    )


def normalize(values):
    centre = jnp.mean(values, axis=-1, keepdims=True)
    shifted = values - centre
    spread = jnp.mean(shifted * shifted, axis=-1, keepdims=True)
    inv = lax.rsqrt(spread + EPS)
    return shifted * inv, inv


def normalize_back(grad, normed, inv):
    first = jnp.mean(grad, axis=-1, keepdims=True)
    second = jnp.mean(grad * normed, axis=-1, keepdims=True)
    return (grad - first - normed * second) * inv


def total_rows(values):
    return jnp.sum(values, axis=0, keepdims=True)


def gather_ctx(own, pieces, ctx):
    rows = pieces[0].shape[0]
    for j, ref in enumerate(pieces):
        first = pl.multiple_of(xor(own, j) * rows, 64)
        ctx[pl.ds(first, rows), :] = ref[...]


def student_kernel(
    pref, c0, c1, c2, c3, x, w_out, w_up, w_down, b_out, b_up, b_down, gain, shift,
    ctx, act_one, normed_one, inv_one, gelu, slope, result, normed_two, inv_two,
    acc, mid,
):
    step = pl.program_id(0)

    @pl.when(step == 0)
    def _():
        gather_ctx(pref[0], (c0, c1, c2, c3), ctx)
        res = x[...].astype(F32) + (dot(ctx[...], w_out[...], 0, 1) + b_out[...])
        normed, inv = normalize(res)
        normed_one[...] = normed
        inv_one[...] = inv
        middle = normed * gain[0:1] + shift[0:1]
        mid[...] = middle
        act_one[...] = jnp.clip(middle, -CLIP, CLIP).astype(BF)
        acc[...] = jnp.zeros_like(acc)

    pre = dot(act_one[...], w_up[...], 1, 1) + b_up[...]
    cdf = 0.5 * (1.0 + lax.erf(pre * 0.5**0.5))
    act = (pre * cdf).astype(BF)
    gelu[...] = act
    slope[...] = (cdf + pre * (jnp.exp(pre * pre * -0.5) * 0.3989422804014327)).astype(BF)
    acc[...] += dot(act, w_down[...], 1, 1)

    @pl.when(step == pl.num_programs(0) - 1)
    def _():
        normed, inv = normalize(mid[...] + (acc[...] + b_down[...]))
        normed_two[...] = normed
        inv_two[...] = inv
        result[...] = (normed * gain[1:2] + shift[1:2]).astype(BF)


def ffn_specs(tok, width, hidden):
    up = pl.BlockSpec((FC, width), lambda c, i: (c, 0))
    down = pl.BlockSpec((width, FC), lambda c, i: (0, c))
    wide = pl.BlockSpec((tok, FC), lambda c, i: (0, c))
    row = pl.BlockSpec((1, FC), lambda c, i: (0, c))
    return up, down, wide, row


def student_ffn(pref, pieces, x, w_out, w_up, w_down, b_out, b_up, b_down, gain, shift):
    tok, width = x.shape
    hidden = w_up.shape[0]
    up, down, wide, row = ffn_specs(tok, width, hidden)
    full, one = whole((tok, width)), whole((tok, 1))
    return call(
        student_kernel,
        pref,
        list(pieces) + [x, w_out, w_up, w_down, b_out, b_up, b_down, gain, shift],
        [whole(pieces[0].shape)] * 4
        + [full, whole(w_out.shape), up, down, whole((1, width)), row, whole((1, width))]
        + [whole((2, width))] * 2,
        [
            shape_of((width, tok), BF),
            shape_of((tok, width), BF),
            shape_of((tok, width), F32),
            shape_of((tok, 1), F32),
            shape_of((tok, hidden), BF),
            shape_of((tok, hidden), BF),
            shape_of((tok, width), BF),
            shape_of((tok, width), F32),
            shape_of((tok, 1), F32),
        ],
        [whole((width, tok)), full, full, one, wide, wide, full, full, one],
        (hidden // FC,),
        [pltpu.VMEM((tok, width), F32)] * 2,
        2 * tok * width * (2 * hidden + width),
        2 * tok * hidden,
    )


def teacher_kernel(
    pref, c0, c1, c2, c3, x, w_out, w_up, w_down, gain, shift, normed_two, inv_two,
    grad_sum, grad_ffn, vectors,
    ctx, acc, mid, act_one,
):
    step = pl.program_id(0)

    @pl.when(step == 0)
    def _():
        gather_ctx(pref[0], (c0, c1, c2, c3), ctx)
        res = x[...].astype(F32) + dot(ctx[...], w_out[...], 0, 1)
        normed, inv = normalize(res)
        mid[...] = normed
        act_one[...] = normed.astype(BF)
        acc[...] = jnp.zeros_like(acc)

    pre = dot(act_one[...], w_up[...], 1, 1)
    act = (pre * (0.5 * (1.0 + lax.erf(pre * 0.5**0.5)))).astype(BF)
    acc[...] += dot(act, w_down[...], 1, 1)

    @pl.when(step == pl.num_programs(0) - 1)
    def _():
        target, _unused = normalize(mid[...] + acc[...])
        normed = normed_two[...]
        diff = normed * gain[1:2] + shift[1:2] - target
        back = normalize_back(diff * gain[1:2], normed, inv_two[...])
        grad_sum[...] = back
        low = back.astype(BF)
        grad_ffn[...] = low
        vectors[0:1] = total_rows(diff * normed)
        vectors[1:2] = total_rows(diff)
        vectors[2:3] = total_rows(low.astype(F32))


def teacher_ffn(pref, pieces, x, w_out, w_up, w_down, gain, shift, normed_two, inv_two):
    tok, width = x.shape
    hidden = w_up.shape[0]
    up, down, wide, row = ffn_specs(tok, width, hidden)
    full, one = whole((tok, width)), whole((tok, 1))
    return call(
        teacher_kernel,
        pref,
        list(pieces) + [x, w_out, w_up, w_down, gain, shift, normed_two, inv_two],
        [whole(pieces[0].shape)] * 4
        + [full, whole(w_out.shape), up, down]
        + [whole((2, width))] * 2
        + [full, one],
        [shape_of((tok, width), F32), shape_of((tok, width), BF), shape_of((3, width), F32)],
        [full, full, whole((3, width))],
        (hidden // FC,),
        [pltpu.VMEM((width, tok), BF)]
        + [pltpu.VMEM((tok, width), F32)] * 2
        + [pltpu.VMEM((tok, width), BF)],
        2 * tok * width * (2 * hidden + width),
        tok * hidden,
    )


def back_kernel(
    pref, grad_ffn, slope, w_up, w_down, grad_sum, normed_one, inv_one, gain, shift, w_out,
    grad_hidden, grad_bias, grad_res, grad_attn, g0, g1, g2, g3, vectors,
    acc, ctx,
):
    step = pl.program_id(0)

    @pl.when(step == 0)
    def _():
        acc[...] = jnp.zeros_like(acc)

    low = (dot(grad_ffn[...], w_down[...], 1, 0) * slope[...].astype(F32)).astype(BF)
    grad_hidden[...] = low
    grad_bias[...] = total_rows(low.astype(F32))
    acc[...] += dot(low, w_up[...], 1, 0)

    @pl.when(step == pl.num_programs(0) - 1)
    def _():
        normed = normed_one[...]
        middle = normed * gain[0:1] + shift[0:1]
        grad = grad_sum[...] + jnp.where(jnp.abs(middle) < CLIP, acc[...], 0.0)
        back = normalize_back(grad * gain[0:1], normed, inv_one[...])
        grad_res[...] = back
        attn = back.astype(BF)
        grad_attn[...] = attn
        vectors[0:1] = total_rows(grad * normed)
        vectors[1:2] = total_rows(grad)
        vectors[2:3] = total_rows(attn.astype(F32))
        ctx[...] = dot(w_out[...], attn, 0, 1).astype(BF)
        rows = g0.shape[0]
        for j, ref in enumerate((g0, g1, g2, g3)):
            first = pl.multiple_of(xor(pref[0], j) * rows, 64)
            ref[...] = ctx[pl.ds(first, rows), :]


def student_back(pref, grad_ffn, slope, w_up, w_down, grad_sum, normed_one, inv_one, gain, shift, w_out):
    tok, width = grad_ffn.shape
    hidden = w_up.shape[0]
    up, down, wide, row = ffn_specs(tok, width, hidden)
    full, one = whole((tok, width)), whole((tok, 1))
    return call(
        back_kernel,
        pref,
        [grad_ffn, slope, w_up, w_down, grad_sum, normed_one, inv_one, gain, shift, w_out],
        [full, wide, up, down, full, full, one] + [whole((2, width))] * 2 + [whole(w_out.shape)],
        [
            shape_of((tok, hidden), BF),
            shape_of((1, hidden), F32),
            shape_of((tok, width), F32),
            shape_of((tok, width), BF),
        ]
        + [shape_of((width // 4, tok), BF)] * 4
        + [shape_of((3, width), F32)],
        [wide, row, full, full] + [whole((width // 4, tok))] * 4 + [whole((3, width))],
        (hidden // FC,),
        [pltpu.VMEM((tok, width), F32), pltpu.VMEM((width, tok), BF)],
        2 * tok * width * (2 * hidden + width),
    )


def weight_grad_kernel(
    pref, grad_ffn, gelu, grad_hidden, act_one, grad_attn, ctx, grad_down, grad_up, grad_out
):
    @pl.when(pl.program_id(0) == 0)
    def _():
        value = dot(grad_attn[...], ctx[...], 0, 1).astype(BF)
        grad_out[...] = value.reshape(grad_out.shape)

    value = dot(grad_ffn[...], gelu[...], 0, 0).astype(BF)
    grad_down[...] = value.reshape(grad_down.shape)
    value = dot(grad_hidden[...], act_one[...], 0, 0).astype(BF)
    grad_up[...] = value.reshape(grad_up.shape)


def weight_grads(pref, grad_ffn, gelu, grad_hidden, act_one, grad_attn, ctx):
    tok, width = grad_ffn.shape
    hidden = gelu.shape[1]
    count, half = hidden // width, width // 2
    wide = pl.BlockSpec((tok, width), lambda c, i: (0, c))
    full = whole((tok, width))
    return call(
        weight_grad_kernel,
        pref,
        [grad_ffn, gelu, grad_hidden, act_one, grad_attn, ctx],
        [full, wide, wide, full, full, whole((width, tok))],
        [
            shape_of((2, count, half, width), BF),
            shape_of((2 * count, half, width), BF),
            shape_of((2, half, width), BF),
        ],
        [
            pl.BlockSpec((2, 1, half, width), lambda c, i: (0, c, 0, 0)),
            pl.BlockSpec((2, half, width), lambda c, i: (c, 0, 0)),
            whole((2, half, width)),
        ],
        (count,),
        [],
        2 * tok * width * (2 * hidden + width),
    )


def qkv_grad_kernel(pref, d0, d1, d2, d3, x0, x1, x2, x3, out, sums):
    own = pref[0]
    total = None
    count = None
    ones = jnp.ones((8, d0.shape[1]), BF)
    for grad, x in zip((d0, d1, d2, d3), (x0, x1, x2, x3)):
        value = grad[...]
        part = dot(value, jnp.clip(x[...], -CLIP, CLIP), 1, 0)
        line = dot(ones, value, 1, 1)
        total = part if total is None else total + part
        count = line if count is None else count + line
    out[...] = total.astype(BF)
    sums[...] = jnp.zeros_like(sums)
    rows = out.shape[0]
    for j in range(4):

        @pl.when(own == j)
        def _():
            sums[:, j * rows : (j + 1) * rows] = count


def qkv_grad(pref, grads, slots):
    tok, width = slots[0].shape
    rows = grads[0].shape[1]
    return call(
        qkv_grad_kernel,
        pref,
        list(grads) + list(slots),
        [pl.BlockSpec((None, rows, tok), lambda o, i: (o, 0, 0))] * 4 + [whole((tok, width))] * 4,
        [shape_of((3, rows, width), BF), shape_of((3, 8, width), F32)],
        [
            pl.BlockSpec((None, rows, width), lambda o, i: (o, 0, 0)),
            pl.BlockSpec((None, 8, width), lambda o, i: (o, 0, 0)),
        ],
        (3,),
        [],
        2 * 4 * tok * width * 3 * rows,
    )


def input_grad_kernel(pref, e0, e1, e2, e3, wq, wk, wv, grad_res, x, out, acc):
    slot = pl.program_id(0)

    @pl.when(slot == 0)
    def _():
        acc[...] = jnp.zeros_like(acc)

    for j, ref in enumerate((e0, e1, e2, e3)):

        @pl.when(slot == j)
        def _():
            part = dot(ref[0], wq[...], 0, 0)
            part = part + dot(ref[1], wk[...], 0, 0)
            acc[...] += part + dot(ref[2], wv[...], 0, 0)

    @pl.when(slot == 3)
    def _():
        size = jnp.abs(x[...].astype(F32))
        pull = jnp.where(size < CLIP, 1.0, jnp.where(size == CLIP, 0.5, 0.0))
        out[...] = (grad_res[...] + acc[...] * pull).astype(BF)


def input_grad(pref, pieces, weight, grad_res, x):
    tok, width = x.shape
    rows = pieces[0].shape[1]
    full = whole((tok, width))
    return call(
        input_grad_kernel,
        pref,
        list(pieces) + [weight] * 3 + [grad_res, x],
        [whole((3, rows, tok))] * 4
        + [
            pl.BlockSpec((rows, width), lambda j, i, o=o: (o * 4 + lax.bitwise_xor(i[0], j), 0))
            for o in range(3)
        ]
        + [full, full],
        shape_of((tok, width), BF),
        full,
        (4,),
        [pltpu.VMEM((tok, width), F32)],
        2 * 4 * tok * width * 3 * rows,
    )


def place(bit):
    name, mask = bit
    at = lax.axis_index(name)
    upper = lax.rem(lax.div(at, jnp.int32(mask)), jnp.int32(2))
    return upper, {name: at + mask * (1 - 2 * upper)}


def greet(bits):
    barrier = pltpu.get_barrier_semaphore()
    for bit in bits:
        pl.semaphore_signal(
            barrier, inc=1, device_id=place(bit)[1], device_id_type=pl.DeviceIdType.MESH
        )
    pl.semaphore_wait(barrier, len(bits))


class Copies:
    def __init__(self, send, recv, local):
        self.send, self.recv, self.local_sem = send, recv, local
        self.sent, self.planned, self.kept = [], 0, 0

    def plan(self, source, target, device):
        n = self.planned
        self.planned += 1
        return pltpu.make_async_remote_copy(
            src_ref=source,
            dst_ref=target,
            send_sem=self.send.at[n],
            recv_sem=self.recv.at[n],
            device_id=device,
            device_id_type=pl.DeviceIdType.MESH,
        )

    def remote(self, source, target, device):
        copy = self.plan(source, target, device)
        copy.start()
        self.sent.append(copy)
        return copy

    def plan_local(self, source, target):
        self.kept += 1
        return pltpu.make_async_copy(source, target, self.local_sem.at[self.kept - 1])

    def local(self, source, target):
        copy = self.plan_local(source, target)
        copy.start()
        return copy

    def finish(self):
        for copy in self.sent:
            copy.wait_send()


def window(ref, region):
    row, rows, col, cols = region
    return ref.at[pl.ds(row, rows), pl.ds(col, cols)]


def add_window(target, left, right, region, start):
    row, rows, col, cols = region
    step = 48 if rows % 48 == 0 else 16

    def body(i, carry):
        there = pl.ds(pl.multiple_of(row + i * step, 16), step)
        here = pl.ds(pl.multiple_of(start + i * step, 16), step)
        value = left[there, pl.ds(col, cols)].astype(F32) + right[here, :cols].astype(F32)
        target[there, pl.ds(col, cols)] = value.astype(target.dtype)
        return carry

    lax.fori_loop(0, rows // step, body, 0)


def scatter_sum(copies, work, far, full, bits):
    rows, cols = work.shape
    region, used, parts = (0, rows, 0, cols), 0, []
    for n, bit in enumerate(bits):
        upper, device = place(bit)
        row, rows, col, cols = region
        if (rows // 2) % 16 == 0:
            rows //= 2
            kept = (pl.multiple_of(row + upper * rows, 16), rows, col, cols)
            sent = (pl.multiple_of(row + (1 - upper) * rows, 16), rows, col, cols)
        else:
            cols //= 2
            kept = (row, rows, pl.multiple_of(col + upper * cols, 128), cols)
            sent = (row, rows, pl.multiple_of(col + (1 - upper) * cols, 128), cols)
        slot = far.at[pl.ds(used, rows), pl.ds(0, cols)]
        copy = copies.remote(window(work, sent), slot, device)
        yield
        copy.wait_recv()
        add_window(full if n == len(bits) - 1 else work, work, far, kept, used)
        used += rows
        region = kept
        parts.append((bit, kept))
    return parts


def sum_flow(copies, own, other, work, near, far, full, result, core, bits):
    copy = copies.remote(other, near, place(core)[1])
    load = copies.local(own, work)
    yield
    copy.wait_recv()
    load.wait()
    add_window(work, work, near, (0, work.shape[0], 0, work.shape[1]), 0)
    parts = yield from scatter_sum(copies, work, far, full, bits)
    for bit, kept in reversed(parts):
        copy = copies.remote(window(full, kept), window(full, kept), place(bit)[1])
        yield
        copy.wait_recv()
    store = copies.local(full, result)
    yield
    store.wait()


def vector_flow(copies, sums, far, bits):
    for n, bit in enumerate(bits):
        yield
        copy = copies.remote(sums.at[n], far.at[n], place(bit)[1])
        yield
        copy.wait_recv()
        sums[n + 1] = sums[n] + far[n]


def run_flows(flows, step):
    events = []
    for delay, flow in flows:
        next(flow)
        events.append([delay, len(events), flow])
    while events:
        events.sort(key=lambda e: e[:2])
        event = events[0]
        try:
            next(event[2])
            event[0] += step
        except StopIteration:
            events.pop(0)


def rotate(items, count):
    count %= len(items)
    return items[count:] + items[:count]


def sum_kernel(
    dp, seq, core, down, up, out, two, one, bias, heads, down_sum, up_sum, out_sum, totals,
    work, near, far, full, sums, sums_far, send, recv, local,
):
    greet(dp + seq + [core])
    copies = Copies(send, recv, local)
    side_of = place(core)[0]
    count, half, width = down.shape[1:]
    pieces = [(up.at[side_of, p], up.at[1 - side_of, p], up_sum.at[p]) for p in range(count)]
    pieces += [
        (
            down.at[side_of, p],
            down.at[1 - side_of, p],
            down_sum.at[:, pl.ds(p * width, width)],
        )
        for p in range(count)
    ]
    pieces.append((out.at[side_of], out.at[1 - side_of], out_sum))
    first = dp + seq[:1]
    flows = []
    for n, (own, other, result) in enumerate(pieces):
        bits = rotate(first, n) + seq[1:]
        flow = sum_flow(
            copies, own, other, work.at[n], near.at[n], far.at[n], full.at[n], result, core, bits
        )
        flows.append((n // len(first), flow))
    sums[0] = jnp.zeros(sums.shape[1:], F32)
    sums[0, 0:1] = heads[0, 0:1]
    sums[0, 1:2] = heads[2, 0:1]
    sums[0, 2:3] = one[2:3]
    sums[0, 3:4] = two[2:3]
    sums[0, 4:5] = one[0:1]
    sums[0, 5:6] = two[0:1]
    sums[0, 6:7] = one[1:2]
    sums[0, 7:8] = two[1:2]
    for p in range(count):
        sums[0, 8 + p : 9 + p] = bias[:, p * width : (p + 1) * width]
    flows.append((0.5, vector_flow(copies, sums, sums_far, [core] + dp + seq)))
    run_flows(flows, 1.5)
    totals[...] = sums[sums.shape[0] - 1]
    copies.finish()


def remote_call(kernel, args, in_specs, outs, out_specs, scratch, copies, local, number):
    sems = pltpu.SemaphoreType.DMA
    return pl.pallas_call(
        kernel,
        in_specs=in_specs,
        out_specs=out_specs,
        out_shape=outs,
        scratch_shapes=scratch + [sems((copies,)), sems((copies,)), sems((local,))],
        compiler_params=pltpu.CompilerParams(
            vmem_limit_bytes=VMEM_LIMIT, collective_id=number, has_side_effects=True
        ),
        cost_estimate=pl.CostEstimate(flops=5 * 10**10, bytes_accessed=10**8, transcendentals=0),
    )(*args)


ANY = pl.BlockSpec(memory_space=pl.ANY)
IN_VMEM = pl.BlockSpec(memory_space=pltpu.VMEM)


def sum_grads(dp, seq, core, down, up, out, two, one, bias, heads):
    sides, count, half, width = down.shape
    pieces, steps = 2 * count + 1, len(dp) + len(seq)
    lines = 16
    return remote_call(
        lambda *refs: sum_kernel(dp, seq, core, *refs),
        [down, up, out, two, one, bias, heads],
        [ANY] * 3 + [IN_VMEM] * 4,
        [
            shape_of((half, count * width), BF),
            shape_of((count, half, width), BF),
            shape_of((half, width), BF),
            shape_of((lines, width), F32),
        ],
        [ANY] * 3 + [IN_VMEM],
        [pltpu.VMEM((pieces, half, width), BF)] * 4
        + [pltpu.VMEM((steps + 2, lines, width), F32), pltpu.VMEM((steps + 1, lines, width), F32)],
        pieces * (1 + 2 * steps) + steps + 1,
        2 * pieces,
        1,
    )


def head_sum_kernel(dp, seq, core, heads, result, work, far, full, send, recv, local):
    greet(dp + seq + [core])
    copies = Copies(send, recv, local)
    side_of, partner = place(core)
    along = place(seq[0])[0]
    rows = dp + seq[1:]

    def flow(n):
        if n == 1:
            copy = copies.remote(heads.at[2 - 2 * side_of], work.at[n], partner)
            yield
            copy.wait_recv()
        else:
            load = copies.local(heads.at[n // 2 + side_of], work.at[n])
            yield
            load.wait()
        bits = (rotate(dp, n) if n < 2 else dp) + seq[1:]
        mine = full.at[2 * n + along]
        parts = yield from scatter_sum(copies, work.at[n], far.at[n], mine, bits)
        steps = [(bit, kept, False) for bit, kept in reversed(parts)]
        cut = len(steps) if n == 2 else 1
        held = steps[cut][1] if n < 2 else (0, mine.shape[0], 0, mine.shape[1])
        steps = steps[:cut] + [(seq[0], held, False)] + [(b, k, True) for b, k, _ in steps[cut:]]
        for bit, (row, size, col, cols), both in steps:
            first, count = (2 * n, 2) if both else (2 * n + along, 1)
            part = full.at[pl.ds(first, count), pl.ds(row, size), pl.ds(col, cols)]
            copy = copies.remote(part, part, place(bit)[1])
            yield
            copy.wait_recv()
        store = copies.local(full.at[pl.ds(2 * n, 2)], result.at[pl.ds(2 * n, 2)])
        yield
        store.wait()

    run_flows([(0, flow(0)), (0, flow(2)), (0, flow(1))], 1.0)
    copies.finish()


def head_sums_of(dp, seq, core, heads):
    _, rows, width = heads.shape
    steps = len(dp) + len(seq) - 1
    return remote_call(
        lambda *refs: head_sum_kernel(dp, seq, core, *refs),
        [heads],
        [ANY],
        shape_of((6, rows, width), BF),
        ANY,
        [pltpu.VMEM((3, rows, width), BF)] * 2 + [pltpu.VMEM((6, rows, width), BF)],
        3 * (2 * steps + 1) + 1,
        5,
        2,
    )


def binarize_rows(source, target):
    rows, cols = target.shape
    step = 96 if cols < 2048 else 32

    def body(i, carry):
        at = pl.ds(pl.multiple_of(i * step, 16), step)
        value = source[at, :]
        scale = jnp.sum(jnp.abs(value), axis=1, keepdims=True) * (1.0 / cols)
        signed = jnp.where(value > 0, scale, jnp.where(value < 0, -scale, 0.0))
        target[at, :] = signed.astype(BF)
        return carry

    lax.fori_loop(0, rows // step, body, 0)


def entry_kernel(
    seq, core, hidden, teach, segments, l_qkv, l_out, l_up, l_down, t_qkv, t_out, t_up, t_down, bias,
    o_pref, o_qkv, x0, x1, x2, x3, o_teach, b_qkv, b_out, b_up, b_down, e_qkv, e_out, e_up, e_down,
    xs, held, w_qkv, w_out, w_up, w_down, f_qkv, f_out, f_up, f_down,
    s_qkv, s_out, s_up, s_down, proj, others, send, recv, local,
):
    tok, width = hidden.shape
    parts, size = 4, tok // 4
    along, next_chip = place(seq[0])
    side_of, sibling = place(core)
    half = lax.div(lax.axis_index("seq"), jnp.int32(2))
    stays = half == side_of
    moves = half != side_of
    partner = {"seq": 2 * side_of + along, "fsdp": half}
    mesh = pl.DeviceIdType.MESH

    barrier = pltpu.get_barrier_semaphore()
    for device in (next_chip, sibling):
        pl.semaphore_signal(barrier, inc=1, device_id=device, device_id_type=mesh)

    @pl.when(moves)
    def _():
        pl.semaphore_signal(barrier, inc=1, device_id=partner, device_id_type=mesh)
        pl.semaphore_wait(barrier, 3)

    @pl.when(stays)
    def _():
        pl.semaphore_wait(barrier, 2)

    copies = Copies(send, recv, local)
    cuts = [pl.ds(c * size, size) for c in range(parts)]
    swap = [copies.plan(hidden.at[cut], xs.at[0, cut], partner) for cut in cuts]
    load = [copies.plan_local(hidden.at[cut], xs.at[0, cut]) for cut in cuts]
    over = [copies.plan(xs.at[0, cut], xs.at[1, cut], next_chip) for cut in cuts]
    beside = [copies.plan(xs.at[0, cut], xs.at[2, cut], sibling) for cut in cuts]
    relay = [copies.plan(xs.at[1, cut], xs.at[3, cut], sibling) for cut in cuts]
    t_swap = copies.plan(teach, held, partner)
    t_load = copies.plan_local(teach, held)
    seg_copy = copies.remote(segments, others, sibling)

    @pl.when(moves)
    def _():
        for copy in swap:
            copy.start()

    @pl.when(stays)
    def _():
        for copy in load:
            copy.start()
        t_load.start()

    latent = [
        (copies.local(source, target), target)
        for source, target in ((l_qkv, f_qkv), (l_out, f_out), (l_up, f_up), (l_down, f_down))
    ]
    staged = [
        (copies.local(source, target), target, result)
        for source, target, result in (
            (t_qkv, s_qkv, e_qkv),
            (t_out, s_out, e_out),
            (t_up, s_up, e_up),
            (t_down, s_down, e_down),
        )
    ]

    @pl.when(stays)
    def _():
        for c in range(parts):
            load[c].wait()
            over[c].start()
            beside[c].start()

    rows_qkv = l_qkv.shape[0]
    mine = w_qkv.at[pl.ds(pl.multiple_of(side_of * rows_qkv, 16), rows_qkv)]
    latent[0][0].wait()
    binarize_rows(f_qkv, mine)
    qkv_copy = copies.remote(mine, mine, sibling)
    stores, arrivals = [], []
    for (copy, source), target, result in zip(
        latent[1:], (w_out, w_up, w_down), (b_out, b_up, b_down)
    ):
        copy.wait()
        binarize_rows(source, target)
        arrivals.append(copies.remote(target, result.at[side_of], sibling))
        stores.append(copies.local(target, result.at[side_of]))
    for source, (_, _, result) in zip((t_qkv, t_out, t_up, t_down), staged):
        arrivals.append(copies.remote(source, result.at[side_of], sibling))
    for copy, target, result in staged:
        copy.wait()
        stores.append(copies.local(target, result.at[side_of]))

    @pl.when(moves)
    def _():
        for c in range(parts):
            swap[c].wait_recv()
            over[c].start()
            beside[c].start()
        t_swap.start()

    qkv_copy.wait_recv()
    stores.append(copies.local(w_qkv, b_qkv))
    rows = width // 4
    own = along + 2 * side_of

    def project(slot):
        act = jnp.clip(xs[slot], -CLIP, CLIP)
        first = (1 - along if slot % 2 else along) + 2 * (1 - side_of if slot // 2 else side_of)
        there = pl.ds(pl.multiple_of(first * tok, 128), tok)
        for part in range(3):
            at = pl.multiple_of(part * width + own * rows, 16)
            value = dot(w_qkv[pl.ds(at, rows), :], act, 1, 1)
            if part != 1:
                value = value + bias[part // 2, pl.ds(pl.multiple_of(own * rows, 8), rows), :]
            proj[part * rows : (part + 1) * rows, there] = value.astype(BF)
        stores.append(copies.local(proj.at[:, there], o_qkv.at[:, there]))
        stores.append(copies.local(xs.at[slot], (x0, x1, x2, x3)[slot]))

    seg_copy.wait_recv()
    counts = [jnp.sum(jnp.where(segments[...] == k, 1.0, 0.0)) for k in (1, 2, 3)]
    theirs = [jnp.sum(jnp.where(others[...] == k, 1.0, 0.0)) for k in (1, 2, 3)]
    first, second, third = [
        jnp.where(stays, a, b).astype(jnp.int32) for a, b in zip(counts, theirs)
    ]
    o_pref[0] = own
    o_pref[1] = jnp.where(first == LONG, 0, jnp.where(second == LONG, first, first + second))
    o_pref[2] = jnp.where(first == LONG, second, jnp.where(second == LONG, third, first))

    project(0)
    for copy in beside:
        copy.wait_recv()
    project(2)
    for c in range(parts):
        over[c].wait_recv()
        relay[c].start()
    project(1)
    for copy in relay:
        copy.wait_recv()
    project(3)

    @pl.when(moves)
    def _():
        t_swap.wait_recv()

    @pl.when(stays)
    def _():
        t_load.wait()

    stores.append(copies.local(held, o_teach))
    for copy in arrivals:
        copy.wait_recv()
    for copy in stores:
        copy.wait()

    @pl.when(moves)
    def _():
        for copy in swap + [t_swap]:
            copy.wait_send()

    for copy in over + beside + relay:
        copy.wait_send()
    copies.finish()


def entry(seq, core, hidden, teach, segments, latents, teachers, bias):
    tok, width = hidden.shape
    halves = [w.shape for w in latents]
    sides = [shape_of((2,) + shape, BF) for shape in halves]
    own = [pltpu.VMEM(shape, BF) for shape in halves]
    sides[0] = shape_of((2 * halves[0][0], halves[0][1]), BF)
    sides_t = [shape_of((2,) + shape, BF) for shape in halves]
    outs = remote_call(
        lambda *refs: entry_kernel(seq, core, *refs),
        [hidden, teach, segments] + list(latents) + list(teachers) + [bias],
        [ANY] * 2 + [IN_VMEM] + [ANY] * 8 + [IN_VMEM],
        [shape_of((3,), jnp.int32), shape_of((3 * width // 4, 4 * tok), BF)]
        + [shape_of((tok, width), BF)] * 5
        + sides
        + sides_t,
        [pl.BlockSpec(memory_space=pltpu.SMEM)] + [ANY] * 14,
        [pltpu.VMEM((4, tok, width), BF), pltpu.VMEM((tok, width), BF)]
        + [pltpu.VMEM(sides[0].shape, BF)]
        + own[1:]
        + [pltpu.VMEM(shape, F32) for shape in halves]
        + own
        + [pltpu.VMEM((3 * width // 4, 4 * tok), BF), pltpu.VMEM(segments.shape, jnp.int32)],
        26,
        30,
        3,
    )
    pref, qkv, x0, x1, x2, x3, teach = outs[:7]
    weights = [w.reshape((-1, w.shape[-1])) for w in outs[7:]]
    return pref, qkv, (x0, x1, x2, x3), teach, weights[:4], weights[4:]


def binarize(latent):
    row_scale = jnp.mean(jnp.abs(latent), axis=1, keepdims=True)
    return (row_scale * jnp.sign(latent)).astype(BF)


def segment_info(segments):
    sizes_of = [jnp.sum((segments == k).astype(jnp.int32)) for k in (1, 2, 3)]
    first, second, third = sizes_of
    shift = jnp.where(first == LONG, 0, jnp.where(second == LONG, first, first + second))
    border = jnp.where(first == LONG, second, jnp.where(second == LONG, third, first))
    return jnp.stack([shift, border])


def quarters(own):
    along = to_slot(own, 1)
    return (own, along, to_slot(own, 2), to_slot(along, 2))


def exchange(pieces):
    return (pieces[0],) + tuple(to_slot(pieces[j], j) for j in (1, 2, 3))


def on_device(
    hidden, teacher_hidden, segments, latent_qkv, latent_out, latent_up, latent_down,
    biases, up_bias, norm_gains, norm_shifts, teacher_qkv, teacher_out, teacher_up, teacher_down,
):
    seq_at, fsdp_at = lax.axis_index("seq"), lax.axis_index("fsdp")
    fsdp = lax.axis_size("fsdp")
    core = fsdp_at % 2
    own = (seq_at % 2 + 2 * core).astype(jnp.int32)
    width = hidden.shape[2]

    bias_cols = biases[:2].reshape(2, width, 1)
    latents = (latent_qkv, latent_out, latent_up, latent_down)
    teachers = (teacher_qkv, teacher_out, teacher_up, teacher_down)
    if fsdp == 2:
        pref, qkv, x_slots, teach, bins, t_weights = entry(
            bit_list("seq"), bit_list("fsdp")[0], hidden[0], teacher_hidden[0], segments,
            latents, teachers, bias_cols,
        )
        x = x_slots[0]
    else:
        info = segment_info(segments)
        info = jnp.where(core == seq_at // 2, info, flip(info, fsdp=1))
        pref = jnp.concatenate([own[None], info]).astype(jnp.int32)
        x = swap_groups(hidden[0])
        x_slots = quarters(x)
        bins = [gather_rows(binarize(w)) for w in latents]
        teach = swap_groups(teacher_hidden[0])
        t_weights = [gather_rows(w) for w in teachers]
        qkv = qkv_project(pref, x_slots, bins[0], bias_cols)
    bin_qkv, bin_out, bin_up, bin_down = bins
    t_qkv, t_out, t_up, t_down = t_weights
    t_along, t_beside = to_slot(teach, 1), to_slot(teach, 2)
    *ctx_slots, ctx_full, lse = attention(pref, qkv)
    t_along, ctx_slots = lax.optimization_barrier((t_along, ctx_slots))
    t_slots = (teach, t_along, t_beside, to_slot(t_along, 2))
    ctx_pieces = exchange(ctx_slots)

    t_heads = qkv_project(pref, t_slots, t_qkv, None)
    *tctx_slots, _unused, _unused_too = attention(pref, t_heads)
    tctx_slots, ctx_pieces = lax.optimization_barrier((tctx_slots, ctx_pieces))
    tctx_pieces = exchange(tctx_slots)

    gain, shift = norm_gains, norm_shifts
    (
        ctx, act_one, normed_one, inv_one, gelu, slope, result, normed_two, inv_two,
    ) = student_ffn(
        pref, ctx_pieces, x, bin_out, bin_up, bin_down,
        biases[2:3], up_bias[None], biases[3:4], gain, shift,
    )
    student_out = swap_groups(result)
    grad_sum, grad_ffn, vec_two = teacher_ffn(
        pref, tctx_pieces, teach, t_out, t_up, t_down, gain, shift, normed_two, inv_two
    )
    grad_hidden, grad_up_bias, grad_res, grad_attn, *gctx_slots, vec_one = student_back(
        pref, grad_ffn, slope, bin_up, bin_down, grad_sum, normed_one, inv_one, gain, shift, bin_out
    )
    gctx_pieces = exchange(gctx_slots)
    grad_down, grad_up, grad_out = weight_grads(
        pref, grad_ffn, gelu, grad_hidden, act_one, grad_attn, ctx
    )
    dp_bits, seq_bits, fsdp_bits = bit_list("dp"), bit_list("seq"), bit_list("fsdp")
    dqkv_slots = attention_back(pref, qkv, gctx_pieces, ctx_full, lse)
    dqkv_pieces = exchange(dqkv_slots)
    grad_heads, head_sums = qkv_grad(pref, dqkv_slots, x_slots)
    rows, hidden_units = width // 4, up_bias.shape[0]
    _, count, half, _ = grad_down.shape

    if fsdp == 2:
        total_down, total_up, total_out, vectors = sum_grads(
            dp_bits,
            seq_bits,
            fsdp_bits[0],
            grad_down,
            grad_up.reshape(grad_down.shape),
            grad_out,
            vec_two,
            vec_one,
            grad_up_bias,
            head_sums,
        )
        total_up = total_up.reshape(-1, width)
        hidden_grad = swap_groups(input_grad(pref, dqkv_pieces, bin_qkv, grad_res, x))
        total_qkv = head_sums_of(dp_bits, seq_bits, fsdp_bits[0], grad_heads).reshape(-1, width)
    else:
        hidden_grad = swap_groups(input_grad(pref, dqkv_pieces, bin_qkv, grad_res, x))

        def reduce_grad(value, bits):
            for bit in reversed(fsdp_bits):
                value = halve(value, bit)
            return all_reduce(value, bits)

        grad_down = grad_down.transpose(0, 2, 1, 3).reshape(width, hidden_units)
        total_down = reduce_grad(grad_down, dp_bits + seq_bits)
        total_up = reduce_grad(grad_up.reshape(hidden_units, width), dp_bits[::-1] + seq_bits)
        total_out = reduce_grad(
            grad_out.reshape(width, width), seq_bits[:1] + dp_bits + seq_bits[1:]
        )
        blocks = all_reduce(
            grad_heads.reshape(3 * rows, width), dp_bits + seq_bits[1:] + fsdp_bits[1:]
        )
        blocks = blocks.reshape(1, 3, rows, width)
        blocks = double(double(blocks, seq_bits[0]), fsdp_bits[0])
        whole_qkv = blocks.transpose(1, 0, 2, 3).reshape(3 * width, width)
        part = 3 * width // fsdp
        total_qkv = lax.dynamic_slice_in_dim(whole_qkv, fsdp_at * part, part, 0)
        vectors = jnp.concatenate(
            [
                head_sums[0, :1],
                head_sums[2, :1],
                vec_one[2:3],
                vec_two[2:3],
                vec_one[0:1],
                vec_two[0:1],
                vec_one[1:2],
                vec_two[1:2],
                grad_up_bias.reshape(-1, width),
            ]
        )
        vectors = sum_small(vectors, dp_bits + seq_bits + fsdp_bits)
    hid_bias = vectors[8 : 8 + hidden_units // width].reshape(-1)
    share, hid_share = width // fsdp, hid_bias.shape[0] // fsdp
    cols = lax.dynamic_slice_in_dim(vectors[:8], fsdp_at * share, share, 1)
    return (
        student_out[None],
        hidden_grad[None],
        total_qkv.astype(F32),
        total_out.astype(F32),
        total_up.astype(F32),
        total_down.astype(F32),
        cols[0:4],
        lax.dynamic_slice_in_dim(hid_bias, fsdp_at * hid_share, hid_share, 0),
        cols[4:6],
        cols[6:8],
    )


def solution(mesh):
    tokens = P(("dp", "fsdp"), "seq", None)
    rows = P("fsdp", None)
    return jax.shard_map(
        on_device,
        mesh=mesh,
        in_specs=(tokens, tokens, P(("dp", "fsdp"), None)) + (rows,) * 4 + (P(),) * 4 + (rows,) * 4,
        out_specs=(tokens, tokens)
        + (rows,) * 4
        + (P(None, "fsdp"), P("fsdp"), P(None, "fsdp"), P(None, "fsdp")),
        check_vma=False,
    )
```

```python
import jax
import jax.numpy as jnp
from jax import lax
from jax.experimental import pallas as pl
from jax.experimental.pallas import tpu as pltpu
from jax.sharding import PartitionSpec as P

HEADS = 12
PROMPT = 1024
LONG = 1024
CLIP = 2.5
EPS = 1e-05
AXES = ("dp", "seq", "fsdp")
BF = jnp.bfloat16
F32 = jnp.float32
LOG2E = 1.4426950408889634
QB = 512
KC = 256
KB = 512
FC = 512
AUG = 16
VMEM_LIMIT = 56 * 2**20


def dot(left, right, left_dim, right_dim):
    return lax.dot_general(
        left, right, (((left_dim,), (right_dim,)), ((), ())), preferred_element_type=F32
    )


def xor(first, second):
    return lax.bitwise_xor(first, jnp.int32(second))


def sizes():
    return tuple(lax.axis_size(name) for name in AXES)


def permute(values, target):
    dp, seq, fsdp = sizes()
    pairs = []
    for d in range(dp):
        for s in range(seq):
            for f in range(fsdp):
                td, ts, tf = target(d, s, f)
                pairs.append(((d * seq + s) * fsdp + f, (td * seq + ts) * fsdp + tf))
    return lax.ppermute(values, AXES, pairs)


def flip(values, dp=0, seq=0, fsdp=0):
    return permute(values, lambda d, s, f: (d ^ dp, s ^ seq, f ^ fsdp))


def swap_groups(values):
    return permute(
        values, lambda d, s, f: (d, 2 * (f % 2) + s % 2, f - f % 2 + s // 2)
    )


def to_slot(values, slot):
    return flip(values, seq=slot & 1, fsdp=slot >> 1)


def bit_list(name):
    count = lax.axis_size(name)
    out, bit = [], 1
    while bit < count:
        out.append((name, bit))
        bit *= 2
    return out


def flip_bit(values, bit):
    return flip(values, **{bit[0]: bit[1]})


def side(bit):
    return lax.bitwise_and(lax.axis_index(bit[0]), bit[1]) != 0


def halve(values, bit):
    upper = side(bit).astype(jnp.int32)
    half = values.shape[0] // 2
    sent = lax.dynamic_slice_in_dim(values, (1 - upper) * half, half, 0)
    kept = lax.dynamic_slice_in_dim(values, upper * half, half, 0)
    got = flip_bit(sent, bit)
    return (kept.astype(F32) + got.astype(F32)).astype(values.dtype)


def double(values, bit):
    got = flip_bit(values, bit)
    return jnp.where(
        side(bit),
        jnp.concatenate([got, values], axis=0),
        jnp.concatenate([values, got], axis=0),
    )


def gather_rows(values):
    for bit in bit_list("fsdp"):
        values = double(values, bit)
    return values


def all_reduce(values, bits):
    for bit in bits:
        values = halve(values, bit)
    for bit in reversed(bits):
        values = double(values, bit)
    return values


def sum_small(values, bits):
    for bit in bits:
        values = values + flip_bit(values, bit)
    return values


def whole(shape):
    return pl.BlockSpec(shape, lambda *_: (0,) * len(shape))


def call(kernel, pref, args, in_specs, outs, out_specs, grid, scratch, flops, trans=0):
    moved = sum(a.size * a.dtype.itemsize for a in args)
    moved += sum(o.size * o.dtype.itemsize for o in jax.tree.leaves(outs))
    return pl.pallas_call(
        kernel,
        grid_spec=pltpu.PrefetchScalarGridSpec(
            num_scalar_prefetch=1,
            grid=grid,
            in_specs=in_specs,
            out_specs=out_specs,
            scratch_shapes=scratch,
        ),
        out_shape=outs,
        compiler_params=pltpu.CompilerParams(vmem_limit_bytes=VMEM_LIMIT),
        cost_estimate=pl.CostEstimate(flops=flops, bytes_accessed=moved, transcendentals=trans),
    )(pref, *args)


def shape_of(shape, dtype):
    return jax.ShapeDtypeStruct(shape, dtype)


def qkv_kernel(student, pref, x0, x1, x2, x3, wq, wk, wv, *rest):
    slot = pl.program_id(0)
    out = rest[-1]
    rows = wq.shape[0]
    for j, ref in enumerate((x0, x1, x2, x3)):

        @pl.when(slot == j)
        def _():
            act = ref[...]
            if student:
                act = jnp.clip(act, -CLIP, CLIP)
            for part, weight in enumerate((wq, wk, wv)):
                value = dot(weight[...], act, 1, 1)
                if student and part != 1:
                    value = value + rest[0][part // 2]
                out[part * rows : (part + 1) * rows, :] = value.astype(BF)


def qkv_project(pref, slots, weight, bias):
    tok, width = slots[0].shape
    rows = weight.shape[0] // 12
    specs = [whole((tok, width))] * 4
    specs += [
        pl.BlockSpec((rows, width), lambda j, i, o=o: (o * 4 + i[0], 0)) for o in range(3)
    ]
    args = list(slots) + [weight] * 3
    if bias is not None:
        specs.append(pl.BlockSpec((2, rows, 1), lambda j, i: (0, i[0], 0)))
        args.append(bias)
    return call(
        lambda *refs: qkv_kernel(bias is not None, *refs),
        pref,
        args,
        specs,
        shape_of((3 * rows, 4 * tok), BF),
        pl.BlockSpec((3 * rows, tok), lambda j, i: (0, lax.bitwise_xor(i[0], j))),
        (4,),
        [],
        2 * 4 * tok * width * 3 * rows,
    )


def roll_cont(values, shift):
    return jnp.concatenate(
        [values[:, :PROMPT], pltpu.roll(values[:, PROMPT:], shift, 1)], axis=1
    )


def block_list(total, rows):
    blocks = [(i, [(0, PROMPT)]) for i in range(0, PROMPT, rows)]
    blocks += [(i, [(0, PROMPT + LONG)]) for i in range(PROMPT, PROMPT + LONG, rows)]
    blocks += [
        (i, [(0, PROMPT), (PROMPT + LONG, total)]) for i in range(PROMPT + LONG, total, rows)
    ]
    return blocks


def same_segment(shape, key_axis, key_start, query_start, border):
    keys = lax.broadcasted_iota(jnp.int32, shape, key_axis) + key_start
    queries = lax.broadcasted_iota(jnp.int32, shape, 1 - key_axis) + query_start
    return (keys < border) == (queries < border)


def attention_kernel(scale, kept, pref, q_ref, k_ref, v_ref, o0, o1, o2, o3, cf_ref, lse_ref, *rest):
    if kept:
        qs, ks, vs, cs, st = rest
    else:
        cs, st, qs, ks, vs = rest
    own, shift, border = pref[0], pref[1], pref[2]
    total = q_ref.shape[1]
    cont = total - PROMPT
    others = PROMPT + LONG
    back = lax.rem(cont - shift, cont)
    qs[...] = roll_cont(q_ref[...].astype(F32), back).astype(BF)
    ks[...] = roll_cont(k_ref[...].astype(F32), back).astype(BF)
    vs[...] = roll_cont(v_ref[...].astype(F32), back).astype(BF)
    blocks = []
    for start, parts in block_list(total, QB):
        chunks = [key for lo, hi in parts for key in range(lo, hi, KC)]
        blocks.append((start, chunks))
    top, acc, norm = {}, {}, {}

    def scores(n, i):
        start, chunks = blocks[n]
        key = chunks[i]
        value = dot(ks[:, key : key + KC], qs[:, start : start + QB], 0, 0) * scale
        if key >= others:
            mask = same_segment((KC, QB), 0, key - others, start - others, border)
            value = jnp.where(mask, value, -1e30)
        st[n % 2, i * KC : (i + 1) * KC, :] = value
        peak = jnp.max(value, axis=0, keepdims=True)
        top[n] = jnp.maximum(top[n], peak) if n in top else peak

    def weigh(n, i):
        key = blocks[n][1][i]
        prob = jnp.exp2(st[n % 2, i * KC : (i + 1) * KC, :] - top[n])
        part = jnp.sum(prob, axis=0, keepdims=True)
        value = dot(vs[:, key : key + KC], prob.astype(BF), 1, 0)
        acc[n] = acc[n] + value if n in acc else value
        norm[n] = norm[n] + part if n in norm else part

    for i in range(len(blocks[0][1])):
        scores(0, i)
    for n, (start, chunks) in enumerate(blocks):
        ahead = len(blocks[n + 1][1]) if n + 1 < len(blocks) else 0
        for i in range(max(len(chunks), ahead)):
            if i < ahead:
                scores(n + 1, i)
            if i < len(chunks):
                weigh(n, i)
        cf_ref[:, start : start + QB] = acc[n] / norm[n]
        lse_ref[:, start : start + QB] = top[n] + jnp.log2(norm[n])
    cs[...] = roll_cont(cf_ref[...], shift).astype(BF)
    tok = total // 4
    for j, out in enumerate((o0, o1, o2, o3)):
        first = pl.multiple_of(xor(own, j) * tok, 128)
        out[...] = cs[:, pl.ds(first, tok)]


def attention(pref, qkv, kept):
    total = qkv.shape[1]
    heads = HEADS // 4
    hdim = qkv.shape[0] // (3 * heads)
    rows = qkv.shape[0] // 3
    scale = LOG2E / hdim**0.5
    return call(
        lambda *refs: attention_kernel(scale, kept, *refs),
        pref,
        [qkv] * 3,
        [pl.BlockSpec((hdim, total), lambda h, i, o=o: (h + o * heads, 0)) for o in range(3)],
        [shape_of((rows, total // 4), BF)] * 4
        + [shape_of((rows, total), F32), shape_of((heads, 1, total), F32)]
        + [shape_of((rows, total), BF)] * (3 if kept else 0),
        [pl.BlockSpec((hdim, total // 4), lambda h, i: (h, 0))] * 4
        + [
            pl.BlockSpec((hdim, total), lambda h, i: (h, 0)),
            pl.BlockSpec((None, 1, total), lambda h, i: (h, 0, 0)),
        ]
        + [pl.BlockSpec((hdim, total), lambda h, i: (h, 0))] * (3 if kept else 0),
        (heads,),
        [pltpu.VMEM((hdim, total), BF), pltpu.VMEM((2, PROMPT + LONG, QB), F32)]
        + [pltpu.VMEM((hdim, total), BF)] * (0 if kept else 3),
        16 * 10**9,
        12 * 10**6,
    )


def thirds(values):
    high = values.astype(BF).astype(F32)
    middle = (values - high).astype(BF).astype(F32)
    low = values - high - middle
    row = lax.broadcasted_iota(jnp.int32, (AUG, values.shape[1]), 0)
    value = jnp.where(row == 0, high, jnp.where(row == 1, middle, jnp.where(row == 2, low, 0.0)))
    return value.astype(BF)


def attention_back_kernel(
    scale, pref, q_ref, k_ref, v_ref, g0, g1, g2, g3, cf_ref, lse_ref,
    d0, d1, d2, d3, qa, ka, va, ga, gs, dqs, dks, dvs,
):
    own, shift, border = pref[0], pref[1], pref[2]
    hdim, total = q_ref.shape
    tok = total // 4
    cont = total - PROMPT
    others = PROMPT + LONG
    back = lax.rem(cont - shift, cont)
    for j, ref in enumerate((g0, g1, g2, g3)):
        first = pl.multiple_of(xor(own, j) * tok, 128)
        gs[:, pl.ds(first, tok)] = ref[...].astype(F32)
    qa[:hdim, :] = roll_cont(q_ref[...].astype(F32), back).astype(BF)
    ka[:hdim, :] = roll_cont(k_ref[...].astype(F32), back).astype(BF)
    va[:hdim, :] = roll_cont(v_ref[...].astype(F32), back).astype(BF)
    grad = roll_cont(gs[...], back)
    ga[:hdim, :] = grad.astype(BF)
    ga[hdim:, :] = thirds(-jnp.sum(grad * cf_ref[...], axis=0, keepdims=True))
    qa[hdim:, :] = thirds(lse_ref[...] * (-1.0 / scale))
    row = lax.broadcasted_iota(jnp.int32, (AUG, total), 0)
    ones = jnp.where(row < 3, 1.0, 0.0).astype(BF)
    ka[hdim:, :] = ones
    va[hdim:, :] = ones
    seen = set()
    for start, parts in block_list(total, QB):
        queries = slice(start, start + QB)
        grad_q = None
        for lo, hi in parts:
            for key in range(lo, hi, KB):
                keys = slice(key, key + KB)
                value = dot(qa[:, queries], ka[:, keys], 0, 0) * scale
                if lo >= others:
                    mask = same_segment((QB, KB), 1, key - others, start - others, border)
                    value = jnp.where(mask, value, -1e30)
                prob = jnp.exp2(value)
                grad_p = dot(ga[:, queries], va[:, keys], 0, 0)
                grad_s = (prob * grad_p).astype(BF)
                grad_v = dot(ga[:hdim, queries], prob.astype(BF), 1, 0)
                grad_k = dot(qa[:hdim, queries], grad_s, 1, 0)
                part = dot(ka[:hdim, keys], grad_s, 1, 1)
                grad_q = part if grad_q is None else grad_q + part
                if key in seen:
                    dvs[:, keys] += grad_v
                    dks[:, keys] += grad_k
                else:
                    dvs[:, keys] = grad_v
                    dks[:, keys] = grad_k
                    seen.add(key)
        dqs[:, queries] = grad_q
    inv = 1.0 / hdim**0.5
    for part, (ref, factor) in enumerate(((dqs, inv), (dks, inv), (dvs, 1.0))):
        gs[...] = roll_cont(ref[...] * factor, shift)
        for j, out in enumerate((d0, d1, d2, d3)):
            first = pl.multiple_of(xor(own, j) * tok, 128)
            out[part] = gs[:, pl.ds(first, tok)].astype(BF)


def attention_back(pref, qkv, grads, ctx, lse):
    total = qkv.shape[1]
    heads = HEADS // 4
    hdim = qkv.shape[0] // (3 * heads)
    rows = qkv.shape[0] // 3
    scale = LOG2E / hdim**0.5
    quarter = pl.BlockSpec((hdim, total // 4), lambda h, i: (h, 0))
    return call(
        lambda *refs: attention_back_kernel(scale, *refs),
        pref,
        [qkv] * 3 + list(grads) + [ctx, lse],
        [pl.BlockSpec((hdim, total), lambda h, i, o=o: (h + o * heads, 0)) for o in range(3)]
        + [quarter] * 4
        + [
            pl.BlockSpec((hdim, total), lambda h, i: (h, 0)),
            pl.BlockSpec((None, 1, total), lambda h, i: (h, 0, 0)),
        ],
        [shape_of((3, rows, total // 4), BF)] * 4,
        [pl.BlockSpec((3, hdim, total // 4), lambda h, i: (0, h, 0))] * 4,
        (heads,),
        [pltpu.VMEM((hdim + AUG, total), BF)] * 4 + [pltpu.VMEM((hdim, total), F32)] * 4,
        30 * 10**9,
        12 * 10**6,
    )


def normalize(values):
    centre = jnp.mean(values, axis=-1, keepdims=True)
    shifted = values - centre
    spread = jnp.mean(shifted * shifted, axis=-1, keepdims=True)
    inv = lax.rsqrt(spread + EPS)
    return shifted * inv, inv


def normalize_back(grad, normed, inv):
    first = jnp.mean(grad, axis=-1, keepdims=True)
    second = jnp.mean(grad * normed, axis=-1, keepdims=True)
    return (grad - first - normed * second) * inv


def total_rows(values):
    return jnp.sum(values, axis=0, keepdims=True)


def gather_ctx(own, pieces, ctx):
    rows = pieces[0].shape[0]
    for j, ref in enumerate(pieces):
        first = pl.multiple_of(xor(own, j) * rows, 64)
        ctx[pl.ds(first, rows), :] = ref[...]


def student_kernel(
    pref, c0, c1, c2, c3, x, w_out, w_up, w_down, b_out, b_up, b_down, gain, shift,
    ctx, act_one, normed_one, inv_one, gelu, slope, result, normed_two, inv_two,
    acc, mid,
):
    step = pl.program_id(0)

    @pl.when(step == 0)
    def _():
        gather_ctx(pref[0], (c0, c1, c2, c3), ctx)
        res = x[...].astype(F32) + (dot(ctx[...], w_out[...], 0, 1) + b_out[...])
        normed, inv = normalize(res)
        normed_one[...] = normed
        inv_one[...] = inv
        middle = normed * gain[0:1] + shift[0:1]
        mid[...] = middle
        act_one[...] = jnp.clip(middle, -CLIP, CLIP).astype(BF)
        acc[...] = jnp.zeros_like(acc)

    pre = dot(act_one[...], w_up[...], 1, 1) + b_up[...]
    cdf = 0.5 * (1.0 + lax.erf(pre * 0.5**0.5))
    act = (pre * cdf).astype(BF)
    gelu[...] = act
    slope[...] = (cdf + pre * (jnp.exp(pre * pre * -0.5) * 0.3989422804014327)).astype(BF)
    acc[...] += dot(act, w_down[...], 1, 1)

    @pl.when(step == pl.num_programs(0) - 1)
    def _():
        normed, inv = normalize(mid[...] + (acc[...] + b_down[...]))
        normed_two[...] = normed
        inv_two[...] = inv
        result[...] = (normed * gain[1:2] + shift[1:2]).astype(BF)


def ffn_specs(tok, width, hidden):
    up = pl.BlockSpec((FC, width), lambda c, i: (c, 0))
    down = pl.BlockSpec((width, FC), lambda c, i: (0, c))
    wide = pl.BlockSpec((tok, FC), lambda c, i: (0, c))
    row = pl.BlockSpec((1, FC), lambda c, i: (0, c))
    return up, down, wide, row


def student_ffn(pref, pieces, x, w_out, w_up, w_down, b_out, b_up, b_down, gain, shift):
    tok, width = x.shape
    hidden = w_up.shape[0]
    up, down, wide, row = ffn_specs(tok, width, hidden)
    full, one = whole((tok, width)), whole((tok, 1))
    return call(
        student_kernel,
        pref,
        list(pieces) + [x, w_out, w_up, w_down, b_out, b_up, b_down, gain, shift],
        [whole(pieces[0].shape)] * 4
        + [full, whole(w_out.shape), up, down, whole((1, width)), row, whole((1, width))]
        + [whole((2, width))] * 2,
        [
            shape_of((width, tok), BF),
            shape_of((tok, width), BF),
            shape_of((tok, width), F32),
            shape_of((tok, 1), F32),
            shape_of((tok, hidden), BF),
            shape_of((tok, hidden), BF),
            shape_of((tok, width), BF),
            shape_of((tok, width), F32),
            shape_of((tok, 1), F32),
        ],
        [whole((width, tok)), full, full, one, wide, wide, full, full, one],
        (hidden // FC,),
        [pltpu.VMEM((tok, width), F32)] * 2,
        2 * tok * width * (2 * hidden + width),
        2 * tok * hidden,
    )


def teacher_kernel(
    pref, c0, c1, c2, c3, x, w_out, w_up, w_down, gain, shift, normed_two, inv_two,
    grad_sum, grad_ffn, vectors,
    ctx, acc, mid, act_one,
):
    step = pl.program_id(0)

    @pl.when(step == 0)
    def _():
        gather_ctx(pref[0], (c0, c1, c2, c3), ctx)
        res = x[...].astype(F32) + dot(ctx[...], w_out[...], 0, 1)
        normed, inv = normalize(res)
        mid[...] = normed
        act_one[...] = normed.astype(BF)
        acc[...] = jnp.zeros_like(acc)

    pre = dot(act_one[...], w_up[...], 1, 1)
    act = (pre * (0.5 * (1.0 + lax.erf(pre * 0.5**0.5)))).astype(BF)
    acc[...] += dot(act, w_down[...], 1, 1)

    @pl.when(step == pl.num_programs(0) - 1)
    def _():
        target, _unused = normalize(mid[...] + acc[...])
        normed = normed_two[...]
        diff = normed * gain[1:2] + shift[1:2] - target
        back = normalize_back(diff * gain[1:2], normed, inv_two[...])
        grad_sum[...] = back
        low = back.astype(BF)
        grad_ffn[...] = low
        vectors[0:1] = total_rows(diff * normed)
        vectors[1:2] = total_rows(diff)
        vectors[2:3] = total_rows(low.astype(F32))


def teacher_ffn(pref, pieces, x, w_out, w_up, w_down, gain, shift, normed_two, inv_two):
    tok, width = x.shape
    hidden = w_up.shape[0]
    up, down, wide, row = ffn_specs(tok, width, hidden)
    full, one = whole((tok, width)), whole((tok, 1))
    return call(
        teacher_kernel,
        pref,
        list(pieces) + [x, w_out, w_up, w_down, gain, shift, normed_two, inv_two],
        [whole(pieces[0].shape)] * 4
        + [full, whole(w_out.shape), up, down]
        + [whole((2, width))] * 2
        + [full, one],
        [shape_of((tok, width), F32), shape_of((tok, width), BF), shape_of((3, width), F32)],
        [full, full, whole((3, width))],
        (hidden // FC,),
        [pltpu.VMEM((width, tok), BF)]
        + [pltpu.VMEM((tok, width), F32)] * 2
        + [pltpu.VMEM((tok, width), BF)],
        2 * tok * width * (2 * hidden + width),
        tok * hidden,
    )


def back_kernel(
    pref, grad_ffn, slope, w_up, w_down, grad_sum, normed_one, inv_one, gain, shift, w_out,
    grad_hidden, grad_bias, grad_res, grad_attn, g0, g1, g2, g3, vectors,
    acc, ctx,
):
    step = pl.program_id(0)

    @pl.when(step == 0)
    def _():
        acc[...] = jnp.zeros_like(acc)

    low = (dot(grad_ffn[...], w_down[...], 1, 0) * slope[...].astype(F32)).astype(BF)
    grad_hidden[...] = low
    grad_bias[...] = total_rows(low.astype(F32))
    acc[...] += dot(low, w_up[...], 1, 0)

    @pl.when(step == pl.num_programs(0) - 1)
    def _():
        normed = normed_one[...]
        middle = normed * gain[0:1] + shift[0:1]
        grad = grad_sum[...] + jnp.where(jnp.abs(middle) < CLIP, acc[...], 0.0)
        back = normalize_back(grad * gain[0:1], normed, inv_one[...])
        grad_res[...] = back
        attn = back.astype(BF)
        grad_attn[...] = attn
        vectors[0:1] = total_rows(grad * normed)
        vectors[1:2] = total_rows(grad)
        vectors[2:3] = total_rows(attn.astype(F32))
        ctx[...] = dot(w_out[...], attn, 0, 1).astype(BF)
        rows = g0.shape[0]
        for j, ref in enumerate((g0, g1, g2, g3)):
            first = pl.multiple_of(xor(pref[0], j) * rows, 64)
            ref[...] = ctx[pl.ds(first, rows), :]


def student_back(pref, grad_ffn, slope, w_up, w_down, grad_sum, normed_one, inv_one, gain, shift, w_out):
    tok, width = grad_ffn.shape
    hidden = w_up.shape[0]
    up, down, wide, row = ffn_specs(tok, width, hidden)
    full, one = whole((tok, width)), whole((tok, 1))
    return call(
        back_kernel,
        pref,
        [grad_ffn, slope, w_up, w_down, grad_sum, normed_one, inv_one, gain, shift, w_out],
        [full, wide, up, down, full, full, one] + [whole((2, width))] * 2 + [whole(w_out.shape)],
        [
            shape_of((tok, hidden), BF),
            shape_of((1, hidden), F32),
            shape_of((tok, width), F32),
            shape_of((tok, width), BF),
        ]
        + [shape_of((width // 4, tok), BF)] * 4
        + [shape_of((3, width), F32)],
        [wide, row, full, full] + [whole((width // 4, tok))] * 4 + [whole((3, width))],
        (hidden // FC,),
        [pltpu.VMEM((tok, width), F32), pltpu.VMEM((width, tok), BF)],
        2 * tok * width * (2 * hidden + width),
    )


def weight_grad_kernel(
    pref, grad_ffn, gelu, grad_hidden, act_one, grad_attn, ctx, grad_down, grad_up, grad_out
):
    @pl.when(pl.program_id(0) == 0)
    def _():
        value = dot(grad_attn[...], ctx[...], 0, 1).astype(BF)
        grad_out[...] = value.reshape(grad_out.shape)

    value = dot(grad_ffn[...], gelu[...], 0, 0).astype(BF)
    grad_down[...] = value.reshape(grad_down.shape)
    value = dot(grad_hidden[...], act_one[...], 0, 0).astype(BF)
    grad_up[...] = value.reshape(grad_up.shape)


def weight_grads(pref, grad_ffn, gelu, grad_hidden, act_one, grad_attn, ctx):
    tok, width = grad_ffn.shape
    hidden = gelu.shape[1]
    count, half = hidden // width, width // 2
    wide = pl.BlockSpec((tok, width), lambda c, i: (0, c))
    full = whole((tok, width))
    return call(
        weight_grad_kernel,
        pref,
        [grad_ffn, gelu, grad_hidden, act_one, grad_attn, ctx],
        [full, wide, wide, full, full, whole((width, tok))],
        [
            shape_of((2, count, half, width), BF),
            shape_of((2 * count, half, width), BF),
            shape_of((2, half, width), BF),
        ],
        [
            pl.BlockSpec((2, 1, half, width), lambda c, i: (0, c, 0, 0)),
            pl.BlockSpec((2, half, width), lambda c, i: (c, 0, 0)),
            whole((2, half, width)),
        ],
        (count,),
        [],
        2 * tok * width * (2 * hidden + width),
    )


def qkv_grad_kernel(pref, d0, d1, d2, d3, x0, x1, x2, x3, out, sums):
    own = pref[0]
    total = None
    count = None
    ones = jnp.ones((8, d0.shape[1]), BF)
    for grad, x in zip((d0, d1, d2, d3), (x0, x1, x2, x3)):
        value = grad[...]
        part = dot(value, jnp.clip(x[...], -CLIP, CLIP), 1, 0)
        line = dot(ones, value, 1, 1)
        total = part if total is None else total + part
        count = line if count is None else count + line
    out[...] = total.astype(BF)
    sums[...] = jnp.zeros_like(sums)
    rows = out.shape[0]
    for j in range(4):

        @pl.when(own == j)
        def _():
            sums[:, j * rows : (j + 1) * rows] = count


def qkv_grad(pref, grads, slots):
    tok, width = slots[0].shape
    rows = grads[0].shape[1]
    return call(
        qkv_grad_kernel,
        pref,
        list(grads) + list(slots),
        [pl.BlockSpec((None, rows, tok), lambda o, i: (o, 0, 0))] * 4 + [whole((tok, width))] * 4,
        [shape_of((3, rows, width), BF), shape_of((3, 8, width), F32)],
        [
            pl.BlockSpec((None, rows, width), lambda o, i: (o, 0, 0)),
            pl.BlockSpec((None, 8, width), lambda o, i: (o, 0, 0)),
        ],
        (3,),
        [],
        2 * 4 * tok * width * 3 * rows,
    )


def input_grad_kernel(pref, e0, e1, e2, e3, wq, wk, wv, grad_res, x, out, acc):
    slot = pl.program_id(0)

    @pl.when(slot == 0)
    def _():
        acc[...] = jnp.zeros_like(acc)

    for j, ref in enumerate((e0, e1, e2, e3)):

        @pl.when(slot == j)
        def _():
            part = dot(ref[0], wq[...], 0, 0)
            part = part + dot(ref[1], wk[...], 0, 0)
            acc[...] += part + dot(ref[2], wv[...], 0, 0)

    @pl.when(slot == 3)
    def _():
        size = jnp.abs(x[...].astype(F32))
        pull = jnp.where(size < CLIP, 1.0, jnp.where(size == CLIP, 0.5, 0.0))
        out[...] = (grad_res[...] + acc[...] * pull).astype(BF)


def input_grad(pref, pieces, weight, grad_res, x):
    tok, width = x.shape
    rows = pieces[0].shape[1]
    full = whole((tok, width))
    return call(
        input_grad_kernel,
        pref,
        list(pieces) + [weight] * 3 + [grad_res, x],
        [whole((3, rows, tok))] * 4
        + [
            pl.BlockSpec((rows, width), lambda j, i, o=o: (o * 4 + lax.bitwise_xor(i[0], j), 0))
            for o in range(3)
        ]
        + [full, full],
        shape_of((tok, width), BF),
        full,
        (4,),
        [pltpu.VMEM((tok, width), F32)],
        2 * 4 * tok * width * 3 * rows,
    )


def place(bit):
    name, mask = bit
    at = lax.axis_index(name)
    upper = lax.rem(lax.div(at, jnp.int32(mask)), jnp.int32(2))
    return upper, {name: at + mask * (1 - 2 * upper)}


class Copies:
    def __init__(self, send, recv, local):
        self.send, self.recv, self.local_sem = send, recv, local
        self.sent, self.planned, self.kept = [], 0, 0

    def plan(self, source, target, device):
        n = self.planned
        self.planned += 1
        return pltpu.make_async_remote_copy(
            src_ref=source,
            dst_ref=target,
            send_sem=self.send.at[n],
            recv_sem=self.recv.at[n],
            device_id=device,
            device_id_type=pl.DeviceIdType.MESH,
        )

    def remote(self, source, target, device):
        copy = self.plan(source, target, device)
        copy.start()
        self.sent.append(copy)
        return copy

    def plan_local(self, source, target):
        self.kept += 1
        return pltpu.make_async_copy(source, target, self.local_sem.at[self.kept - 1])

    def local(self, source, target):
        copy = self.plan_local(source, target)
        copy.start()
        return copy

    def finish(self):
        for copy in self.sent:
            copy.wait_send()


def window(ref, region):
    row, rows, col, cols = region
    return ref.at[pl.ds(row, rows), pl.ds(col, cols)]


def add_window(target, left, right, region, start):
    row, rows, col, cols = region
    step = 48 if rows % 48 == 0 else 16

    def body(i, carry):
        there = pl.ds(pl.multiple_of(row + i * step, 16), step)
        here = pl.ds(pl.multiple_of(start + i * step, 16), step)
        value = left[there, pl.ds(col, cols)].astype(F32) + right[here, :cols].astype(F32)
        target[there, pl.ds(col, cols)] = value.astype(target.dtype)
        return carry

    lax.fori_loop(0, rows // step, body, 0)


def scatter_sum(copies, work, far, full, bits):
    rows, cols = work.shape
    region, used, parts = (0, rows, 0, cols), 0, []
    for n, bit in enumerate(bits):
        upper, device = place(bit)
        row, rows, col, cols = region
        if (rows // 2) % 16 == 0:
            rows //= 2
            kept = (pl.multiple_of(row + upper * rows, 16), rows, col, cols)
            sent = (pl.multiple_of(row + (1 - upper) * rows, 16), rows, col, cols)
        else:
            cols //= 2
            kept = (row, rows, pl.multiple_of(col + upper * cols, 128), cols)
            sent = (row, rows, pl.multiple_of(col + (1 - upper) * cols, 128), cols)
        slot = far.at[pl.ds(used, rows), pl.ds(0, cols)]
        copy = copies.remote(window(work, sent), slot, device)
        yield
        copy.wait_recv()
        add_window(full if n == len(bits) - 1 else work, work, far, kept, used)
        used += rows
        region = kept
        parts.append((bit, kept))
    return parts


def sum_flow(copies, own, other, work, near, far, full, result, core, bits):
    copy = copies.remote(other, near, place(core)[1])
    load = copies.local(own, work)
    yield
    copy.wait_recv()
    load.wait()
    add_window(work, work, near, (0, work.shape[0], 0, work.shape[1]), 0)
    parts = yield from scatter_sum(copies, work, far, full, bits)
    for bit, kept in reversed(parts):
        copy = copies.remote(window(full, kept), window(full, kept), place(bit)[1])
        yield
        copy.wait_recv()
    store = copies.local(full, result)
    yield
    store.wait()


def vector_flow(copies, sums, far, bits):
    for n, bit in enumerate(bits):
        yield
        copy = copies.remote(sums.at[n], far.at[n], place(bit)[1])
        yield
        copy.wait_recv()
        sums[n + 1] = sums[n] + far[n]


def rotate(items, count):
    count %= len(items)
    return items[count:] + items[:count]


def remote_call(kernel, args, in_specs, outs, out_specs, scratch, copies, local, number):
    sems = pltpu.SemaphoreType.DMA
    return pl.pallas_call(
        kernel,
        in_specs=in_specs,
        out_specs=out_specs,
        out_shape=outs,
        scratch_shapes=scratch + [sems((copies,)), sems((copies,)), sems((local,))],
        compiler_params=pltpu.CompilerParams(
            vmem_limit_bytes=VMEM_LIMIT, collective_id=number, has_side_effects=True
        ),
        cost_estimate=pl.CostEstimate(flops=5 * 10**10, bytes_accessed=10**8, transcendentals=0),
    )(*args)


ANY = pl.BlockSpec(memory_space=pl.ANY)
IN_VMEM = pl.BlockSpec(memory_space=pltpu.VMEM)


def binarize_rows(source, target):
    rows, cols = target.shape
    step = 96 if cols < 2048 else 32

    def body(i, carry):
        at = pl.ds(pl.multiple_of(i * step, 16), step)
        value = source[at, :]
        scale = jnp.sum(jnp.abs(value), axis=1, keepdims=True) * (1.0 / cols)
        signed = jnp.where(value > 0, scale, jnp.where(value < 0, -scale, 0.0))
        target[at, :] = signed.astype(BF)
        return carry

    lax.fori_loop(0, rows // step, body, 0)


def entry_kernel(
    seq, core, hidden, teach, segments, l_qkv, l_out, l_up, l_down, t_qkv, t_out, t_up, t_down, bias,
    o_pref, o_qkv, x0, x1, x2, x3, o_teach, b_qkv, b_out, b_up, b_down, e_qkv, e_out, e_up, e_down,
    xs, held, w_qkv, w_out, w_up, w_down, f_qkv, f_out, f_up, f_down,
    s_qkv, s_out, s_up, s_down, proj, others, send, recv, local,
):
    tok, width = hidden.shape
    parts, size = 4, tok // 4
    along, next_chip = place(seq[0])
    side_of, sibling = place(core)
    half = lax.div(lax.axis_index("seq"), jnp.int32(2))
    stays = half == side_of
    moves = half != side_of
    partner = {"seq": 2 * side_of + along, "fsdp": half}
    mesh = pl.DeviceIdType.MESH

    barrier = pltpu.get_barrier_semaphore()
    for device in (next_chip, sibling):
        pl.semaphore_signal(barrier, inc=1, device_id=device, device_id_type=mesh)

    @pl.when(moves)
    def _():
        pl.semaphore_signal(barrier, inc=1, device_id=partner, device_id_type=mesh)
        pl.semaphore_wait(barrier, 3)

    @pl.when(stays)
    def _():
        pl.semaphore_wait(barrier, 2)

    copies = Copies(send, recv, local)
    cuts = [pl.ds(c * size, size) for c in range(parts)]
    swap = [copies.plan(hidden.at[cut], xs.at[0, cut], partner) for cut in cuts]
    load = [copies.plan_local(hidden.at[cut], xs.at[0, cut]) for cut in cuts]
    over = [copies.plan(xs.at[0, cut], xs.at[1, cut], next_chip) for cut in cuts]
    beside = [copies.plan(xs.at[0, cut], xs.at[2, cut], sibling) for cut in cuts]
    relay = [copies.plan(xs.at[1, cut], xs.at[3, cut], sibling) for cut in cuts]
    t_swap = copies.plan(teach, held, partner)
    t_load = copies.plan_local(teach, held)
    seg_copy = copies.remote(segments, others, sibling)

    @pl.when(moves)
    def _():
        for copy in swap:
            copy.start()

    @pl.when(stays)
    def _():
        for copy in load:
            copy.start()
        t_load.start()

    latent = [
        (copies.local(source, target), target)
        for source, target in ((l_qkv, f_qkv), (l_out, f_out), (l_up, f_up), (l_down, f_down))
    ]
    staged = [
        (copies.local(source, target), target, result)
        for source, target, result in (
            (t_qkv, s_qkv, e_qkv),
            (t_out, s_out, e_out),
            (t_up, s_up, e_up),
            (t_down, s_down, e_down),
        )
    ]

    @pl.when(stays)
    def _():
        for c in range(parts):
            load[c].wait()
            over[c].start()
            beside[c].start()

    rows_qkv = l_qkv.shape[0]
    mine = w_qkv.at[pl.ds(pl.multiple_of(side_of * rows_qkv, 16), rows_qkv)]
    latent[0][0].wait()
    binarize_rows(f_qkv, mine)
    qkv_copy = copies.remote(mine, mine, sibling)
    stores, arrivals = [], []
    for (copy, source), target, result in zip(
        latent[1:], (w_out, w_up, w_down), (b_out, b_up, b_down)
    ):
        copy.wait()
        binarize_rows(source, target)
        arrivals.append(copies.remote(target, result.at[side_of], sibling))
        stores.append(copies.local(target, result.at[side_of]))
    for source, (_, _, result) in zip((t_qkv, t_out, t_up, t_down), staged):
        arrivals.append(copies.remote(source, result.at[side_of], sibling))
    for copy, target, result in staged:
        copy.wait()
        stores.append(copies.local(target, result.at[side_of]))

    @pl.when(moves)
    def _():
        for c in range(parts):
            swap[c].wait_recv()
            over[c].start()
            beside[c].start()
        t_swap.start()

    qkv_copy.wait_recv()
    stores.append(copies.local(w_qkv, b_qkv))
    rows = width // 4
    own = along + 2 * side_of

    def project(slot):
        act = jnp.clip(xs[slot], -CLIP, CLIP)
        first = (1 - along if slot % 2 else along) + 2 * (1 - side_of if slot // 2 else side_of)
        there = pl.ds(pl.multiple_of(first * tok, 128), tok)
        for part in range(3):
            at = pl.multiple_of(part * width + own * rows, 16)
            value = dot(w_qkv[pl.ds(at, rows), :], act, 1, 1)
            if part != 1:
                value = value + bias[part // 2, pl.ds(pl.multiple_of(own * rows, 8), rows), :]
            proj[part * rows : (part + 1) * rows, there] = value.astype(BF)
        stores.append(copies.local(proj.at[:, there], o_qkv.at[:, there]))
        stores.append(copies.local(xs.at[slot], (x0, x1, x2, x3)[slot]))

    seg_copy.wait_recv()
    counts = [jnp.sum(jnp.where(segments[...] == k, 1.0, 0.0)) for k in (1, 2, 3)]
    theirs = [jnp.sum(jnp.where(others[...] == k, 1.0, 0.0)) for k in (1, 2, 3)]
    first, second, third = [
        jnp.where(stays, a, b).astype(jnp.int32) for a, b in zip(counts, theirs)
    ]
    o_pref[0] = own
    o_pref[1] = jnp.where(first == LONG, 0, jnp.where(second == LONG, first, first + second))
    o_pref[2] = jnp.where(first == LONG, second, jnp.where(second == LONG, third, first))

    project(0)
    for copy in beside:
        copy.wait_recv()
    project(2)
    for c in range(parts):
        over[c].wait_recv()
        relay[c].start()
    project(1)
    for copy in relay:
        copy.wait_recv()
    project(3)

    @pl.when(moves)
    def _():
        t_swap.wait_recv()

    @pl.when(stays)
    def _():
        t_load.wait()

    stores.append(copies.local(held, o_teach))
    for copy in arrivals:
        copy.wait_recv()
    for copy in stores:
        copy.wait()

    @pl.when(moves)
    def _():
        for copy in swap + [t_swap]:
            copy.wait_send()

    for copy in over + beside + relay:
        copy.wait_send()
    copies.finish()


def entry(seq, core, hidden, teach, segments, latents, teachers, bias):
    tok, width = hidden.shape
    halves = [w.shape for w in latents]
    sides = [shape_of((2,) + shape, BF) for shape in halves]
    own = [pltpu.VMEM(shape, BF) for shape in halves]
    sides[0] = shape_of((2 * halves[0][0], halves[0][1]), BF)
    sides_t = [shape_of((2,) + shape, BF) for shape in halves]
    outs = remote_call(
        lambda *refs: entry_kernel(seq, core, *refs),
        [hidden, teach, segments] + list(latents) + list(teachers) + [bias],
        [ANY] * 2 + [IN_VMEM] + [ANY] * 8 + [IN_VMEM],
        [shape_of((3,), jnp.int32), shape_of((3 * width // 4, 4 * tok), BF)]
        + [shape_of((tok, width), BF)] * 5
        + sides
        + sides_t,
        [pl.BlockSpec(memory_space=pltpu.SMEM)] + [ANY] * 14,
        [pltpu.VMEM((4, tok, width), BF), pltpu.VMEM((tok, width), BF)]
        + [pltpu.VMEM(sides[0].shape, BF)]
        + own[1:]
        + [pltpu.VMEM(shape, F32) for shape in halves]
        + own
        + [pltpu.VMEM((3 * width // 4, 4 * tok), BF), pltpu.VMEM(segments.shape, jnp.int32)],
        26,
        30,
        3,
    )
    pref, qkv, x0, x1, x2, x3, teach = outs[:7]
    weights = [w.reshape((-1, w.shape[-1])) for w in outs[7:]]
    return pref, qkv, (x0, x1, x2, x3), teach, weights[:4], weights[4:]


class Pump:
    def __init__(self, step):
        self.step, self.events = step, []

    def add(self, time, flow):
        gap = next(flow)
        self.events.append([time + (gap or 0), len(self.events), flow])

    def run(self, time=1e9):
        while self.events:
            event = min(self.events, key=lambda e: e[:2])
            if event[0] > time:
                return
            try:
                gap = next(event[2])
                event[0] += self.step if gap is None else gap
            except StopIteration:
                self.events.remove(event)


def head_flow(copies, n, gh, work, far, full, result, seq, core, dp):
    side_of, partner = place(core)
    along = place(seq[0])[0]
    if n == 1:
        copy = copies.remote(gh.at[2 - 2 * side_of], work, partner)
        yield
        copy.wait_recv()
    else:
        load = copies.local(gh.at[n // 2 + side_of], work)
        yield
        load.wait()
    bits = (rotate(dp, n) if n < 2 else dp) + seq[1:]
    mine = full.at[2 * n + along]
    parts = yield from scatter_sum(copies, work, far, mine, bits)
    steps = [(bit, kept, False) for bit, kept in reversed(parts)]
    cut = len(steps) if n == 2 else 1
    held = steps[cut][1] if n < 2 else (0, mine.shape[0], 0, mine.shape[1])
    steps = steps[:cut] + [(seq[0], held, False)] + [(b, k, True) for b, k, _ in steps[cut:]]
    for bit, (row, size, col, cols), both in steps:
        first, count = (2 * n, 2) if both else (2 * n + along, 1)
        part = full.at[pl.ds(first, count), pl.ds(row, size), pl.ds(col, cols)]
        copy = copies.remote(part, part, place(bit)[1])
        yield
        copy.wait_recv()
    store = copies.local(full.at[pl.ds(2 * n, 2)], result.at[pl.ds(2 * n, 2)])
    yield
    store.wait()


def tail_kernel(
    dp, seq, core, scale, pref, down, up, out, two, one, bias,
    q_in, k_in, v_in, g0, g1, g2, g3, cf_in, lse, x0, x1, x2, x3, w_in, res_in,
    down_sum, up_sum, out_sum, totals, qkv_sum, hidden_out,
    work, near, far, full, sums, sums_far, gh, h_work, h_far, h_full,
    qs, ks, vs, gp, cf, xs, weight, res, qa, ka, va, ga, gs, dqs, dks, dvs, dn, er, acc, hid,
    send, recv, local,
):
    shift, border = pref[1], pref[2]
    heads_all, total = qs.shape
    hdim = qa.shape[0] - AUG
    heads = heads_all // hdim
    tok = total // 4
    width = xs.shape[2]
    cont, others = total - PROMPT, PROMPT + LONG
    back = lax.rem(cont - shift, cont)
    along, next_chip = place(seq[0])
    side_of, sibling = place(core)
    across = {**next_chip, **sibling}
    half = lax.div(lax.axis_index("seq"), jnp.int32(2))
    stays, moves = half == side_of, half != side_of
    partner = {"seq": 2 * side_of + along, "fsdp": half}
    own = along + 2 * side_of

    def place_of(slot):
        return (1 - along if slot % 2 else along) + 2 * (1 - side_of if slot // 2 else side_of)

    copies = Copies(send, recv, local)
    first_loads = [
        copies.local(source, target)
        for source, target in (
            (g0, gp.at[0]), (g1, gp.at[1]), (g2, gp.at[2]), (g3, gp.at[3]),
            (q_in, qs), (k_in, ks), (v_in, vs), (cf_in, cf),
        )
    ]

    mesh = pl.DeviceIdType.MESH
    barrier = pltpu.get_barrier_semaphore()
    friends = [place(bit)[1] for bit in dp + seq] + [sibling, across]
    for device in friends:
        pl.semaphore_signal(barrier, inc=1, device_id=device, device_id_type=mesh)

    @pl.when(moves)
    def _():
        pl.semaphore_signal(barrier, inc=1, device_id=partner, device_id_type=mesh)
        pl.semaphore_wait(barrier, len(friends) + 1)

    @pl.when(stays)
    def _():
        pl.semaphore_wait(barrier, len(friends))

    pump = Pump(6.5)
    count, rows_half = down.shape[1:3]
    ups = [(up.at[side_of, p], up.at[1 - side_of, p], up_sum.at[p]) for p in range(count)]
    downs = [
        (
            down.at[side_of, p],
            down.at[1 - side_of, p],
            down_sum.at[:, pl.ds(p * width, width)],
        )
        for p in range(count)
    ]
    queue = [(dp + seq, p, k) for k, p in enumerate(ups)]
    queue += [(dp[::-1] + seq, p, k) for k, p in enumerate(downs)]
    queue.append((seq[:1] + dp + seq[1:], (out.at[side_of], out.at[1 - side_of], out_sum), 1))
    queue.sort(key=lambda item: item[2])
    for n, (bits, (mine, theirs, result), k) in enumerate(queue):
        flow = sum_flow(
            copies, mine, theirs, work.at[n], near.at[n], far.at[n], full.at[n], result, core, bits
        )
        pump.add(2.0 + 5 * k, flow)

    late_loads = [
        copies.local(source, target)
        for source, target in (
            (x0, xs.at[0]), (x1, xs.at[1]), (x2, xs.at[2]), (x3, xs.at[3]),
            (w_in, weight), (res_in, res),
        )
    ]
    for copy in first_loads:
        copy.wait()

    row = lax.broadcasted_iota(jnp.int32, (AUG, total), 0)
    ones = jnp.where(row < 3, 1.0, 0.0).astype(BF)
    ka[hdim:, :] = ones
    va[hdim:, :] = ones
    clock = 1.0
    pieces = {1: [], 2: [], 3: []}
    devices = {1: next_chip, 2: sibling, 3: across}
    for h in range(heads):
        lines = slice(h * hdim, (h + 1) * hdim)
        for j in range(4):
            gs[:, pl.ds(pl.multiple_of(place_of(j) * tok, 128), tok)] = gp[j, lines, :].astype(F32)
        qa[:hdim, :] = qs[lines, :]
        ka[:hdim, :] = ks[lines, :]
        va[:hdim, :] = vs[lines, :]
        grad = roll_cont(gs[...], back)
        ga[:hdim, :] = grad.astype(BF)
        ga[hdim:, :] = thirds(-jnp.sum(grad * cf[lines, :], axis=0, keepdims=True))
        qa[hdim:, :] = thirds(lse[h] * (-1.0 / scale))
        seen = set()
        for start, parts in block_list(total, QB):
            queries = slice(start, start + QB)
            grad_q = None
            for lo, hi in parts:
                for key in range(lo, hi, KB):
                    keys = slice(key, key + KB)
                    value = dot(qa[:, queries], ka[:, keys], 0, 0) * scale
                    if lo >= others:
                        mask = same_segment((QB, KB), 1, key - others, start - others, border)
                        value = jnp.where(mask, value, -1e30)
                    prob = jnp.exp2(value)
                    grad_p = dot(ga[:, queries], va[:, keys], 0, 0)
                    grad_s = (prob * grad_p).astype(BF)
                    grad_v = dot(ga[:hdim, queries], prob.astype(BF), 1, 0)
                    grad_k = dot(qa[:hdim, queries], grad_s, 1, 0)
                    part = dot(ka[:hdim, keys], grad_s, 1, 1)
                    grad_q = part if grad_q is None else grad_q + part
                    if key in seen:
                        dvs[:, keys] += grad_v
                        dks[:, keys] += grad_k
                    else:
                        dvs[:, keys] = grad_v
                        dks[:, keys] = grad_k
                        seen.add(key)
                    clock += 0.65
            dqs[:, queries] = grad_q
            pump.run(clock)
        inv = 1.0 / hdim**0.5
        for part, (ref, factor) in enumerate(((dqs, inv), (dks, inv), (dvs, 1.0))):
            gs[...] = roll_cont(ref[...] * factor, shift)
            for j in range(4):
                there = pl.ds(pl.multiple_of(place_of(j) * tok, 128), tok)
                dn[j, part, lines, :] = gs[:, there].astype(BF)
        for j in (1, 3, 2):
            at = pl.ds(h * hdim, hdim)
            copy = copies.remote(dn.at[j, :, at, :], er.at[j - 1, :, at, :], devices[j])
            pieces[j].append(copy)
        clock += 1.5
        pump.run(clock)

    for copy in late_loads:
        copy.wait()
    rows = width // 4
    one_rows = jnp.ones((8, tok), BF)
    counts = []
    for o in range(3):
        value, line = None, None
        for j in range(4):
            part = dot(dn[j, o], jnp.clip(xs[j], -CLIP, CLIP), 1, 0)
            ends = dot(one_rows, dn[j, o], 1, 1)
            value = part if value is None else value + part
            line = ends if line is None else line + ends
        gh[o] = value.astype(BF)
        counts.append(line)
        clock += 2.7
        pump.run(clock)
    sums[0] = jnp.zeros(sums.shape[1:], F32)
    for j in range(4):

        @pl.when(own == j)
        def _():
            sums[0, 0:1, j * rows : (j + 1) * rows] = counts[0][0:1]
            sums[0, 1:2, j * rows : (j + 1) * rows] = counts[2][0:1]

    sums[0, 2:3] = one[2:3]
    sums[0, 3:4] = two[2:3]
    sums[0, 4:5] = one[0:1]
    sums[0, 5:6] = two[0:1]
    sums[0, 6:7] = one[1:2]
    sums[0, 7:8] = two[1:2]
    for p in range(count):
        sums[0, 8 + p : 9 + p] = bias[:, p * width : (p + 1) * width]

    swap = copies.plan(hid, hidden_out, partner)
    keep = copies.plan_local(hid, hidden_out)

    def hidden_flow():
        yield 0.0
        for gap, j in ((2.0, 0), (5.0, 2), (3.0, 1), (0.0, 3)):
            for copy in pieces.get(j, []):
                copy.wait_recv()
            part = None
            for o in range(3):
                at = pl.multiple_of(o * width + place_of(j) * rows, 16)
                source = dn[0, o] if j == 0 else er[j - 1, o]
                piece = dot(source, weight[pl.ds(at, rows), :], 0, 0)
                part = piece if part is None else part + piece
            if j == 0:
                acc[...] = part
            elif j != 3:
                acc[...] += part
            else:
                size = jnp.abs(xs[0].astype(F32))
                pull = jnp.where(size < CLIP, 1.0, jnp.where(size == CLIP, 0.5, 0.0))
                hid[...] = (res[...] + (acc[...] + part) * pull).astype(BF)
            yield gap

        @pl.when(moves)
        def _():
            swap.start()

        @pl.when(stays)
        def _():
            keep.start()

        yield 30.0

        @pl.when(moves)
        def _():
            swap.wait_recv()
            swap.wait_send()

        @pl.when(stays)
        def _():
            keep.wait()

    pump.add(clock, hidden_flow())
    for n in (0, 2, 1):
        flow = head_flow(
            copies, n, gh, h_work.at[n], h_far.at[n], h_full, qkv_sum, seq, core, dp
        )
        pump.add(clock + 1, flow)
    pump.add(clock + 1, vector_flow(copies, sums, sums_far, [core] + dp + seq))
    pump.run()
    totals[...] = sums[sums.shape[0] - 1]
    copies.finish()


def tail(
    dp, seq, core, pref, down, up, out, two, one, bias, rolled, grads, cf, lse, slots, weight, res
):
    sides, count, half, width = down.shape
    pieces, steps, lines = 2 * count + 1, len(dp) + len(seq), 16
    rows, total = rolled[0].shape
    tok = total // 4
    heads = HEADS // 4
    hdim = rows // heads
    scale = LOG2E / hdim**0.5
    smem = pl.BlockSpec(memory_space=pltpu.SMEM)
    return remote_call(
        lambda *refs: tail_kernel(dp, seq, core, scale, *refs),
        [pref, down, up, out, two, one, bias]
        + list(rolled)
        + list(grads)
        + [cf, lse]
        + list(slots)
        + [weight, res],
        [smem] + [ANY] * 3 + [IN_VMEM] * 3 + [ANY] * 8 + [IN_VMEM] + [ANY] * 6,
        [
            shape_of((half, count * width), BF),
            shape_of((count, half, width), BF),
            shape_of((half, width), BF),
            shape_of((lines, width), F32),
            shape_of((6, rows, width), BF),
            shape_of((tok, width), BF),
        ],
        [ANY] * 3 + [IN_VMEM] + [ANY] * 2,
        [pltpu.VMEM((pieces, half, width), BF)] * 4
        + [pltpu.VMEM((steps + 2, lines, width), F32), pltpu.VMEM((steps + 1, lines, width), F32)]
        + [pltpu.VMEM((3, rows, width), BF)] * 3
        + [pltpu.VMEM((6, rows, width), BF)]
        + [pltpu.VMEM((rows, total), BF)] * 3
        + [pltpu.VMEM((4, rows, tok), BF), pltpu.VMEM((rows, total), F32)]
        + [pltpu.VMEM((4, tok, width), BF), pltpu.VMEM(weight.shape, BF)]
        + [pltpu.VMEM((tok, width), F32)]
        + [pltpu.VMEM((hdim + AUG, total), BF)] * 4
        + [pltpu.VMEM((hdim, total), F32)] * 4
        + [pltpu.VMEM((4, 3, rows, tok), BF), pltpu.VMEM((3, 3, rows, tok), BF)]
        + [pltpu.VMEM((tok, width), F32), pltpu.VMEM((tok, width), BF)],
        pieces * (1 + 2 * steps) + steps + 1 + 3 * heads + 1 + 3 * (2 * steps - 1) + 1,
        2 * pieces + 14 + 1 + 5,
        4,
    )


def binarize(latent):
    row_scale = jnp.mean(jnp.abs(latent), axis=1, keepdims=True)
    return (row_scale * jnp.sign(latent)).astype(BF)


def segment_info(segments):
    sizes_of = [jnp.sum((segments == k).astype(jnp.int32)) for k in (1, 2, 3)]
    first, second, third = sizes_of
    shift = jnp.where(first == LONG, 0, jnp.where(second == LONG, first, first + second))
    border = jnp.where(first == LONG, second, jnp.where(second == LONG, third, first))
    return jnp.stack([shift, border])


def quarters(own):
    along = to_slot(own, 1)
    return (own, along, to_slot(own, 2), to_slot(along, 2))


def exchange(pieces):
    return (pieces[0],) + tuple(to_slot(pieces[j], j) for j in (1, 2, 3))


def on_device(
    hidden, teacher_hidden, segments, latent_qkv, latent_out, latent_up, latent_down,
    biases, up_bias, norm_gains, norm_shifts, teacher_qkv, teacher_out, teacher_up, teacher_down,
):
    seq_at, fsdp_at = lax.axis_index("seq"), lax.axis_index("fsdp")
    fsdp = lax.axis_size("fsdp")
    core = fsdp_at % 2
    own = (seq_at % 2 + 2 * core).astype(jnp.int32)
    width = hidden.shape[2]

    bias_cols = biases[:2].reshape(2, width, 1)
    latents = (latent_qkv, latent_out, latent_up, latent_down)
    teachers = (teacher_qkv, teacher_out, teacher_up, teacher_down)
    if fsdp == 2:
        pref, qkv, x_slots, teach, bins, t_weights = entry(
            bit_list("seq"), bit_list("fsdp")[0], hidden[0], teacher_hidden[0], segments,
            latents, teachers, bias_cols,
        )
        x = x_slots[0]
    else:
        info = segment_info(segments)
        info = jnp.where(core == seq_at // 2, info, flip(info, fsdp=1))
        pref = jnp.concatenate([own[None], info]).astype(jnp.int32)
        x = swap_groups(hidden[0])
        x_slots = quarters(x)
        bins = [gather_rows(binarize(w)) for w in latents]
        teach = swap_groups(teacher_hidden[0])
        t_weights = [gather_rows(w) for w in teachers]
        qkv = qkv_project(pref, x_slots, bins[0], bias_cols)
    bin_qkv, bin_out, bin_up, bin_down = bins
    t_qkv, t_out, t_up, t_down = t_weights
    t_along, t_beside = to_slot(teach, 1), to_slot(teach, 2)
    *ctx_slots, ctx_full, lse, q_roll, k_roll, v_roll = attention(pref, qkv, True)
    t_along, ctx_slots = lax.optimization_barrier((t_along, ctx_slots))
    t_slots = (teach, t_along, t_beside, to_slot(t_along, 2))
    ctx_pieces = exchange(ctx_slots)

    t_heads = qkv_project(pref, t_slots, t_qkv, None)
    *tctx_slots, _unused, _unused_too = attention(pref, t_heads, False)
    tctx_slots, ctx_pieces = lax.optimization_barrier((tctx_slots, ctx_pieces))
    tctx_pieces = exchange(tctx_slots)

    gain, shift = norm_gains, norm_shifts
    (
        ctx, act_one, normed_one, inv_one, gelu, slope, result, normed_two, inv_two,
    ) = student_ffn(
        pref, ctx_pieces, x, bin_out, bin_up, bin_down,
        biases[2:3], up_bias[None], biases[3:4], gain, shift,
    )
    student_out = swap_groups(result)
    grad_sum, grad_ffn, vec_two = teacher_ffn(
        pref, tctx_pieces, teach, t_out, t_up, t_down, gain, shift, normed_two, inv_two
    )
    grad_hidden, grad_up_bias, grad_res, grad_attn, *gctx_slots, vec_one = student_back(
        pref, grad_ffn, slope, bin_up, bin_down, grad_sum, normed_one, inv_one, gain, shift, bin_out
    )
    gctx_pieces = exchange(gctx_slots)
    grad_down, grad_up, grad_out = weight_grads(
        pref, grad_ffn, gelu, grad_hidden, act_one, grad_attn, ctx
    )
    dp_bits, seq_bits, fsdp_bits = bit_list("dp"), bit_list("seq"), bit_list("fsdp")
    rows, hidden_units = width // 4, up_bias.shape[0]

    if fsdp == 2:
        total_down, total_up, total_out, vectors, total_qkv, hidden_grad = tail(
            dp_bits, seq_bits, fsdp_bits[0], pref,
            grad_down, grad_up.reshape(grad_down.shape), grad_out, vec_two, vec_one, grad_up_bias,
            (q_roll, k_roll, v_roll), gctx_pieces, ctx_full, lse, x_slots, bin_qkv, grad_res,
        )
        total_up = total_up.reshape(-1, width)
        total_qkv = total_qkv.reshape(-1, width)
    else:
        dqkv_slots = attention_back(pref, qkv, gctx_pieces, ctx_full, lse)
        dqkv_pieces = exchange(dqkv_slots)
        grad_heads, head_sums = qkv_grad(pref, dqkv_slots, x_slots)
        hidden_grad = swap_groups(input_grad(pref, dqkv_pieces, bin_qkv, grad_res, x))

        def reduce_grad(value, bits):
            for bit in reversed(fsdp_bits):
                value = halve(value, bit)
            return all_reduce(value, bits)

        grad_down = grad_down.transpose(0, 2, 1, 3).reshape(width, hidden_units)
        total_down = reduce_grad(grad_down, dp_bits + seq_bits)
        total_up = reduce_grad(grad_up.reshape(hidden_units, width), dp_bits[::-1] + seq_bits)
        total_out = reduce_grad(
            grad_out.reshape(width, width), seq_bits[:1] + dp_bits + seq_bits[1:]
        )
        blocks = all_reduce(
            grad_heads.reshape(3 * rows, width), dp_bits + seq_bits[1:] + fsdp_bits[1:]
        )
        blocks = blocks.reshape(1, 3, rows, width)
        blocks = double(double(blocks, seq_bits[0]), fsdp_bits[0])
        whole_qkv = blocks.transpose(1, 0, 2, 3).reshape(3 * width, width)
        part = 3 * width // fsdp
        total_qkv = lax.dynamic_slice_in_dim(whole_qkv, fsdp_at * part, part, 0)
        vectors = jnp.concatenate(
            [
                head_sums[0, :1],
                head_sums[2, :1],
                vec_one[2:3],
                vec_two[2:3],
                vec_one[0:1],
                vec_two[0:1],
                vec_one[1:2],
                vec_two[1:2],
                grad_up_bias.reshape(-1, width),
            ]
        )
        vectors = sum_small(vectors, dp_bits + seq_bits + fsdp_bits)
    hid_bias = vectors[8 : 8 + hidden_units // width].reshape(-1)
    share, hid_share = width // fsdp, hid_bias.shape[0] // fsdp
    cols = lax.dynamic_slice_in_dim(vectors[:8], fsdp_at * share, share, 1)
    return (
        student_out[None],
        hidden_grad[None],
        total_qkv.astype(F32),
        total_out.astype(F32),
        total_up.astype(F32),
        total_down.astype(F32),
        cols[0:4],
        lax.dynamic_slice_in_dim(hid_bias, fsdp_at * hid_share, hid_share, 0),
        cols[4:6],
        cols[6:8],
    )


def solution(mesh):
    tokens = P(("dp", "fsdp"), "seq", None)
    rows = P("fsdp", None)
    return jax.shard_map(
        on_device,
        mesh=mesh,
        in_specs=(tokens, tokens, P(("dp", "fsdp"), None)) + (rows,) * 4 + (P(),) * 4 + (rows,) * 4,
        out_specs=(tokens, tokens)
        + (rows,) * 4
        + (P(None, "fsdp"), P("fsdp"), P(None, "fsdp"), P(None, "fsdp")),
        check_vma=False,
    )
```

```python
import jax
import jax.numpy as jnp
from jax import lax
from jax.experimental import pallas as pl
from jax.experimental.pallas import tpu as pltpu
from jax.sharding import PartitionSpec as P

HEADS = 12
PROMPT = 1024
LONG = 1024
CLIP = 2.5
EPS = 1e-05
AXES = ("dp", "seq", "fsdp")
BF = jnp.bfloat16
F32 = jnp.float32
LOG2E = 1.4426950408889634
QB = 512
KC = 256
KB = 512
FC = 1024
AUG = 16
VMEM_LIMIT = 56 * 2**20
ORDERS = ((0, 1, 2), (1, 0, 2), (0, 2, 1), (1, 2, 0), (2, 0, 1), (2, 1, 0))
PIECE_PLAN = (
    (2, 20.0, 95.4, 86.9),
    (0, 170.2, 97.1, 111.4),
    (1, 20.8, 80.9, 96.5),
    (3, 19.5, 100.8, 153.8),
    (1, 294.8, 80.8, 122.2),
    (0, 19.9, 101.0, 166.8),
    (4, 10.7, 73.5, 199.5),
    (1, 169.6, 90.3, 133.2),
    (3, 33.7, 57.9, 88.5),
)
HEAD_PLAN = (
    (0, 1, 24.6, 50.5, 104.3),
    (1, 1, 29.3, 52.8, 136.5),
    (0, 3, 312.0, 93.4, 93.4),
)
HIDDEN_PLAN = (0.0, (203.8, 62.6, 390.1, 383.5))
VECTOR_PLAN = (7.8, 182.0)


def dot(left, right, left_dim, right_dim):
    return lax.dot_general(
        left, right, (((left_dim,), (right_dim,)), ((), ())), preferred_element_type=F32
    )


def xor(first, second):
    return lax.bitwise_xor(first, jnp.int32(second))


def sizes():
    return tuple(lax.axis_size(name) for name in AXES)


def permute(values, target):
    dp, seq, fsdp = sizes()
    pairs = []
    for d in range(dp):
        for s in range(seq):
            for f in range(fsdp):
                td, ts, tf = target(d, s, f)
                pairs.append(((d * seq + s) * fsdp + f, (td * seq + ts) * fsdp + tf))
    return lax.ppermute(values, AXES, pairs)


def flip(values, dp=0, seq=0, fsdp=0):
    return permute(values, lambda d, s, f: (d ^ dp, s ^ seq, f ^ fsdp))


def swap_groups(values):
    return permute(
        values, lambda d, s, f: (d, 2 * (f % 2) + s % 2, f - f % 2 + s // 2)
    )


def to_slot(values, slot):
    return flip(values, seq=slot & 1, fsdp=slot >> 1)


def bit_list(name):
    count = lax.axis_size(name)
    out, bit = [], 1
    while bit < count:
        out.append((name, bit))
        bit *= 2
    return out


def flip_bit(values, bit):
    return flip(values, **{bit[0]: bit[1]})


def side(bit):
    return lax.bitwise_and(lax.axis_index(bit[0]), bit[1]) != 0


def halve(values, bit):
    upper = side(bit).astype(jnp.int32)
    half = values.shape[0] // 2
    sent = lax.dynamic_slice_in_dim(values, (1 - upper) * half, half, 0)
    kept = lax.dynamic_slice_in_dim(values, upper * half, half, 0)
    got = flip_bit(sent, bit)
    return (kept.astype(F32) + got.astype(F32)).astype(values.dtype)


def double(values, bit):
    got = flip_bit(values, bit)
    return jnp.where(
        side(bit),
        jnp.concatenate([got, values], axis=0),
        jnp.concatenate([values, got], axis=0),
    )


def gather_rows(values):
    for bit in bit_list("fsdp"):
        values = double(values, bit)
    return values


def all_reduce(values, bits):
    for bit in bits:
        values = halve(values, bit)
    for bit in reversed(bits):
        values = double(values, bit)
    return values


def sum_small(values, bits):
    for bit in bits:
        values = values + flip_bit(values, bit)
    return values


def whole(shape):
    return pl.BlockSpec(shape, lambda *_: (0,) * len(shape))


def call(kernel, pref, args, in_specs, outs, out_specs, grid, scratch, flops, trans=0):
    moved = sum(a.size * a.dtype.itemsize for a in args)
    moved += sum(o.size * o.dtype.itemsize for o in jax.tree.leaves(outs))
    return pl.pallas_call(
        kernel,
        grid_spec=pltpu.PrefetchScalarGridSpec(
            num_scalar_prefetch=1,
            grid=grid,
            in_specs=in_specs,
            out_specs=out_specs,
            scratch_shapes=scratch,
        ),
        out_shape=outs,
        compiler_params=pltpu.CompilerParams(vmem_limit_bytes=VMEM_LIMIT),
        cost_estimate=pl.CostEstimate(flops=flops, bytes_accessed=moved, transcendentals=trans),
    )(pref, *args)


def shape_of(shape, dtype):
    return jax.ShapeDtypeStruct(shape, dtype)


def qkv_kernel(student, pref, x0, x1, x2, x3, wq, wk, wv, *rest):
    slot = pl.program_id(0)
    out = rest[-1]
    rows = wq.shape[0]
    for j, ref in enumerate((x0, x1, x2, x3)):

        @pl.when(slot == j)
        def _():
            act = ref[...]
            if student:
                act = jnp.clip(act, -CLIP, CLIP)
            for part, weight in enumerate((wq, wk, wv)):
                value = dot(weight[...], act, 1, 1)
                if student and part != 1:
                    value = value + rest[0][part // 2]
                out[part * rows : (part + 1) * rows, :] = value.astype(BF)


def qkv_project(pref, slots, weight, bias):
    tok, width = slots[0].shape
    rows = weight.shape[0] // 12
    specs = [whole((tok, width))] * 4
    specs += [
        pl.BlockSpec((rows, width), lambda j, i, o=o: (o * 4 + i[0], 0)) for o in range(3)
    ]
    args = list(slots) + [weight] * 3
    if bias is not None:
        specs.append(pl.BlockSpec((2, rows, 1), lambda j, i: (0, i[0], 0)))
        args.append(bias)
    return call(
        lambda *refs: qkv_kernel(bias is not None, *refs),
        pref,
        args,
        specs,
        shape_of((3 * rows, 4 * tok), BF),
        pl.BlockSpec((3 * rows, tok), lambda j, i: (0, lax.bitwise_xor(i[0], j))),
        (4,),
        [],
        2 * 4 * tok * width * 3 * rows,
    )


def roll_cont(values, shift):
    return jnp.concatenate(
        [values[:, :PROMPT], pltpu.roll(values[:, PROMPT:], shift, 1)], axis=1
    )


def block_list(total, rows):
    blocks = [(i, [(0, PROMPT)]) for i in range(0, PROMPT, rows)]
    blocks += [(i, [(0, PROMPT + LONG)]) for i in range(PROMPT, PROMPT + LONG, rows)]
    blocks += [
        (i, [(0, PROMPT), (PROMPT + LONG, total)]) for i in range(PROMPT + LONG, total, rows)
    ]
    return blocks


def same_segment(shape, key_axis, key_start, query_start, border):
    keys = lax.broadcasted_iota(jnp.int32, shape, key_axis) + key_start
    queries = lax.broadcasted_iota(jnp.int32, shape, 1 - key_axis) + query_start
    return (keys < border) == (queries < border)


def attention_kernel(scale, kept, pref, q_ref, k_ref, v_ref, o0, o1, o2, o3, cf_ref, lse_ref, *rest):
    if kept:
        qs, ks, vs, cs, st = rest
    else:
        cs, st, qs, ks, vs = rest
    own, shift, border = pref[0], pref[1], pref[2]
    total = q_ref.shape[1]
    cont = total - PROMPT
    others = PROMPT + LONG
    back = lax.rem(cont - shift, cont)
    qs[...] = roll_cont(q_ref[...].astype(F32), back).astype(BF)
    ks[...] = roll_cont(k_ref[...].astype(F32), back).astype(BF)
    vs[...] = roll_cont(v_ref[...].astype(F32), back).astype(BF)
    blocks = []
    for start, parts in block_list(total, QB):
        chunks = [key for lo, hi in parts for key in range(lo, hi, KC)]
        blocks.append((start, chunks))
    top, acc, norm = {}, {}, {}

    def scores(n, i):
        start, chunks = blocks[n]
        key = chunks[i]
        value = dot(ks[:, key : key + KC], qs[:, start : start + QB], 0, 0) * scale
        if key >= others:
            mask = same_segment((KC, QB), 0, key - others, start - others, border)
            value = jnp.where(mask, value, -1e30)
        st[n % 2, i * KC : (i + 1) * KC, :] = value
        peak = jnp.max(value, axis=0, keepdims=True)
        top[n] = jnp.maximum(top[n], peak) if n in top else peak

    def weigh(n, i):
        key = blocks[n][1][i]
        prob = jnp.exp2(st[n % 2, i * KC : (i + 1) * KC, :] - top[n])
        part = jnp.sum(prob, axis=0, keepdims=True)
        value = dot(vs[:, key : key + KC], prob.astype(BF), 1, 0)
        acc[n] = acc[n] + value if n in acc else value
        norm[n] = norm[n] + part if n in norm else part

    for i in range(len(blocks[0][1])):
        scores(0, i)
    for n, (start, chunks) in enumerate(blocks):
        ahead = len(blocks[n + 1][1]) if n + 1 < len(blocks) else 0
        for i in range(max(len(chunks), ahead)):
            if i < ahead:
                scores(n + 1, i)
            if i < len(chunks):
                weigh(n, i)
        cf_ref[:, start : start + QB] = acc[n] / norm[n]
        lse_ref[:, start : start + QB] = top[n] + jnp.log2(norm[n])
    cs[...] = roll_cont(cf_ref[...], shift).astype(BF)
    tok = total // 4
    for j, out in enumerate((o0, o1, o2, o3)):
        first = pl.multiple_of(xor(own, j) * tok, 128)
        out[...] = cs[:, pl.ds(first, tok)]


def attention(pref, qkv, kept):
    total = qkv.shape[1]
    heads = HEADS // 4
    hdim = qkv.shape[0] // (3 * heads)
    rows = qkv.shape[0] // 3
    scale = LOG2E / hdim**0.5
    return call(
        lambda *refs: attention_kernel(scale, kept, *refs),
        pref,
        [qkv] * 3,
        [pl.BlockSpec((hdim, total), lambda h, i, o=o: (h + o * heads, 0)) for o in range(3)],
        [shape_of((rows, total // 4), BF)] * 4
        + [shape_of((rows, total), F32), shape_of((heads, 1, total), F32)]
        + [shape_of((rows, total), BF)] * (3 if kept else 0),
        [pl.BlockSpec((hdim, total // 4), lambda h, i: (h, 0))] * 4
        + [
            pl.BlockSpec((hdim, total), lambda h, i: (h, 0)),
            pl.BlockSpec((None, 1, total), lambda h, i: (h, 0, 0)),
        ]
        + [pl.BlockSpec((hdim, total), lambda h, i: (h, 0))] * (3 if kept else 0),
        (heads,),
        [pltpu.VMEM((hdim, total), BF), pltpu.VMEM((2, PROMPT + LONG, QB), F32)]
        + [pltpu.VMEM((hdim, total), BF)] * (0 if kept else 3),
        16 * 10**9,
        12 * 10**6,
    )


def thirds(values):
    high = values.astype(BF).astype(F32)
    middle = (values - high).astype(BF).astype(F32)
    low = values - high - middle
    row = lax.broadcasted_iota(jnp.int32, (AUG, values.shape[1]), 0)
    value = jnp.where(row == 0, high, jnp.where(row == 1, middle, jnp.where(row == 2, low, 0.0)))
    return value.astype(BF)


def attention_back_kernel(
    scale, pref, q_ref, k_ref, v_ref, g0, g1, g2, g3, cf_ref, lse_ref,
    d0, d1, d2, d3, qa, ka, va, ga, gs, dqs, dks, dvs,
):
    own, shift, border = pref[0], pref[1], pref[2]
    hdim, total = q_ref.shape
    tok = total // 4
    cont = total - PROMPT
    others = PROMPT + LONG
    back = lax.rem(cont - shift, cont)
    for j, ref in enumerate((g0, g1, g2, g3)):
        first = pl.multiple_of(xor(own, j) * tok, 128)
        gs[:, pl.ds(first, tok)] = ref[...].astype(F32)
    qa[:hdim, :] = roll_cont(q_ref[...].astype(F32), back).astype(BF)
    ka[:hdim, :] = roll_cont(k_ref[...].astype(F32), back).astype(BF)
    va[:hdim, :] = roll_cont(v_ref[...].astype(F32), back).astype(BF)
    grad = roll_cont(gs[...], back)
    ga[:hdim, :] = grad.astype(BF)
    ga[hdim:, :] = thirds(-jnp.sum(grad * cf_ref[...], axis=0, keepdims=True))
    qa[hdim:, :] = thirds(lse_ref[...] * (-1.0 / scale))
    row = lax.broadcasted_iota(jnp.int32, (AUG, total), 0)
    ones = jnp.where(row < 3, 1.0, 0.0).astype(BF)
    ka[hdim:, :] = ones
    va[hdim:, :] = ones
    seen = set()
    for start, parts in block_list(total, QB):
        queries = slice(start, start + QB)
        grad_q = None
        for lo, hi in parts:
            for key in range(lo, hi, KB):
                keys = slice(key, key + KB)
                value = dot(qa[:, queries], ka[:, keys], 0, 0) * scale
                if lo >= others:
                    mask = same_segment((QB, KB), 1, key - others, start - others, border)
                    value = jnp.where(mask, value, -1e30)
                prob = jnp.exp2(value)
                grad_p = dot(ga[:, queries], va[:, keys], 0, 0)
                grad_s = (prob * grad_p).astype(BF)
                grad_v = dot(ga[:hdim, queries], prob.astype(BF), 1, 0)
                grad_k = dot(qa[:hdim, queries], grad_s, 1, 0)
                part = dot(ka[:hdim, keys], grad_s, 1, 1)
                grad_q = part if grad_q is None else grad_q + part
                if key in seen:
                    dvs[:, keys] += grad_v
                    dks[:, keys] += grad_k
                else:
                    dvs[:, keys] = grad_v
                    dks[:, keys] = grad_k
                    seen.add(key)
        dqs[:, queries] = grad_q
    inv = 1.0 / hdim**0.5
    for part, (ref, factor) in enumerate(((dqs, inv), (dks, inv), (dvs, 1.0))):
        gs[...] = roll_cont(ref[...] * factor, shift)
        for j, out in enumerate((d0, d1, d2, d3)):
            first = pl.multiple_of(xor(own, j) * tok, 128)
            out[part] = gs[:, pl.ds(first, tok)].astype(BF)


def attention_back(pref, qkv, grads, ctx, lse):
    total = qkv.shape[1]
    heads = HEADS // 4
    hdim = qkv.shape[0] // (3 * heads)
    rows = qkv.shape[0] // 3
    scale = LOG2E / hdim**0.5
    quarter = pl.BlockSpec((hdim, total // 4), lambda h, i: (h, 0))
    return call(
        lambda *refs: attention_back_kernel(scale, *refs),
        pref,
        [qkv] * 3 + list(grads) + [ctx, lse],
        [pl.BlockSpec((hdim, total), lambda h, i, o=o: (h + o * heads, 0)) for o in range(3)]
        + [quarter] * 4
        + [
            pl.BlockSpec((hdim, total), lambda h, i: (h, 0)),
            pl.BlockSpec((None, 1, total), lambda h, i: (h, 0, 0)),
        ],
        [shape_of((3, rows, total // 4), BF)] * 4,
        [pl.BlockSpec((3, hdim, total // 4), lambda h, i: (0, h, 0))] * 4,
        (heads,),
        [pltpu.VMEM((hdim + AUG, total), BF)] * 4 + [pltpu.VMEM((hdim, total), F32)] * 4,
        30 * 10**9,
        12 * 10**6,
    )


def normalize(values):
    centre = jnp.mean(values, axis=-1, keepdims=True)
    shifted = values - centre
    spread = jnp.mean(shifted * shifted, axis=-1, keepdims=True)
    inv = lax.rsqrt(spread + EPS)
    return shifted * inv, inv


def normalize_back(grad, normed, inv):
    first = jnp.mean(grad, axis=-1, keepdims=True)
    second = jnp.mean(grad * normed, axis=-1, keepdims=True)
    return (grad - first - normed * second) * inv


def total_rows(values):
    return jnp.sum(values, axis=0, keepdims=True)


def gather_ctx(own, pieces, ctx):
    rows = pieces[0].shape[0]
    for j, ref in enumerate(pieces):
        first = pl.multiple_of(xor(own, j) * rows, 64)
        ctx[pl.ds(first, rows), :] = ref[...]


def student_kernel(
    pref, c0, c1, c2, c3, x, w_out, w_up, w_down, b_out, b_up, b_down, gain, shift,
    ctx, act_one, normed_one, inv_one, gelu, slope, result, normed_two, inv_two,
    acc, mid,
):
    step = pl.program_id(0)

    @pl.when(step == 0)
    def _():
        gather_ctx(pref[0], (c0, c1, c2, c3), ctx)
        res = x[...].astype(F32) + (dot(ctx[...], w_out[...], 0, 1) + b_out[...])
        normed, inv = normalize(res)
        normed_one[...] = normed
        inv_one[...] = inv
        middle = normed * gain[0:1] + shift[0:1]
        mid[...] = middle
        act_one[...] = jnp.clip(middle, -CLIP, CLIP).astype(BF)
        acc[...] = jnp.zeros_like(acc)

    pre = dot(act_one[...], w_up[...], 1, 1) + b_up[...]
    cdf = 0.5 * (1.0 + lax.erf(pre * 0.5**0.5))
    act = (pre * cdf).astype(BF)
    gelu[...] = act
    slope[...] = (cdf + pre * (jnp.exp(pre * pre * -0.5) * 0.3989422804014327)).astype(BF)
    acc[...] += dot(act, w_down[...], 1, 1)

    @pl.when(step == pl.num_programs(0) - 1)
    def _():
        normed, inv = normalize(mid[...] + (acc[...] + b_down[...]))
        normed_two[...] = normed
        inv_two[...] = inv
        result[...] = (normed * gain[1:2] + shift[1:2]).astype(BF)


def ffn_specs(tok, width, hidden):
    up = pl.BlockSpec((FC, width), lambda c, i: (c, 0))
    down = pl.BlockSpec((width, FC), lambda c, i: (0, c))
    wide = pl.BlockSpec((tok, FC), lambda c, i: (0, c))
    row = pl.BlockSpec((1, FC), lambda c, i: (0, c))
    return up, down, wide, row


def student_ffn(pref, pieces, x, w_out, w_up, w_down, b_out, b_up, b_down, gain, shift):
    tok, width = x.shape
    hidden = w_up.shape[0]
    up, down, wide, row = ffn_specs(tok, width, hidden)
    full, one = whole((tok, width)), whole((tok, 1))
    return call(
        student_kernel,
        pref,
        list(pieces) + [x, w_out, w_up, w_down, b_out, b_up, b_down, gain, shift],
        [whole(pieces[0].shape)] * 4
        + [full, whole(w_out.shape), up, down, whole((1, width)), row, whole((1, width))]
        + [whole((2, width))] * 2,
        [
            shape_of((width, tok), BF),
            shape_of((tok, width), BF),
            shape_of((tok, width), F32),
            shape_of((tok, 1), F32),
            shape_of((tok, hidden), BF),
            shape_of((tok, hidden), BF),
            shape_of((tok, width), BF),
            shape_of((tok, width), F32),
            shape_of((tok, 1), F32),
        ],
        [whole((width, tok)), full, full, one, wide, wide, full, full, one],
        (hidden // FC,),
        [pltpu.VMEM((tok, width), F32)] * 2,
        2 * tok * width * (2 * hidden + width),
        2 * tok * hidden,
    )


def teacher_kernel(
    pref, c0, c1, c2, c3, x, w_out, w_up, w_down, gain, shift, normed_two, inv_two,
    grad_sum, grad_ffn, vectors,
    ctx, acc, mid, act_one,
):
    step = pl.program_id(0)

    @pl.when(step == 0)
    def _():
        gather_ctx(pref[0], (c0, c1, c2, c3), ctx)
        res = x[...].astype(F32) + dot(ctx[...], w_out[...], 0, 1)
        normed, inv = normalize(res)
        mid[...] = normed
        act_one[...] = normed.astype(BF)
        acc[...] = jnp.zeros_like(acc)

    pre = dot(act_one[...], w_up[...], 1, 1)
    act = (pre * (0.5 * (1.0 + lax.erf(pre * 0.5**0.5)))).astype(BF)
    acc[...] += dot(act, w_down[...], 1, 1)

    @pl.when(step == pl.num_programs(0) - 1)
    def _():
        target, _unused = normalize(mid[...] + acc[...])
        normed = normed_two[...]
        diff = normed * gain[1:2] + shift[1:2] - target
        back = normalize_back(diff * gain[1:2], normed, inv_two[...])
        grad_sum[...] = back
        low = back.astype(BF)
        grad_ffn[...] = low
        vectors[0:1] = total_rows(diff * normed)
        vectors[1:2] = total_rows(diff)
        vectors[2:3] = total_rows(low.astype(F32))


def teacher_ffn(pref, pieces, x, w_out, w_up, w_down, gain, shift, normed_two, inv_two):
    tok, width = x.shape
    hidden = w_up.shape[0]
    up, down, wide, row = ffn_specs(tok, width, hidden)
    full, one = whole((tok, width)), whole((tok, 1))
    return call(
        teacher_kernel,
        pref,
        list(pieces) + [x, w_out, w_up, w_down, gain, shift, normed_two, inv_two],
        [whole(pieces[0].shape)] * 4
        + [full, whole(w_out.shape), up, down]
        + [whole((2, width))] * 2
        + [full, one],
        [shape_of((tok, width), F32), shape_of((tok, width), BF), shape_of((3, width), F32)],
        [full, full, whole((3, width))],
        (hidden // FC,),
        [pltpu.VMEM((width, tok), BF)]
        + [pltpu.VMEM((tok, width), F32)] * 2
        + [pltpu.VMEM((tok, width), BF)],
        2 * tok * width * (2 * hidden + width),
        tok * hidden,
    )


def back_kernel(
    pref, grad_ffn, slope, w_up, w_down, grad_sum, normed_one, inv_one, gain, shift, w_out,
    grad_hidden, grad_bias, grad_res, grad_attn, g0, g1, g2, g3, vectors,
    acc, ctx,
):
    step = pl.program_id(0)

    @pl.when(step == 0)
    def _():
        acc[...] = jnp.zeros_like(acc)

    low = (dot(grad_ffn[...], w_down[...], 1, 0) * slope[...].astype(F32)).astype(BF)
    grad_hidden[...] = low
    grad_bias[...] = total_rows(low.astype(F32))
    acc[...] += dot(low, w_up[...], 1, 0)

    @pl.when(step == pl.num_programs(0) - 1)
    def _():
        normed = normed_one[...]
        middle = normed * gain[0:1] + shift[0:1]
        grad = grad_sum[...] + jnp.where(jnp.abs(middle) < CLIP, acc[...], 0.0)
        back = normalize_back(grad * gain[0:1], normed, inv_one[...])
        grad_res[...] = back
        attn = back.astype(BF)
        grad_attn[...] = attn
        vectors[0:1] = total_rows(grad * normed)
        vectors[1:2] = total_rows(grad)
        vectors[2:3] = total_rows(attn.astype(F32))
        ctx[...] = dot(w_out[...], attn, 0, 1).astype(BF)
        rows = g0.shape[0]
        for j, ref in enumerate((g0, g1, g2, g3)):
            first = pl.multiple_of(xor(pref[0], j) * rows, 64)
            ref[...] = ctx[pl.ds(first, rows), :]


def student_back(pref, grad_ffn, slope, w_up, w_down, grad_sum, normed_one, inv_one, gain, shift, w_out):
    tok, width = grad_ffn.shape
    hidden = w_up.shape[0]
    up, down, wide, row = ffn_specs(tok, width, hidden)
    full, one = whole((tok, width)), whole((tok, 1))
    return call(
        back_kernel,
        pref,
        [grad_ffn, slope, w_up, w_down, grad_sum, normed_one, inv_one, gain, shift, w_out],
        [full, wide, up, down, full, full, one] + [whole((2, width))] * 2 + [whole(w_out.shape)],
        [
            shape_of((tok, hidden), BF),
            shape_of((1, hidden), F32),
            shape_of((tok, width), F32),
            shape_of((tok, width), BF),
        ]
        + [shape_of((width // 4, tok), BF)] * 4
        + [shape_of((3, width), F32)],
        [wide, row, full, full] + [whole((width // 4, tok))] * 4 + [whole((3, width))],
        (hidden // FC,),
        [pltpu.VMEM((tok, width), F32), pltpu.VMEM((width, tok), BF)],
        2 * tok * width * (2 * hidden + width),
    )


def weight_grad_kernel(
    pref, grad_ffn, gelu, grad_hidden, act_one, grad_attn, ctx, grad_down, grad_up, grad_out
):
    @pl.when(pl.program_id(0) == 0)
    def _():
        value = dot(grad_attn[...], ctx[...], 0, 1).astype(BF)
        grad_out[...] = value.reshape(grad_out.shape)

    value = dot(grad_ffn[...], gelu[...], 0, 0).astype(BF)
    grad_down[...] = value.reshape(grad_down.shape)
    value = dot(grad_hidden[...], act_one[...], 0, 0).astype(BF)
    grad_up[...] = value.reshape(grad_up.shape)


def weight_grads(pref, grad_ffn, gelu, grad_hidden, act_one, grad_attn, ctx):
    tok, width = grad_ffn.shape
    hidden = gelu.shape[1]
    count, half = hidden // width, width // 2
    wide = pl.BlockSpec((tok, width), lambda c, i: (0, c))
    full = whole((tok, width))
    return call(
        weight_grad_kernel,
        pref,
        [grad_ffn, gelu, grad_hidden, act_one, grad_attn, ctx],
        [full, wide, wide, full, full, whole((width, tok))],
        [
            shape_of((2, count, half, width), BF),
            shape_of((2 * count, half, width), BF),
            shape_of((2, half, width), BF),
        ],
        [
            pl.BlockSpec((2, 1, half, width), lambda c, i: (0, c, 0, 0)),
            pl.BlockSpec((2, half, width), lambda c, i: (c, 0, 0)),
            whole((2, half, width)),
        ],
        (count,),
        [],
        2 * tok * width * (2 * hidden + width),
    )


def qkv_grad_kernel(pref, d0, d1, d2, d3, x0, x1, x2, x3, out, sums):
    own = pref[0]
    total = None
    count = None
    ones = jnp.ones((8, d0.shape[1]), BF)
    for grad, x in zip((d0, d1, d2, d3), (x0, x1, x2, x3)):
        value = grad[...]
        part = dot(value, jnp.clip(x[...], -CLIP, CLIP), 1, 0)
        line = dot(ones, value, 1, 1)
        total = part if total is None else total + part
        count = line if count is None else count + line
    out[...] = total.astype(BF)
    sums[...] = jnp.zeros_like(sums)
    rows = out.shape[0]
    for j in range(4):

        @pl.when(own == j)
        def _():
            sums[:, j * rows : (j + 1) * rows] = count


def qkv_grad(pref, grads, slots):
    tok, width = slots[0].shape
    rows = grads[0].shape[1]
    return call(
        qkv_grad_kernel,
        pref,
        list(grads) + list(slots),
        [pl.BlockSpec((None, rows, tok), lambda o, i: (o, 0, 0))] * 4 + [whole((tok, width))] * 4,
        [shape_of((3, rows, width), BF), shape_of((3, 8, width), F32)],
        [
            pl.BlockSpec((None, rows, width), lambda o, i: (o, 0, 0)),
            pl.BlockSpec((None, 8, width), lambda o, i: (o, 0, 0)),
        ],
        (3,),
        [],
        2 * 4 * tok * width * 3 * rows,
    )


def input_grad_kernel(pref, e0, e1, e2, e3, wq, wk, wv, grad_res, x, out, acc):
    slot = pl.program_id(0)

    @pl.when(slot == 0)
    def _():
        acc[...] = jnp.zeros_like(acc)

    for j, ref in enumerate((e0, e1, e2, e3)):

        @pl.when(slot == j)
        def _():
            part = dot(ref[0], wq[...], 0, 0)
            part = part + dot(ref[1], wk[...], 0, 0)
            acc[...] += part + dot(ref[2], wv[...], 0, 0)

    @pl.when(slot == 3)
    def _():
        size = jnp.abs(x[...].astype(F32))
        pull = jnp.where(size < CLIP, 1.0, jnp.where(size == CLIP, 0.5, 0.0))
        out[...] = (grad_res[...] + acc[...] * pull).astype(BF)


def input_grad(pref, pieces, weight, grad_res, x):
    tok, width = x.shape
    rows = pieces[0].shape[1]
    full = whole((tok, width))
    return call(
        input_grad_kernel,
        pref,
        list(pieces) + [weight] * 3 + [grad_res, x],
        [whole((3, rows, tok))] * 4
        + [
            pl.BlockSpec((rows, width), lambda j, i, o=o: (o * 4 + lax.bitwise_xor(i[0], j), 0))
            for o in range(3)
        ]
        + [full, full],
        shape_of((tok, width), BF),
        full,
        (4,),
        [pltpu.VMEM((tok, width), F32)],
        2 * 4 * tok * width * 3 * rows,
    )


def place(bit):
    name, mask = bit
    at = lax.axis_index(name)
    upper = lax.rem(lax.div(at, jnp.int32(mask)), jnp.int32(2))
    return upper, {name: at + mask * (1 - 2 * upper)}


class Copies:
    def __init__(self, send, recv, local):
        self.send, self.recv, self.local_sem = send, recv, local
        self.sent, self.planned, self.kept = [], 0, 0

    def plan(self, source, target, device):
        n = self.planned
        self.planned += 1
        return pltpu.make_async_remote_copy(
            src_ref=source,
            dst_ref=target,
            send_sem=self.send.at[n],
            recv_sem=self.recv.at[n],
            device_id=device,
            device_id_type=pl.DeviceIdType.MESH,
        )

    def remote(self, source, target, device):
        copy = self.plan(source, target, device)
        copy.start()
        self.sent.append(copy)
        return copy

    def plan_local(self, source, target):
        self.kept += 1
        return pltpu.make_async_copy(source, target, self.local_sem.at[self.kept - 1])

    def local(self, source, target):
        copy = self.plan_local(source, target)
        copy.start()
        return copy

    def finish(self):
        for copy in self.sent:
            copy.wait_send()


def window(ref, region):
    row, rows, col, cols = region
    return ref.at[pl.ds(row, rows), pl.ds(col, cols)]


def add_window(target, left, right, region, start):
    row, rows, col, cols = region
    step = 48 if rows % 48 == 0 else 16

    def body(i, carry):
        there = pl.ds(pl.multiple_of(row + i * step, 16), step)
        here = pl.ds(pl.multiple_of(start + i * step, 16), step)
        target[there, pl.ds(col, cols)] = left[there, pl.ds(col, cols)] + right[here, :cols]
        return carry

    lax.fori_loop(0, rows // step, body, 0)


def scatter_sum(copies, work, far, full, bits):
    rows, cols = work.shape
    region, used, parts = (0, rows, 0, cols), 0, []
    for n, bit in enumerate(bits):
        upper, device = place(bit)
        row, rows, col, cols = region
        if (rows // 2) % 16 == 0:
            rows //= 2
            kept = (pl.multiple_of(row + upper * rows, 16), rows, col, cols)
            sent = (pl.multiple_of(row + (1 - upper) * rows, 16), rows, col, cols)
        else:
            cols //= 2
            kept = (row, rows, pl.multiple_of(col + upper * cols, 128), cols)
            sent = (row, rows, pl.multiple_of(col + (1 - upper) * cols, 128), cols)
        slot = far.at[pl.ds(used, rows), pl.ds(0, cols)]
        copy = copies.remote(window(work, sent), slot, device)
        yield
        copy.wait_recv()
        add_window(full if n == len(bits) - 1 else work, work, far, kept, used)
        used += rows
        region = kept
        parts.append((bit, kept))
    return parts


def sum_flow(copies, own, other, work, near, far, full, result, core, bits):
    copy = copies.remote(other, near, place(core)[1])
    load = copies.local(own, work)
    yield
    copy.wait_recv()
    load.wait()
    add_window(work, work, near, (0, work.shape[0], 0, work.shape[1]), 0)
    parts = yield from scatter_sum(copies, work, far, full, bits)
    for bit, kept in reversed(parts):
        copy = copies.remote(window(full, kept), window(full, kept), place(bit)[1])
        yield
        copy.wait_recv()
    store = copies.local(full, result)
    yield
    store.wait()


def vector_flow(copies, sums, far, bits):
    for n, bit in enumerate(bits):
        yield
        copy = copies.remote(sums.at[n], far.at[n], place(bit)[1])
        yield
        copy.wait_recv()
        sums[n + 1] = sums[n] + far[n]


def remote_call(kernel, args, in_specs, outs, out_specs, scratch, copies, local, number):
    sems = pltpu.SemaphoreType.DMA
    return pl.pallas_call(
        kernel,
        in_specs=in_specs,
        out_specs=out_specs,
        out_shape=outs,
        scratch_shapes=scratch + [sems((copies,)), sems((copies,)), sems((local,))],
        compiler_params=pltpu.CompilerParams(
            vmem_limit_bytes=VMEM_LIMIT, collective_id=number, has_side_effects=True
        ),
        cost_estimate=pl.CostEstimate(flops=5 * 10**10, bytes_accessed=10**8, transcendentals=0),
    )(*args)


ANY = pl.BlockSpec(memory_space=pl.ANY)
IN_VMEM = pl.BlockSpec(memory_space=pltpu.VMEM)


def binarize_rows(source, target):
    rows, cols = target.shape
    step = 96 if cols < 2048 else 32

    def body(i, carry):
        at = pl.ds(pl.multiple_of(i * step, 16), step)
        value = source[at, :]
        scale = jnp.sum(jnp.abs(value), axis=1, keepdims=True) * (1.0 / cols)
        signed = jnp.where(value > 0, scale, jnp.where(value < 0, -scale, 0.0))
        target[at, :] = signed.astype(BF)
        return carry

    lax.fori_loop(0, rows // step, body, 0)


def entry_kernel(
    seq, core, hidden, teach, segments, l_qkv, l_out, l_up, l_down, t_qkv, t_out, t_up, t_down, bias,
    o_pref, o_qkv, x0, x1, x2, x3, o_teach, b_qkv, b_out, b_up, b_down, e_qkv, e_out, e_up, e_down,
    xs, held, w_qkv, w_out, w_up, w_down, f_qkv, f_out, f_up, f_down,
    s_qkv, s_out, s_up, s_down, proj, others, send, recv, local,
):
    tok, width = hidden.shape
    parts, size = 4, tok // 4
    along, next_chip = place(seq[0])
    side_of, sibling = place(core)
    half = lax.div(lax.axis_index("seq"), jnp.int32(2))
    stays = half == side_of
    moves = half != side_of
    partner = {"seq": 2 * side_of + along, "fsdp": half}
    mesh = pl.DeviceIdType.MESH

    barrier = pltpu.get_barrier_semaphore()
    for device in (next_chip, sibling):
        pl.semaphore_signal(barrier, inc=1, device_id=device, device_id_type=mesh)

    @pl.when(moves)
    def _():
        pl.semaphore_signal(barrier, inc=1, device_id=partner, device_id_type=mesh)
        pl.semaphore_wait(barrier, 3)

    @pl.when(stays)
    def _():
        pl.semaphore_wait(barrier, 2)

    copies = Copies(send, recv, local)
    cuts = [pl.ds(c * size, size) for c in range(parts)]
    swap = [copies.plan(hidden.at[cut], xs.at[0, cut], partner) for cut in cuts]
    load = [copies.plan_local(hidden.at[cut], xs.at[0, cut]) for cut in cuts]
    over = [copies.plan(xs.at[0, cut], xs.at[1, cut], next_chip) for cut in cuts]
    beside = [copies.plan(xs.at[0, cut], xs.at[2, cut], sibling) for cut in cuts]
    relay = [copies.plan(xs.at[1, cut], xs.at[3, cut], sibling) for cut in cuts]
    t_swap = copies.plan(teach, held, partner)
    t_load = copies.plan_local(teach, held)
    seg_copy = copies.remote(segments, others, sibling)

    @pl.when(moves)
    def _():
        for copy in swap:
            copy.start()

    @pl.when(stays)
    def _():
        for copy in load:
            copy.start()
        t_load.start()

    latent = [
        (copies.local(source, target), target)
        for source, target in ((l_qkv, f_qkv), (l_out, f_out), (l_up, f_up), (l_down, f_down))
    ]
    staged = [
        (copies.local(source, target), target, result)
        for source, target, result in (
            (t_qkv, s_qkv, e_qkv),
            (t_out, s_out, e_out),
            (t_up, s_up, e_up),
            (t_down, s_down, e_down),
        )
    ]

    @pl.when(stays)
    def _():
        for c in range(parts):
            load[c].wait()
            over[c].start()
            beside[c].start()

    rows_qkv = l_qkv.shape[0]
    mine = w_qkv.at[pl.ds(pl.multiple_of(side_of * rows_qkv, 16), rows_qkv)]
    latent[0][0].wait()
    binarize_rows(f_qkv, mine)
    qkv_copy = copies.remote(mine, mine, sibling)
    stores, arrivals = [], []
    for (copy, source), target, result in zip(
        latent[1:], (w_out, w_up, w_down), (b_out, b_up, b_down)
    ):
        copy.wait()
        binarize_rows(source, target)
        arrivals.append(copies.remote(target, result.at[side_of], sibling))
        stores.append(copies.local(target, result.at[side_of]))
    for source, (_, _, result) in zip((t_qkv, t_out, t_up, t_down), staged):
        arrivals.append(copies.remote(source, result.at[side_of], sibling))
    for copy, target, result in staged:
        copy.wait()
        stores.append(copies.local(target, result.at[side_of]))

    @pl.when(moves)
    def _():
        for c in range(parts):
            swap[c].wait_recv()
            over[c].start()
            beside[c].start()
        t_swap.start()

    qkv_copy.wait_recv()
    stores.append(copies.local(w_qkv, b_qkv))
    rows = width // 4
    own = along + 2 * side_of

    def project(slot):
        act = jnp.clip(xs[slot], -CLIP, CLIP)
        first = (1 - along if slot % 2 else along) + 2 * (1 - side_of if slot // 2 else side_of)
        there = pl.ds(pl.multiple_of(first * tok, 128), tok)
        for part in range(3):
            at = pl.multiple_of(part * width + own * rows, 16)
            value = dot(w_qkv[pl.ds(at, rows), :], act, 1, 1)
            if part != 1:
                value = value + bias[part // 2, pl.ds(pl.multiple_of(own * rows, 8), rows), :]
            proj[part * rows : (part + 1) * rows, there] = value.astype(BF)
        stores.append(copies.local(proj.at[:, there], o_qkv.at[:, there]))
        stores.append(copies.local(xs.at[slot], (x0, x1, x2, x3)[slot]))

    seg_copy.wait_recv()
    counts = [jnp.sum(jnp.where(segments[...] == k, 1.0, 0.0)) for k in (1, 2, 3)]
    theirs = [jnp.sum(jnp.where(others[...] == k, 1.0, 0.0)) for k in (1, 2, 3)]
    first, second, third = [
        jnp.where(stays, a, b).astype(jnp.int32) for a, b in zip(counts, theirs)
    ]
    o_pref[0] = own
    o_pref[1] = jnp.where(first == LONG, 0, jnp.where(second == LONG, first, first + second))
    o_pref[2] = jnp.where(first == LONG, second, jnp.where(second == LONG, third, first))

    project(0)
    for copy in beside:
        copy.wait_recv()
    project(2)
    for c in range(parts):
        over[c].wait_recv()
        relay[c].start()
    project(1)
    for copy in relay:
        copy.wait_recv()
    project(3)

    @pl.when(moves)
    def _():
        t_swap.wait_recv()

    @pl.when(stays)
    def _():
        t_load.wait()

    stores.append(copies.local(held, o_teach))
    for copy in arrivals:
        copy.wait_recv()
    for copy in stores:
        copy.wait()

    @pl.when(moves)
    def _():
        for copy in swap + [t_swap]:
            copy.wait_send()

    for copy in over + beside + relay:
        copy.wait_send()
    copies.finish()


def entry(seq, core, hidden, teach, segments, latents, teachers, bias):
    tok, width = hidden.shape
    halves = [w.shape for w in latents]
    sides = [shape_of((2,) + shape, BF) for shape in halves]
    own = [pltpu.VMEM(shape, BF) for shape in halves]
    sides[0] = shape_of((2 * halves[0][0], halves[0][1]), BF)
    sides_t = [shape_of((2,) + shape, BF) for shape in halves]
    outs = remote_call(
        lambda *refs: entry_kernel(seq, core, *refs),
        [hidden, teach, segments] + list(latents) + list(teachers) + [bias],
        [ANY] * 2 + [IN_VMEM] + [ANY] * 8 + [IN_VMEM],
        [shape_of((3,), jnp.int32), shape_of((3 * width // 4, 4 * tok), BF)]
        + [shape_of((tok, width), BF)] * 5
        + sides
        + sides_t,
        [pl.BlockSpec(memory_space=pltpu.SMEM)] + [ANY] * 14,
        [pltpu.VMEM((4, tok, width), BF), pltpu.VMEM((tok, width), BF)]
        + [pltpu.VMEM(sides[0].shape, BF)]
        + own[1:]
        + [pltpu.VMEM(shape, F32) for shape in halves]
        + own
        + [pltpu.VMEM((3 * width // 4, 4 * tok), BF), pltpu.VMEM(segments.shape, jnp.int32)],
        26,
        30,
        3,
    )
    pref, qkv, x0, x1, x2, x3, teach = outs[:7]
    weights = [w.reshape((-1, w.shape[-1])) for w in outs[7:]]
    return pref, qkv, (x0, x1, x2, x3), teach, weights[:4], weights[4:]


class Pump:
    def __init__(self):
        self.events, self.added = [], 0

    def add(self, time, flow, first, then, turn):
        gap = next(flow)
        self.events.append([time + (gap or 0.0), self.added, flow, 0, (first, then, turn)])
        self.added += 1

    def run(self, time=1e9):
        while self.events:
            event = min(self.events, key=lambda e: e[:2])
            if event[0] > time:
                return
            try:
                gap = next(event[2])
            except StopIteration:
                self.events.remove(event)
                continue
            event[3] += 1
            first, then, turn = event[4]
            if gap is None:
                gap = first if event[3] <= turn else then
            event[0] += gap


def head_flow(copies, n, gh, work, far, full, result, seq, core, dp):
    side_of, partner = place(core)
    along = place(seq[0])[0]
    if n == 1:
        copy = copies.remote(gh.at[2 - 2 * side_of], work, partner)
        yield
        copy.wait_recv()
    else:
        load = copies.local(gh.at[n // 2 + side_of], work)
        yield
        load.wait()
    turned, cut = HEAD_PLAN[n][:2]
    bits = (dp[::-1] if turned else dp) + seq[1:]
    mine = full.at[2 * n + along]
    parts = yield from scatter_sum(copies, work, far, mine, bits)
    steps = [(bit, kept, False) for bit, kept in reversed(parts)]
    cut = min(cut, len(steps))
    held = steps[cut][1] if cut < len(steps) else (0, mine.shape[0], 0, mine.shape[1])
    steps = steps[:cut] + [(seq[0], held, False)] + [(b, k, True) for b, k, _ in steps[cut:]]
    for bit, (row, size, col, cols), both in steps:
        first, count = (2 * n, 2) if both else (2 * n + along, 1)
        part = full.at[pl.ds(first, count), pl.ds(row, size), pl.ds(col, cols)]
        copy = copies.remote(part, part, place(bit)[1])
        yield
        copy.wait_recv()
    store = copies.local(full.at[pl.ds(2 * n, 2)], result.at[pl.ds(2 * n, 2)])
    yield
    store.wait()


def tail_kernel(
    dp, seq, core, scale, pref, down, up, out, two, one, bias,
    q_in, k_in, v_in, g0, g1, g2, g3, cf_in, lse, x0, x1, x2, x3, w_in, res_in,
    down_sum, up_sum, out_sum, totals, qkv_sum, hidden_out,
    work, near, far, full, sums, sums_far, gh, h_work, h_far, h_full,
    qs, ks, vs, gp, cf, xs, weight, res, qa, ka, va, ga, gs, dqs, dks, dvs, dn, er, acc, hid,
    send, recv, local,
):
    shift, border = pref[1], pref[2]
    heads_all, total = qs.shape
    hdim = qa.shape[0] - AUG
    heads = heads_all // hdim
    tok = total // 4
    width = xs.shape[2]
    cont, others = total - PROMPT, PROMPT + LONG
    back = lax.rem(cont - shift, cont)
    along, next_chip = place(seq[0])
    side_of, sibling = place(core)
    across = {**next_chip, **sibling}
    half = lax.div(lax.axis_index("seq"), jnp.int32(2))
    stays, moves = half == side_of, half != side_of
    partner = {"seq": 2 * side_of + along, "fsdp": half}
    own = along + 2 * side_of

    def place_of(slot):
        return (1 - along if slot % 2 else along) + 2 * (1 - side_of if slot // 2 else side_of)

    copies = Copies(send, recv, local)
    first_loads = [
        copies.local(source, target)
        for source, target in (
            (g0, gp.at[0]), (g1, gp.at[1]), (g2, gp.at[2]), (g3, gp.at[3]),
            (q_in, qs), (k_in, ks), (v_in, vs), (cf_in, cf),
        )
    ]

    mesh = pl.DeviceIdType.MESH
    barrier = pltpu.get_barrier_semaphore()
    friends = [place(bit)[1] for bit in dp + seq] + [sibling, across]
    for device in friends:
        pl.semaphore_signal(barrier, inc=1, device_id=device, device_id_type=mesh)

    @pl.when(moves)
    def _():
        pl.semaphore_signal(barrier, inc=1, device_id=partner, device_id_type=mesh)
        pl.semaphore_wait(barrier, len(friends) + 1)

    @pl.when(stays)
    def _():
        pl.semaphore_wait(barrier, len(friends))

    pump = Pump()
    count, rows_half = down.shape[1:3]
    ups = [(up.at[side_of, p], up.at[1 - side_of, p], up_sum.at[p]) for p in range(count)]
    downs = [
        (
            down.at[side_of, p],
            down.at[1 - side_of, p],
            down_sum.at[:, pl.ds(p * width, width)],
        )
        for p in range(count)
    ]
    queue = ups + downs + [(out.at[side_of], out.at[1 - side_of], out_sum)]
    near_bits = dp + seq[:1]
    orders = [tuple(near_bits[i] for i in order) for order in ORDERS]
    for n, (mine, theirs, result) in enumerate(queue):
        order, time, first, then = PIECE_PLAN[n % len(PIECE_PLAN)]
        bits = list(orders[order]) + seq[1:]
        flow = sum_flow(
            copies, mine, theirs, work.at[n], near.at[n], far.at[n], full.at[n], result, core, bits
        )
        pump.add(time, flow, first, then, 1 + len(bits))

    late_loads = [
        copies.local(source, target)
        for source, target in (
            (x0, xs.at[0]), (x1, xs.at[1]), (x2, xs.at[2]), (x3, xs.at[3]),
            (w_in, weight), (res_in, res),
        )
    ]
    for copy in first_loads:
        copy.wait()

    row = lax.broadcasted_iota(jnp.int32, (AUG, total), 0)
    ones = jnp.where(row < 3, 1.0, 0.0).astype(BF)
    ka[hdim:, :] = ones
    va[hdim:, :] = ones
    clock = 1.0
    pieces = {1: [], 2: [], 3: []}
    devices = {1: next_chip, 2: sibling, 3: across}
    for h in range(heads):
        lines = slice(h * hdim, (h + 1) * hdim)
        for j in range(4):
            gs[:, pl.ds(pl.multiple_of(place_of(j) * tok, 128), tok)] = gp[j, lines, :].astype(F32)
        qa[:hdim, :] = qs[lines, :]
        ka[:hdim, :] = ks[lines, :]
        va[:hdim, :] = vs[lines, :]
        grad = roll_cont(gs[...], back)
        ga[:hdim, :] = grad.astype(BF)
        ga[hdim:, :] = thirds(-jnp.sum(grad * cf[lines, :], axis=0, keepdims=True))
        qa[hdim:, :] = thirds(lse[h] * (-1.0 / scale))
        seen = set()
        for start, parts in block_list(total, QB):
            queries = slice(start, start + QB)
            grad_q = None
            for lo, hi in parts:
                for key in range(lo, hi, KB):
                    keys = slice(key, key + KB)
                    value = dot(qa[:, queries], ka[:, keys], 0, 0) * scale
                    if lo >= others:
                        mask = same_segment((QB, KB), 1, key - others, start - others, border)
                        value = jnp.where(mask, value, -1e30)
                    prob = jnp.exp2(value)
                    grad_p = dot(ga[:, queries], va[:, keys], 0, 0)
                    grad_s = (prob * grad_p).astype(BF)
                    grad_v = dot(ga[:hdim, queries], prob.astype(BF), 1, 0)
                    grad_k = dot(qa[:hdim, queries], grad_s, 1, 0)
                    part = dot(ka[:hdim, keys], grad_s, 1, 1)
                    grad_q = part if grad_q is None else grad_q + part
                    if key in seen:
                        dvs[:, keys] += grad_v
                        dks[:, keys] += grad_k
                    else:
                        dvs[:, keys] = grad_v
                        dks[:, keys] = grad_k
                        seen.add(key)
                    clock += 0.65
            dqs[:, queries] = grad_q
            pump.run(clock)
        inv = 1.0 / hdim**0.5
        for part, (ref, factor) in enumerate(((dqs, inv), (dks, inv), (dvs, 1.0))):
            gs[...] = roll_cont(ref[...] * factor, shift)
            for j in range(4):
                there = pl.ds(pl.multiple_of(place_of(j) * tok, 128), tok)
                dn[j, part, lines, :] = gs[:, there].astype(BF)
        for j in (1, 3, 2):
            at = pl.ds(h * hdim, hdim)
            copy = copies.remote(dn.at[j, :, at, :], er.at[j - 1, :, at, :], devices[j])
            pieces[j].append(copy)
        clock += 1.5
        pump.run(clock)

    for copy in late_loads:
        copy.wait()
    rows = width // 4
    one_rows = jnp.ones((8, tok), BF)
    counts = []
    for o in range(3):
        value, line = None, None
        for j in range(4):
            part = dot(dn[j, o], jnp.clip(xs[j], -CLIP, CLIP), 1, 0)
            ends = dot(one_rows, dn[j, o], 1, 1)
            value = part if value is None else value + part
            line = ends if line is None else line + ends
        gh[o] = value.astype(BF)
        counts.append(line)
        clock += 2.7
        pump.run(clock)
    sums[0] = jnp.zeros(sums.shape[1:], F32)
    for j in range(4):

        @pl.when(own == j)
        def _():
            sums[0, 0:1, j * rows : (j + 1) * rows] = counts[0][0:1]
            sums[0, 1:2, j * rows : (j + 1) * rows] = counts[2][0:1]

    sums[0, 2:3] = one[2:3]
    sums[0, 3:4] = two[2:3]
    sums[0, 4:5] = one[0:1]
    sums[0, 5:6] = two[0:1]
    sums[0, 6:7] = one[1:2]
    sums[0, 7:8] = two[1:2]
    for p in range(count):
        sums[0, 8 + p : 9 + p] = bias[:, p * width : (p + 1) * width]

    swap = copies.plan(hid, hidden_out, partner)
    keep = copies.plan_local(hid, hidden_out)

    def hidden_flow():
        yield 0.0
        gaps = HIDDEN_PLAN[1]
        for gap, j in zip(gaps, (0, 2, 1, 3)):
            for copy in pieces.get(j, []):
                copy.wait_recv()
            part = None
            for o in range(3):
                at = pl.multiple_of(o * width + place_of(j) * rows, 16)
                source = dn[0, o] if j == 0 else er[j - 1, o]
                piece = dot(source, weight[pl.ds(at, rows), :], 0, 0)
                part = piece if part is None else part + piece
            if j == 0:
                acc[...] = part
            elif j != 3:
                acc[...] += part
            else:
                size = jnp.abs(xs[0].astype(F32))
                pull = jnp.where(size < CLIP, 1.0, jnp.where(size == CLIP, 0.5, 0.0))
                hid[...] = (res[...] + (acc[...] + part) * pull).astype(BF)
            if j != 3:
                yield gap

        @pl.when(moves)
        def _():
            swap.start()

        @pl.when(stays)
        def _():
            keep.start()

        yield gaps[3]

        @pl.when(moves)
        def _():
            swap.wait_recv()
            swap.wait_send()

        @pl.when(stays)
        def _():
            keep.wait()

    pump.add(clock + HIDDEN_PLAN[0], hidden_flow(), 0.0, 0.0, 0)
    for n in (0, 2, 1):
        flow = head_flow(
            copies, n, gh, h_work.at[n], h_far.at[n], h_full, qkv_sum, seq, core, dp
        )
        time, first, then = HEAD_PLAN[n][2:]
        pump.add(clock + time, flow, first, then, 4)
    time, gap = VECTOR_PLAN
    pump.add(clock + time, vector_flow(copies, sums, sums_far, [core] + dp + seq), gap, gap, 0)
    pump.run()
    totals[...] = sums[sums.shape[0] - 1]
    copies.finish()


def tail(
    dp, seq, core, pref, down, up, out, two, one, bias, rolled, grads, cf, lse, slots, weight, res
):
    sides, count, half, width = down.shape
    pieces, steps, lines = 2 * count + 1, len(dp) + len(seq), 16
    rows, total = rolled[0].shape
    tok = total // 4
    heads = HEADS // 4
    hdim = rows // heads
    scale = LOG2E / hdim**0.5
    smem = pl.BlockSpec(memory_space=pltpu.SMEM)
    return remote_call(
        lambda *refs: tail_kernel(dp, seq, core, scale, *refs),
        [pref, down, up, out, two, one, bias]
        + list(rolled)
        + list(grads)
        + [cf, lse]
        + list(slots)
        + [weight, res],
        [smem] + [ANY] * 3 + [IN_VMEM] * 3 + [ANY] * 8 + [IN_VMEM] + [ANY] * 6,
        [
            shape_of((half, count * width), BF),
            shape_of((count, half, width), BF),
            shape_of((half, width), BF),
            shape_of((lines, width), F32),
            shape_of((6, rows, width), BF),
            shape_of((tok, width), BF),
        ],
        [ANY] * 3 + [IN_VMEM] + [ANY] * 2,
        [pltpu.VMEM((pieces, half, width), BF)] * 4
        + [pltpu.VMEM((steps + 2, lines, width), F32), pltpu.VMEM((steps + 1, lines, width), F32)]
        + [pltpu.VMEM((3, rows, width), BF)] * 3
        + [pltpu.VMEM((6, rows, width), BF)]
        + [pltpu.VMEM((rows, total), BF)] * 3
        + [pltpu.VMEM((4, rows, tok), BF), pltpu.VMEM((rows, total), F32)]
        + [pltpu.VMEM((4, tok, width), BF), pltpu.VMEM(weight.shape, BF)]
        + [pltpu.VMEM((tok, width), F32)]
        + [pltpu.VMEM((hdim + AUG, total), BF)] * 4
        + [pltpu.VMEM((hdim, total), F32)] * 4
        + [pltpu.VMEM((4, 3, rows, tok), BF), pltpu.VMEM((3, 3, rows, tok), BF)]
        + [pltpu.VMEM((tok, width), F32), pltpu.VMEM((tok, width), BF)],
        pieces * (1 + 2 * steps) + steps + 1 + 3 * heads + 1 + 3 * (2 * steps - 1) + 1,
        2 * pieces + 14 + 1 + 5,
        4,
    )


def binarize(latent):
    row_scale = jnp.mean(jnp.abs(latent), axis=1, keepdims=True)
    return (row_scale * jnp.sign(latent)).astype(BF)


def segment_info(segments):
    sizes_of = [jnp.sum((segments == k).astype(jnp.int32)) for k in (1, 2, 3)]
    first, second, third = sizes_of
    shift = jnp.where(first == LONG, 0, jnp.where(second == LONG, first, first + second))
    border = jnp.where(first == LONG, second, jnp.where(second == LONG, third, first))
    return jnp.stack([shift, border])


def quarters(own):
    along = to_slot(own, 1)
    return (own, along, to_slot(own, 2), to_slot(along, 2))


def exchange(pieces):
    return (pieces[0],) + tuple(to_slot(pieces[j], j) for j in (1, 2, 3))


def on_device(
    hidden, teacher_hidden, segments, latent_qkv, latent_out, latent_up, latent_down,
    biases, up_bias, norm_gains, norm_shifts, teacher_qkv, teacher_out, teacher_up, teacher_down,
):
    seq_at, fsdp_at = lax.axis_index("seq"), lax.axis_index("fsdp")
    fsdp = lax.axis_size("fsdp")
    core = fsdp_at % 2
    own = (seq_at % 2 + 2 * core).astype(jnp.int32)
    width = hidden.shape[2]

    bias_cols = biases[:2].reshape(2, width, 1)
    latents = (latent_qkv, latent_out, latent_up, latent_down)
    teachers = (teacher_qkv, teacher_out, teacher_up, teacher_down)
    if fsdp == 2:
        pref, qkv, x_slots, teach, bins, t_weights = entry(
            bit_list("seq"), bit_list("fsdp")[0], hidden[0], teacher_hidden[0], segments,
            latents, teachers, bias_cols,
        )
        x = x_slots[0]
    else:
        info = segment_info(segments)
        info = jnp.where(core == seq_at // 2, info, flip(info, fsdp=1))
        pref = jnp.concatenate([own[None], info]).astype(jnp.int32)
        x = swap_groups(hidden[0])
        x_slots = quarters(x)
        bins = [gather_rows(binarize(w)) for w in latents]
        teach = swap_groups(teacher_hidden[0])
        t_weights = [gather_rows(w) for w in teachers]
        qkv = qkv_project(pref, x_slots, bins[0], bias_cols)
    bin_qkv, bin_out, bin_up, bin_down = bins
    t_qkv, t_out, t_up, t_down = t_weights
    t_along, t_beside = to_slot(teach, 1), to_slot(teach, 2)
    *ctx_slots, ctx_full, lse, q_roll, k_roll, v_roll = attention(pref, qkv, True)
    t_along, ctx_slots = lax.optimization_barrier((t_along, ctx_slots))
    t_slots = (teach, t_along, t_beside, to_slot(t_along, 2))
    ctx_pieces = exchange(ctx_slots)

    t_heads = qkv_project(pref, t_slots, t_qkv, None)
    *tctx_slots, _unused, _unused_too = attention(pref, t_heads, False)
    tctx_slots, ctx_pieces = lax.optimization_barrier((tctx_slots, ctx_pieces))
    tctx_pieces = exchange(tctx_slots)

    gain, shift = norm_gains, norm_shifts
    (
        ctx, act_one, normed_one, inv_one, gelu, slope, result, normed_two, inv_two,
    ) = student_ffn(
        pref, ctx_pieces, x, bin_out, bin_up, bin_down,
        biases[2:3], up_bias[None], biases[3:4], gain, shift,
    )
    student_out = swap_groups(result)
    grad_sum, grad_ffn, vec_two = teacher_ffn(
        pref, tctx_pieces, teach, t_out, t_up, t_down, gain, shift, normed_two, inv_two
    )
    grad_hidden, grad_up_bias, grad_res, grad_attn, *gctx_slots, vec_one = student_back(
        pref, grad_ffn, slope, bin_up, bin_down, grad_sum, normed_one, inv_one, gain, shift, bin_out
    )
    gctx_pieces = exchange(gctx_slots)
    grad_down, grad_up, grad_out = weight_grads(
        pref, grad_ffn, gelu, grad_hidden, act_one, grad_attn, ctx
    )
    dp_bits, seq_bits, fsdp_bits = bit_list("dp"), bit_list("seq"), bit_list("fsdp")
    rows, hidden_units = width // 4, up_bias.shape[0]

    if fsdp == 2:
        total_down, total_up, total_out, vectors, total_qkv, hidden_grad = tail(
            dp_bits, seq_bits, fsdp_bits[0], pref,
            grad_down, grad_up.reshape(grad_down.shape), grad_out, vec_two, vec_one, grad_up_bias,
            (q_roll, k_roll, v_roll), gctx_pieces, ctx_full, lse, x_slots, bin_qkv, grad_res,
        )
        total_up = total_up.reshape(-1, width)
        total_qkv = total_qkv.reshape(-1, width)
    else:
        dqkv_slots = attention_back(pref, qkv, gctx_pieces, ctx_full, lse)
        dqkv_pieces = exchange(dqkv_slots)
        grad_heads, head_sums = qkv_grad(pref, dqkv_slots, x_slots)
        hidden_grad = swap_groups(input_grad(pref, dqkv_pieces, bin_qkv, grad_res, x))

        def reduce_grad(value, bits):
            for bit in reversed(fsdp_bits):
                value = halve(value, bit)
            return all_reduce(value, bits)

        grad_down = grad_down.transpose(0, 2, 1, 3).reshape(width, hidden_units)
        total_down = reduce_grad(grad_down, dp_bits + seq_bits)
        total_up = reduce_grad(grad_up.reshape(hidden_units, width), dp_bits[::-1] + seq_bits)
        total_out = reduce_grad(
            grad_out.reshape(width, width), seq_bits[:1] + dp_bits + seq_bits[1:]
        )
        blocks = all_reduce(
            grad_heads.reshape(3 * rows, width), dp_bits + seq_bits[1:] + fsdp_bits[1:]
        )
        blocks = blocks.reshape(1, 3, rows, width)
        blocks = double(double(blocks, seq_bits[0]), fsdp_bits[0])
        whole_qkv = blocks.transpose(1, 0, 2, 3).reshape(3 * width, width)
        part = 3 * width // fsdp
        total_qkv = lax.dynamic_slice_in_dim(whole_qkv, fsdp_at * part, part, 0)
        vectors = jnp.concatenate(
            [
                head_sums[0, :1],
                head_sums[2, :1],
                vec_one[2:3],
                vec_two[2:3],
                vec_one[0:1],
                vec_two[0:1],
                vec_one[1:2],
                vec_two[1:2],
                grad_up_bias.reshape(-1, width),
            ]
        )
        vectors = sum_small(vectors, dp_bits + seq_bits + fsdp_bits)
    hid_bias = vectors[8 : 8 + hidden_units // width].reshape(-1)
    share, hid_share = width // fsdp, hid_bias.shape[0] // fsdp
    cols = lax.dynamic_slice_in_dim(vectors[:8], fsdp_at * share, share, 1)
    return (
        student_out[None],
        hidden_grad[None],
        total_qkv.astype(F32),
        total_out.astype(F32),
        total_up.astype(F32),
        total_down.astype(F32),
        cols[0:4],
        lax.dynamic_slice_in_dim(hid_bias, fsdp_at * hid_share, hid_share, 0),
        cols[4:6],
        cols[6:8],
    )


def solution(mesh):
    tokens = P(("dp", "fsdp"), "seq", None)
    rows = P("fsdp", None)
    return jax.shard_map(
        on_device,
        mesh=mesh,
        in_specs=(tokens, tokens, P(("dp", "fsdp"), None)) + (rows,) * 4 + (P(),) * 4 + (rows,) * 4,
        out_specs=(tokens, tokens)
        + (rows,) * 4
        + (P(None, "fsdp"), P("fsdp"), P(None, "fsdp"), P(None, "fsdp")),
        check_vma=False,
    )
```

```python
import jax
import jax.numpy as jnp
from jax import lax
from jax.experimental import pallas as pl
from jax.experimental.pallas import tpu as pltpu
from jax.sharding import PartitionSpec as P

HEADS = 12
PROMPT = 1024
LONG = 1024
CLIP = 2.5
EPS = 1e-05
AXES = ("dp", "seq", "fsdp")
BF = jnp.bfloat16
F32 = jnp.float32
LOG2E = 1.4426950408889634
QB = 512
KC = 256
KB = 512
FC = 1024
AUG = 16
VMEM_LIMIT = 56 * 2**20
ORDERS = ((0, 1, 2), (1, 0, 2), (0, 2, 1), (1, 2, 0), (2, 0, 1), (2, 1, 0))
PIECE_PLAN = (
    (2, 20.0, 95.4, 86.9),
    (0, 170.2, 97.1, 111.4),
    (1, 20.8, 80.9, 96.5),
    (3, 19.5, 100.8, 153.8),
    (1, 294.8, 80.8, 122.2),
    (0, 19.9, 101.0, 166.8),
    (4, 10.7, 73.5, 199.5),
    (1, 169.6, 90.3, 133.2),
    (3, 33.7, 57.9, 88.5),
)
HEAD_PLAN = (
    (0, 1, 24.6, 50.5, 104.3),
    (1, 1, 29.3, 52.8, 136.5),
    (0, 3, 312.0, 93.4, 93.4),
)
HIDDEN_PLAN = (0.0, (203.8, 62.6, 390.1, 383.5))
VECTOR_PLAN = (7.8, 182.0)


def dot(left, right, left_dim, right_dim):
    return lax.dot_general(
        left, right, (((left_dim,), (right_dim,)), ((), ())), preferred_element_type=F32
    )


def xor(first, second):
    return lax.bitwise_xor(first, jnp.int32(second))


def sizes():
    return tuple(lax.axis_size(name) for name in AXES)


def permute(values, target):
    dp, seq, fsdp = sizes()
    pairs = []
    for d in range(dp):
        for s in range(seq):
            for f in range(fsdp):
                td, ts, tf = target(d, s, f)
                pairs.append(((d * seq + s) * fsdp + f, (td * seq + ts) * fsdp + tf))
    return lax.ppermute(values, AXES, pairs)


def flip(values, dp=0, seq=0, fsdp=0):
    return permute(values, lambda d, s, f: (d ^ dp, s ^ seq, f ^ fsdp))


def swap_groups(values):
    return permute(
        values, lambda d, s, f: (d, 2 * (f % 2) + s % 2, f - f % 2 + s // 2)
    )


def to_slot(values, slot):
    return flip(values, seq=slot & 1, fsdp=slot >> 1)


def bit_list(name):
    count = lax.axis_size(name)
    out, bit = [], 1
    while bit < count:
        out.append((name, bit))
        bit *= 2
    return out


def flip_bit(values, bit):
    return flip(values, **{bit[0]: bit[1]})


def side(bit):
    return lax.bitwise_and(lax.axis_index(bit[0]), bit[1]) != 0


def halve(values, bit):
    upper = side(bit).astype(jnp.int32)
    half = values.shape[0] // 2
    sent = lax.dynamic_slice_in_dim(values, (1 - upper) * half, half, 0)
    kept = lax.dynamic_slice_in_dim(values, upper * half, half, 0)
    got = flip_bit(sent, bit)
    return (kept.astype(F32) + got.astype(F32)).astype(values.dtype)


def double(values, bit):
    got = flip_bit(values, bit)
    return jnp.where(
        side(bit),
        jnp.concatenate([got, values], axis=0),
        jnp.concatenate([values, got], axis=0),
    )


def gather_rows(values):
    for bit in bit_list("fsdp"):
        values = double(values, bit)
    return values


def all_reduce(values, bits):
    for bit in bits:
        values = halve(values, bit)
    for bit in reversed(bits):
        values = double(values, bit)
    return values


def sum_small(values, bits):
    for bit in bits:
        values = values + flip_bit(values, bit)
    return values


def whole(shape):
    return pl.BlockSpec(shape, lambda *_: (0,) * len(shape))


def call(kernel, pref, args, in_specs, outs, out_specs, grid, scratch, flops, trans=0):
    moved = sum(a.size * a.dtype.itemsize for a in args)
    moved += sum(o.size * o.dtype.itemsize for o in jax.tree.leaves(outs))
    return pl.pallas_call(
        kernel,
        grid_spec=pltpu.PrefetchScalarGridSpec(
            num_scalar_prefetch=1,
            grid=grid,
            in_specs=in_specs,
            out_specs=out_specs,
            scratch_shapes=scratch,
        ),
        out_shape=outs,
        compiler_params=pltpu.CompilerParams(vmem_limit_bytes=VMEM_LIMIT),
        cost_estimate=pl.CostEstimate(flops=flops, bytes_accessed=moved, transcendentals=trans),
    )(pref, *args)


def shape_of(shape, dtype):
    return jax.ShapeDtypeStruct(shape, dtype)


def qkv_kernel(student, pref, x0, x1, x2, x3, wq, wk, wv, *rest):
    slot = pl.program_id(0)
    out = rest[-1]
    rows = wq.shape[0]
    for j, ref in enumerate((x0, x1, x2, x3)):

        @pl.when(slot == j)
        def _():
            act = ref[...]
            if student:
                act = jnp.clip(act, -CLIP, CLIP)
            for part, weight in enumerate((wq, wk, wv)):
                value = dot(weight[...], act, 1, 1)
                if student and part != 1:
                    value = value + rest[0][part // 2]
                out[part * rows : (part + 1) * rows, :] = value.astype(BF)


def qkv_project(pref, slots, weight, bias):
    tok, width = slots[0].shape
    rows = weight.shape[0] // 12
    specs = [whole((tok, width))] * 4
    specs += [
        pl.BlockSpec((rows, width), lambda j, i, o=o: (o * 4 + i[0], 0)) for o in range(3)
    ]
    args = list(slots) + [weight] * 3
    if bias is not None:
        specs.append(pl.BlockSpec((2, rows, 1), lambda j, i: (0, i[0], 0)))
        args.append(bias)
    return call(
        lambda *refs: qkv_kernel(bias is not None, *refs),
        pref,
        args,
        specs,
        shape_of((3 * rows, 4 * tok), BF),
        pl.BlockSpec((3 * rows, tok), lambda j, i: (0, lax.bitwise_xor(i[0], j))),
        (4,),
        [],
        2 * 4 * tok * width * 3 * rows,
    )


def roll_cont(values, shift):
    return jnp.concatenate(
        [values[:, :PROMPT], pltpu.roll(values[:, PROMPT:], shift, 1)], axis=1
    )


def block_list(total, rows):
    blocks = [(i, [(0, PROMPT)]) for i in range(0, PROMPT, rows)]
    blocks += [(i, [(0, PROMPT + LONG)]) for i in range(PROMPT, PROMPT + LONG, rows)]
    blocks += [
        (i, [(0, PROMPT), (PROMPT + LONG, total)]) for i in range(PROMPT + LONG, total, rows)
    ]
    return blocks


def same_segment(shape, key_axis, key_start, query_start, border):
    keys = lax.broadcasted_iota(jnp.int32, shape, key_axis) + key_start
    queries = lax.broadcasted_iota(jnp.int32, shape, 1 - key_axis) + query_start
    return (keys < border) == (queries < border)


def attention_kernel(scale, kept, pref, q_ref, k_ref, v_ref, o0, o1, o2, o3, cf_ref, lse_ref, *rest):
    if kept:
        qs, ks, vs, cs, st = rest
    else:
        cs, st, qs, ks, vs = rest
    own, shift, border = pref[0], pref[1], pref[2]
    total = q_ref.shape[1]
    cont = total - PROMPT
    others = PROMPT + LONG
    back = lax.rem(cont - shift, cont)
    qs[...] = roll_cont(q_ref[...].astype(F32), back).astype(BF)
    ks[...] = roll_cont(k_ref[...].astype(F32), back).astype(BF)
    vs[...] = roll_cont(v_ref[...].astype(F32), back).astype(BF)
    blocks = []
    for start, parts in block_list(total, QB):
        chunks = [key for lo, hi in parts for key in range(lo, hi, KC)]
        blocks.append((start, chunks))
    top, acc, norm = {}, {}, {}

    def scores(n, i):
        start, chunks = blocks[n]
        key = chunks[i]
        value = dot(ks[:, key : key + KC], qs[:, start : start + QB], 0, 0) * scale
        if key >= others:
            mask = same_segment((KC, QB), 0, key - others, start - others, border)
            value = jnp.where(mask, value, -1e30)
        st[n % 2, i * KC : (i + 1) * KC, :] = value
        peak = jnp.max(value, axis=0, keepdims=True)
        top[n] = jnp.maximum(top[n], peak) if n in top else peak

    def weigh(n, i):
        key = blocks[n][1][i]
        prob = jnp.exp2(st[n % 2, i * KC : (i + 1) * KC, :] - top[n])
        part = jnp.sum(prob, axis=0, keepdims=True)
        value = dot(vs[:, key : key + KC], prob.astype(BF), 1, 0)
        acc[n] = acc[n] + value if n in acc else value
        norm[n] = norm[n] + part if n in norm else part

    for i in range(len(blocks[0][1])):
        scores(0, i)
    for n, (start, chunks) in enumerate(blocks):
        ahead = len(blocks[n + 1][1]) if n + 1 < len(blocks) else 0
        for i in range(max(len(chunks), ahead)):
            if i < ahead:
                scores(n + 1, i)
            if i < len(chunks):
                weigh(n, i)
        cf_ref[:, start : start + QB] = acc[n] / norm[n]
        lse_ref[:, start : start + QB] = top[n] + jnp.log2(norm[n])
    cs[...] = roll_cont(cf_ref[...], shift).astype(BF)
    tok = total // 4
    for j, out in enumerate((o0, o1, o2, o3)):
        first = pl.multiple_of(xor(own, j) * tok, 128)
        out[...] = cs[:, pl.ds(first, tok)]


def attention(pref, qkv, kept):
    total = qkv.shape[1]
    heads = HEADS // 4
    hdim = qkv.shape[0] // (3 * heads)
    rows = qkv.shape[0] // 3
    scale = LOG2E / hdim**0.5
    return call(
        lambda *refs: attention_kernel(scale, kept, *refs),
        pref,
        [qkv] * 3,
        [pl.BlockSpec((hdim, total), lambda h, i, o=o: (h + o * heads, 0)) for o in range(3)],
        [shape_of((rows, total // 4), BF)] * 4
        + [shape_of((rows, total), F32), shape_of((heads, 1, total), F32)]
        + [shape_of((rows, total), BF)] * (3 if kept else 0),
        [pl.BlockSpec((hdim, total // 4), lambda h, i: (h, 0))] * 4
        + [
            pl.BlockSpec((hdim, total), lambda h, i: (h, 0)),
            pl.BlockSpec((None, 1, total), lambda h, i: (h, 0, 0)),
        ]
        + [pl.BlockSpec((hdim, total), lambda h, i: (h, 0))] * (3 if kept else 0),
        (heads,),
        [pltpu.VMEM((hdim, total), BF), pltpu.VMEM((2, PROMPT + LONG, QB), F32)]
        + [pltpu.VMEM((hdim, total), BF)] * (0 if kept else 3),
        16 * 10**9,
        12 * 10**6,
    )


def thirds(values):
    high = values.astype(BF).astype(F32)
    middle = (values - high).astype(BF).astype(F32)
    low = values - high - middle
    row = lax.broadcasted_iota(jnp.int32, (AUG, values.shape[1]), 0)
    value = jnp.where(row == 0, high, jnp.where(row == 1, middle, jnp.where(row == 2, low, 0.0)))
    return value.astype(BF)


def attention_back_kernel(
    scale, pref, q_ref, k_ref, v_ref, g0, g1, g2, g3, cf_ref, lse_ref,
    d0, d1, d2, d3, qa, ka, va, ga, gs, dqs, dks, dvs,
):
    own, shift, border = pref[0], pref[1], pref[2]
    hdim, total = q_ref.shape
    tok = total // 4
    cont = total - PROMPT
    others = PROMPT + LONG
    back = lax.rem(cont - shift, cont)
    for j, ref in enumerate((g0, g1, g2, g3)):
        first = pl.multiple_of(xor(own, j) * tok, 128)
        gs[:, pl.ds(first, tok)] = ref[...].astype(F32)
    qa[:hdim, :] = roll_cont(q_ref[...].astype(F32), back).astype(BF)
    ka[:hdim, :] = roll_cont(k_ref[...].astype(F32), back).astype(BF)
    va[:hdim, :] = roll_cont(v_ref[...].astype(F32), back).astype(BF)
    grad = roll_cont(gs[...], back)
    ga[:hdim, :] = grad.astype(BF)
    ga[hdim:, :] = thirds(-jnp.sum(grad * cf_ref[...], axis=0, keepdims=True))
    qa[hdim:, :] = thirds(lse_ref[...] * (-1.0 / scale))
    row = lax.broadcasted_iota(jnp.int32, (AUG, total), 0)
    ones = jnp.where(row < 3, 1.0, 0.0).astype(BF)
    ka[hdim:, :] = ones
    va[hdim:, :] = ones
    seen = set()
    for start, parts in block_list(total, QB):
        queries = slice(start, start + QB)
        grad_q = None
        for lo, hi in parts:
            for key in range(lo, hi, KB):
                keys = slice(key, key + KB)
                value = dot(qa[:, queries], ka[:, keys], 0, 0) * scale
                if lo >= others:
                    mask = same_segment((QB, KB), 1, key - others, start - others, border)
                    value = jnp.where(mask, value, -1e30)
                prob = jnp.exp2(value)
                grad_p = dot(ga[:, queries], va[:, keys], 0, 0)
                grad_s = (prob * grad_p).astype(BF)
                grad_v = dot(ga[:hdim, queries], prob.astype(BF), 1, 0)
                grad_k = dot(qa[:hdim, queries], grad_s, 1, 0)
                part = dot(ka[:hdim, keys], grad_s, 1, 1)
                grad_q = part if grad_q is None else grad_q + part
                if key in seen:
                    dvs[:, keys] += grad_v
                    dks[:, keys] += grad_k
                else:
                    dvs[:, keys] = grad_v
                    dks[:, keys] = grad_k
                    seen.add(key)
        dqs[:, queries] = grad_q
    inv = 1.0 / hdim**0.5
    for part, (ref, factor) in enumerate(((dqs, inv), (dks, inv), (dvs, 1.0))):
        gs[...] = roll_cont(ref[...] * factor, shift)
        for j, out in enumerate((d0, d1, d2, d3)):
            first = pl.multiple_of(xor(own, j) * tok, 128)
            out[part] = gs[:, pl.ds(first, tok)].astype(BF)


def attention_back(pref, qkv, grads, ctx, lse):
    total = qkv.shape[1]
    heads = HEADS // 4
    hdim = qkv.shape[0] // (3 * heads)
    rows = qkv.shape[0] // 3
    scale = LOG2E / hdim**0.5
    quarter = pl.BlockSpec((hdim, total // 4), lambda h, i: (h, 0))
    return call(
        lambda *refs: attention_back_kernel(scale, *refs),
        pref,
        [qkv] * 3 + list(grads) + [ctx, lse],
        [pl.BlockSpec((hdim, total), lambda h, i, o=o: (h + o * heads, 0)) for o in range(3)]
        + [quarter] * 4
        + [
            pl.BlockSpec((hdim, total), lambda h, i: (h, 0)),
            pl.BlockSpec((None, 1, total), lambda h, i: (h, 0, 0)),
        ],
        [shape_of((3, rows, total // 4), BF)] * 4,
        [pl.BlockSpec((3, hdim, total // 4), lambda h, i: (0, h, 0))] * 4,
        (heads,),
        [pltpu.VMEM((hdim + AUG, total), BF)] * 4 + [pltpu.VMEM((hdim, total), F32)] * 4,
        30 * 10**9,
        12 * 10**6,
    )


def normalize(values):
    centre = jnp.mean(values, axis=-1, keepdims=True)
    shifted = values - centre
    spread = jnp.mean(shifted * shifted, axis=-1, keepdims=True)
    inv = lax.rsqrt(spread + EPS)
    return shifted * inv, inv


def normalize_back(grad, normed, inv):
    first = jnp.mean(grad, axis=-1, keepdims=True)
    second = jnp.mean(grad * normed, axis=-1, keepdims=True)
    return (grad - first - normed * second) * inv


def total_rows(values):
    return jnp.sum(values, axis=0, keepdims=True)


def gather_ctx(own, pieces, ctx):
    rows = pieces[0].shape[0]
    for j, ref in enumerate(pieces):
        first = pl.multiple_of(xor(own, j) * rows, 64)
        ctx[pl.ds(first, rows), :] = ref[...]


def student_kernel(
    pref, c0, c1, c2, c3, x, w_out, w_up, w_down, b_out, b_up, b_down, gain, shift,
    ctx, act_one, normed_one, inv_one, gelu, slope, result, normed_two, inv_two,
    acc, mid,
):
    step = pl.program_id(0)

    @pl.when(step == 0)
    def _():
        gather_ctx(pref[0], (c0, c1, c2, c3), ctx)
        res = x[...].astype(F32) + (dot(ctx[...], w_out[...], 0, 1) + b_out[...])
        normed, inv = normalize(res)
        normed_one[...] = normed
        inv_one[...] = inv
        middle = normed * gain[0:1] + shift[0:1]
        mid[...] = middle
        act_one[...] = jnp.clip(middle, -CLIP, CLIP).astype(BF)
        acc[...] = jnp.zeros_like(acc)

    pre = dot(act_one[...], w_up[...], 1, 1) + b_up[...]
    cdf = 0.5 * (1.0 + lax.erf(pre * 0.5**0.5))
    act = (pre * cdf).astype(BF)
    gelu[...] = act
    slope[...] = (cdf + pre * (jnp.exp(pre * pre * -0.5) * 0.3989422804014327)).astype(BF)
    acc[...] += dot(act, w_down[...], 1, 1)

    @pl.when(step == pl.num_programs(0) - 1)
    def _():
        normed, inv = normalize(mid[...] + (acc[...] + b_down[...]))
        normed_two[...] = normed
        inv_two[...] = inv
        result[...] = (normed * gain[1:2] + shift[1:2]).astype(BF)


def ffn_specs(tok, width, hidden):
    up = pl.BlockSpec((FC, width), lambda c, i: (c, 0))
    down = pl.BlockSpec((width, FC), lambda c, i: (0, c))
    wide = pl.BlockSpec((tok, FC), lambda c, i: (0, c))
    row = pl.BlockSpec((1, FC), lambda c, i: (0, c))
    return up, down, wide, row


def student_ffn(pref, pieces, x, w_out, w_up, w_down, b_out, b_up, b_down, gain, shift):
    tok, width = x.shape
    hidden = w_up.shape[0]
    up, down, wide, row = ffn_specs(tok, width, hidden)
    full, one = whole((tok, width)), whole((tok, 1))
    return call(
        student_kernel,
        pref,
        list(pieces) + [x, w_out, w_up, w_down, b_out, b_up, b_down, gain, shift],
        [whole(pieces[0].shape)] * 4
        + [full, whole(w_out.shape), up, down, whole((1, width)), row, whole((1, width))]
        + [whole((2, width))] * 2,
        [
            shape_of((width, tok), BF),
            shape_of((tok, width), BF),
            shape_of((tok, width), F32),
            shape_of((tok, 1), F32),
            shape_of((tok, hidden), BF),
            shape_of((tok, hidden), BF),
            shape_of((tok, width), BF),
            shape_of((tok, width), F32),
            shape_of((tok, 1), F32),
        ],
        [whole((width, tok)), full, full, one, wide, wide, full, full, one],
        (hidden // FC,),
        [pltpu.VMEM((tok, width), F32)] * 2,
        2 * tok * width * (2 * hidden + width),
        2 * tok * hidden,
    )


def teacher_kernel(
    pref, c0, c1, c2, c3, x, w_out, w_up, w_down, gain, shift, normed_two, inv_two,
    grad_sum, grad_ffn, vectors,
    ctx, acc, mid, act_one,
):
    step = pl.program_id(0)

    @pl.when(step == 0)
    def _():
        gather_ctx(pref[0], (c0, c1, c2, c3), ctx)
        res = x[...].astype(F32) + dot(ctx[...], w_out[...], 0, 1)
        normed, inv = normalize(res)
        mid[...] = normed
        act_one[...] = normed.astype(BF)
        acc[...] = jnp.zeros_like(acc)

    pre = dot(act_one[...], w_up[...], 1, 1)
    act = (pre * (0.5 * (1.0 + lax.erf(pre * 0.5**0.5)))).astype(BF)
    acc[...] += dot(act, w_down[...], 1, 1)

    @pl.when(step == pl.num_programs(0) - 1)
    def _():
        target, _unused = normalize(mid[...] + acc[...])
        normed = normed_two[...]
        diff = normed * gain[1:2] + shift[1:2] - target
        back = normalize_back(diff * gain[1:2], normed, inv_two[...])
        grad_sum[...] = back
        low = back.astype(BF)
        grad_ffn[...] = low
        vectors[0:1] = total_rows(diff * normed)
        vectors[1:2] = total_rows(diff)
        vectors[2:3] = total_rows(low.astype(F32))


def teacher_ffn(pref, pieces, x, w_out, w_up, w_down, gain, shift, normed_two, inv_two):
    tok, width = x.shape
    hidden = w_up.shape[0]
    up, down, wide, row = ffn_specs(tok, width, hidden)
    full, one = whole((tok, width)), whole((tok, 1))
    return call(
        teacher_kernel,
        pref,
        list(pieces) + [x, w_out, w_up, w_down, gain, shift, normed_two, inv_two],
        [whole(pieces[0].shape)] * 4
        + [full, whole(w_out.shape), up, down]
        + [whole((2, width))] * 2
        + [full, one],
        [shape_of((tok, width), F32), shape_of((tok, width), BF), shape_of((3, width), F32)],
        [full, full, whole((3, width))],
        (hidden // FC,),
        [pltpu.VMEM((width, tok), BF)]
        + [pltpu.VMEM((tok, width), F32)] * 2
        + [pltpu.VMEM((tok, width), BF)],
        2 * tok * width * (2 * hidden + width),
        tok * hidden,
    )


def back_kernel(
    pref, grad_ffn, slope, w_up, w_down, grad_sum, normed_one, inv_one, gain, shift, w_out,
    grad_hidden, grad_bias, grad_res, grad_attn, g0, g1, g2, g3, vectors,
    acc, ctx,
):
    step = pl.program_id(0)

    @pl.when(step == 0)
    def _():
        acc[...] = jnp.zeros_like(acc)

    low = (dot(grad_ffn[...], w_down[...], 1, 0) * slope[...].astype(F32)).astype(BF)
    grad_hidden[...] = low
    grad_bias[...] = total_rows(low.astype(F32))
    acc[...] += dot(low, w_up[...], 1, 0)

    @pl.when(step == pl.num_programs(0) - 1)
    def _():
        normed = normed_one[...]
        middle = normed * gain[0:1] + shift[0:1]
        grad = grad_sum[...] + jnp.where(jnp.abs(middle) < CLIP, acc[...], 0.0)
        back = normalize_back(grad * gain[0:1], normed, inv_one[...])
        grad_res[...] = back
        attn = back.astype(BF)
        grad_attn[...] = attn
        vectors[0:1] = total_rows(grad * normed)
        vectors[1:2] = total_rows(grad)
        vectors[2:3] = total_rows(attn.astype(F32))
        ctx[...] = dot(w_out[...], attn, 0, 1).astype(BF)
        rows = g0.shape[0]
        for j, ref in enumerate((g0, g1, g2, g3)):
            first = pl.multiple_of(xor(pref[0], j) * rows, 64)
            ref[...] = ctx[pl.ds(first, rows), :]


def student_back(pref, grad_ffn, slope, w_up, w_down, grad_sum, normed_one, inv_one, gain, shift, w_out):
    tok, width = grad_ffn.shape
    hidden = w_up.shape[0]
    up, down, wide, row = ffn_specs(tok, width, hidden)
    full, one = whole((tok, width)), whole((tok, 1))
    return call(
        back_kernel,
        pref,
        [grad_ffn, slope, w_up, w_down, grad_sum, normed_one, inv_one, gain, shift, w_out],
        [full, wide, up, down, full, full, one] + [whole((2, width))] * 2 + [whole(w_out.shape)],
        [
            shape_of((tok, hidden), BF),
            shape_of((1, hidden), F32),
            shape_of((tok, width), F32),
            shape_of((tok, width), BF),
        ]
        + [shape_of((width // 4, tok), BF)] * 4
        + [shape_of((3, width), F32)],
        [wide, row, full, full] + [whole((width // 4, tok))] * 4 + [whole((3, width))],
        (hidden // FC,),
        [pltpu.VMEM((tok, width), F32), pltpu.VMEM((width, tok), BF)],
        2 * tok * width * (2 * hidden + width),
    )


def weight_grad_kernel(
    pref, grad_ffn, gelu, grad_hidden, act_one, grad_attn, ctx, grad_down, grad_up, grad_out, turned
):
    @pl.when(pl.program_id(0) == 0)
    def _():
        turned[...] = grad_ffn[...].T
        value = dot(grad_attn[...], ctx[...], 0, 1).astype(BF)
        grad_out[...] = value.reshape(grad_out.shape)

    value = dot(turned[...], gelu[...], 1, 0).astype(BF)
    grad_down[...] = value.reshape(grad_down.shape)
    value = dot(grad_hidden[...], act_one[...], 0, 0).astype(BF)
    grad_up[...] = value.reshape(grad_up.shape)


def weight_grads(pref, grad_ffn, gelu, grad_hidden, act_one, grad_attn, ctx):
    tok, width = grad_ffn.shape
    hidden = gelu.shape[1]
    count, half = hidden // width, width // 2
    wide = pl.BlockSpec((tok, width), lambda c, i: (0, c))
    full = whole((tok, width))
    return call(
        weight_grad_kernel,
        pref,
        [grad_ffn, gelu, grad_hidden, act_one, grad_attn, ctx],
        [full, wide, wide, full, full, whole((width, tok))],
        [
            shape_of((2, count, half, width), BF),
            shape_of((2 * count, half, width), BF),
            shape_of((2, half, width), BF),
        ],
        [
            pl.BlockSpec((2, 1, half, width), lambda c, i: (0, c, 0, 0)),
            pl.BlockSpec((2, half, width), lambda c, i: (c, 0, 0)),
            whole((2, half, width)),
        ],
        (count,),
        [pltpu.VMEM((width, tok), BF)],
        2 * tok * width * (2 * hidden + width),
    )


def qkv_grad_kernel(pref, d0, d1, d2, d3, x0, x1, x2, x3, out, sums):
    own = pref[0]
    total = None
    count = None
    ones = jnp.ones((8, d0.shape[1]), BF)
    for grad, x in zip((d0, d1, d2, d3), (x0, x1, x2, x3)):
        value = grad[...]
        part = dot(value, jnp.clip(x[...], -CLIP, CLIP), 1, 0)
        line = dot(ones, value, 1, 1)
        total = part if total is None else total + part
        count = line if count is None else count + line
    out[...] = total.astype(BF)
    sums[...] = jnp.zeros_like(sums)
    rows = out.shape[0]
    for j in range(4):

        @pl.when(own == j)
        def _():
            sums[:, j * rows : (j + 1) * rows] = count


def qkv_grad(pref, grads, slots):
    tok, width = slots[0].shape
    rows = grads[0].shape[1]
    return call(
        qkv_grad_kernel,
        pref,
        list(grads) + list(slots),
        [pl.BlockSpec((None, rows, tok), lambda o, i: (o, 0, 0))] * 4 + [whole((tok, width))] * 4,
        [shape_of((3, rows, width), BF), shape_of((3, 8, width), F32)],
        [
            pl.BlockSpec((None, rows, width), lambda o, i: (o, 0, 0)),
            pl.BlockSpec((None, 8, width), lambda o, i: (o, 0, 0)),
        ],
        (3,),
        [],
        2 * 4 * tok * width * 3 * rows,
    )


def input_grad_kernel(pref, e0, e1, e2, e3, wq, wk, wv, grad_res, x, out, acc):
    slot = pl.program_id(0)

    @pl.when(slot == 0)
    def _():
        acc[...] = jnp.zeros_like(acc)

    for j, ref in enumerate((e0, e1, e2, e3)):

        @pl.when(slot == j)
        def _():
            part = dot(ref[0], wq[...], 0, 0)
            part = part + dot(ref[1], wk[...], 0, 0)
            acc[...] += part + dot(ref[2], wv[...], 0, 0)

    @pl.when(slot == 3)
    def _():
        size = jnp.abs(x[...].astype(F32))
        pull = jnp.where(size < CLIP, 1.0, jnp.where(size == CLIP, 0.5, 0.0))
        out[...] = (grad_res[...] + acc[...] * pull).astype(BF)


def input_grad(pref, pieces, weight, grad_res, x):
    tok, width = x.shape
    rows = pieces[0].shape[1]
    full = whole((tok, width))
    return call(
        input_grad_kernel,
        pref,
        list(pieces) + [weight] * 3 + [grad_res, x],
        [whole((3, rows, tok))] * 4
        + [
            pl.BlockSpec((rows, width), lambda j, i, o=o: (o * 4 + lax.bitwise_xor(i[0], j), 0))
            for o in range(3)
        ]
        + [full, full],
        shape_of((tok, width), BF),
        full,
        (4,),
        [pltpu.VMEM((tok, width), F32)],
        2 * 4 * tok * width * 3 * rows,
    )


def place(bit):
    name, mask = bit
    at = lax.axis_index(name)
    upper = lax.rem(lax.div(at, jnp.int32(mask)), jnp.int32(2))
    return upper, {name: at + mask * (1 - 2 * upper)}


class Copies:
    def __init__(self, send, recv, local):
        self.send, self.recv, self.local_sem = send, recv, local
        self.sent, self.planned, self.kept = [], 0, 0

    def plan(self, source, target, device):
        n = self.planned
        self.planned += 1
        return pltpu.make_async_remote_copy(
            src_ref=source,
            dst_ref=target,
            send_sem=self.send.at[n],
            recv_sem=self.recv.at[n],
            device_id=device,
            device_id_type=pl.DeviceIdType.MESH,
        )

    def remote(self, source, target, device):
        copy = self.plan(source, target, device)
        copy.start()
        self.sent.append(copy)
        return copy

    def plan_local(self, source, target):
        self.kept += 1
        return pltpu.make_async_copy(source, target, self.local_sem.at[self.kept - 1])

    def local(self, source, target):
        copy = self.plan_local(source, target)
        copy.start()
        return copy

    def finish(self):
        for copy in self.sent:
            copy.wait_send()


def window(ref, region):
    row, rows, col, cols = region
    return ref.at[pl.ds(row, rows), pl.ds(col, cols)]


def add_window(target, left, right, region, start):
    row, rows, col, cols = region
    step = 48 if rows % 48 == 0 else 16

    def body(i, carry):
        there = pl.ds(pl.multiple_of(row + i * step, 16), step)
        here = pl.ds(pl.multiple_of(start + i * step, 16), step)
        target[there, pl.ds(col, cols)] = left[there, pl.ds(col, cols)] + right[here, :cols]
        return carry

    lax.fori_loop(0, rows // step, body, 0)


def scatter_sum(copies, work, far, full, bits):
    rows, cols = work.shape
    region, used, parts = (0, rows, 0, cols), 0, []
    for n, bit in enumerate(bits):
        upper, device = place(bit)
        row, rows, col, cols = region
        if (rows // 2) % 16 == 0:
            rows //= 2
            kept = (pl.multiple_of(row + upper * rows, 16), rows, col, cols)
            sent = (pl.multiple_of(row + (1 - upper) * rows, 16), rows, col, cols)
        else:
            cols //= 2
            kept = (row, rows, pl.multiple_of(col + upper * cols, 128), cols)
            sent = (row, rows, pl.multiple_of(col + (1 - upper) * cols, 128), cols)
        slot = far.at[pl.ds(used, rows), pl.ds(0, cols)]
        copy = copies.remote(window(work, sent), slot, device)
        yield
        copy.wait_recv()
        add_window(full if n == len(bits) - 1 else work, work, far, kept, used)
        used += rows
        region = kept
        parts.append((bit, kept))
    return parts


def sum_flow(copies, own, other, work, near, far, full, result, core, bits):
    copy = copies.remote(other, near, place(core)[1])
    load = copies.local(own, work)
    yield
    copy.wait_recv()
    load.wait()
    add_window(work, work, near, (0, work.shape[0], 0, work.shape[1]), 0)
    parts = yield from scatter_sum(copies, work, far, full, bits)
    for bit, kept in reversed(parts):
        copy = copies.remote(window(full, kept), window(full, kept), place(bit)[1])
        yield
        copy.wait_recv()
    store = copies.local(full, result)
    yield
    store.wait()


def vector_flow(copies, sums, far, bits):
    for n, bit in enumerate(bits):
        yield
        copy = copies.remote(sums.at[n], far.at[n], place(bit)[1])
        yield
        copy.wait_recv()
        sums[n + 1] = sums[n] + far[n]


def remote_call(kernel, args, in_specs, outs, out_specs, scratch, copies, local, number):
    sems = pltpu.SemaphoreType.DMA
    return pl.pallas_call(
        kernel,
        in_specs=in_specs,
        out_specs=out_specs,
        out_shape=outs,
        scratch_shapes=scratch + [sems((copies,)), sems((copies,)), sems((local,))],
        compiler_params=pltpu.CompilerParams(
            vmem_limit_bytes=VMEM_LIMIT, collective_id=number, has_side_effects=True
        ),
        cost_estimate=pl.CostEstimate(flops=5 * 10**10, bytes_accessed=10**8, transcendentals=0),
    )(*args)


ANY = pl.BlockSpec(memory_space=pl.ANY)
IN_VMEM = pl.BlockSpec(memory_space=pltpu.VMEM)


def binarize_rows(source, target):
    rows, cols = target.shape
    step = 96 if cols < 2048 else 32

    def body(i, carry):
        at = pl.ds(pl.multiple_of(i * step, 16), step)
        value = source[at, :]
        scale = jnp.sum(jnp.abs(value), axis=1, keepdims=True) * (1.0 / cols)
        signed = jnp.where(value > 0, scale, jnp.where(value < 0, -scale, 0.0))
        target[at, :] = signed.astype(BF)
        return carry

    lax.fori_loop(0, rows // step, body, 0)


def entry_kernel(
    seq, core, hidden, teach, segments, l_qkv, l_out, l_up, l_down, t_qkv, t_out, t_up, t_down, bias,
    o_pref, o_qkv, x0, x1, x2, x3, o_teach, b_qkv, b_out, b_up, b_down, e_qkv, e_out, e_up, e_down,
    xs, held, w_qkv, w_out, w_up, w_down, f_qkv, f_out, f_up, f_down,
    s_qkv, s_out, s_up, s_down, proj, others, send, recv, local,
):
    tok, width = hidden.shape
    parts, size = 4, tok // 4
    along, next_chip = place(seq[0])
    side_of, sibling = place(core)
    half = lax.div(lax.axis_index("seq"), jnp.int32(2))
    stays = half == side_of
    moves = half != side_of
    partner = {"seq": 2 * side_of + along, "fsdp": half}
    mesh = pl.DeviceIdType.MESH

    barrier = pltpu.get_barrier_semaphore()
    for device in (next_chip, sibling):
        pl.semaphore_signal(barrier, inc=1, device_id=device, device_id_type=mesh)

    @pl.when(moves)
    def _():
        pl.semaphore_signal(barrier, inc=1, device_id=partner, device_id_type=mesh)
        pl.semaphore_wait(barrier, 3)

    @pl.when(stays)
    def _():
        pl.semaphore_wait(barrier, 2)

    copies = Copies(send, recv, local)
    cuts = [pl.ds(c * size, size) for c in range(parts)]
    swap = [copies.plan(hidden.at[cut], xs.at[0, cut], partner) for cut in cuts]
    load = [copies.plan_local(hidden.at[cut], xs.at[0, cut]) for cut in cuts]
    over = [copies.plan(xs.at[0, cut], xs.at[1, cut], next_chip) for cut in cuts]
    beside = [copies.plan(xs.at[0, cut], xs.at[2, cut], sibling) for cut in cuts]
    relay = [copies.plan(xs.at[1, cut], xs.at[3, cut], sibling) for cut in cuts]
    t_swap = copies.plan(teach, held, partner)
    t_load = copies.plan_local(teach, held)
    seg_copy = copies.remote(segments, others, sibling)

    @pl.when(moves)
    def _():
        for copy in swap:
            copy.start()

    @pl.when(stays)
    def _():
        for copy in load:
            copy.start()
        t_load.start()

    latent = [
        (copies.local(source, target), target)
        for source, target in ((l_qkv, f_qkv), (l_out, f_out), (l_up, f_up), (l_down, f_down))
    ]
    staged = [
        (copies.local(source, target), target, result)
        for source, target, result in (
            (t_qkv, s_qkv, e_qkv),
            (t_out, s_out, e_out),
            (t_up, s_up, e_up),
            (t_down, s_down, e_down),
        )
    ]

    @pl.when(stays)
    def _():
        for c in range(parts):
            load[c].wait()
            over[c].start()
            beside[c].start()

    rows_qkv = l_qkv.shape[0]
    mine = w_qkv.at[pl.ds(pl.multiple_of(side_of * rows_qkv, 16), rows_qkv)]
    latent[0][0].wait()
    binarize_rows(f_qkv, mine)
    qkv_copy = copies.remote(mine, mine, sibling)
    stores, arrivals = [], []
    for (copy, source), target, result in zip(
        latent[1:], (w_out, w_up, w_down), (b_out, b_up, b_down)
    ):
        copy.wait()
        binarize_rows(source, target)
        arrivals.append(copies.remote(target, result.at[side_of], sibling))
        stores.append(copies.local(target, result.at[side_of]))
    for source, (_, _, result) in zip((t_qkv, t_out, t_up, t_down), staged):
        arrivals.append(copies.remote(source, result.at[side_of], sibling))
    for copy, target, result in staged:
        copy.wait()
        stores.append(copies.local(target, result.at[side_of]))

    @pl.when(moves)
    def _():
        for c in range(parts):
            swap[c].wait_recv()
            over[c].start()
            beside[c].start()
        t_swap.start()

    qkv_copy.wait_recv()
    stores.append(copies.local(w_qkv, b_qkv))
    rows = width // 4
    own = along + 2 * side_of

    row = lax.broadcasted_iota(jnp.int32, (AUG, tok), 0)
    ones = jnp.where(row < 3, 1.0, 0.0).astype(BF)
    shifts = []
    for part in range(2):
        line = bias[part : part + 1, 0:rows]
        for j in range(1, 4):
            line = jnp.where(own == j, bias[part : part + 1, j * rows : (j + 1) * rows], line)
        shifts.append(dot(thirds(line), ones, 0, 0))

    def project(slot):
        act = jnp.clip(xs[slot], -CLIP, CLIP)
        first = (1 - along if slot % 2 else along) + 2 * (1 - side_of if slot // 2 else side_of)
        there = pl.ds(pl.multiple_of(first * tok, 128), tok)
        for part in range(3):
            at = pl.multiple_of(part * width + own * rows, 16)
            value = dot(w_qkv[pl.ds(at, rows), :], act, 1, 1)
            if part != 1:
                value = value + shifts[part // 2]
            proj[part * rows : (part + 1) * rows, there] = value.astype(BF)
        stores.append(copies.local(proj.at[:, there], o_qkv.at[:, there]))
        stores.append(copies.local(xs.at[slot], (x0, x1, x2, x3)[slot]))

    seg_copy.wait_recv()
    counts = [jnp.sum(jnp.where(segments[...] == k, 1.0, 0.0)) for k in (1, 2, 3)]
    theirs = [jnp.sum(jnp.where(others[...] == k, 1.0, 0.0)) for k in (1, 2, 3)]
    first, second, third = [
        jnp.where(stays, a, b).astype(jnp.int32) for a, b in zip(counts, theirs)
    ]
    o_pref[0] = own
    o_pref[1] = jnp.where(first == LONG, 0, jnp.where(second == LONG, first, first + second))
    o_pref[2] = jnp.where(first == LONG, second, jnp.where(second == LONG, third, first))

    project(0)
    for copy in beside:
        copy.wait_recv()
    project(2)
    for c in range(parts):
        over[c].wait_recv()
        relay[c].start()
    project(1)
    for copy in relay:
        copy.wait_recv()
    project(3)

    @pl.when(moves)
    def _():
        t_swap.wait_recv()

    @pl.when(stays)
    def _():
        t_load.wait()

    stores.append(copies.local(held, o_teach))
    for copy in arrivals:
        copy.wait_recv()
    for copy in stores:
        copy.wait()

    @pl.when(moves)
    def _():
        for copy in swap + [t_swap]:
            copy.wait_send()

    for copy in over + beside + relay:
        copy.wait_send()
    copies.finish()


def entry(seq, core, hidden, teach, segments, latents, teachers, bias):
    tok, width = hidden.shape
    halves = [w.shape for w in latents]
    sides = [shape_of((2,) + shape, BF) for shape in halves]
    own = [pltpu.VMEM(shape, BF) for shape in halves]
    sides[0] = shape_of((2 * halves[0][0], halves[0][1]), BF)
    sides_t = [shape_of((2,) + shape, BF) for shape in halves]
    outs = remote_call(
        lambda *refs: entry_kernel(seq, core, *refs),
        [hidden, teach, segments] + list(latents) + list(teachers) + [bias],
        [ANY] * 2 + [IN_VMEM] + [ANY] * 8 + [IN_VMEM],
        [shape_of((3,), jnp.int32), shape_of((3 * width // 4, 4 * tok), BF)]
        + [shape_of((tok, width), BF)] * 5
        + sides
        + sides_t,
        [pl.BlockSpec(memory_space=pltpu.SMEM)] + [ANY] * 14,
        [pltpu.VMEM((4, tok, width), BF), pltpu.VMEM((tok, width), BF)]
        + [pltpu.VMEM(sides[0].shape, BF)]
        + own[1:]
        + [pltpu.VMEM(shape, F32) for shape in halves]
        + own
        + [pltpu.VMEM((3 * width // 4, 4 * tok), BF), pltpu.VMEM(segments.shape, jnp.int32)],
        26,
        30,
        3,
    )
    pref, qkv, x0, x1, x2, x3, teach = outs[:7]
    weights = [w.reshape((-1, w.shape[-1])) for w in outs[7:]]
    return pref, qkv, (x0, x1, x2, x3), teach, weights[:4], weights[4:]


class Pump:
    def __init__(self):
        self.events, self.added = [], 0

    def add(self, time, flow, first, then, turn):
        gap = next(flow)
        self.events.append([time + (gap or 0.0), self.added, flow, 0, (first, then, turn)])
        self.added += 1

    def run(self, time=1e9):
        while self.events:
            event = min(self.events, key=lambda e: e[:2])
            if event[0] > time:
                return
            try:
                gap = next(event[2])
            except StopIteration:
                self.events.remove(event)
                continue
            event[3] += 1
            first, then, turn = event[4]
            if gap is None:
                gap = first if event[3] <= turn else then
            event[0] += gap


def head_flow(copies, n, gh, work, far, full, result, seq, core, dp):
    side_of, partner = place(core)
    along = place(seq[0])[0]
    if n == 1:
        copy = copies.remote(gh.at[2 - 2 * side_of], work, partner)
        yield
        copy.wait_recv()
    else:
        load = copies.local(gh.at[n // 2 + side_of], work)
        yield
        load.wait()
    turned, cut = HEAD_PLAN[n][:2]
    bits = (dp[::-1] if turned else dp) + seq[1:]
    mine = full.at[2 * n + along]
    parts = yield from scatter_sum(copies, work, far, mine, bits)
    steps = [(bit, kept, False) for bit, kept in reversed(parts)]
    cut = min(cut, len(steps))
    held = steps[cut][1] if cut < len(steps) else (0, mine.shape[0], 0, mine.shape[1])
    steps = steps[:cut] + [(seq[0], held, False)] + [(b, k, True) for b, k, _ in steps[cut:]]
    for bit, (row, size, col, cols), both in steps:
        first, count = (2 * n, 2) if both else (2 * n + along, 1)
        part = full.at[pl.ds(first, count), pl.ds(row, size), pl.ds(col, cols)]
        copy = copies.remote(part, part, place(bit)[1])
        yield
        copy.wait_recv()
    store = copies.local(full.at[pl.ds(2 * n, 2)], result.at[pl.ds(2 * n, 2)])
    yield
    store.wait()


def tail_kernel(
    dp, seq, core, scale, pref, down, up, out, two, one, bias,
    q_in, k_in, v_in, g0, g1, g2, g3, cf_in, lse, x0, x1, x2, x3, w_in, res_in,
    down_sum, up_sum, out_sum, totals, qkv_sum, hidden_out,
    work, near, far, full, sums, sums_far, gh, h_work, h_far, h_full,
    qs, ks, vs, gp, cf, xs, weight, res, qa, ka, va, ga, gs, dqs, dks, dvs, dn, er, acc, hid,
    send, recv, local,
):
    shift, border = pref[1], pref[2]
    heads_all, total = qs.shape
    hdim = qa.shape[0] - AUG
    heads = heads_all // hdim
    tok = total // 4
    width = xs.shape[2]
    cont, others = total - PROMPT, PROMPT + LONG
    back = lax.rem(cont - shift, cont)
    along, next_chip = place(seq[0])
    side_of, sibling = place(core)
    across = {**next_chip, **sibling}
    half = lax.div(lax.axis_index("seq"), jnp.int32(2))
    stays, moves = half == side_of, half != side_of
    partner = {"seq": 2 * side_of + along, "fsdp": half}
    own = along + 2 * side_of

    def place_of(slot):
        return (1 - along if slot % 2 else along) + 2 * (1 - side_of if slot // 2 else side_of)

    copies = Copies(send, recv, local)
    first_loads = [
        copies.local(source, target)
        for source, target in (
            (g0, gp.at[0]), (g1, gp.at[1]), (g2, gp.at[2]), (g3, gp.at[3]),
            (q_in, qs), (k_in, ks), (v_in, vs), (cf_in, cf),
        )
    ]

    mesh = pl.DeviceIdType.MESH
    barrier = pltpu.get_barrier_semaphore()
    friends = [place(bit)[1] for bit in dp + seq] + [sibling, across]
    for device in friends:
        pl.semaphore_signal(barrier, inc=1, device_id=device, device_id_type=mesh)

    @pl.when(moves)
    def _():
        pl.semaphore_signal(barrier, inc=1, device_id=partner, device_id_type=mesh)
        pl.semaphore_wait(barrier, len(friends) + 1)

    @pl.when(stays)
    def _():
        pl.semaphore_wait(barrier, len(friends))

    pump = Pump()
    count, rows_half = down.shape[1:3]
    ups = [(up.at[side_of, p], up.at[1 - side_of, p], up_sum.at[p]) for p in range(count)]
    downs = [
        (
            down.at[side_of, p],
            down.at[1 - side_of, p],
            down_sum.at[:, pl.ds(p * width, width)],
        )
        for p in range(count)
    ]
    queue = ups + downs + [(out.at[side_of], out.at[1 - side_of], out_sum)]
    near_bits = dp + seq[:1]
    orders = [tuple(near_bits[i] for i in order) for order in ORDERS]
    for n, (mine, theirs, result) in enumerate(queue):
        order, time, first, then = PIECE_PLAN[n % len(PIECE_PLAN)]
        bits = list(orders[order]) + seq[1:]
        flow = sum_flow(
            copies, mine, theirs, work.at[n], near.at[n], far.at[n], full.at[n], result, core, bits
        )
        pump.add(time, flow, first, then, 1 + len(bits))

    late_loads = [
        copies.local(source, target)
        for source, target in (
            (x0, xs.at[0]), (x1, xs.at[1]), (x2, xs.at[2]), (x3, xs.at[3]),
            (w_in, weight), (res_in, res),
        )
    ]
    for copy in first_loads:
        copy.wait()

    row = lax.broadcasted_iota(jnp.int32, (AUG, total), 0)
    ones = jnp.where(row < 3, 1.0, 0.0).astype(BF)
    ka[hdim:, :] = ones
    va[hdim:, :] = ones
    clock = 1.0
    pieces = {1: [], 2: [], 3: []}
    devices = {1: next_chip, 2: sibling, 3: across}
    for h in range(heads):
        lines = slice(h * hdim, (h + 1) * hdim)
        for j in range(4):
            gs[:, pl.ds(pl.multiple_of(place_of(j) * tok, 128), tok)] = gp[j, lines, :].astype(F32)
        qa[:hdim, :] = qs[lines, :]
        ka[:hdim, :] = ks[lines, :]
        va[:hdim, :] = vs[lines, :]
        grad = roll_cont(gs[...], back)
        ga[:hdim, :] = grad.astype(BF)
        ga[hdim:, :] = thirds(-jnp.sum(grad * cf[lines, :], axis=0, keepdims=True))
        qa[hdim:, :] = thirds(lse[h] * (-1.0 / scale))
        seen = set()
        for start, parts in block_list(total, QB):
            queries = slice(start, start + QB)
            grad_q = None
            for lo, hi in parts:
                for key in range(lo, hi, KB):
                    keys = slice(key, key + KB)
                    value = dot(qa[:, queries], ka[:, keys], 0, 0) * scale
                    if lo >= others:
                        mask = same_segment((QB, KB), 1, key - others, start - others, border)
                        value = jnp.where(mask, value, -1e30)
                    prob = jnp.exp2(value)
                    grad_p = dot(ga[:, queries], va[:, keys], 0, 0)
                    grad_s = (prob * grad_p).astype(BF)
                    grad_v = dot(ga[:hdim, queries], prob.astype(BF), 1, 0)
                    grad_k = dot(qa[:hdim, queries], grad_s, 1, 0)
                    part = dot(ka[:hdim, keys], grad_s, 1, 1)
                    grad_q = part if grad_q is None else grad_q + part
                    if key in seen:
                        dvs[:, keys] += grad_v
                        dks[:, keys] += grad_k
                    else:
                        dvs[:, keys] = grad_v
                        dks[:, keys] = grad_k
                        seen.add(key)
                    clock += 0.65
            dqs[:, queries] = grad_q
            pump.run(clock)
        inv = 1.0 / hdim**0.5
        for part, (ref, factor) in enumerate(((dqs, inv), (dks, inv), (dvs, 1.0))):
            gs[...] = roll_cont(ref[...] * factor, shift)
            for j in range(4):
                there = pl.ds(pl.multiple_of(place_of(j) * tok, 128), tok)
                dn[j, part, lines, :] = gs[:, there].astype(BF)
        for j in (1, 3, 2):
            at = pl.ds(h * hdim, hdim)
            copy = copies.remote(dn.at[j, :, at, :], er.at[j - 1, :, at, :], devices[j])
            pieces[j].append(copy)
        clock += 1.5
        pump.run(clock)

    for copy in late_loads:
        copy.wait()
    rows = width // 4
    one_rows = jnp.ones((8, tok), BF)
    counts = []
    for o in range(3):
        value, line = None, None
        for j in range(4):
            part = dot(dn[j, o], jnp.clip(xs[j], -CLIP, CLIP), 1, 0)
            ends = dot(one_rows, dn[j, o], 1, 1)
            value = part if value is None else value + part
            line = ends if line is None else line + ends
        gh[o] = value.astype(BF)
        counts.append(line)
        clock += 2.7
        pump.run(clock)
    sums[0] = jnp.zeros(sums.shape[1:], F32)
    for j in range(4):

        @pl.when(own == j)
        def _():
            sums[0, 0:1, j * rows : (j + 1) * rows] = counts[0][0:1]
            sums[0, 1:2, j * rows : (j + 1) * rows] = counts[2][0:1]

    sums[0, 2:3] = one[2:3]
    sums[0, 3:4] = two[2:3]
    sums[0, 4:5] = one[0:1]
    sums[0, 5:6] = two[0:1]
    sums[0, 6:7] = one[1:2]
    sums[0, 7:8] = two[1:2]
    for p in range(count):
        sums[0, 8 + p : 9 + p] = bias[:, p * width : (p + 1) * width]

    swap = copies.plan(hid, hidden_out, partner)
    keep = copies.plan_local(hid, hidden_out)

    def hidden_flow():
        yield 0.0
        gaps = HIDDEN_PLAN[1]
        for gap, j in zip(gaps, (0, 2, 1, 3)):
            for copy in pieces.get(j, []):
                copy.wait_recv()
            part = None
            for o in range(3):
                at = pl.multiple_of(o * width + place_of(j) * rows, 16)
                source = dn[0, o] if j == 0 else er[j - 1, o]
                piece = dot(source, weight[pl.ds(at, rows), :], 0, 0)
                part = piece if part is None else part + piece
            if j == 0:
                acc[...] = part
            elif j != 3:
                acc[...] += part
            else:
                size = jnp.abs(xs[0].astype(F32))
                pull = jnp.where(size < CLIP, 1.0, jnp.where(size == CLIP, 0.5, 0.0))
                hid[...] = (res[...] + (acc[...] + part) * pull).astype(BF)
            if j != 3:
                yield gap

        @pl.when(moves)
        def _():
            swap.start()

        @pl.when(stays)
        def _():
            keep.start()

        yield gaps[3]

        @pl.when(moves)
        def _():
            swap.wait_recv()
            swap.wait_send()

        @pl.when(stays)
        def _():
            keep.wait()

    pump.add(clock + HIDDEN_PLAN[0], hidden_flow(), 0.0, 0.0, 0)
    for n in (0, 2, 1):
        flow = head_flow(
            copies, n, gh, h_work.at[n], h_far.at[n], h_full, qkv_sum, seq, core, dp
        )
        time, first, then = HEAD_PLAN[n][2:]
        pump.add(clock + time, flow, first, then, 4)
    time, gap = VECTOR_PLAN
    pump.add(clock + time, vector_flow(copies, sums, sums_far, [core] + dp + seq), gap, gap, 0)
    pump.run()
    totals[...] = sums[sums.shape[0] - 1]
    copies.finish()


def tail(
    dp, seq, core, pref, down, up, out, two, one, bias, rolled, grads, cf, lse, slots, weight, res
):
    sides, count, half, width = down.shape
    pieces, steps, lines = 2 * count + 1, len(dp) + len(seq), 16
    rows, total = rolled[0].shape
    tok = total // 4
    heads = HEADS // 4
    hdim = rows // heads
    scale = LOG2E / hdim**0.5
    smem = pl.BlockSpec(memory_space=pltpu.SMEM)
    return remote_call(
        lambda *refs: tail_kernel(dp, seq, core, scale, *refs),
        [pref, down, up, out, two, one, bias]
        + list(rolled)
        + list(grads)
        + [cf, lse]
        + list(slots)
        + [weight, res],
        [smem] + [ANY] * 3 + [IN_VMEM] * 3 + [ANY] * 8 + [IN_VMEM] + [ANY] * 6,
        [
            shape_of((half, count * width), BF),
            shape_of((count, half, width), BF),
            shape_of((half, width), BF),
            shape_of((lines, width), F32),
            shape_of((6, rows, width), BF),
            shape_of((tok, width), BF),
        ],
        [ANY] * 3 + [IN_VMEM] + [ANY] * 2,
        [pltpu.VMEM((pieces, half, width), BF)] * 4
        + [pltpu.VMEM((steps + 2, lines, width), F32), pltpu.VMEM((steps + 1, lines, width), F32)]
        + [pltpu.VMEM((3, rows, width), BF)] * 3
        + [pltpu.VMEM((6, rows, width), BF)]
        + [pltpu.VMEM((rows, total), BF)] * 3
        + [pltpu.VMEM((4, rows, tok), BF), pltpu.VMEM((rows, total), F32)]
        + [pltpu.VMEM((4, tok, width), BF), pltpu.VMEM(weight.shape, BF)]
        + [pltpu.VMEM((tok, width), F32)]
        + [pltpu.VMEM((hdim + AUG, total), BF)] * 4
        + [pltpu.VMEM((hdim, total), F32)] * 4
        + [pltpu.VMEM((4, 3, rows, tok), BF), pltpu.VMEM((3, 3, rows, tok), BF)]
        + [pltpu.VMEM((tok, width), F32), pltpu.VMEM((tok, width), BF)],
        pieces * (1 + 2 * steps) + steps + 1 + 3 * heads + 1 + 3 * (2 * steps - 1) + 1,
        2 * pieces + 14 + 1 + 5,
        4,
    )


def widen_kernel(*refs):
    half = len(refs) // 2
    for source, target in zip(refs[:half], refs[half:]):
        target[...] = source[...].astype(F32)


def widen(values, steps):
    specs = [pl.BlockSpec((v.shape[0] // steps, v.shape[1]), lambda i: (i, 0)) for v in values]
    return pl.pallas_call(
        widen_kernel,
        grid=(steps,),
        in_specs=specs,
        out_specs=specs,
        out_shape=[shape_of(v.shape, F32) for v in values],
        compiler_params=pltpu.CompilerParams(vmem_limit_bytes=VMEM_LIMIT),
        cost_estimate=pl.CostEstimate(
            flops=0, bytes_accessed=6 * sum(v.size for v in values), transcendentals=0
        ),
    )(*values)


def binarize(latent):
    row_scale = jnp.mean(jnp.abs(latent), axis=1, keepdims=True)
    return (row_scale * jnp.sign(latent)).astype(BF)


def segment_info(segments):
    sizes_of = [jnp.sum((segments == k).astype(jnp.int32)) for k in (1, 2, 3)]
    first, second, third = sizes_of
    shift = jnp.where(first == LONG, 0, jnp.where(second == LONG, first, first + second))
    border = jnp.where(first == LONG, second, jnp.where(second == LONG, third, first))
    return jnp.stack([shift, border])


def quarters(own):
    along = to_slot(own, 1)
    return (own, along, to_slot(own, 2), to_slot(along, 2))


def exchange(pieces):
    return (pieces[0],) + tuple(to_slot(pieces[j], j) for j in (1, 2, 3))


def on_device(
    hidden, teacher_hidden, segments, latent_qkv, latent_out, latent_up, latent_down,
    biases, up_bias, norm_gains, norm_shifts, teacher_qkv, teacher_out, teacher_up, teacher_down,
):
    seq_at, fsdp_at = lax.axis_index("seq"), lax.axis_index("fsdp")
    fsdp = lax.axis_size("fsdp")
    core = fsdp_at % 2
    own = (seq_at % 2 + 2 * core).astype(jnp.int32)
    width = hidden.shape[2]

    latents = (latent_qkv, latent_out, latent_up, latent_down)
    teachers = (teacher_qkv, teacher_out, teacher_up, teacher_down)
    if fsdp == 2:
        pref, qkv, x_slots, teach, bins, t_weights = entry(
            bit_list("seq"), bit_list("fsdp")[0], hidden[0], teacher_hidden[0], segments,
            latents, teachers, biases,
        )
        x = x_slots[0]
    else:
        info = segment_info(segments)
        info = jnp.where(core == seq_at // 2, info, flip(info, fsdp=1))
        pref = jnp.concatenate([own[None], info]).astype(jnp.int32)
        x = swap_groups(hidden[0])
        x_slots = quarters(x)
        bins = [gather_rows(binarize(w)) for w in latents]
        teach = swap_groups(teacher_hidden[0])
        t_weights = [gather_rows(w) for w in teachers]
        qkv = qkv_project(pref, x_slots, bins[0], biases[:2].reshape(2, width, 1))
    bin_qkv, bin_out, bin_up, bin_down = bins
    t_qkv, t_out, t_up, t_down = t_weights
    t_along, t_beside = to_slot(teach, 1), to_slot(teach, 2)
    *ctx_slots, ctx_full, lse, q_roll, k_roll, v_roll = attention(pref, qkv, True)
    t_along, ctx_slots = lax.optimization_barrier((t_along, ctx_slots))
    t_slots = (teach, t_along, t_beside, to_slot(t_along, 2))
    ctx_pieces = exchange(ctx_slots)

    t_heads = qkv_project(pref, t_slots, t_qkv, None)
    *tctx_slots, _unused, _unused_too = attention(pref, t_heads, False)
    tctx_slots, ctx_pieces = lax.optimization_barrier((tctx_slots, ctx_pieces))
    tctx_pieces = exchange(tctx_slots)

    gain, shift = norm_gains, norm_shifts
    (
        ctx, act_one, normed_one, inv_one, gelu, slope, result, normed_two, inv_two,
    ) = student_ffn(
        pref, ctx_pieces, x, bin_out, bin_up, bin_down,
        biases[2:3], up_bias[None], biases[3:4], gain, shift,
    )
    student_out = swap_groups(result)
    grad_sum, grad_ffn, vec_two = teacher_ffn(
        pref, tctx_pieces, teach, t_out, t_up, t_down, gain, shift, normed_two, inv_two
    )
    grad_hidden, grad_up_bias, grad_res, grad_attn, *gctx_slots, vec_one = student_back(
        pref, grad_ffn, slope, bin_up, bin_down, grad_sum, normed_one, inv_one, gain, shift, bin_out
    )
    gctx_pieces = exchange(gctx_slots)
    grad_down, grad_up, grad_out = weight_grads(
        pref, grad_ffn, gelu, grad_hidden, act_one, grad_attn, ctx
    )
    dp_bits, seq_bits, fsdp_bits = bit_list("dp"), bit_list("seq"), bit_list("fsdp")
    rows, hidden_units = width // 4, up_bias.shape[0]

    if fsdp == 2:
        total_down, total_up, total_out, vectors, total_qkv, hidden_grad = tail(
            dp_bits, seq_bits, fsdp_bits[0], pref,
            grad_down, grad_up.reshape(grad_down.shape), grad_out, vec_two, vec_one, grad_up_bias,
            (q_roll, k_roll, v_roll), gctx_pieces, ctx_full, lse, x_slots, bin_qkv, grad_res,
        )
        total_up = total_up.reshape(-1, width)
        total_qkv = total_qkv.reshape(-1, width)
        total_qkv, total_out, total_up, total_down = widen(
            (total_qkv, total_out, total_up, total_down), 6
        )
    else:
        dqkv_slots = attention_back(pref, qkv, gctx_pieces, ctx_full, lse)
        dqkv_pieces = exchange(dqkv_slots)
        grad_heads, head_sums = qkv_grad(pref, dqkv_slots, x_slots)
        hidden_grad = swap_groups(input_grad(pref, dqkv_pieces, bin_qkv, grad_res, x))

        def reduce_grad(value, bits):
            for bit in reversed(fsdp_bits):
                value = halve(value, bit)
            return all_reduce(value, bits)

        grad_down = grad_down.transpose(0, 2, 1, 3).reshape(width, hidden_units)
        total_down = reduce_grad(grad_down, dp_bits + seq_bits)
        total_up = reduce_grad(grad_up.reshape(hidden_units, width), dp_bits[::-1] + seq_bits)
        total_out = reduce_grad(
            grad_out.reshape(width, width), seq_bits[:1] + dp_bits + seq_bits[1:]
        )
        blocks = all_reduce(
            grad_heads.reshape(3 * rows, width), dp_bits + seq_bits[1:] + fsdp_bits[1:]
        )
        blocks = blocks.reshape(1, 3, rows, width)
        blocks = double(double(blocks, seq_bits[0]), fsdp_bits[0])
        whole_qkv = blocks.transpose(1, 0, 2, 3).reshape(3 * width, width)
        part = 3 * width // fsdp
        total_qkv = lax.dynamic_slice_in_dim(whole_qkv, fsdp_at * part, part, 0)
        vectors = jnp.concatenate(
            [
                head_sums[0, :1],
                head_sums[2, :1],
                vec_one[2:3],
                vec_two[2:3],
                vec_one[0:1],
                vec_two[0:1],
                vec_one[1:2],
                vec_two[1:2],
                grad_up_bias.reshape(-1, width),
            ]
        )
        vectors = sum_small(vectors, dp_bits + seq_bits + fsdp_bits)
    hid_bias = vectors[8 : 8 + hidden_units // width].reshape(-1)
    share, hid_share = width // fsdp, hid_bias.shape[0] // fsdp
    cols = lax.dynamic_slice_in_dim(vectors[:8], fsdp_at * share, share, 1)
    return (
        student_out[None],
        hidden_grad[None],
        total_qkv.astype(F32),
        total_out.astype(F32),
        total_up.astype(F32),
        total_down.astype(F32),
        cols[0:4],
        lax.dynamic_slice_in_dim(hid_bias, fsdp_at * hid_share, hid_share, 0),
        cols[4:6],
        cols[6:8],
    )


def solution(mesh):
    tokens = P(("dp", "fsdp"), "seq", None)
    rows = P("fsdp", None)
    return jax.shard_map(
        on_device,
        mesh=mesh,
        in_specs=(tokens, tokens, P(("dp", "fsdp"), None)) + (rows,) * 4 + (P(),) * 4 + (rows,) * 4,
        out_specs=(tokens, tokens)
        + (rows,) * 4
        + (P(None, "fsdp"), P("fsdp"), P(None, "fsdp"), P(None, "fsdp")),
        check_vma=False,
    )
```

```python
import jax
import jax.numpy as jnp
from jax import lax
from jax.experimental import pallas as pl
from jax.experimental.pallas import tpu as pltpu
from jax.sharding import PartitionSpec as P

HEADS = 12
PROMPT = 1024
LONG = 1024
CLIP = 2.5
EPS = 1e-05
AXES = ("dp", "seq", "fsdp")
BF = jnp.bfloat16
F32 = jnp.float32
LOG2E = 1.4426950408889634
QB = 512
KC = 256
KB = 512
FC = 1024
AUG = 16
VMEM_LIMIT = 56 * 2**20
TAIL_LIMIT = 60 * 2**20
ORDERS = ((0, 1, 2), (1, 0, 2), (0, 2, 1), (1, 2, 0), (2, 0, 1), (2, 1, 0))
PIECE_PLAN = (
    (0, 6.2, 33.2, 64.8),
    (2, 13.6, 75.8, 115.6),
    (1, 87.9, 109.7, 109.9),
    (1, 18.5, 61.3, 92.2),
    (4, 8.4, 94.5, 125.6),
    (0, 9.7, 53.1, 89.3),
    (0, 30.0, 114.5, 110.0),
    (1, 23.6, 99.1, 76.0),
    (1, 15.8, 49.7, 87.1),
)
HEAD_PLAN = (
    (1, 1, 238.2, 90.7, 81.4),
    (0, 3, 170.9, 119.6, 73.4),
    (1, 1, 16.1, 96.9, 77.0),
)
HIDDEN_PLAN = (0.0, (416.8, 50.8, 134.5, 451.6))
VECTOR_PLAN = (75.4, 88.5)


def dot(left, right, left_dim, right_dim):
    return lax.dot_general(
        left, right, (((left_dim,), (right_dim,)), ((), ())), preferred_element_type=F32
    )


def xor(first, second):
    return lax.bitwise_xor(first, jnp.int32(second))


def sizes():
    return tuple(lax.axis_size(name) for name in AXES)


def permute(values, target):
    dp, seq, fsdp = sizes()
    pairs = []
    for d in range(dp):
        for s in range(seq):
            for f in range(fsdp):
                td, ts, tf = target(d, s, f)
                pairs.append(((d * seq + s) * fsdp + f, (td * seq + ts) * fsdp + tf))
    return lax.ppermute(values, AXES, pairs)


def flip(values, dp=0, seq=0, fsdp=0):
    return permute(values, lambda d, s, f: (d ^ dp, s ^ seq, f ^ fsdp))


def swap_groups(values):
    return permute(
        values, lambda d, s, f: (d, 2 * (f % 2) + s % 2, f - f % 2 + s // 2)
    )


def to_slot(values, slot):
    return flip(values, seq=slot & 1, fsdp=slot >> 1)


def bit_list(name):
    count = lax.axis_size(name)
    out, bit = [], 1
    while bit < count:
        out.append((name, bit))
        bit *= 2
    return out


def flip_bit(values, bit):
    return flip(values, **{bit[0]: bit[1]})


def side(bit):
    return lax.bitwise_and(lax.axis_index(bit[0]), bit[1]) != 0


def halve(values, bit):
    upper = side(bit).astype(jnp.int32)
    half = values.shape[0] // 2
    sent = lax.dynamic_slice_in_dim(values, (1 - upper) * half, half, 0)
    kept = lax.dynamic_slice_in_dim(values, upper * half, half, 0)
    got = flip_bit(sent, bit)
    return (kept.astype(F32) + got.astype(F32)).astype(values.dtype)


def double(values, bit):
    got = flip_bit(values, bit)
    return jnp.where(
        side(bit),
        jnp.concatenate([got, values], axis=0),
        jnp.concatenate([values, got], axis=0),
    )


def gather_rows(values):
    for bit in bit_list("fsdp"):
        values = double(values, bit)
    return values


def all_reduce(values, bits):
    for bit in bits:
        values = halve(values, bit)
    for bit in reversed(bits):
        values = double(values, bit)
    return values


def sum_small(values, bits):
    for bit in bits:
        values = values + flip_bit(values, bit)
    return values


def whole(shape):
    return pl.BlockSpec(shape, lambda *_: (0,) * len(shape))


def call(kernel, pref, args, in_specs, outs, out_specs, grid, scratch, flops, trans=0):
    moved = sum(a.size * a.dtype.itemsize for a in args)
    moved += sum(o.size * o.dtype.itemsize for o in jax.tree.leaves(outs))
    return pl.pallas_call(
        kernel,
        grid_spec=pltpu.PrefetchScalarGridSpec(
            num_scalar_prefetch=1,
            grid=grid,
            in_specs=in_specs,
            out_specs=out_specs,
            scratch_shapes=scratch,
        ),
        out_shape=outs,
        compiler_params=pltpu.CompilerParams(vmem_limit_bytes=VMEM_LIMIT),
        cost_estimate=pl.CostEstimate(flops=flops, bytes_accessed=moved, transcendentals=trans),
    )(pref, *args)


def shape_of(shape, dtype):
    return jax.ShapeDtypeStruct(shape, dtype)


def qkv_kernel(student, pref, x0, x1, x2, x3, wq, wk, wv, *rest):
    slot = pl.program_id(0)
    out = rest[-1]
    rows = wq.shape[0]
    for j, ref in enumerate((x0, x1, x2, x3)):

        @pl.when(slot == j)
        def _():
            act = ref[...]
            if student:
                act = jnp.clip(act, -CLIP, CLIP)
            for part, weight in enumerate((wq, wk, wv)):
                value = dot(weight[...], act, 1, 1)
                if student and part != 1:
                    value = value + rest[0][part // 2]
                out[part * rows : (part + 1) * rows, :] = value.astype(BF)


def qkv_project(pref, slots, weight, bias):
    tok, width = slots[0].shape
    rows = weight.shape[0] // 12
    specs = [whole((tok, width))] * 4
    specs += [
        pl.BlockSpec((rows, width), lambda j, i, o=o: (o * 4 + i[0], 0)) for o in range(3)
    ]
    args = list(slots) + [weight] * 3
    if bias is not None:
        specs.append(pl.BlockSpec((2, rows, 1), lambda j, i: (0, i[0], 0)))
        args.append(bias)
    return call(
        lambda *refs: qkv_kernel(bias is not None, *refs),
        pref,
        args,
        specs,
        shape_of((3 * rows, 4 * tok), BF),
        pl.BlockSpec((3 * rows, tok), lambda j, i: (0, lax.bitwise_xor(i[0], j))),
        (4,),
        [],
        2 * 4 * tok * width * 3 * rows,
    )


def roll_cont(values, shift):
    return jnp.concatenate(
        [values[:, :PROMPT], pltpu.roll(values[:, PROMPT:], shift, 1)], axis=1
    )


def block_list(total, rows):
    blocks = [(i, [(0, PROMPT)]) for i in range(0, PROMPT, rows)]
    blocks += [(i, [(0, PROMPT + LONG)]) for i in range(PROMPT, PROMPT + LONG, rows)]
    blocks += [
        (i, [(0, PROMPT), (PROMPT + LONG, total)]) for i in range(PROMPT + LONG, total, rows)
    ]
    return blocks


def same_segment(shape, key_axis, key_start, query_start, border):
    keys = lax.broadcasted_iota(jnp.int32, shape, key_axis) + key_start
    queries = lax.broadcasted_iota(jnp.int32, shape, 1 - key_axis) + query_start
    return (keys < border) == (queries < border)


def attention_kernel(scale, kept, pref, q_ref, k_ref, v_ref, o0, o1, o2, o3, cf_ref, lse_ref, *rest):
    if kept:
        qs, ks, vs, cs, st = rest
    else:
        cs, st, qs, ks, vs = rest
    own, shift, border = pref[0], pref[1], pref[2]
    total = q_ref.shape[1]
    cont = total - PROMPT
    others = PROMPT + LONG
    back = lax.rem(cont - shift, cont)
    qs[...] = roll_cont(q_ref[...].astype(F32), back).astype(BF)
    ks[...] = roll_cont(k_ref[...].astype(F32), back).astype(BF)
    vs[...] = roll_cont(v_ref[...].astype(F32), back).astype(BF)
    blocks = []
    for start, parts in block_list(total, QB):
        chunks = [key for lo, hi in parts for key in range(lo, hi, KC)]
        blocks.append((start, chunks))
    top, acc, norm = {}, {}, {}

    def scores(n, i):
        start, chunks = blocks[n]
        key = chunks[i]
        value = dot(ks[:, key : key + KC], qs[:, start : start + QB], 0, 0) * scale
        if key >= others:
            mask = same_segment((KC, QB), 0, key - others, start - others, border)
            value = jnp.where(mask, value, -1e30)
        st[n % 2, i * KC : (i + 1) * KC, :] = value
        peak = jnp.max(value, axis=0, keepdims=True)
        top[n] = jnp.maximum(top[n], peak) if n in top else peak

    def weigh(n, i):
        key = blocks[n][1][i]
        prob = jnp.exp2(st[n % 2, i * KC : (i + 1) * KC, :] - top[n])
        part = jnp.sum(prob, axis=0, keepdims=True)
        value = dot(vs[:, key : key + KC], prob.astype(BF), 1, 0)
        acc[n] = acc[n] + value if n in acc else value
        norm[n] = norm[n] + part if n in norm else part

    for i in range(len(blocks[0][1])):
        scores(0, i)
    for n, (start, chunks) in enumerate(blocks):
        ahead = len(blocks[n + 1][1]) if n + 1 < len(blocks) else 0
        for i in range(max(len(chunks), ahead)):
            if i < ahead:
                scores(n + 1, i)
            if i < len(chunks):
                weigh(n, i)
        cf_ref[:, start : start + QB] = acc[n] / norm[n]
        lse_ref[:, start : start + QB] = top[n] + jnp.log2(norm[n])
    cs[...] = roll_cont(cf_ref[...], shift).astype(BF)
    tok = total // 4
    for j, out in enumerate((o0, o1, o2, o3)):
        first = pl.multiple_of(xor(own, j) * tok, 128)
        out[...] = cs[:, pl.ds(first, tok)]


def attention(pref, qkv, kept):
    total = qkv.shape[1]
    heads = HEADS // 4
    hdim = qkv.shape[0] // (3 * heads)
    rows = qkv.shape[0] // 3
    scale = LOG2E / hdim**0.5
    return call(
        lambda *refs: attention_kernel(scale, kept, *refs),
        pref,
        [qkv] * 3,
        [pl.BlockSpec((hdim, total), lambda h, i, o=o: (h + o * heads, 0)) for o in range(3)],
        [shape_of((rows, total // 4), BF)] * 4
        + [shape_of((rows, total), F32), shape_of((heads, 1, total), F32)]
        + [shape_of((rows, total), BF)] * (3 if kept else 0),
        [pl.BlockSpec((hdim, total // 4), lambda h, i: (h, 0))] * 4
        + [
            pl.BlockSpec((hdim, total), lambda h, i: (h, 0)),
            pl.BlockSpec((None, 1, total), lambda h, i: (h, 0, 0)),
        ]
        + [pl.BlockSpec((hdim, total), lambda h, i: (h, 0))] * (3 if kept else 0),
        (heads,),
        [pltpu.VMEM((hdim, total), BF), pltpu.VMEM((2, PROMPT + LONG, QB), F32)]
        + [pltpu.VMEM((hdim, total), BF)] * (0 if kept else 3),
        16 * 10**9,
        12 * 10**6,
    )


def thirds(values):
    high = values.astype(BF).astype(F32)
    middle = (values - high).astype(BF).astype(F32)
    low = values - high - middle
    row = lax.broadcasted_iota(jnp.int32, (AUG, values.shape[1]), 0)
    value = jnp.where(row == 0, high, jnp.where(row == 1, middle, jnp.where(row == 2, low, 0.0)))
    return value.astype(BF)


def attention_back_kernel(
    scale, pref, q_ref, k_ref, v_ref, g0, g1, g2, g3, cf_ref, lse_ref,
    d0, d1, d2, d3, qa, ka, va, ga, gs, dqs, dks, dvs,
):
    own, shift, border = pref[0], pref[1], pref[2]
    hdim, total = q_ref.shape
    tok = total // 4
    cont = total - PROMPT
    others = PROMPT + LONG
    back = lax.rem(cont - shift, cont)
    for j, ref in enumerate((g0, g1, g2, g3)):
        first = pl.multiple_of(xor(own, j) * tok, 128)
        gs[:, pl.ds(first, tok)] = ref[...].astype(F32)
    qa[:hdim, :] = roll_cont(q_ref[...].astype(F32), back).astype(BF)
    ka[:hdim, :] = roll_cont(k_ref[...].astype(F32), back).astype(BF)
    va[:hdim, :] = roll_cont(v_ref[...].astype(F32), back).astype(BF)
    grad = roll_cont(gs[...], back)
    ga[:hdim, :] = grad.astype(BF)
    ga[hdim:, :] = thirds(-jnp.sum(grad * cf_ref[...], axis=0, keepdims=True))
    qa[hdim:, :] = thirds(lse_ref[...] * (-1.0 / scale))
    row = lax.broadcasted_iota(jnp.int32, (AUG, total), 0)
    ones = jnp.where(row < 3, 1.0, 0.0).astype(BF)
    ka[hdim:, :] = ones
    va[hdim:, :] = ones
    seen = set()
    for start, parts in block_list(total, QB):
        queries = slice(start, start + QB)
        grad_q = None
        for lo, hi in parts:
            for key in range(lo, hi, KB):
                keys = slice(key, key + KB)
                value = dot(qa[:, queries], ka[:, keys], 0, 0) * scale
                if lo >= others:
                    mask = same_segment((QB, KB), 1, key - others, start - others, border)
                    value = jnp.where(mask, value, -1e30)
                prob = jnp.exp2(value)
                grad_p = dot(ga[:, queries], va[:, keys], 0, 0)
                grad_s = (prob * grad_p).astype(BF)
                grad_v = dot(ga[:hdim, queries], prob.astype(BF), 1, 0)
                grad_k = dot(qa[:hdim, queries], grad_s, 1, 0)
                part = dot(ka[:hdim, keys], grad_s, 1, 1)
                grad_q = part if grad_q is None else grad_q + part
                if key in seen:
                    dvs[:, keys] += grad_v
                    dks[:, keys] += grad_k
                else:
                    dvs[:, keys] = grad_v
                    dks[:, keys] = grad_k
                    seen.add(key)
        dqs[:, queries] = grad_q
    inv = 1.0 / hdim**0.5
    for part, (ref, factor) in enumerate(((dqs, inv), (dks, inv), (dvs, 1.0))):
        gs[...] = roll_cont(ref[...] * factor, shift)
        for j, out in enumerate((d0, d1, d2, d3)):
            first = pl.multiple_of(xor(own, j) * tok, 128)
            out[part] = gs[:, pl.ds(first, tok)].astype(BF)


def attention_back(pref, qkv, grads, ctx, lse):
    total = qkv.shape[1]
    heads = HEADS // 4
    hdim = qkv.shape[0] // (3 * heads)
    rows = qkv.shape[0] // 3
    scale = LOG2E / hdim**0.5
    quarter = pl.BlockSpec((hdim, total // 4), lambda h, i: (h, 0))
    return call(
        lambda *refs: attention_back_kernel(scale, *refs),
        pref,
        [qkv] * 3 + list(grads) + [ctx, lse],
        [pl.BlockSpec((hdim, total), lambda h, i, o=o: (h + o * heads, 0)) for o in range(3)]
        + [quarter] * 4
        + [
            pl.BlockSpec((hdim, total), lambda h, i: (h, 0)),
            pl.BlockSpec((None, 1, total), lambda h, i: (h, 0, 0)),
        ],
        [shape_of((3, rows, total // 4), BF)] * 4,
        [pl.BlockSpec((3, hdim, total // 4), lambda h, i: (0, h, 0))] * 4,
        (heads,),
        [pltpu.VMEM((hdim + AUG, total), BF)] * 4 + [pltpu.VMEM((hdim, total), F32)] * 4,
        30 * 10**9,
        12 * 10**6,
    )


def normalize(values):
    centre = jnp.mean(values, axis=-1, keepdims=True)
    shifted = values - centre
    spread = jnp.mean(shifted * shifted, axis=-1, keepdims=True)
    inv = lax.rsqrt(spread + EPS)
    return shifted * inv, inv


def normalize_back(grad, normed, inv):
    first = jnp.mean(grad, axis=-1, keepdims=True)
    second = jnp.mean(grad * normed, axis=-1, keepdims=True)
    return (grad - first - normed * second) * inv


def total_rows(values):
    return jnp.sum(values, axis=0, keepdims=True)


def gather_ctx(own, pieces, ctx):
    rows = pieces[0].shape[0]
    for j, ref in enumerate(pieces):
        first = pl.multiple_of(xor(own, j) * rows, 64)
        ctx[pl.ds(first, rows), :] = ref[...]


def student_kernel(
    pref, c0, c1, c2, c3, x, w_out, w_up, w_down, b_out, b_up, b_down, gain, shift,
    ctx, act_one, normed_one, inv_one, gelu, slope, result, normed_two, inv_two,
    acc, mid,
):
    step = pl.program_id(0)

    @pl.when(step == 0)
    def _():
        gather_ctx(pref[0], (c0, c1, c2, c3), ctx)
        res = x[...].astype(F32) + (dot(ctx[...], w_out[...], 0, 1) + b_out[...])
        normed, inv = normalize(res)
        normed_one[...] = normed
        inv_one[...] = inv
        middle = normed * gain[0:1] + shift[0:1]
        mid[...] = middle
        act_one[...] = jnp.clip(middle, -CLIP, CLIP).astype(BF)
        acc[...] = jnp.zeros_like(acc)

    pre = dot(act_one[...], w_up[...], 1, 1) + b_up[...]
    cdf = 0.5 * (1.0 + lax.erf(pre * 0.5**0.5))
    act = (pre * cdf).astype(BF)
    gelu[...] = act
    slope[...] = (cdf + pre * (jnp.exp(pre * pre * -0.5) * 0.3989422804014327)).astype(BF)
    acc[...] += dot(act, w_down[...], 1, 1)

    @pl.when(step == pl.num_programs(0) - 1)
    def _():
        normed, inv = normalize(mid[...] + (acc[...] + b_down[...]))
        normed_two[...] = normed
        inv_two[...] = inv
        result[...] = (normed * gain[1:2] + shift[1:2]).astype(BF)


def ffn_specs(tok, width, hidden):
    up = pl.BlockSpec((FC, width), lambda c, i: (c, 0))
    down = pl.BlockSpec((width, FC), lambda c, i: (0, c))
    wide = pl.BlockSpec((tok, FC), lambda c, i: (0, c))
    row = pl.BlockSpec((1, FC), lambda c, i: (0, c))
    return up, down, wide, row


def student_ffn(pref, pieces, x, w_out, w_up, w_down, b_out, b_up, b_down, gain, shift):
    tok, width = x.shape
    hidden = w_up.shape[0]
    up, down, wide, row = ffn_specs(tok, width, hidden)
    full, one = whole((tok, width)), whole((tok, 1))
    return call(
        student_kernel,
        pref,
        list(pieces) + [x, w_out, w_up, w_down, b_out, b_up, b_down, gain, shift],
        [whole(pieces[0].shape)] * 4
        + [full, whole(w_out.shape), up, down, whole((1, width)), row, whole((1, width))]
        + [whole((2, width))] * 2,
        [
            shape_of((width, tok), BF),
            shape_of((tok, width), BF),
            shape_of((tok, width), F32),
            shape_of((tok, 1), F32),
            shape_of((tok, hidden), BF),
            shape_of((tok, hidden), BF),
            shape_of((tok, width), BF),
            shape_of((tok, width), F32),
            shape_of((tok, 1), F32),
        ],
        [whole((width, tok)), full, full, one, wide, wide, full, full, one],
        (hidden // FC,),
        [pltpu.VMEM((tok, width), F32)] * 2,
        2 * tok * width * (2 * hidden + width),
        2 * tok * hidden,
    )


def teacher_kernel(
    pref, c0, c1, c2, c3, x, w_out, w_up, w_down, gain, shift, normed_two, inv_two,
    grad_sum, grad_ffn, vectors,
    ctx, acc, mid, act_one,
):
    step = pl.program_id(0)

    @pl.when(step == 0)
    def _():
        gather_ctx(pref[0], (c0, c1, c2, c3), ctx)
        res = x[...].astype(F32) + dot(ctx[...], w_out[...], 0, 1)
        normed, inv = normalize(res)
        mid[...] = normed
        act_one[...] = normed.astype(BF)
        acc[...] = jnp.zeros_like(acc)

    pre = dot(act_one[...], w_up[...], 1, 1)
    act = (pre * (0.5 * (1.0 + lax.erf(pre * 0.5**0.5)))).astype(BF)
    acc[...] += dot(act, w_down[...], 1, 1)

    @pl.when(step == pl.num_programs(0) - 1)
    def _():
        target, _unused = normalize(mid[...] + acc[...])
        normed = normed_two[...]
        diff = normed * gain[1:2] + shift[1:2] - target
        back = normalize_back(diff * gain[1:2], normed, inv_two[...])
        grad_sum[...] = back
        low = back.astype(BF)
        grad_ffn[...] = low
        vectors[0:1] = total_rows(diff * normed)
        vectors[1:2] = total_rows(diff)
        vectors[2:3] = total_rows(low.astype(F32))


def teacher_ffn(pref, pieces, x, w_out, w_up, w_down, gain, shift, normed_two, inv_two):
    tok, width = x.shape
    hidden = w_up.shape[0]
    up, down, wide, row = ffn_specs(tok, width, hidden)
    full, one = whole((tok, width)), whole((tok, 1))
    return call(
        teacher_kernel,
        pref,
        list(pieces) + [x, w_out, w_up, w_down, gain, shift, normed_two, inv_two],
        [whole(pieces[0].shape)] * 4
        + [full, whole(w_out.shape), up, down]
        + [whole((2, width))] * 2
        + [full, one],
        [shape_of((tok, width), F32), shape_of((tok, width), BF), shape_of((3, width), F32)],
        [full, full, whole((3, width))],
        (hidden // FC,),
        [pltpu.VMEM((width, tok), BF)]
        + [pltpu.VMEM((tok, width), F32)] * 2
        + [pltpu.VMEM((tok, width), BF)],
        2 * tok * width * (2 * hidden + width),
        tok * hidden,
    )


def back_kernel(
    pref, grad_ffn, slope, w_up, w_down, grad_sum, normed_one, inv_one, gain, shift, w_out,
    grad_hidden, grad_bias, grad_res, grad_attn, g0, g1, g2, g3, vectors,
    acc, ctx,
):
    step = pl.program_id(0)

    @pl.when(step == 0)
    def _():
        acc[...] = jnp.zeros_like(acc)

    low = (dot(grad_ffn[...], w_down[...], 1, 0) * slope[...].astype(F32)).astype(BF)
    grad_hidden[...] = low
    grad_bias[...] = total_rows(low.astype(F32))
    acc[...] += dot(low, w_up[...], 1, 0)

    @pl.when(step == pl.num_programs(0) - 1)
    def _():
        normed = normed_one[...]
        middle = normed * gain[0:1] + shift[0:1]
        grad = grad_sum[...] + jnp.where(jnp.abs(middle) < CLIP, acc[...], 0.0)
        back = normalize_back(grad * gain[0:1], normed, inv_one[...])
        grad_res[...] = back
        attn = back.astype(BF)
        grad_attn[...] = attn
        vectors[0:1] = total_rows(grad * normed)
        vectors[1:2] = total_rows(grad)
        vectors[2:3] = total_rows(attn.astype(F32))
        ctx[...] = dot(w_out[...], attn, 0, 1).astype(BF)
        rows = g0.shape[0]
        for j, ref in enumerate((g0, g1, g2, g3)):
            first = pl.multiple_of(xor(pref[0], j) * rows, 64)
            ref[...] = ctx[pl.ds(first, rows), :]


def student_back(pref, grad_ffn, slope, w_up, w_down, grad_sum, normed_one, inv_one, gain, shift, w_out):
    tok, width = grad_ffn.shape
    hidden = w_up.shape[0]
    up, down, wide, row = ffn_specs(tok, width, hidden)
    full, one = whole((tok, width)), whole((tok, 1))
    return call(
        back_kernel,
        pref,
        [grad_ffn, slope, w_up, w_down, grad_sum, normed_one, inv_one, gain, shift, w_out],
        [full, wide, up, down, full, full, one] + [whole((2, width))] * 2 + [whole(w_out.shape)],
        [
            shape_of((tok, hidden), BF),
            shape_of((1, hidden), F32),
            shape_of((tok, width), F32),
            shape_of((tok, width), BF),
        ]
        + [shape_of((width // 4, tok), BF)] * 4
        + [shape_of((3, width), F32)],
        [wide, row, full, full] + [whole((width // 4, tok))] * 4 + [whole((3, width))],
        (hidden // FC,),
        [pltpu.VMEM((tok, width), F32), pltpu.VMEM((width, tok), BF)],
        2 * tok * width * (2 * hidden + width),
    )


def weight_grad_kernel(
    pref, grad_ffn, gelu, grad_hidden, act_one, grad_attn, ctx, grad_down, grad_up, grad_out, turned
):
    @pl.when(pl.program_id(0) == 0)
    def _():
        turned[...] = grad_ffn[...].T
        value = dot(grad_attn[...], ctx[...], 0, 1).astype(BF)
        grad_out[...] = value.reshape(grad_out.shape)

    value = dot(turned[...], gelu[...], 1, 0).astype(BF)
    grad_down[...] = value.reshape(grad_down.shape)
    value = dot(grad_hidden[...], act_one[...], 0, 0).astype(BF)
    grad_up[...] = value.reshape(grad_up.shape)


def weight_grads(pref, grad_ffn, gelu, grad_hidden, act_one, grad_attn, ctx):
    tok, width = grad_ffn.shape
    hidden = gelu.shape[1]
    count, half = hidden // width, width // 2
    wide = pl.BlockSpec((tok, width), lambda c, i: (0, c))
    full = whole((tok, width))
    return call(
        weight_grad_kernel,
        pref,
        [grad_ffn, gelu, grad_hidden, act_one, grad_attn, ctx],
        [full, wide, wide, full, full, whole((width, tok))],
        [
            shape_of((2, count, half, width), BF),
            shape_of((2 * count, half, width), BF),
            shape_of((2, half, width), BF),
        ],
        [
            pl.BlockSpec((2, 1, half, width), lambda c, i: (0, c, 0, 0)),
            pl.BlockSpec((2, half, width), lambda c, i: (c, 0, 0)),
            whole((2, half, width)),
        ],
        (count,),
        [pltpu.VMEM((width, tok), BF)],
        2 * tok * width * (2 * hidden + width),
    )


def qkv_grad_kernel(pref, d0, d1, d2, d3, x0, x1, x2, x3, out, sums):
    own = pref[0]
    total = None
    count = None
    ones = jnp.ones((8, d0.shape[1]), BF)
    for grad, x in zip((d0, d1, d2, d3), (x0, x1, x2, x3)):
        value = grad[...]
        part = dot(value, jnp.clip(x[...], -CLIP, CLIP), 1, 0)
        line = dot(ones, value, 1, 1)
        total = part if total is None else total + part
        count = line if count is None else count + line
    out[...] = total.astype(BF)
    sums[...] = jnp.zeros_like(sums)
    rows = out.shape[0]
    for j in range(4):

        @pl.when(own == j)
        def _():
            sums[:, j * rows : (j + 1) * rows] = count


def qkv_grad(pref, grads, slots):
    tok, width = slots[0].shape
    rows = grads[0].shape[1]
    return call(
        qkv_grad_kernel,
        pref,
        list(grads) + list(slots),
        [pl.BlockSpec((None, rows, tok), lambda o, i: (o, 0, 0))] * 4 + [whole((tok, width))] * 4,
        [shape_of((3, rows, width), BF), shape_of((3, 8, width), F32)],
        [
            pl.BlockSpec((None, rows, width), lambda o, i: (o, 0, 0)),
            pl.BlockSpec((None, 8, width), lambda o, i: (o, 0, 0)),
        ],
        (3,),
        [],
        2 * 4 * tok * width * 3 * rows,
    )


def input_grad_kernel(pref, e0, e1, e2, e3, wq, wk, wv, grad_res, x, out, acc):
    slot = pl.program_id(0)

    @pl.when(slot == 0)
    def _():
        acc[...] = jnp.zeros_like(acc)

    for j, ref in enumerate((e0, e1, e2, e3)):

        @pl.when(slot == j)
        def _():
            part = dot(ref[0], wq[...], 0, 0)
            part = part + dot(ref[1], wk[...], 0, 0)
            acc[...] += part + dot(ref[2], wv[...], 0, 0)

    @pl.when(slot == 3)
    def _():
        size = jnp.abs(x[...].astype(F32))
        pull = jnp.where(size < CLIP, 1.0, jnp.where(size == CLIP, 0.5, 0.0))
        out[...] = (grad_res[...] + acc[...] * pull).astype(BF)


def input_grad(pref, pieces, weight, grad_res, x):
    tok, width = x.shape
    rows = pieces[0].shape[1]
    full = whole((tok, width))
    return call(
        input_grad_kernel,
        pref,
        list(pieces) + [weight] * 3 + [grad_res, x],
        [whole((3, rows, tok))] * 4
        + [
            pl.BlockSpec((rows, width), lambda j, i, o=o: (o * 4 + lax.bitwise_xor(i[0], j), 0))
            for o in range(3)
        ]
        + [full, full],
        shape_of((tok, width), BF),
        full,
        (4,),
        [pltpu.VMEM((tok, width), F32)],
        2 * 4 * tok * width * 3 * rows,
    )


def place(bit):
    name, mask = bit
    at = lax.axis_index(name)
    upper = lax.rem(lax.div(at, jnp.int32(mask)), jnp.int32(2))
    return upper, {name: at + mask * (1 - 2 * upper)}


class Copies:
    def __init__(self, send, recv, local):
        self.send, self.recv, self.local_sem = send, recv, local
        self.sent, self.planned, self.kept = [], 0, 0

    def plan(self, source, target, device):
        n = self.planned
        self.planned += 1
        return pltpu.make_async_remote_copy(
            src_ref=source,
            dst_ref=target,
            send_sem=self.send.at[n],
            recv_sem=self.recv.at[n],
            device_id=device,
            device_id_type=pl.DeviceIdType.MESH,
        )

    def remote(self, source, target, device):
        copy = self.plan(source, target, device)
        copy.start()
        self.sent.append(copy)
        return copy

    def plan_local(self, source, target):
        self.kept += 1
        return pltpu.make_async_copy(source, target, self.local_sem.at[self.kept - 1])

    def local(self, source, target):
        copy = self.plan_local(source, target)
        copy.start()
        return copy

    def finish(self):
        for copy in self.sent:
            copy.wait_send()


def window(ref, region):
    row, rows, col, cols = region
    return ref.at[pl.ds(row, rows), pl.ds(col, cols)]


def add_window(target, left, right, region, start):
    row, rows, col, cols = region
    step = 48 if rows % 48 == 0 else 16

    def body(i, carry):
        there = pl.ds(pl.multiple_of(row + i * step, 16), step)
        here = pl.ds(pl.multiple_of(start + i * step, 16), step)
        target[there, pl.ds(col, cols)] = left[there, pl.ds(col, cols)] + right[here, :cols]
        return carry

    lax.fori_loop(0, rows // step, body, 0)


def scatter_sum(copies, work, far, full, bits):
    rows, cols = work.shape
    region, used, parts = (0, rows, 0, cols), 0, []
    for n, bit in enumerate(bits):
        upper, device = place(bit)
        row, rows, col, cols = region
        if (rows // 2) % 16 == 0:
            rows //= 2
            kept = (pl.multiple_of(row + upper * rows, 16), rows, col, cols)
            sent = (pl.multiple_of(row + (1 - upper) * rows, 16), rows, col, cols)
        else:
            cols //= 2
            kept = (row, rows, pl.multiple_of(col + upper * cols, 128), cols)
            sent = (row, rows, pl.multiple_of(col + (1 - upper) * cols, 128), cols)
        slot = far.at[pl.ds(used, rows), pl.ds(0, cols)]
        copy = copies.remote(window(work, sent), slot, device)
        yield
        copy.wait_recv()
        add_window(full if n == len(bits) - 1 else work, work, far, kept, used)
        used += rows
        region = kept
        parts.append((bit, kept))
    return parts


def sum_flow(copies, own, other, work, near, far, full, result, core, bits):
    copy = copies.remote(other, near, place(core)[1])
    load = copies.local(own, work)
    yield
    copy.wait_recv()
    load.wait()
    add_window(work, work, near, (0, work.shape[0], 0, work.shape[1]), 0)
    parts = yield from scatter_sum(copies, work, far, full, bits)
    for bit, kept in reversed(parts):
        copy = copies.remote(window(full, kept), window(full, kept), place(bit)[1])
        yield
        copy.wait_recv()
    store = copies.local(full, result)
    yield
    store.wait()


def vector_flow(copies, sums, far, bits):
    for n, bit in enumerate(bits):
        yield
        copy = copies.remote(sums.at[n], far.at[n], place(bit)[1])
        yield
        copy.wait_recv()
        sums[n + 1] = sums[n] + far[n]


def remote_call(kernel, args, in_specs, outs, out_specs, scratch, copies, local, number, limit=VMEM_LIMIT):
    sems = pltpu.SemaphoreType.DMA
    return pl.pallas_call(
        kernel,
        in_specs=in_specs,
        out_specs=out_specs,
        out_shape=outs,
        scratch_shapes=scratch + [sems((copies,)), sems((copies,)), sems((local,))],
        compiler_params=pltpu.CompilerParams(
            vmem_limit_bytes=limit, collective_id=number, has_side_effects=True
        ),
        cost_estimate=pl.CostEstimate(flops=5 * 10**10, bytes_accessed=10**8, transcendentals=0),
    )(*args)


ANY = pl.BlockSpec(memory_space=pl.ANY)
IN_VMEM = pl.BlockSpec(memory_space=pltpu.VMEM)


def binarize_rows(source, target):
    rows, cols = target.shape
    step = 96 if cols < 2048 else 32

    def body(i, carry):
        at = pl.ds(pl.multiple_of(i * step, 16), step)
        value = source[at, :]
        scale = jnp.sum(jnp.abs(value), axis=1, keepdims=True) * (1.0 / cols)
        signed = jnp.where(value > 0, scale, jnp.where(value < 0, -scale, 0.0))
        target[at, :] = signed.astype(BF)
        return carry

    lax.fori_loop(0, rows // step, body, 0)


def entry_kernel(
    seq, core, hidden, teach, segments, l_qkv, l_out, l_up, l_down, t_qkv, t_out, t_up, t_down, bias,
    o_pref, o_qkv, x0, x1, x2, x3, o_teach, b_qkv, b_out, b_up, b_down, e_qkv, e_out, e_up, e_down,
    xs, held, w_qkv, w_out, w_up, w_down, f_qkv, f_out, f_up, f_down,
    s_qkv, s_out, s_up, s_down, proj, others, send, recv, local,
):
    tok, width = hidden.shape
    parts, size = 4, tok // 4
    along, next_chip = place(seq[0])
    side_of, sibling = place(core)
    half = lax.div(lax.axis_index("seq"), jnp.int32(2))
    stays = half == side_of
    moves = half != side_of
    partner = {"seq": 2 * side_of + along, "fsdp": half}
    mesh = pl.DeviceIdType.MESH

    barrier = pltpu.get_barrier_semaphore()
    for device in (next_chip, sibling):
        pl.semaphore_signal(barrier, inc=1, device_id=device, device_id_type=mesh)

    @pl.when(moves)
    def _():
        pl.semaphore_signal(barrier, inc=1, device_id=partner, device_id_type=mesh)
        pl.semaphore_wait(barrier, 3)

    @pl.when(stays)
    def _():
        pl.semaphore_wait(barrier, 2)

    copies = Copies(send, recv, local)
    cuts = [pl.ds(c * size, size) for c in range(parts)]
    swap = [copies.plan(hidden.at[cut], xs.at[0, cut], partner) for cut in cuts]
    load = [copies.plan_local(hidden.at[cut], xs.at[0, cut]) for cut in cuts]
    over = [copies.plan(xs.at[0, cut], xs.at[1, cut], next_chip) for cut in cuts]
    beside = [copies.plan(xs.at[0, cut], xs.at[2, cut], sibling) for cut in cuts]
    relay = [copies.plan(xs.at[1, cut], xs.at[3, cut], sibling) for cut in cuts]
    t_swap = copies.plan(teach, held, partner)
    t_load = copies.plan_local(teach, held)
    seg_copy = copies.remote(segments, others, sibling)

    @pl.when(moves)
    def _():
        for copy in swap:
            copy.start()

    @pl.when(stays)
    def _():
        for copy in load:
            copy.start()
        t_load.start()

    latent = [
        (copies.local(source, target), target)
        for source, target in ((l_qkv, f_qkv), (l_out, f_out), (l_up, f_up), (l_down, f_down))
    ]
    staged = [
        (copies.local(source, target), target, result)
        for source, target, result in (
            (t_qkv, s_qkv, e_qkv),
            (t_out, s_out, e_out),
            (t_up, s_up, e_up),
            (t_down, s_down, e_down),
        )
    ]

    @pl.when(stays)
    def _():
        for c in range(parts):
            load[c].wait()
            over[c].start()
            beside[c].start()

    rows_qkv = l_qkv.shape[0]
    mine = w_qkv.at[pl.ds(pl.multiple_of(side_of * rows_qkv, 16), rows_qkv)]
    latent[0][0].wait()
    binarize_rows(f_qkv, mine)
    qkv_copy = copies.remote(mine, mine, sibling)
    stores, arrivals = [], []
    for (copy, source), target, result in zip(
        latent[1:], (w_out, w_up, w_down), (b_out, b_up, b_down)
    ):
        copy.wait()
        binarize_rows(source, target)
        arrivals.append(copies.remote(target, result.at[side_of], sibling))
        stores.append(copies.local(target, result.at[side_of]))
    for source, (_, _, result) in zip((t_qkv, t_out, t_up, t_down), staged):
        arrivals.append(copies.remote(source, result.at[side_of], sibling))
    for copy, target, result in staged:
        copy.wait()
        stores.append(copies.local(target, result.at[side_of]))

    @pl.when(moves)
    def _():
        for c in range(parts):
            swap[c].wait_recv()
            over[c].start()
            beside[c].start()
        t_swap.start()

    qkv_copy.wait_recv()
    stores.append(copies.local(w_qkv, b_qkv))
    rows = width // 4
    own = along + 2 * side_of

    row = lax.broadcasted_iota(jnp.int32, (AUG, tok), 0)
    ones = jnp.where(row < 3, 1.0, 0.0).astype(BF)
    shifts = []
    for part in range(2):
        line = bias[part : part + 1, 0:rows]
        for j in range(1, 4):
            line = jnp.where(own == j, bias[part : part + 1, j * rows : (j + 1) * rows], line)
        shifts.append(dot(thirds(line), ones, 0, 0))

    def project(slot):
        act = jnp.clip(xs[slot], -CLIP, CLIP)
        first = (1 - along if slot % 2 else along) + 2 * (1 - side_of if slot // 2 else side_of)
        there = pl.ds(pl.multiple_of(first * tok, 128), tok)
        for part in range(3):
            at = pl.multiple_of(part * width + own * rows, 16)
            value = dot(w_qkv[pl.ds(at, rows), :], act, 1, 1)
            if part != 1:
                value = value + shifts[part // 2]
            proj[part * rows : (part + 1) * rows, there] = value.astype(BF)
        stores.append(copies.local(proj.at[:, there], o_qkv.at[:, there]))
        stores.append(copies.local(xs.at[slot], (x0, x1, x2, x3)[slot]))

    seg_copy.wait_recv()
    counts = [jnp.sum(jnp.where(segments[...] == k, 1.0, 0.0)) for k in (1, 2, 3)]
    theirs = [jnp.sum(jnp.where(others[...] == k, 1.0, 0.0)) for k in (1, 2, 3)]
    first, second, third = [
        jnp.where(stays, a, b).astype(jnp.int32) for a, b in zip(counts, theirs)
    ]
    o_pref[0] = own
    o_pref[1] = jnp.where(first == LONG, 0, jnp.where(second == LONG, first, first + second))
    o_pref[2] = jnp.where(first == LONG, second, jnp.where(second == LONG, third, first))

    project(0)
    for copy in beside:
        copy.wait_recv()
    project(2)
    for c in range(parts):
        over[c].wait_recv()
        relay[c].start()
    project(1)
    for copy in relay:
        copy.wait_recv()
    project(3)

    @pl.when(moves)
    def _():
        t_swap.wait_recv()

    @pl.when(stays)
    def _():
        t_load.wait()

    stores.append(copies.local(held, o_teach))
    for copy in arrivals:
        copy.wait_recv()
    for copy in stores:
        copy.wait()

    @pl.when(moves)
    def _():
        for copy in swap + [t_swap]:
            copy.wait_send()

    for copy in over + beside + relay:
        copy.wait_send()
    copies.finish()


def entry(seq, core, hidden, teach, segments, latents, teachers, bias):
    tok, width = hidden.shape
    halves = [w.shape for w in latents]
    sides = [shape_of((2,) + shape, BF) for shape in halves]
    own = [pltpu.VMEM(shape, BF) for shape in halves]
    sides[0] = shape_of((2 * halves[0][0], halves[0][1]), BF)
    sides_t = [shape_of((2,) + shape, BF) for shape in halves]
    outs = remote_call(
        lambda *refs: entry_kernel(seq, core, *refs),
        [hidden, teach, segments] + list(latents) + list(teachers) + [bias],
        [ANY] * 2 + [IN_VMEM] + [ANY] * 8 + [IN_VMEM],
        [shape_of((3,), jnp.int32), shape_of((3 * width // 4, 4 * tok), BF)]
        + [shape_of((tok, width), BF)] * 5
        + sides
        + sides_t,
        [pl.BlockSpec(memory_space=pltpu.SMEM)] + [ANY] * 14,
        [pltpu.VMEM((4, tok, width), BF), pltpu.VMEM((tok, width), BF)]
        + [pltpu.VMEM(sides[0].shape, BF)]
        + own[1:]
        + [pltpu.VMEM(shape, F32) for shape in halves]
        + own
        + [pltpu.VMEM((3 * width // 4, 4 * tok), BF), pltpu.VMEM(segments.shape, jnp.int32)],
        26,
        30,
        3,
    )
    pref, qkv, x0, x1, x2, x3, teach = outs[:7]
    weights = [w.reshape((-1, w.shape[-1])) for w in outs[7:]]
    return pref, qkv, (x0, x1, x2, x3), teach, weights[:4], weights[4:]


class Pump:
    def __init__(self):
        self.events, self.added = [], 0

    def add(self, time, flow, first, then, turn):
        gap = next(flow)
        self.events.append([time + (gap or 0.0), self.added, flow, 0, (first, then, turn)])
        self.added += 1

    def run(self, time=1e9):
        while self.events:
            event = min(self.events, key=lambda e: e[:2])
            if event[0] > time:
                return
            try:
                gap = next(event[2])
            except StopIteration:
                self.events.remove(event)
                continue
            event[3] += 1
            first, then, turn = event[4]
            if gap is None:
                gap = first if event[3] <= turn else then
            event[0] += gap


def head_flow(copies, n, gh, work, far, full, result, seq, core, dp):
    side_of, partner = place(core)
    along = place(seq[0])[0]
    if n == 1:
        copy = copies.remote(gh.at[2 - 2 * side_of], work, partner)
        yield
        copy.wait_recv()
    else:
        load = copies.local(gh.at[n // 2 + side_of], work)
        yield
        load.wait()
    turned, cut = HEAD_PLAN[n][:2]
    bits = (dp[::-1] if turned else dp) + seq[1:]
    mine = full.at[2 * n + along]
    parts = yield from scatter_sum(copies, work, far, mine, bits)
    steps = [(bit, kept, False) for bit, kept in reversed(parts)]
    cut = min(cut, len(steps))
    held = steps[cut][1] if cut < len(steps) else (0, mine.shape[0], 0, mine.shape[1])
    steps = steps[:cut] + [(seq[0], held, False)] + [(b, k, True) for b, k, _ in steps[cut:]]
    for bit, (row, size, col, cols), both in steps:
        first, count = (2 * n, 2) if both else (2 * n + along, 1)
        part = full.at[pl.ds(first, count), pl.ds(row, size), pl.ds(col, cols)]
        copy = copies.remote(part, part, place(bit)[1])
        yield
        copy.wait_recv()
    store = copies.local(full.at[pl.ds(2 * n, 2)], result.at[pl.ds(2 * n, 2)])
    yield
    store.wait()


def tail_kernel(
    dp, seq, core, scale, pref, down, up, out, two, one, bias,
    q_in, k_in, v_in, g0, g1, g2, g3, cf_in, lse, x0, x1, x2, x3, w_in, res_in,
    down_sum, up_sum, out_sum, totals, qkv_sum, hidden_out,
    work, near, far, full, sums, sums_far, gh, h_work, h_far, h_full,
    qs, ks, vs, gp, cf, xs, weight, res, qa, ka, va, ga, gs, dqs, dks, dvs, dn, er, acc, hid,
    send, recv, local,
):
    shift, border = pref[1], pref[2]
    heads_all, total = qs.shape
    hdim = qa.shape[0] - AUG
    heads = heads_all // hdim
    tok = total // 4
    width = xs.shape[2]
    cont, others = total - PROMPT, PROMPT + LONG
    back = lax.rem(cont - shift, cont)
    along, next_chip = place(seq[0])
    side_of, sibling = place(core)
    across = {**next_chip, **sibling}
    half = lax.div(lax.axis_index("seq"), jnp.int32(2))
    stays, moves = half == side_of, half != side_of
    partner = {"seq": 2 * side_of + along, "fsdp": half}
    own = along + 2 * side_of

    def place_of(slot):
        return (1 - along if slot % 2 else along) + 2 * (1 - side_of if slot // 2 else side_of)

    copies = Copies(send, recv, local)
    first_loads = [
        copies.local(source, target)
        for source, target in (
            (g0, gp.at[0]), (g1, gp.at[1]), (g2, gp.at[2]), (g3, gp.at[3]),
            (q_in, qs), (k_in, ks), (v_in, vs), (cf_in, cf),
        )
    ]

    mesh = pl.DeviceIdType.MESH
    barrier = pltpu.get_barrier_semaphore()
    friends = [place(bit)[1] for bit in dp + seq] + [sibling, across]
    for device in friends:
        pl.semaphore_signal(barrier, inc=1, device_id=device, device_id_type=mesh)

    @pl.when(moves)
    def _():
        pl.semaphore_signal(barrier, inc=1, device_id=partner, device_id_type=mesh)
        pl.semaphore_wait(barrier, len(friends) + 1)

    @pl.when(stays)
    def _():
        pl.semaphore_wait(barrier, len(friends))

    pump = Pump()
    count, rows_half = down.shape[1:3]
    ups = [(up.at[side_of, p], up.at[1 - side_of, p], up_sum.at[p]) for p in range(count)]
    downs = [
        (
            down.at[side_of, p],
            down.at[1 - side_of, p],
            down_sum.at[:, pl.ds(p * width, width)],
        )
        for p in range(count)
    ]
    queue = ups + downs + [(out.at[side_of], out.at[1 - side_of], out_sum)]
    near_bits = dp + seq[:1]
    orders = [tuple(near_bits[i] for i in order) for order in ORDERS]
    for n, (mine, theirs, result) in enumerate(queue):
        order, time, first, then = PIECE_PLAN[n % len(PIECE_PLAN)]
        bits = list(orders[order]) + seq[1:]
        flow = sum_flow(
            copies, mine, theirs, work.at[n], near.at[n], far.at[n], full.at[n], result, core, bits
        )
        pump.add(time, flow, first, then, 1 + len(bits))

    late_loads = [
        copies.local(source, target)
        for source, target in (
            (x0, xs.at[0]), (x1, xs.at[1]), (x2, xs.at[2]), (x3, xs.at[3]),
            (w_in, weight), (res_in, res),
        )
    ]
    for copy in first_loads:
        copy.wait()

    row = lax.broadcasted_iota(jnp.int32, (AUG, total), 0)
    ones = jnp.where(row < 3, 1.0, 0.0).astype(BF)
    ka[hdim:, :] = ones
    va[hdim:, :] = ones
    clock = 1.0
    pieces = {1: [], 2: [], 3: []}
    devices = {1: next_chip, 2: sibling, 3: across}
    for h in range(heads):
        lines = slice(h * hdim, (h + 1) * hdim)
        for j in range(4):
            gs[:, pl.ds(pl.multiple_of(place_of(j) * tok, 128), tok)] = gp[j, lines, :].astype(F32)
        qa[:hdim, :] = qs[lines, :]
        ka[:hdim, :] = ks[lines, :]
        va[:hdim, :] = vs[lines, :]
        grad = roll_cont(gs[...], back)
        ga[:hdim, :] = grad.astype(BF)
        ga[hdim:, :] = thirds(-jnp.sum(grad * cf[lines, :], axis=0, keepdims=True))
        qa[hdim:, :] = thirds(lse[h] * (-1.0 / scale))
        seen = set()
        for start, parts in block_list(total, QB):
            queries = slice(start, start + QB)
            grad_q = None
            for lo, hi in parts:
                for key in range(lo, hi, KB):
                    keys = slice(key, key + KB)
                    value = dot(qa[:, queries], ka[:, keys], 0, 0) * scale
                    if lo >= others:
                        mask = same_segment((QB, KB), 1, key - others, start - others, border)
                        value = jnp.where(mask, value, -1e30)
                    prob = jnp.exp2(value)
                    grad_p = dot(ga[:, queries], va[:, keys], 0, 0)
                    grad_s = (prob * grad_p).astype(BF)
                    grad_v = dot(ga[:hdim, queries], prob.astype(BF), 1, 0)
                    grad_k = dot(qa[:hdim, queries], grad_s, 1, 0)
                    part = dot(ka[:hdim, keys], grad_s, 1, 1)
                    grad_q = part if grad_q is None else grad_q + part
                    if key in seen:
                        dvs[:, keys] += grad_v
                        dks[:, keys] += grad_k
                    else:
                        dvs[:, keys] = grad_v
                        dks[:, keys] = grad_k
                        seen.add(key)
                    clock += 0.65
            dqs[:, queries] = grad_q
            pump.run(clock)
        inv = 1.0 / hdim**0.5
        for part, (ref, factor) in enumerate(((dqs, inv), (dks, inv), (dvs, 1.0))):
            gs[...] = roll_cont(ref[...] * factor, shift)
            for j in range(4):
                there = pl.ds(pl.multiple_of(place_of(j) * tok, 128), tok)
                dn[j, part, lines, :] = gs[:, there].astype(BF)
        for j in (1, 3, 2):
            at = pl.ds(h * hdim, hdim)
            copy = copies.remote(dn.at[j, :, at, :], er.at[j - 1, :, at, :], devices[j])
            pieces[j].append(copy)
        clock += 1.5
        pump.run(clock)

    for copy in late_loads:
        copy.wait()
    rows = width // 4
    one_rows = jnp.ones((8, tok), BF)
    counts = []
    for o in range(3):
        value, line = None, None
        for j in range(4):
            part = dot(dn[j, o], jnp.clip(xs[j], -CLIP, CLIP), 1, 0)
            ends = dot(one_rows, dn[j, o], 1, 1)
            value = part if value is None else value + part
            line = ends if line is None else line + ends
        gh[o] = value.astype(BF)
        counts.append(line)
        clock += 2.7
        pump.run(clock)
    sums[0] = jnp.zeros(sums.shape[1:], F32)
    for j in range(4):

        @pl.when(own == j)
        def _():
            sums[0, 0:1, j * rows : (j + 1) * rows] = counts[0][0:1]
            sums[0, 1:2, j * rows : (j + 1) * rows] = counts[2][0:1]

    sums[0, 2:3] = one[2:3]
    sums[0, 3:4] = two[2:3]
    sums[0, 4:5] = one[0:1]
    sums[0, 5:6] = two[0:1]
    sums[0, 6:7] = one[1:2]
    sums[0, 7:8] = two[1:2]
    for p in range(count):
        sums[0, 8 + p : 9 + p] = bias[:, p * width : (p + 1) * width]

    swap = copies.plan(hid, hidden_out, partner)
    keep = copies.plan_local(hid, hidden_out)

    def hidden_flow():
        yield 0.0
        gaps = HIDDEN_PLAN[1]
        for gap, j in zip(gaps, (0, 2, 1, 3)):
            for copy in pieces.get(j, []):
                copy.wait_recv()
            part = None
            for o in range(3):
                at = pl.multiple_of(o * width + place_of(j) * rows, 16)
                source = dn[0, o] if j == 0 else er[j - 1, o]
                piece = dot(source, weight[pl.ds(at, rows), :], 0, 0)
                part = piece if part is None else part + piece
            if j == 0:
                acc[...] = part
            elif j != 3:
                acc[...] += part
            else:
                size = jnp.abs(xs[0].astype(F32))
                pull = jnp.where(size < CLIP, 1.0, jnp.where(size == CLIP, 0.5, 0.0))
                hid[...] = (res[...] + (acc[...] + part) * pull).astype(BF)
            if j != 3:
                yield gap

        @pl.when(moves)
        def _():
            swap.start()

        @pl.when(stays)
        def _():
            keep.start()

        yield gaps[3]

        @pl.when(moves)
        def _():
            swap.wait_recv()
            swap.wait_send()

        @pl.when(stays)
        def _():
            keep.wait()

    pump.add(clock + HIDDEN_PLAN[0], hidden_flow(), 0.0, 0.0, 0)
    for n in (0, 2, 1):
        flow = head_flow(
            copies, n, gh, h_work.at[n], h_far.at[n], h_full, qkv_sum, seq, core, dp
        )
        time, first, then = HEAD_PLAN[n][2:]
        pump.add(clock + time, flow, first, then, 4)
    time, gap = VECTOR_PLAN
    pump.add(clock + time, vector_flow(copies, sums, sums_far, [core] + dp + seq), gap, gap, 0)
    pump.run()
    totals[...] = sums[sums.shape[0] - 1]
    copies.finish()


def tail(
    dp, seq, core, pref, down, up, out, two, one, bias, rolled, grads, cf, lse, slots, weight, res
):
    sides, count, half, width = down.shape
    pieces, steps, lines = 2 * count + 1, len(dp) + len(seq), 16
    rows, total = rolled[0].shape
    tok = total // 4
    heads = HEADS // 4
    hdim = rows // heads
    scale = LOG2E / hdim**0.5
    smem = pl.BlockSpec(memory_space=pltpu.SMEM)
    return remote_call(
        lambda *refs: tail_kernel(dp, seq, core, scale, *refs),
        [pref, down, up, out, two, one, bias]
        + list(rolled)
        + list(grads)
        + [cf, lse]
        + list(slots)
        + [weight, res],
        [smem] + [ANY] * 3 + [IN_VMEM] * 3 + [ANY] * 8 + [IN_VMEM] + [ANY] * 6,
        [
            shape_of((half, count * width), BF),
            shape_of((count, half, width), BF),
            shape_of((half, width), BF),
            shape_of((lines, width), F32),
            shape_of((6, rows, width), BF),
            shape_of((tok, width), BF),
        ],
        [ANY] * 3 + [IN_VMEM] + [ANY] * 2,
        [pltpu.VMEM((pieces, half, width), BF)] * 4
        + [pltpu.VMEM((steps + 2, lines, width), F32), pltpu.VMEM((steps + 1, lines, width), F32)]
        + [pltpu.VMEM((3, rows, width), BF)] * 3
        + [pltpu.VMEM((6, rows, width), BF)]
        + [pltpu.VMEM((rows, total), BF)] * 3
        + [pltpu.VMEM((4, rows, tok), BF), pltpu.VMEM((rows, total), F32)]
        + [pltpu.VMEM((4, tok, width), BF), pltpu.VMEM(weight.shape, BF)]
        + [pltpu.VMEM((tok, width), F32)]
        + [pltpu.VMEM((hdim + AUG, total), BF)] * 4
        + [pltpu.VMEM((hdim, total), F32)] * 4
        + [pltpu.VMEM((4, 3, rows, tok), BF), pltpu.VMEM((3, 3, rows, tok), BF)]
        + [pltpu.VMEM((tok, width), F32), pltpu.VMEM((tok, width), BF)],
        pieces * (1 + 2 * steps) + steps + 1 + 3 * heads + 1 + 3 * (2 * steps - 1) + 1,
        2 * pieces + 14 + 1 + 5,
        4,
        TAIL_LIMIT,
    )


def widen_kernel(*refs):
    half = len(refs) // 2
    for source, target in zip(refs[:half], refs[half:]):
        target[...] = source[...].astype(F32)


def widen(values, steps):
    specs = [pl.BlockSpec((v.shape[0] // steps, v.shape[1]), lambda i: (i, 0)) for v in values]
    return pl.pallas_call(
        widen_kernel,
        grid=(steps,),
        in_specs=specs,
        out_specs=specs,
        out_shape=[shape_of(v.shape, F32) for v in values],
        compiler_params=pltpu.CompilerParams(vmem_limit_bytes=VMEM_LIMIT),
        cost_estimate=pl.CostEstimate(
            flops=0, bytes_accessed=6 * sum(v.size for v in values), transcendentals=0
        ),
    )(*values)


def binarize(latent):
    row_scale = jnp.mean(jnp.abs(latent), axis=1, keepdims=True)
    return (row_scale * jnp.sign(latent)).astype(BF)


def segment_info(segments):
    sizes_of = [jnp.sum((segments == k).astype(jnp.int32)) for k in (1, 2, 3)]
    first, second, third = sizes_of
    shift = jnp.where(first == LONG, 0, jnp.where(second == LONG, first, first + second))
    border = jnp.where(first == LONG, second, jnp.where(second == LONG, third, first))
    return jnp.stack([shift, border])


def quarters(own):
    along = to_slot(own, 1)
    return (own, along, to_slot(own, 2), to_slot(along, 2))


def exchange(pieces):
    return (pieces[0],) + tuple(to_slot(pieces[j], j) for j in (1, 2, 3))


def on_device(
    hidden, teacher_hidden, segments, latent_qkv, latent_out, latent_up, latent_down,
    biases, up_bias, norm_gains, norm_shifts, teacher_qkv, teacher_out, teacher_up, teacher_down,
):
    seq_at, fsdp_at = lax.axis_index("seq"), lax.axis_index("fsdp")
    fsdp = lax.axis_size("fsdp")
    core = fsdp_at % 2
    own = (seq_at % 2 + 2 * core).astype(jnp.int32)
    width = hidden.shape[2]

    latents = (latent_qkv, latent_out, latent_up, latent_down)
    teachers = (teacher_qkv, teacher_out, teacher_up, teacher_down)
    if fsdp == 2:
        pref, qkv, x_slots, teach, bins, t_weights = entry(
            bit_list("seq"), bit_list("fsdp")[0], hidden[0], teacher_hidden[0], segments,
            latents, teachers, biases,
        )
        x = x_slots[0]
    else:
        info = segment_info(segments)
        info = jnp.where(core == seq_at // 2, info, flip(info, fsdp=1))
        pref = jnp.concatenate([own[None], info]).astype(jnp.int32)
        x = swap_groups(hidden[0])
        x_slots = quarters(x)
        bins = [gather_rows(binarize(w)) for w in latents]
        teach = swap_groups(teacher_hidden[0])
        t_weights = [gather_rows(w) for w in teachers]
        qkv = qkv_project(pref, x_slots, bins[0], biases[:2].reshape(2, width, 1))
    bin_qkv, bin_out, bin_up, bin_down = bins
    t_qkv, t_out, t_up, t_down = t_weights
    t_along, t_beside = to_slot(teach, 1), to_slot(teach, 2)
    *ctx_slots, ctx_full, lse, q_roll, k_roll, v_roll = attention(pref, qkv, True)
    t_along, ctx_slots = lax.optimization_barrier((t_along, ctx_slots))
    t_slots = (teach, t_along, t_beside, to_slot(t_along, 2))
    ctx_pieces = exchange(ctx_slots)

    t_heads = qkv_project(pref, t_slots, t_qkv, None)
    *tctx_slots, _unused, _unused_too = attention(pref, t_heads, False)
    tctx_slots, ctx_pieces = lax.optimization_barrier((tctx_slots, ctx_pieces))
    tctx_pieces = exchange(tctx_slots)

    gain, shift = norm_gains, norm_shifts
    (
        ctx, act_one, normed_one, inv_one, gelu, slope, result, normed_two, inv_two,
    ) = student_ffn(
        pref, ctx_pieces, x, bin_out, bin_up, bin_down,
        biases[2:3], up_bias[None], biases[3:4], gain, shift,
    )
    student_out = swap_groups(result)
    grad_sum, grad_ffn, vec_two = teacher_ffn(
        pref, tctx_pieces, teach, t_out, t_up, t_down, gain, shift, normed_two, inv_two
    )
    grad_hidden, grad_up_bias, grad_res, grad_attn, *gctx_slots, vec_one = student_back(
        pref, grad_ffn, slope, bin_up, bin_down, grad_sum, normed_one, inv_one, gain, shift, bin_out
    )
    gctx_pieces = exchange(gctx_slots)
    grad_down, grad_up, grad_out = weight_grads(
        pref, grad_ffn, gelu, grad_hidden, act_one, grad_attn, ctx
    )
    dp_bits, seq_bits, fsdp_bits = bit_list("dp"), bit_list("seq"), bit_list("fsdp")
    rows, hidden_units = width // 4, up_bias.shape[0]

    if fsdp == 2:
        total_down, total_up, total_out, vectors, total_qkv, hidden_grad = tail(
            dp_bits, seq_bits, fsdp_bits[0], pref,
            grad_down, grad_up.reshape(grad_down.shape), grad_out, vec_two, vec_one, grad_up_bias,
            (q_roll, k_roll, v_roll), gctx_pieces, ctx_full, lse, x_slots, bin_qkv, grad_res,
        )
        total_up = total_up.reshape(-1, width)
        total_qkv = total_qkv.reshape(-1, width)
        total_qkv, total_out, total_up, total_down = widen(
            (total_qkv, total_out, total_up, total_down), 6
        )
    else:
        dqkv_slots = attention_back(pref, qkv, gctx_pieces, ctx_full, lse)
        dqkv_pieces = exchange(dqkv_slots)
        grad_heads, head_sums = qkv_grad(pref, dqkv_slots, x_slots)
        hidden_grad = swap_groups(input_grad(pref, dqkv_pieces, bin_qkv, grad_res, x))

        def reduce_grad(value, bits):
            for bit in reversed(fsdp_bits):
                value = halve(value, bit)
            return all_reduce(value, bits)

        grad_down = grad_down.transpose(0, 2, 1, 3).reshape(width, hidden_units)
        total_down = reduce_grad(grad_down, dp_bits + seq_bits)
        total_up = reduce_grad(grad_up.reshape(hidden_units, width), dp_bits[::-1] + seq_bits)
        total_out = reduce_grad(
            grad_out.reshape(width, width), seq_bits[:1] + dp_bits + seq_bits[1:]
        )
        blocks = all_reduce(
            grad_heads.reshape(3 * rows, width), dp_bits + seq_bits[1:] + fsdp_bits[1:]
        )
        blocks = blocks.reshape(1, 3, rows, width)
        blocks = double(double(blocks, seq_bits[0]), fsdp_bits[0])
        whole_qkv = blocks.transpose(1, 0, 2, 3).reshape(3 * width, width)
        part = 3 * width // fsdp
        total_qkv = lax.dynamic_slice_in_dim(whole_qkv, fsdp_at * part, part, 0)
        vectors = jnp.concatenate(
            [
                head_sums[0, :1],
                head_sums[2, :1],
                vec_one[2:3],
                vec_two[2:3],
                vec_one[0:1],
                vec_two[0:1],
                vec_one[1:2],
                vec_two[1:2],
                grad_up_bias.reshape(-1, width),
            ]
        )
        vectors = sum_small(vectors, dp_bits + seq_bits + fsdp_bits)
    hid_bias = vectors[8 : 8 + hidden_units // width].reshape(-1)
    share, hid_share = width // fsdp, hid_bias.shape[0] // fsdp
    cols = lax.dynamic_slice_in_dim(vectors[:8], fsdp_at * share, share, 1)
    return (
        student_out[None],
        hidden_grad[None],
        total_qkv.astype(F32),
        total_out.astype(F32),
        total_up.astype(F32),
        total_down.astype(F32),
        cols[0:4],
        lax.dynamic_slice_in_dim(hid_bias, fsdp_at * hid_share, hid_share, 0),
        cols[4:6],
        cols[6:8],
    )


def solution(mesh):
    tokens = P(("dp", "fsdp"), "seq", None)
    rows = P("fsdp", None)
    return jax.shard_map(
        on_device,
        mesh=mesh,
        in_specs=(tokens, tokens, P(("dp", "fsdp"), None)) + (rows,) * 4 + (P(),) * 4 + (rows,) * 4,
        out_specs=(tokens, tokens)
        + (rows,) * 4
        + (P(None, "fsdp"), P("fsdp"), P(None, "fsdp"), P(None, "fsdp")),
        check_vma=False,
    )
```

```python
import jax
import jax.numpy as jnp
from jax import lax
from jax.experimental import pallas as pl
from jax.experimental.pallas import tpu as pltpu
from jax.sharding import PartitionSpec as P

HEADS = 12
PROMPT = 1024
LONG = 1024
CLIP = 2.5
EPS = 1e-05
AXES = ("dp", "seq", "fsdp")
BF = jnp.bfloat16
F32 = jnp.float32
LOG2E = 1.4426950408889634
QB = 512
KC = 256
KB = 512
FC = 1024
AUG = 16
VMEM_LIMIT = 56 * 2**20
TAIL_LIMIT = 60 * 2**20
ORDERS = ((0, 1, 2), (1, 0, 2), (0, 2, 1), (1, 2, 0), (2, 0, 1), (2, 1, 0))
PIECE_PLAN = (
    (0, 6.2, 33.2, 64.8),
    (2, 13.6, 75.8, 115.6),
    (1, 87.9, 109.7, 109.9),
    (1, 18.5, 61.3, 92.2),
    (4, 8.4, 94.5, 125.6),
    (0, 9.7, 53.1, 89.3),
    (0, 30.0, 114.5, 110.0),
    (1, 23.6, 99.1, 76.0),
    (1, 15.8, 49.7, 87.1),
)
HEAD_PLAN = (
    (1, 1, 238.2, 90.7, 81.4),
    (0, 3, 170.9, 119.6, 73.4),
    (1, 1, 16.1, 96.9, 77.0),
)
HIDDEN_PLAN = (0.0, (416.8, 50.8, 134.5, 451.6))
VECTOR_PLAN = (75.4, 88.5)


def dot(left, right, left_dim, right_dim):
    return lax.dot_general(
        left, right, (((left_dim,), (right_dim,)), ((), ())), preferred_element_type=F32
    )


def xor(first, second):
    return lax.bitwise_xor(first, jnp.int32(second))


def sizes():
    return tuple(lax.axis_size(name) for name in AXES)


def permute(values, target):
    dp, seq, fsdp = sizes()
    pairs = []
    for d in range(dp):
        for s in range(seq):
            for f in range(fsdp):
                td, ts, tf = target(d, s, f)
                pairs.append(((d * seq + s) * fsdp + f, (td * seq + ts) * fsdp + tf))
    return lax.ppermute(values, AXES, pairs)


def flip(values, dp=0, seq=0, fsdp=0):
    return permute(values, lambda d, s, f: (d ^ dp, s ^ seq, f ^ fsdp))


def swap_groups(values):
    return permute(
        values, lambda d, s, f: (d, 2 * (f % 2) + s % 2, f - f % 2 + s // 2)
    )


def to_slot(values, slot):
    return flip(values, seq=slot & 1, fsdp=slot >> 1)


def bit_list(name):
    count = lax.axis_size(name)
    out, bit = [], 1
    while bit < count:
        out.append((name, bit))
        bit *= 2
    return out


def flip_bit(values, bit):
    return flip(values, **{bit[0]: bit[1]})


def side(bit):
    return lax.bitwise_and(lax.axis_index(bit[0]), bit[1]) != 0


def halve(values, bit):
    upper = side(bit).astype(jnp.int32)
    half = values.shape[0] // 2
    sent = lax.dynamic_slice_in_dim(values, (1 - upper) * half, half, 0)
    kept = lax.dynamic_slice_in_dim(values, upper * half, half, 0)
    got = flip_bit(sent, bit)
    return (kept.astype(F32) + got.astype(F32)).astype(values.dtype)


def double(values, bit):
    got = flip_bit(values, bit)
    return jnp.where(
        side(bit),
        jnp.concatenate([got, values], axis=0),
        jnp.concatenate([values, got], axis=0),
    )


def gather_rows(values):
    for bit in bit_list("fsdp"):
        values = double(values, bit)
    return values


def all_reduce(values, bits):
    for bit in bits:
        values = halve(values, bit)
    for bit in reversed(bits):
        values = double(values, bit)
    return values


def sum_small(values, bits):
    for bit in bits:
        values = values + flip_bit(values, bit)
    return values


def whole(shape):
    return pl.BlockSpec(shape, lambda *_: (0,) * len(shape))


def call(kernel, pref, args, in_specs, outs, out_specs, grid, scratch, flops, trans=0):
    moved = sum(a.size * a.dtype.itemsize for a in args)
    moved += sum(o.size * o.dtype.itemsize for o in jax.tree.leaves(outs))
    return pl.pallas_call(
        kernel,
        grid_spec=pltpu.PrefetchScalarGridSpec(
            num_scalar_prefetch=1,
            grid=grid,
            in_specs=in_specs,
            out_specs=out_specs,
            scratch_shapes=scratch,
        ),
        out_shape=outs,
        compiler_params=pltpu.CompilerParams(vmem_limit_bytes=VMEM_LIMIT),
        cost_estimate=pl.CostEstimate(flops=flops, bytes_accessed=moved, transcendentals=trans),
    )(pref, *args)


def shape_of(shape, dtype):
    return jax.ShapeDtypeStruct(shape, dtype)


def qkv_kernel(student, pref, x0, x1, x2, x3, wq, wk, wv, *rest):
    slot = pl.program_id(0)
    out = rest[-1]
    rows = wq.shape[0]
    for j, ref in enumerate((x0, x1, x2, x3)):

        @pl.when(slot == j)
        def _():
            act = ref[...]
            if student:
                act = jnp.clip(act, -CLIP, CLIP)
            for part, weight in enumerate((wq, wk, wv)):
                value = dot(weight[...], act, 1, 1)
                if student and part != 1:
                    value = value + rest[0][part // 2]
                out[part * rows : (part + 1) * rows, :] = value.astype(BF)


def qkv_project(pref, slots, weight, bias):
    tok, width = slots[0].shape
    rows = weight.shape[0] // 12
    specs = [whole((tok, width))] * 4
    specs += [
        pl.BlockSpec((rows, width), lambda j, i, o=o: (o * 4 + i[0], 0)) for o in range(3)
    ]
    args = list(slots) + [weight] * 3
    if bias is not None:
        specs.append(pl.BlockSpec((2, rows, 1), lambda j, i: (0, i[0], 0)))
        args.append(bias)
    return call(
        lambda *refs: qkv_kernel(bias is not None, *refs),
        pref,
        args,
        specs,
        shape_of((3 * rows, 4 * tok), BF),
        pl.BlockSpec((3 * rows, tok), lambda j, i: (0, lax.bitwise_xor(i[0], j))),
        (4,),
        [],
        2 * 4 * tok * width * 3 * rows,
    )


def roll_cont(values, shift):
    return jnp.concatenate(
        [values[:, :PROMPT], pltpu.roll(values[:, PROMPT:], shift, 1)], axis=1
    )


def block_list(total, rows):
    blocks = [(i, [(0, PROMPT)]) for i in range(0, PROMPT, rows)]
    blocks += [(i, [(0, PROMPT + LONG)]) for i in range(PROMPT, PROMPT + LONG, rows)]
    blocks += [
        (i, [(0, PROMPT), (PROMPT + LONG, total)]) for i in range(PROMPT + LONG, total, rows)
    ]
    return blocks


def same_segment(shape, key_axis, key_start, query_start, border):
    keys = lax.broadcasted_iota(jnp.int32, shape, key_axis) + key_start
    queries = lax.broadcasted_iota(jnp.int32, shape, 1 - key_axis) + query_start
    return (keys < border) == (queries < border)


def attention_kernel(scale, kept, pref, q_ref, k_ref, v_ref, o0, o1, o2, o3, cf_ref, lse_ref, *rest):
    if kept:
        qs, ks, vs, cs, st = rest
    else:
        cs, st, qs, ks, vs = rest
    own, shift, border = pref[0], pref[1], pref[2]
    total = q_ref.shape[1]
    cont = total - PROMPT
    others = PROMPT + LONG
    back = lax.rem(cont - shift, cont)
    qs[...] = roll_cont(q_ref[...].astype(F32), back).astype(BF)
    ks[...] = roll_cont(k_ref[...].astype(F32), back).astype(BF)
    vs[...] = roll_cont(v_ref[...].astype(F32), back).astype(BF)
    blocks = []
    for start, parts in block_list(total, QB):
        chunks = [key for lo, hi in parts for key in range(lo, hi, KC)]
        blocks.append((start, chunks))
    top, acc, norm = {}, {}, {}

    def scores(n, i):
        start, chunks = blocks[n]
        key = chunks[i]
        value = dot(ks[:, key : key + KC], qs[:, start : start + QB], 0, 0) * scale
        if key >= others:
            mask = same_segment((KC, QB), 0, key - others, start - others, border)
            value = jnp.where(mask, value, -1e30)
        st[n % 2, i * KC : (i + 1) * KC, :] = value
        peak = jnp.max(value, axis=0, keepdims=True)
        top[n] = jnp.maximum(top[n], peak) if n in top else peak

    def weigh(n, i):
        key = blocks[n][1][i]
        prob = jnp.exp2(st[n % 2, i * KC : (i + 1) * KC, :] - top[n])
        part = jnp.sum(prob, axis=0, keepdims=True)
        value = dot(vs[:, key : key + KC], prob.astype(BF), 1, 0)
        acc[n] = acc[n] + value if n in acc else value
        norm[n] = norm[n] + part if n in norm else part

    for i in range(len(blocks[0][1])):
        scores(0, i)
    for n, (start, chunks) in enumerate(blocks):
        ahead = len(blocks[n + 1][1]) if n + 1 < len(blocks) else 0
        for i in range(max(len(chunks), ahead)):
            if i < ahead:
                scores(n + 1, i)
            if i < len(chunks):
                weigh(n, i)
        cf_ref[:, start : start + QB] = acc[n] / norm[n]
        lse_ref[:, start : start + QB] = top[n] + jnp.log2(norm[n])
    cs[...] = roll_cont(cf_ref[...], shift).astype(BF)
    tok = total // 4
    for j, out in enumerate((o0, o1, o2, o3)):
        first = pl.multiple_of(xor(own, j) * tok, 128)
        out[...] = cs[:, pl.ds(first, tok)]


def attention(pref, qkv, kept):
    total = qkv.shape[1]
    heads = HEADS // 4
    hdim = qkv.shape[0] // (3 * heads)
    rows = qkv.shape[0] // 3
    scale = LOG2E / hdim**0.5
    return call(
        lambda *refs: attention_kernel(scale, kept, *refs),
        pref,
        [qkv] * 3,
        [pl.BlockSpec((hdim, total), lambda h, i, o=o: (h + o * heads, 0)) for o in range(3)],
        [shape_of((rows, total // 4), BF)] * 4
        + [shape_of((rows, total), F32), shape_of((heads, 1, total), F32)]
        + [shape_of((rows, total), BF)] * (3 if kept else 0),
        [pl.BlockSpec((hdim, total // 4), lambda h, i: (h, 0))] * 4
        + [
            pl.BlockSpec((hdim, total), lambda h, i: (h, 0)),
            pl.BlockSpec((None, 1, total), lambda h, i: (h, 0, 0)),
        ]
        + [pl.BlockSpec((hdim, total), lambda h, i: (h, 0))] * (3 if kept else 0),
        (heads,),
        [pltpu.VMEM((hdim, total), BF), pltpu.VMEM((2, PROMPT + LONG, QB), F32)]
        + [pltpu.VMEM((hdim, total), BF)] * (0 if kept else 3),
        16 * 10**9,
        12 * 10**6,
    )


def thirds(values):
    high = values.astype(BF).astype(F32)
    middle = (values - high).astype(BF).astype(F32)
    low = values - high - middle
    row = lax.broadcasted_iota(jnp.int32, (AUG, values.shape[1]), 0)
    value = jnp.where(row == 0, high, jnp.where(row == 1, middle, jnp.where(row == 2, low, 0.0)))
    return value.astype(BF)


def attention_back_kernel(
    scale, pref, q_ref, k_ref, v_ref, g0, g1, g2, g3, cf_ref, lse_ref,
    d0, d1, d2, d3, qa, ka, va, ga, gs, dqs, dks, dvs,
):
    own, shift, border = pref[0], pref[1], pref[2]
    hdim, total = q_ref.shape
    tok = total // 4
    cont = total - PROMPT
    others = PROMPT + LONG
    back = lax.rem(cont - shift, cont)
    for j, ref in enumerate((g0, g1, g2, g3)):
        first = pl.multiple_of(xor(own, j) * tok, 128)
        gs[:, pl.ds(first, tok)] = ref[...].astype(F32)
    qa[:hdim, :] = roll_cont(q_ref[...].astype(F32), back).astype(BF)
    ka[:hdim, :] = roll_cont(k_ref[...].astype(F32), back).astype(BF)
    va[:hdim, :] = roll_cont(v_ref[...].astype(F32), back).astype(BF)
    grad = roll_cont(gs[...], back)
    ga[:hdim, :] = grad.astype(BF)
    ga[hdim:, :] = thirds(-jnp.sum(grad * cf_ref[...], axis=0, keepdims=True))
    qa[hdim:, :] = thirds(lse_ref[...] * (-1.0 / scale))
    row = lax.broadcasted_iota(jnp.int32, (AUG, total), 0)
    ones = jnp.where(row < 3, 1.0, 0.0).astype(BF)
    ka[hdim:, :] = ones
    va[hdim:, :] = ones
    seen = set()
    for start, parts in block_list(total, QB):
        queries = slice(start, start + QB)
        grad_q = None
        for lo, hi in parts:
            for key in range(lo, hi, KB):
                keys = slice(key, key + KB)
                value = dot(qa[:, queries], ka[:, keys], 0, 0) * scale
                if lo >= others:
                    mask = same_segment((QB, KB), 1, key - others, start - others, border)
                    value = jnp.where(mask, value, -1e30)
                prob = jnp.exp2(value)
                grad_p = dot(ga[:, queries], va[:, keys], 0, 0)
                grad_s = (prob * grad_p).astype(BF)
                grad_v = dot(ga[:hdim, queries], prob.astype(BF), 1, 0)
                grad_k = dot(qa[:hdim, queries], grad_s, 1, 0)
                part = dot(ka[:hdim, keys], grad_s, 1, 1)
                grad_q = part if grad_q is None else grad_q + part
                if key in seen:
                    dvs[:, keys] += grad_v
                    dks[:, keys] += grad_k
                else:
                    dvs[:, keys] = grad_v
                    dks[:, keys] = grad_k
                    seen.add(key)
        dqs[:, queries] = grad_q
    inv = 1.0 / hdim**0.5
    for part, (ref, factor) in enumerate(((dqs, inv), (dks, inv), (dvs, 1.0))):
        gs[...] = roll_cont(ref[...] * factor, shift)
        for j, out in enumerate((d0, d1, d2, d3)):
            first = pl.multiple_of(xor(own, j) * tok, 128)
            out[part] = gs[:, pl.ds(first, tok)].astype(BF)


def attention_back(pref, qkv, grads, ctx, lse):
    total = qkv.shape[1]
    heads = HEADS // 4
    hdim = qkv.shape[0] // (3 * heads)
    rows = qkv.shape[0] // 3
    scale = LOG2E / hdim**0.5
    quarter = pl.BlockSpec((hdim, total // 4), lambda h, i: (h, 0))
    return call(
        lambda *refs: attention_back_kernel(scale, *refs),
        pref,
        [qkv] * 3 + list(grads) + [ctx, lse],
        [pl.BlockSpec((hdim, total), lambda h, i, o=o: (h + o * heads, 0)) for o in range(3)]
        + [quarter] * 4
        + [
            pl.BlockSpec((hdim, total), lambda h, i: (h, 0)),
            pl.BlockSpec((None, 1, total), lambda h, i: (h, 0, 0)),
        ],
        [shape_of((3, rows, total // 4), BF)] * 4,
        [pl.BlockSpec((3, hdim, total // 4), lambda h, i: (0, h, 0))] * 4,
        (heads,),
        [pltpu.VMEM((hdim + AUG, total), BF)] * 4 + [pltpu.VMEM((hdim, total), F32)] * 4,
        30 * 10**9,
        12 * 10**6,
    )


def normalize(values):
    centre = jnp.mean(values, axis=-1, keepdims=True)
    shifted = values - centre
    spread = jnp.mean(shifted * shifted, axis=-1, keepdims=True)
    inv = lax.rsqrt(spread + EPS)
    return shifted * inv, inv


def normalize_back(grad, normed, inv):
    first = jnp.mean(grad, axis=-1, keepdims=True)
    second = jnp.mean(grad * normed, axis=-1, keepdims=True)
    return (grad - first - normed * second) * inv


def total_rows(values):
    return jnp.sum(values, axis=0, keepdims=True)


def gather_ctx(own, pieces, ctx):
    rows = pieces[0].shape[0]
    for j, ref in enumerate(pieces):
        first = pl.multiple_of(xor(own, j) * rows, 64)
        ctx[pl.ds(first, rows), :] = ref[...]


def student_kernel(
    pref, c0, c1, c2, c3, x, w_out, w_up, w_down, b_out, b_up, b_down, gain, shift,
    ctx, act_one, normed_one, inv_one, gelu, slope, result, normed_two, inv_two,
    acc, mid,
):
    step = pl.program_id(0)

    @pl.when(step == 0)
    def _():
        gather_ctx(pref[0], (c0, c1, c2, c3), ctx)
        res = x[...].astype(F32) + (dot(ctx[...], w_out[...], 0, 1) + b_out[...])
        normed, inv = normalize(res)
        normed_one[...] = normed
        inv_one[...] = inv
        middle = normed * gain[0:1] + shift[0:1]
        mid[...] = middle
        act_one[...] = jnp.clip(middle, -CLIP, CLIP).astype(BF)
        acc[...] = jnp.zeros_like(acc)

    pre = dot(act_one[...], w_up[...], 1, 1) + b_up[...]
    cdf = 0.5 * (1.0 + lax.erf(pre * 0.5**0.5))
    act = (pre * cdf).astype(BF)
    gelu[...] = act
    slope[...] = (cdf + pre * (jnp.exp(pre * pre * -0.5) * 0.3989422804014327)).astype(BF)
    acc[...] += dot(act, w_down[...], 1, 1)

    @pl.when(step == pl.num_programs(0) - 1)
    def _():
        normed, inv = normalize(mid[...] + (acc[...] + b_down[...]))
        normed_two[...] = normed
        inv_two[...] = inv
        result[...] = (normed * gain[1:2] + shift[1:2]).astype(BF)


def ffn_specs(tok, width, hidden):
    up = pl.BlockSpec((FC, width), lambda c, i: (c, 0))
    down = pl.BlockSpec((width, FC), lambda c, i: (0, c))
    wide = pl.BlockSpec((tok, FC), lambda c, i: (0, c))
    row = pl.BlockSpec((1, FC), lambda c, i: (0, c))
    return up, down, wide, row


def student_ffn(pref, pieces, x, w_out, w_up, w_down, b_out, b_up, b_down, gain, shift):
    tok, width = x.shape
    hidden = w_up.shape[0]
    up, down, wide, row = ffn_specs(tok, width, hidden)
    full, one = whole((tok, width)), whole((tok, 1))
    return call(
        student_kernel,
        pref,
        list(pieces) + [x, w_out, w_up, w_down, b_out, b_up, b_down, gain, shift],
        [whole(pieces[0].shape)] * 4
        + [full, whole(w_out.shape), up, down, whole((1, width)), row, whole((1, width))]
        + [whole((2, width))] * 2,
        [
            shape_of((width, tok), BF),
            shape_of((tok, width), BF),
            shape_of((tok, width), F32),
            shape_of((tok, 1), F32),
            shape_of((tok, hidden), BF),
            shape_of((tok, hidden), BF),
            shape_of((tok, width), BF),
            shape_of((tok, width), F32),
            shape_of((tok, 1), F32),
        ],
        [whole((width, tok)), full, full, one, wide, wide, full, full, one],
        (hidden // FC,),
        [pltpu.VMEM((tok, width), F32)] * 2,
        2 * tok * width * (2 * hidden + width),
        2 * tok * hidden,
    )


def teacher_kernel(
    pref, c0, c1, c2, c3, x, w_out, w_up, w_down, gain, shift, normed_two, inv_two,
    grad_sum, grad_ffn, vectors,
    ctx, acc, mid, act_one,
):
    step = pl.program_id(0)

    @pl.when(step == 0)
    def _():
        gather_ctx(pref[0], (c0, c1, c2, c3), ctx)
        res = x[...].astype(F32) + dot(ctx[...], w_out[...], 0, 1)
        normed, inv = normalize(res)
        mid[...] = normed
        act_one[...] = normed.astype(BF)
        acc[...] = jnp.zeros_like(acc)

    pre = dot(act_one[...], w_up[...], 1, 1)
    act = (pre * (0.5 * (1.0 + lax.erf(pre * 0.5**0.5)))).astype(BF)
    acc[...] += dot(act, w_down[...], 1, 1)

    @pl.when(step == pl.num_programs(0) - 1)
    def _():
        target, _unused = normalize(mid[...] + acc[...])
        normed = normed_two[...]
        diff = normed * gain[1:2] + shift[1:2] - target
        back = normalize_back(diff * gain[1:2], normed, inv_two[...])
        grad_sum[...] = back
        low = back.astype(BF)
        grad_ffn[...] = low
        vectors[0:1] = total_rows(diff * normed)
        vectors[1:2] = total_rows(diff)
        vectors[2:3] = total_rows(low.astype(F32))


def teacher_ffn(pref, pieces, x, w_out, w_up, w_down, gain, shift, normed_two, inv_two):
    tok, width = x.shape
    hidden = w_up.shape[0]
    up, down, wide, row = ffn_specs(tok, width, hidden)
    full, one = whole((tok, width)), whole((tok, 1))
    return call(
        teacher_kernel,
        pref,
        list(pieces) + [x, w_out, w_up, w_down, gain, shift, normed_two, inv_two],
        [whole(pieces[0].shape)] * 4
        + [full, whole(w_out.shape), up, down]
        + [whole((2, width))] * 2
        + [full, one],
        [shape_of((tok, width), F32), shape_of((tok, width), BF), shape_of((3, width), F32)],
        [full, full, whole((3, width))],
        (hidden // FC,),
        [pltpu.VMEM((width, tok), BF)]
        + [pltpu.VMEM((tok, width), F32)] * 2
        + [pltpu.VMEM((tok, width), BF)],
        2 * tok * width * (2 * hidden + width),
        tok * hidden,
    )


def back_kernel(
    pref, grad_ffn, slope, w_up, w_down, grad_sum, normed_one, inv_one, gain, shift, w_out,
    grad_hidden, grad_bias, grad_res, grad_attn, g0, g1, g2, g3, vectors,
    acc, ctx,
):
    step = pl.program_id(0)

    @pl.when(step == 0)
    def _():
        acc[...] = jnp.zeros_like(acc)

    low = (dot(grad_ffn[...], w_down[...], 1, 0) * slope[...].astype(F32)).astype(BF)
    grad_hidden[...] = low
    grad_bias[...] = total_rows(low.astype(F32))
    acc[...] += dot(low, w_up[...], 1, 0)

    @pl.when(step == pl.num_programs(0) - 1)
    def _():
        normed = normed_one[...]
        middle = normed * gain[0:1] + shift[0:1]
        grad = grad_sum[...] + jnp.where(jnp.abs(middle) < CLIP, acc[...], 0.0)
        back = normalize_back(grad * gain[0:1], normed, inv_one[...])
        grad_res[...] = back
        attn = back.astype(BF)
        grad_attn[...] = attn
        vectors[0:1] = total_rows(grad * normed)
        vectors[1:2] = total_rows(grad)
        vectors[2:3] = total_rows(attn.astype(F32))
        ctx[...] = dot(w_out[...], attn, 0, 1).astype(BF)
        rows = g0.shape[0]
        for j, ref in enumerate((g0, g1, g2, g3)):
            first = pl.multiple_of(xor(pref[0], j) * rows, 64)
            ref[...] = ctx[pl.ds(first, rows), :]


def student_back(pref, grad_ffn, slope, w_up, w_down, grad_sum, normed_one, inv_one, gain, shift, w_out):
    tok, width = grad_ffn.shape
    hidden = w_up.shape[0]
    up, down, wide, row = ffn_specs(tok, width, hidden)
    full, one = whole((tok, width)), whole((tok, 1))
    return call(
        back_kernel,
        pref,
        [grad_ffn, slope, w_up, w_down, grad_sum, normed_one, inv_one, gain, shift, w_out],
        [full, wide, up, down, full, full, one] + [whole((2, width))] * 2 + [whole(w_out.shape)],
        [
            shape_of((tok, hidden), BF),
            shape_of((1, hidden), F32),
            shape_of((tok, width), F32),
            shape_of((tok, width), BF),
        ]
        + [shape_of((width // 4, tok), BF)] * 4
        + [shape_of((3, width), F32)],
        [wide, row, full, full] + [whole((width // 4, tok))] * 4 + [whole((3, width))],
        (hidden // FC,),
        [pltpu.VMEM((tok, width), F32), pltpu.VMEM((width, tok), BF)],
        2 * tok * width * (2 * hidden + width),
    )


def weight_grad_kernel(
    pref, grad_ffn, gelu, grad_hidden, act_one, grad_attn, ctx, grad_down, grad_up, grad_out, turned
):
    @pl.when(pl.program_id(0) == 0)
    def _():
        turned[...] = grad_ffn[...].T
        value = dot(grad_attn[...], ctx[...], 0, 1).astype(BF)
        grad_out[...] = value.reshape(grad_out.shape)

    value = dot(turned[...], gelu[...], 1, 0).astype(BF)
    grad_down[...] = value.reshape(grad_down.shape)
    value = dot(grad_hidden[...], act_one[...], 0, 0).astype(BF)
    grad_up[...] = value.reshape(grad_up.shape)


def weight_grads(pref, grad_ffn, gelu, grad_hidden, act_one, grad_attn, ctx):
    tok, width = grad_ffn.shape
    hidden = gelu.shape[1]
    count, half = hidden // width, width // 2
    wide = pl.BlockSpec((tok, width), lambda c, i: (0, c))
    full = whole((tok, width))
    return call(
        weight_grad_kernel,
        pref,
        [grad_ffn, gelu, grad_hidden, act_one, grad_attn, ctx],
        [full, wide, wide, full, full, whole((width, tok))],
        [
            shape_of((2, count, half, width), BF),
            shape_of((2 * count, half, width), BF),
            shape_of((2, half, width), BF),
        ],
        [
            pl.BlockSpec((2, 1, half, width), lambda c, i: (0, c, 0, 0)),
            pl.BlockSpec((2, half, width), lambda c, i: (c, 0, 0)),
            whole((2, half, width)),
        ],
        (count,),
        [pltpu.VMEM((width, tok), BF)],
        2 * tok * width * (2 * hidden + width),
    )


def qkv_grad_kernel(pref, d0, d1, d2, d3, x0, x1, x2, x3, out, sums):
    own = pref[0]
    total = None
    count = None
    ones = jnp.ones((8, d0.shape[1]), BF)
    for grad, x in zip((d0, d1, d2, d3), (x0, x1, x2, x3)):
        value = grad[...]
        part = dot(value, jnp.clip(x[...], -CLIP, CLIP), 1, 0)
        line = dot(ones, value, 1, 1)
        total = part if total is None else total + part
        count = line if count is None else count + line
    out[...] = total.astype(BF)
    sums[...] = jnp.zeros_like(sums)
    rows = out.shape[0]
    for j in range(4):

        @pl.when(own == j)
        def _():
            sums[:, j * rows : (j + 1) * rows] = count


def qkv_grad(pref, grads, slots):
    tok, width = slots[0].shape
    rows = grads[0].shape[1]
    return call(
        qkv_grad_kernel,
        pref,
        list(grads) + list(slots),
        [pl.BlockSpec((None, rows, tok), lambda o, i: (o, 0, 0))] * 4 + [whole((tok, width))] * 4,
        [shape_of((3, rows, width), BF), shape_of((3, 8, width), F32)],
        [
            pl.BlockSpec((None, rows, width), lambda o, i: (o, 0, 0)),
            pl.BlockSpec((None, 8, width), lambda o, i: (o, 0, 0)),
        ],
        (3,),
        [],
        2 * 4 * tok * width * 3 * rows,
    )


def input_grad_kernel(pref, e0, e1, e2, e3, wq, wk, wv, grad_res, x, out, acc):
    slot = pl.program_id(0)

    @pl.when(slot == 0)
    def _():
        acc[...] = jnp.zeros_like(acc)

    for j, ref in enumerate((e0, e1, e2, e3)):

        @pl.when(slot == j)
        def _():
            part = dot(ref[0], wq[...], 0, 0)
            part = part + dot(ref[1], wk[...], 0, 0)
            acc[...] += part + dot(ref[2], wv[...], 0, 0)

    @pl.when(slot == 3)
    def _():
        size = jnp.abs(x[...].astype(F32))
        pull = jnp.where(size < CLIP, 1.0, jnp.where(size == CLIP, 0.5, 0.0))
        out[...] = (grad_res[...] + acc[...] * pull).astype(BF)


def input_grad(pref, pieces, weight, grad_res, x):
    tok, width = x.shape
    rows = pieces[0].shape[1]
    full = whole((tok, width))
    return call(
        input_grad_kernel,
        pref,
        list(pieces) + [weight] * 3 + [grad_res, x],
        [whole((3, rows, tok))] * 4
        + [
            pl.BlockSpec((rows, width), lambda j, i, o=o: (o * 4 + lax.bitwise_xor(i[0], j), 0))
            for o in range(3)
        ]
        + [full, full],
        shape_of((tok, width), BF),
        full,
        (4,),
        [pltpu.VMEM((tok, width), F32)],
        2 * 4 * tok * width * 3 * rows,
    )


def place(bit):
    name, mask = bit
    at = lax.axis_index(name)
    upper = lax.rem(lax.div(at, jnp.int32(mask)), jnp.int32(2))
    return upper, {name: at + mask * (1 - 2 * upper)}


class Copies:
    def __init__(self, send, recv, local):
        self.send, self.recv, self.local_sem = send, recv, local
        self.sent, self.planned, self.kept = [], 0, 0

    def plan(self, source, target, device):
        n = self.planned
        self.planned += 1
        return pltpu.make_async_remote_copy(
            src_ref=source,
            dst_ref=target,
            send_sem=self.send.at[n],
            recv_sem=self.recv.at[n],
            device_id=device,
            device_id_type=pl.DeviceIdType.MESH,
        )

    def remote(self, source, target, device):
        copy = self.plan(source, target, device)
        copy.start()
        self.sent.append(copy)
        return copy

    def plan_local(self, source, target):
        self.kept += 1
        return pltpu.make_async_copy(source, target, self.local_sem.at[self.kept - 1])

    def local(self, source, target):
        copy = self.plan_local(source, target)
        copy.start()
        return copy

    def finish(self):
        for copy in self.sent:
            copy.wait_send()


def window(ref, region):
    row, rows, col, cols = region
    return ref.at[pl.ds(row, rows), pl.ds(col, cols)]


def add_window(target, left, right, region, start):
    row, rows, col, cols = region
    step = 48 if rows % 48 == 0 else 16

    def body(i, carry):
        there = pl.ds(pl.multiple_of(row + i * step, 16), step)
        here = pl.ds(pl.multiple_of(start + i * step, 16), step)
        target[there, pl.ds(col, cols)] = left[there, pl.ds(col, cols)] + right[here, :cols]
        return carry

    lax.fori_loop(0, rows // step, body, 0)


def scatter_sum(copies, work, far, full, bits):
    rows, cols = work.shape
    region, used, parts = (0, rows, 0, cols), 0, []
    for n, bit in enumerate(bits):
        upper, device = place(bit)
        row, rows, col, cols = region
        if (rows // 2) % 16 == 0:
            rows //= 2
            kept = (pl.multiple_of(row + upper * rows, 16), rows, col, cols)
            sent = (pl.multiple_of(row + (1 - upper) * rows, 16), rows, col, cols)
        else:
            cols //= 2
            kept = (row, rows, pl.multiple_of(col + upper * cols, 128), cols)
            sent = (row, rows, pl.multiple_of(col + (1 - upper) * cols, 128), cols)
        slot = far.at[pl.ds(used, rows), pl.ds(0, cols)]
        copy = copies.remote(window(work, sent), slot, device)
        yield
        copy.wait_recv()
        add_window(full if n == len(bits) - 1 else work, work, far, kept, used)
        used += rows
        region = kept
        parts.append((bit, kept))
    return parts


def sum_flow(copies, own, other, work, near, far, full, result, core, bits):
    copy = copies.remote(other, near, place(core)[1])
    load = copies.local(own, work)
    yield
    copy.wait_recv()
    load.wait()
    add_window(work, work, near, (0, work.shape[0], 0, work.shape[1]), 0)
    parts = yield from scatter_sum(copies, work, far, full, bits)
    for bit, kept in reversed(parts):
        copy = copies.remote(window(full, kept), window(full, kept), place(bit)[1])
        yield
        copy.wait_recv()
    store = copies.local(full, result)
    yield
    store.wait()


def vector_flow(copies, sums, far, bits):
    for n, bit in enumerate(bits):
        yield
        copy = copies.remote(sums.at[n], far.at[n], place(bit)[1])
        yield
        copy.wait_recv()
        sums[n + 1] = sums[n] + far[n]


def remote_call(kernel, args, in_specs, outs, out_specs, scratch, copies, local, number, limit=VMEM_LIMIT):
    sems = pltpu.SemaphoreType.DMA
    return pl.pallas_call(
        kernel,
        in_specs=in_specs,
        out_specs=out_specs,
        out_shape=outs,
        scratch_shapes=scratch + [sems((copies,)), sems((copies,)), sems((local,))],
        compiler_params=pltpu.CompilerParams(
            vmem_limit_bytes=limit, collective_id=number, has_side_effects=True
        ),
        cost_estimate=pl.CostEstimate(flops=5 * 10**10, bytes_accessed=10**8, transcendentals=0),
    )(*args)


ANY = pl.BlockSpec(memory_space=pl.ANY)
IN_VMEM = pl.BlockSpec(memory_space=pltpu.VMEM)


def binarize_rows(source, target):
    rows, cols = target.shape
    step = 96 if cols < 2048 else 32

    def body(i, carry):
        at = pl.ds(pl.multiple_of(i * step, 16), step)
        value = source[at, :]
        scale = jnp.sum(jnp.abs(value), axis=1, keepdims=True) * (1.0 / cols)
        signed = jnp.where(value > 0, scale, jnp.where(value < 0, -scale, 0.0))
        target[at, :] = signed.astype(BF)
        return carry

    lax.fori_loop(0, rows // step, body, 0)


def entry_kernel(
    seq, core, hidden, teach, segments, l_qkv, l_out, l_up, l_down, t_qkv, t_out, t_up, t_down, bias,
    o_pref, o_qkv, x0, x1, x2, x3, o_teach, b_qkv, b_out, b_up, b_down, e_qkv, e_out, e_up, e_down,
    xs, held, w_qkv, w_out, w_up, w_down, f_qkv, f_out, f_up, f_down,
    s_qkv, s_out, s_up, s_down, proj, others, send, recv, local,
):
    tok, width = hidden.shape
    parts, size = 4, tok // 4
    along, next_chip = place(seq[0])
    side_of, sibling = place(core)
    half = lax.div(lax.axis_index("seq"), jnp.int32(2))
    stays = half == side_of
    moves = half != side_of
    partner = {"seq": 2 * side_of + along, "fsdp": half}
    mesh = pl.DeviceIdType.MESH

    barrier = pltpu.get_barrier_semaphore()
    for device in (next_chip, sibling):
        pl.semaphore_signal(barrier, inc=1, device_id=device, device_id_type=mesh)

    @pl.when(moves)
    def _():
        pl.semaphore_signal(barrier, inc=1, device_id=partner, device_id_type=mesh)
        pl.semaphore_wait(barrier, 3)

    @pl.when(stays)
    def _():
        pl.semaphore_wait(barrier, 2)

    copies = Copies(send, recv, local)
    cuts = [pl.ds(c * size, size) for c in range(parts)]
    swap = [copies.plan(hidden.at[cut], xs.at[0, cut], partner) for cut in cuts]
    load = [copies.plan_local(hidden.at[cut], xs.at[0, cut]) for cut in cuts]
    over = [copies.plan(xs.at[0, cut], xs.at[1, cut], next_chip) for cut in cuts]
    beside = [copies.plan(xs.at[0, cut], xs.at[2, cut], sibling) for cut in cuts]
    relay = [copies.plan(xs.at[1, cut], xs.at[3, cut], sibling) for cut in cuts]
    t_swap = [copies.plan(teach.at[cut], held.at[cut], partner) for cut in cuts]
    t_load = copies.plan_local(teach, held)
    seg_copy = copies.remote(segments, others, sibling)

    @pl.when(moves)
    def _():
        for copy in swap:
            copy.start()

    @pl.when(stays)
    def _():
        for copy in load:
            copy.start()
        t_load.start()

    latent = [
        (copies.local(source, target), target)
        for source, target in ((l_qkv, f_qkv), (l_out, f_out), (l_up, f_up), (l_down, f_down))
    ]
    staged = [
        (copies.local(source, target), target, result)
        for source, target, result in (
            (t_qkv, s_qkv, e_qkv),
            (t_out, s_out, e_out),
            (t_up, s_up, e_up),
            (t_down, s_down, e_down),
        )
    ]

    @pl.when(stays)
    def _():
        for c in range(parts):
            load[c].wait()
            over[c].start()
            beside[c].start()

    rows_qkv = l_qkv.shape[0]
    mine = w_qkv.at[pl.ds(pl.multiple_of(side_of * rows_qkv, 16), rows_qkv)]
    latent[0][0].wait()
    binarize_rows(f_qkv, mine)
    qkv_copy = copies.remote(mine, mine, sibling)
    stores, arrivals = [], []
    for (copy, source), target, result in zip(
        latent[1:], (w_out, w_up, w_down), (b_out, b_up, b_down)
    ):
        copy.wait()
        binarize_rows(source, target)
        arrivals.append(copies.remote(target, result.at[side_of], sibling))
        stores.append(copies.local(target, result.at[side_of]))
    for source, (_, _, result) in zip((t_qkv, t_out, t_up, t_down), staged):
        arrivals.append(copies.remote(source, result.at[side_of], sibling))
    for copy, target, result in staged:
        copy.wait()
        stores.append(copies.local(target, result.at[side_of]))

    @pl.when(moves)
    def _():
        for c in range(parts):
            swap[c].wait_recv()
            over[c].start()
            beside[c].start()
            t_swap[c].start()

    qkv_copy.wait_recv()
    stores.append(copies.local(w_qkv, b_qkv))
    rows = width // 4
    own = along + 2 * side_of

    row = lax.broadcasted_iota(jnp.int32, (AUG, tok), 0)
    ones = jnp.where(row < 3, 1.0, 0.0).astype(BF)
    shifts = []
    for part in range(2):
        line = bias[part : part + 1, 0:rows]
        for j in range(1, 4):
            line = jnp.where(own == j, bias[part : part + 1, j * rows : (j + 1) * rows], line)
        shifts.append(dot(thirds(line), ones, 0, 0))

    def project(slot):
        act = jnp.clip(xs[slot], -CLIP, CLIP)
        first = (1 - along if slot % 2 else along) + 2 * (1 - side_of if slot // 2 else side_of)
        there = pl.ds(pl.multiple_of(first * tok, 128), tok)
        for part in range(3):
            at = pl.multiple_of(part * width + own * rows, 16)
            value = dot(w_qkv[pl.ds(at, rows), :], act, 1, 1)
            if part != 1:
                value = value + shifts[part // 2]
            proj[part * rows : (part + 1) * rows, there] = value.astype(BF)
        stores.append(copies.local(proj.at[:, there], o_qkv.at[:, there]))
        stores.append(copies.local(xs.at[slot], (x0, x1, x2, x3)[slot]))

    seg_copy.wait_recv()
    counts = [jnp.sum(jnp.where(segments[...] == k, 1.0, 0.0)) for k in (1, 2, 3)]
    theirs = [jnp.sum(jnp.where(others[...] == k, 1.0, 0.0)) for k in (1, 2, 3)]
    first, second, third = [
        jnp.where(stays, a, b).astype(jnp.int32) for a, b in zip(counts, theirs)
    ]
    o_pref[0] = own
    o_pref[1] = jnp.where(first == LONG, 0, jnp.where(second == LONG, first, first + second))
    o_pref[2] = jnp.where(first == LONG, second, jnp.where(second == LONG, third, first))

    project(0)
    for copy in beside:
        copy.wait_recv()
    project(2)
    for c in range(parts):
        over[c].wait_recv()
        relay[c].start()
    project(1)
    for copy in relay:
        copy.wait_recv()
    project(3)

    @pl.when(moves)
    def _():
        for copy in t_swap:
            copy.wait_recv()

    @pl.when(stays)
    def _():
        t_load.wait()

    stores.append(copies.local(held, o_teach))
    for copy in arrivals:
        copy.wait_recv()
    for copy in stores:
        copy.wait()

    @pl.when(moves)
    def _():
        for copy in swap + t_swap:
            copy.wait_send()

    for copy in over + beside + relay:
        copy.wait_send()
    copies.finish()


def entry(seq, core, hidden, teach, segments, latents, teachers, bias):
    tok, width = hidden.shape
    halves = [w.shape for w in latents]
    sides = [shape_of((2,) + shape, BF) for shape in halves]
    own = [pltpu.VMEM(shape, BF) for shape in halves]
    sides[0] = shape_of((2 * halves[0][0], halves[0][1]), BF)
    sides_t = [shape_of((2,) + shape, BF) for shape in halves]
    outs = remote_call(
        lambda *refs: entry_kernel(seq, core, *refs),
        [hidden, teach, segments] + list(latents) + list(teachers) + [bias],
        [ANY] * 2 + [IN_VMEM] + [ANY] * 8 + [IN_VMEM],
        [shape_of((3,), jnp.int32), shape_of((3 * width // 4, 4 * tok), BF)]
        + [shape_of((tok, width), BF)] * 5
        + sides
        + sides_t,
        [pl.BlockSpec(memory_space=pltpu.SMEM)] + [ANY] * 14,
        [pltpu.VMEM((4, tok, width), BF), pltpu.VMEM((tok, width), BF)]
        + [pltpu.VMEM(sides[0].shape, BF)]
        + own[1:]
        + [pltpu.VMEM(shape, F32) for shape in halves]
        + own
        + [pltpu.VMEM((3 * width // 4, 4 * tok), BF), pltpu.VMEM(segments.shape, jnp.int32)],
        29,
        30,
        3,
    )
    pref, qkv, x0, x1, x2, x3, teach = outs[:7]
    weights = [w.reshape((-1, w.shape[-1])) for w in outs[7:]]
    return pref, qkv, (x0, x1, x2, x3), teach, weights[:4], weights[4:]


class Pump:
    def __init__(self):
        self.events, self.added = [], 0

    def add(self, time, flow, first, then, turn):
        gap = next(flow)
        self.events.append([time + (gap or 0.0), self.added, flow, 0, (first, then, turn)])
        self.added += 1

    def run(self, time=1e9):
        while self.events:
            event = min(self.events, key=lambda e: e[:2])
            if event[0] > time:
                return
            try:
                gap = next(event[2])
            except StopIteration:
                self.events.remove(event)
                continue
            event[3] += 1
            first, then, turn = event[4]
            if gap is None:
                gap = first if event[3] <= turn else then
            event[0] += gap


def head_flow(copies, n, gh, work, far, full, result, seq, core, dp):
    side_of, partner = place(core)
    along = place(seq[0])[0]
    if n == 1:
        copy = copies.remote(gh.at[2 - 2 * side_of], work, partner)
        yield
        copy.wait_recv()
    else:
        load = copies.local(gh.at[n // 2 + side_of], work)
        yield
        load.wait()
    turned, cut = HEAD_PLAN[n][:2]
    bits = (dp[::-1] if turned else dp) + seq[1:]
    mine = full.at[2 * n + along]
    parts = yield from scatter_sum(copies, work, far, mine, bits)
    steps = [(bit, kept, False) for bit, kept in reversed(parts)]
    cut = min(cut, len(steps))
    held = steps[cut][1] if cut < len(steps) else (0, mine.shape[0], 0, mine.shape[1])
    steps = steps[:cut] + [(seq[0], held, False)] + [(b, k, True) for b, k, _ in steps[cut:]]
    for bit, (row, size, col, cols), both in steps:
        first, count = (2 * n, 2) if both else (2 * n + along, 1)
        part = full.at[pl.ds(first, count), pl.ds(row, size), pl.ds(col, cols)]
        copy = copies.remote(part, part, place(bit)[1])
        yield
        copy.wait_recv()
    store = copies.local(full.at[pl.ds(2 * n, 2)], result.at[pl.ds(2 * n, 2)])
    yield
    store.wait()


def tail_kernel(
    dp, seq, core, scale, pref, down, up, out, two, one, bias,
    q_in, k_in, v_in, g0, g1, g2, g3, cf_in, lse, x0, x1, x2, x3, w_in, res_in,
    down_sum, up_sum, out_sum, totals, qkv_sum, hidden_out,
    work, near, far, full, sums, sums_far, gh, h_work, h_far, h_full,
    qs, ks, vs, gp, cf, xs, weight, res, qa, ka, va, ga, gs, dqs, dks, dvs, dn, er, acc, hid,
    send, recv, local,
):
    shift, border = pref[1], pref[2]
    heads_all, total = qs.shape
    hdim = qa.shape[0] - AUG
    heads = heads_all // hdim
    tok = total // 4
    width = xs.shape[2]
    cont, others = total - PROMPT, PROMPT + LONG
    back = lax.rem(cont - shift, cont)
    along, next_chip = place(seq[0])
    side_of, sibling = place(core)
    across = {**next_chip, **sibling}
    half = lax.div(lax.axis_index("seq"), jnp.int32(2))
    stays, moves = half == side_of, half != side_of
    partner = {"seq": 2 * side_of + along, "fsdp": half}
    own = along + 2 * side_of

    def place_of(slot):
        return (1 - along if slot % 2 else along) + 2 * (1 - side_of if slot // 2 else side_of)

    copies = Copies(send, recv, local)
    first_loads = [
        copies.local(source, target)
        for source, target in (
            (g0, gp.at[0]), (g1, gp.at[1]), (g2, gp.at[2]), (g3, gp.at[3]),
            (q_in, qs), (k_in, ks), (v_in, vs), (cf_in, cf),
        )
    ]

    mesh = pl.DeviceIdType.MESH
    barrier = pltpu.get_barrier_semaphore()
    friends = [place(bit)[1] for bit in dp + seq] + [sibling, across]
    for device in friends:
        pl.semaphore_signal(barrier, inc=1, device_id=device, device_id_type=mesh)

    @pl.when(moves)
    def _():
        pl.semaphore_signal(barrier, inc=1, device_id=partner, device_id_type=mesh)
        pl.semaphore_wait(barrier, len(friends) + 1)

    @pl.when(stays)
    def _():
        pl.semaphore_wait(barrier, len(friends))

    pump = Pump()
    count, rows_half = down.shape[1:3]
    ups = [(up.at[side_of, p], up.at[1 - side_of, p], up_sum.at[p]) for p in range(count)]
    downs = [
        (
            down.at[side_of, p],
            down.at[1 - side_of, p],
            down_sum.at[:, pl.ds(p * width, width)],
        )
        for p in range(count)
    ]
    queue = ups + downs + [(out.at[side_of], out.at[1 - side_of], out_sum)]
    near_bits = dp + seq[:1]
    orders = [tuple(near_bits[i] for i in order) for order in ORDERS]
    for n, (mine, theirs, result) in enumerate(queue):
        order, time, first, then = PIECE_PLAN[n % len(PIECE_PLAN)]
        bits = list(orders[order]) + seq[1:]
        flow = sum_flow(
            copies, mine, theirs, work.at[n], near.at[n], far.at[n], full.at[n], result, core, bits
        )
        pump.add(time, flow, first, then, 1 + len(bits))

    late_loads = [
        copies.local(source, target)
        for source, target in (
            (x0, xs.at[0]), (x1, xs.at[1]), (x2, xs.at[2]), (x3, xs.at[3]),
            (w_in, weight), (res_in, res),
        )
    ]
    for copy in first_loads:
        copy.wait()

    row = lax.broadcasted_iota(jnp.int32, (AUG, total), 0)
    ones = jnp.where(row < 3, 1.0, 0.0).astype(BF)
    ka[hdim:, :] = ones
    va[hdim:, :] = ones
    clock = 1.0
    pieces = {1: [], 2: [], 3: []}
    devices = {1: next_chip, 2: sibling, 3: across}
    for h in range(heads):
        lines = slice(h * hdim, (h + 1) * hdim)
        for j in range(4):
            gs[:, pl.ds(pl.multiple_of(place_of(j) * tok, 128), tok)] = gp[j, lines, :].astype(F32)
        qa[:hdim, :] = qs[lines, :]
        ka[:hdim, :] = ks[lines, :]
        va[:hdim, :] = vs[lines, :]
        grad = roll_cont(gs[...], back)
        ga[:hdim, :] = grad.astype(BF)
        ga[hdim:, :] = thirds(-jnp.sum(grad * cf[lines, :], axis=0, keepdims=True))
        qa[hdim:, :] = thirds(lse[h] * (-1.0 / scale))
        seen = set()
        for start, parts in block_list(total, QB):
            queries = slice(start, start + QB)
            grad_q = None
            for lo, hi in parts:
                for key in range(lo, hi, KB):
                    keys = slice(key, key + KB)
                    value = dot(qa[:, queries], ka[:, keys], 0, 0) * scale
                    if lo >= others:
                        mask = same_segment((QB, KB), 1, key - others, start - others, border)
                        value = jnp.where(mask, value, -1e30)
                    prob = jnp.exp2(value)
                    grad_p = dot(ga[:, queries], va[:, keys], 0, 0)
                    grad_s = (prob * grad_p).astype(BF)
                    grad_v = dot(ga[:hdim, queries], prob.astype(BF), 1, 0)
                    grad_k = dot(qa[:hdim, queries], grad_s, 1, 0)
                    part = dot(ka[:hdim, keys], grad_s, 1, 1)
                    grad_q = part if grad_q is None else grad_q + part
                    if key in seen:
                        dvs[:, keys] += grad_v
                        dks[:, keys] += grad_k
                    else:
                        dvs[:, keys] = grad_v
                        dks[:, keys] = grad_k
                        seen.add(key)
                    clock += 0.65
            dqs[:, queries] = grad_q
            pump.run(clock)
        inv = 1.0 / hdim**0.5
        for part, (ref, factor) in enumerate(((dqs, inv), (dks, inv), (dvs, 1.0))):
            gs[...] = roll_cont(ref[...] * factor, shift)
            for j in range(4):
                there = pl.ds(pl.multiple_of(place_of(j) * tok, 128), tok)
                dn[j, part, lines, :] = gs[:, there].astype(BF)
        for j in (1, 3, 2):
            at = pl.ds(h * hdim, hdim)
            copy = copies.remote(dn.at[j, :, at, :], er.at[j - 1, :, at, :], devices[j])
            pieces[j].append(copy)
        clock += 1.5
        pump.run(clock)

    for copy in late_loads:
        copy.wait()
    rows = width // 4
    one_rows = jnp.ones((8, tok), BF)
    counts = []
    for o in range(3):
        value, line = None, None
        for j in range(4):
            part = dot(dn[j, o], jnp.clip(xs[j], -CLIP, CLIP), 1, 0)
            ends = dot(one_rows, dn[j, o], 1, 1)
            value = part if value is None else value + part
            line = ends if line is None else line + ends
        gh[o] = value.astype(BF)
        counts.append(line)
        clock += 2.7
        pump.run(clock)
    sums[0] = jnp.zeros(sums.shape[1:], F32)
    for j in range(4):

        @pl.when(own == j)
        def _():
            sums[0, 0:1, j * rows : (j + 1) * rows] = counts[0][0:1]
            sums[0, 1:2, j * rows : (j + 1) * rows] = counts[2][0:1]

    sums[0, 2:3] = one[2:3]
    sums[0, 3:4] = two[2:3]
    sums[0, 4:5] = one[0:1]
    sums[0, 5:6] = two[0:1]
    sums[0, 6:7] = one[1:2]
    sums[0, 7:8] = two[1:2]
    for p in range(count):
        sums[0, 8 + p : 9 + p] = bias[:, p * width : (p + 1) * width]

    swap = copies.plan(hid, hidden_out, partner)
    keep = copies.plan_local(hid, hidden_out)

    def hidden_flow():
        yield 0.0
        gaps = HIDDEN_PLAN[1]
        for gap, j in zip(gaps, (0, 2, 1, 3)):
            for copy in pieces.get(j, []):
                copy.wait_recv()
            part = None
            for o in range(3):
                at = pl.multiple_of(o * width + place_of(j) * rows, 16)
                source = dn[0, o] if j == 0 else er[j - 1, o]
                piece = dot(source, weight[pl.ds(at, rows), :], 0, 0)
                part = piece if part is None else part + piece
            if j == 0:
                acc[...] = part
            elif j != 3:
                acc[...] += part
            else:
                size = jnp.abs(xs[0].astype(F32))
                pull = jnp.where(size < CLIP, 1.0, jnp.where(size == CLIP, 0.5, 0.0))
                hid[...] = (res[...] + (acc[...] + part) * pull).astype(BF)
            if j != 3:
                yield gap

        @pl.when(moves)
        def _():
            swap.start()

        @pl.when(stays)
        def _():
            keep.start()

        yield gaps[3]

        @pl.when(moves)
        def _():
            swap.wait_recv()
            swap.wait_send()

        @pl.when(stays)
        def _():
            keep.wait()

    pump.add(clock + HIDDEN_PLAN[0], hidden_flow(), 0.0, 0.0, 0)
    for n in (0, 2, 1):
        flow = head_flow(
            copies, n, gh, h_work.at[n], h_far.at[n], h_full, qkv_sum, seq, core, dp
        )
        time, first, then = HEAD_PLAN[n][2:]
        pump.add(clock + time, flow, first, then, 4)
    time, gap = VECTOR_PLAN
    pump.add(clock + time, vector_flow(copies, sums, sums_far, [core] + dp + seq), gap, gap, 0)
    pump.run()
    totals[...] = sums[sums.shape[0] - 1]
    copies.finish()


def tail(
    dp, seq, core, pref, down, up, out, two, one, bias, rolled, grads, cf, lse, slots, weight, res
):
    sides, count, half, width = down.shape
    pieces, steps, lines = 2 * count + 1, len(dp) + len(seq), 16
    rows, total = rolled[0].shape
    tok = total // 4
    heads = HEADS // 4
    hdim = rows // heads
    scale = LOG2E / hdim**0.5
    smem = pl.BlockSpec(memory_space=pltpu.SMEM)
    return remote_call(
        lambda *refs: tail_kernel(dp, seq, core, scale, *refs),
        [pref, down, up, out, two, one, bias]
        + list(rolled)
        + list(grads)
        + [cf, lse]
        + list(slots)
        + [weight, res],
        [smem] + [ANY] * 3 + [IN_VMEM] * 3 + [ANY] * 8 + [IN_VMEM] + [ANY] * 6,
        [
            shape_of((half, count * width), BF),
            shape_of((count, half, width), BF),
            shape_of((half, width), BF),
            shape_of((lines, width), F32),
            shape_of((6, rows, width), BF),
            shape_of((tok, width), BF),
        ],
        [ANY] * 3 + [IN_VMEM] + [ANY] * 2,
        [pltpu.VMEM((pieces, half, width), BF)] * 4
        + [pltpu.VMEM((steps + 2, lines, width), F32), pltpu.VMEM((steps + 1, lines, width), F32)]
        + [pltpu.VMEM((3, rows, width), BF)] * 3
        + [pltpu.VMEM((6, rows, width), BF)]
        + [pltpu.VMEM((rows, total), BF)] * 3
        + [pltpu.VMEM((4, rows, tok), BF), pltpu.VMEM((rows, total), F32)]
        + [pltpu.VMEM((4, tok, width), BF), pltpu.VMEM(weight.shape, BF)]
        + [pltpu.VMEM((tok, width), F32)]
        + [pltpu.VMEM((hdim + AUG, total), BF)] * 4
        + [pltpu.VMEM((hdim, total), F32)] * 4
        + [pltpu.VMEM((4, 3, rows, tok), BF), pltpu.VMEM((3, 3, rows, tok), BF)]
        + [pltpu.VMEM((tok, width), F32), pltpu.VMEM((tok, width), BF)],
        pieces * (1 + 2 * steps) + steps + 1 + 3 * heads + 1 + 3 * (2 * steps - 1) + 1,
        2 * pieces + 14 + 1 + 5,
        4,
        TAIL_LIMIT,
    )


def widen_kernel(*refs):
    half = len(refs) // 2
    for source, target in zip(refs[:half], refs[half:]):
        target[...] = source[...].astype(F32)


def widen(values, steps):
    specs = [pl.BlockSpec((v.shape[0] // steps, v.shape[1]), lambda i: (i, 0)) for v in values]
    return pl.pallas_call(
        widen_kernel,
        grid=(steps,),
        in_specs=specs,
        out_specs=specs,
        out_shape=[shape_of(v.shape, F32) for v in values],
        compiler_params=pltpu.CompilerParams(vmem_limit_bytes=VMEM_LIMIT),
        cost_estimate=pl.CostEstimate(
            flops=0, bytes_accessed=6 * sum(v.size for v in values), transcendentals=0
        ),
    )(*values)


def binarize(latent):
    row_scale = jnp.mean(jnp.abs(latent), axis=1, keepdims=True)
    return (row_scale * jnp.sign(latent)).astype(BF)


def segment_info(segments):
    sizes_of = [jnp.sum((segments == k).astype(jnp.int32)) for k in (1, 2, 3)]
    first, second, third = sizes_of
    shift = jnp.where(first == LONG, 0, jnp.where(second == LONG, first, first + second))
    border = jnp.where(first == LONG, second, jnp.where(second == LONG, third, first))
    return jnp.stack([shift, border])


def quarters(own):
    along = to_slot(own, 1)
    return (own, along, to_slot(own, 2), to_slot(along, 2))


def exchange(pieces):
    return (pieces[0],) + tuple(to_slot(pieces[j], j) for j in (1, 2, 3))


def on_device(
    hidden, teacher_hidden, segments, latent_qkv, latent_out, latent_up, latent_down,
    biases, up_bias, norm_gains, norm_shifts, teacher_qkv, teacher_out, teacher_up, teacher_down,
):
    seq_at, fsdp_at = lax.axis_index("seq"), lax.axis_index("fsdp")
    fsdp = lax.axis_size("fsdp")
    core = fsdp_at % 2
    own = (seq_at % 2 + 2 * core).astype(jnp.int32)
    width = hidden.shape[2]

    latents = (latent_qkv, latent_out, latent_up, latent_down)
    teachers = (teacher_qkv, teacher_out, teacher_up, teacher_down)
    if fsdp == 2:
        pref, qkv, x_slots, teach, bins, t_weights = entry(
            bit_list("seq"), bit_list("fsdp")[0], hidden[0], teacher_hidden[0], segments,
            latents, teachers, biases,
        )
        x = x_slots[0]
    else:
        info = segment_info(segments)
        info = jnp.where(core == seq_at // 2, info, flip(info, fsdp=1))
        pref = jnp.concatenate([own[None], info]).astype(jnp.int32)
        x = swap_groups(hidden[0])
        x_slots = quarters(x)
        bins = [gather_rows(binarize(w)) for w in latents]
        teach = swap_groups(teacher_hidden[0])
        t_weights = [gather_rows(w) for w in teachers]
        qkv = qkv_project(pref, x_slots, bins[0], biases[:2].reshape(2, width, 1))
    bin_qkv, bin_out, bin_up, bin_down = bins
    t_qkv, t_out, t_up, t_down = t_weights
    t_along, t_beside = to_slot(teach, 1), to_slot(teach, 2)
    *ctx_slots, ctx_full, lse, q_roll, k_roll, v_roll = attention(pref, qkv, True)
    t_along, ctx_slots = lax.optimization_barrier((t_along, ctx_slots))
    t_slots = (teach, t_along, t_beside, to_slot(t_along, 2))
    ctx_pieces = exchange(ctx_slots)

    t_heads = qkv_project(pref, t_slots, t_qkv, None)
    *tctx_slots, _unused, _unused_too = attention(pref, t_heads, False)
    tctx_slots, ctx_pieces = lax.optimization_barrier((tctx_slots, ctx_pieces))
    tctx_pieces = exchange(tctx_slots)

    gain, shift = norm_gains, norm_shifts
    (
        ctx, act_one, normed_one, inv_one, gelu, slope, result, normed_two, inv_two,
    ) = student_ffn(
        pref, ctx_pieces, x, bin_out, bin_up, bin_down,
        biases[2:3], up_bias[None], biases[3:4], gain, shift,
    )
    student_out = swap_groups(result)
    grad_sum, grad_ffn, vec_two = teacher_ffn(
        pref, tctx_pieces, teach, t_out, t_up, t_down, gain, shift, normed_two, inv_two
    )
    grad_hidden, grad_up_bias, grad_res, grad_attn, *gctx_slots, vec_one = student_back(
        pref, grad_ffn, slope, bin_up, bin_down, grad_sum, normed_one, inv_one, gain, shift, bin_out
    )
    gctx_pieces = exchange(gctx_slots)
    grad_down, grad_up, grad_out = weight_grads(
        pref, grad_ffn, gelu, grad_hidden, act_one, grad_attn, ctx
    )
    dp_bits, seq_bits, fsdp_bits = bit_list("dp"), bit_list("seq"), bit_list("fsdp")
    rows, hidden_units = width // 4, up_bias.shape[0]

    if fsdp == 2:
        total_down, total_up, total_out, vectors, total_qkv, hidden_grad = tail(
            dp_bits, seq_bits, fsdp_bits[0], pref,
            grad_down, grad_up.reshape(grad_down.shape), grad_out, vec_two, vec_one, grad_up_bias,
            (q_roll, k_roll, v_roll), gctx_pieces, ctx_full, lse, x_slots, bin_qkv, grad_res,
        )
        total_up = total_up.reshape(-1, width)
        total_qkv = total_qkv.reshape(-1, width)
        total_qkv, total_out, total_up, total_down = widen(
            (total_qkv, total_out, total_up, total_down), 6
        )
    else:
        dqkv_slots = attention_back(pref, qkv, gctx_pieces, ctx_full, lse)
        dqkv_pieces = exchange(dqkv_slots)
        grad_heads, head_sums = qkv_grad(pref, dqkv_slots, x_slots)
        hidden_grad = swap_groups(input_grad(pref, dqkv_pieces, bin_qkv, grad_res, x))

        def reduce_grad(value, bits):
            for bit in reversed(fsdp_bits):
                value = halve(value, bit)
            return all_reduce(value, bits)

        grad_down = grad_down.transpose(0, 2, 1, 3).reshape(width, hidden_units)
        total_down = reduce_grad(grad_down, dp_bits + seq_bits)
        total_up = reduce_grad(grad_up.reshape(hidden_units, width), dp_bits[::-1] + seq_bits)
        total_out = reduce_grad(
            grad_out.reshape(width, width), seq_bits[:1] + dp_bits + seq_bits[1:]
        )
        blocks = all_reduce(
            grad_heads.reshape(3 * rows, width), dp_bits + seq_bits[1:] + fsdp_bits[1:]
        )
        blocks = blocks.reshape(1, 3, rows, width)
        blocks = double(double(blocks, seq_bits[0]), fsdp_bits[0])
        whole_qkv = blocks.transpose(1, 0, 2, 3).reshape(3 * width, width)
        part = 3 * width // fsdp
        total_qkv = lax.dynamic_slice_in_dim(whole_qkv, fsdp_at * part, part, 0)
        vectors = jnp.concatenate(
            [
                head_sums[0, :1],
                head_sums[2, :1],
                vec_one[2:3],
                vec_two[2:3],
                vec_one[0:1],
                vec_two[0:1],
                vec_one[1:2],
                vec_two[1:2],
                grad_up_bias.reshape(-1, width),
            ]
        )
        vectors = sum_small(vectors, dp_bits + seq_bits + fsdp_bits)
    hid_bias = vectors[8 : 8 + hidden_units // width].reshape(-1)
    share, hid_share = width // fsdp, hid_bias.shape[0] // fsdp
    cols = lax.dynamic_slice_in_dim(vectors[:8], fsdp_at * share, share, 1)
    return (
        student_out[None],
        hidden_grad[None],
        total_qkv.astype(F32),
        total_out.astype(F32),
        total_up.astype(F32),
        total_down.astype(F32),
        cols[0:4],
        lax.dynamic_slice_in_dim(hid_bias, fsdp_at * hid_share, hid_share, 0),
        cols[4:6],
        cols[6:8],
    )


def solution(mesh):
    tokens = P(("dp", "fsdp"), "seq", None)
    rows = P("fsdp", None)
    return jax.shard_map(
        on_device,
        mesh=mesh,
        in_specs=(tokens, tokens, P(("dp", "fsdp"), None)) + (rows,) * 4 + (P(),) * 4 + (rows,) * 4,
        out_specs=(tokens, tokens)
        + (rows,) * 4
        + (P(None, "fsdp"), P("fsdp"), P(None, "fsdp"), P(None, "fsdp")),
        check_vma=False,
    )
```
